128 devices in a mesh: dp: 8 (over y, x_lo), mp: 16 (over x_hi, z, core).
Axes of the slice: x: 4 (x_hi: 2, x_lo: 2; x = x_hi * 2 + x_lo), y: 4, z: 4, core: 2. Of those that a mesh axis runs over, the one named last changes fastest.
Arguments:
- hidden_states: bfloat16 [4096, 4096], P('dp', 'mp'), may hold values from -6 to 6
- gate_online: bfloat16 [4096, 14336], P('dp', 'mp'), may hold values from -0.09375 to 0.09375
- up_online: bfloat16 [4096, 14336], P('dp', 'mp'), may hold values from -0.09375 to 0.09375
- down_online: bfloat16 [14336, 4096], P('mp', 'dp'), may hold values from -0.046875 to 0.046875
- gate_previous: bfloat16 [4096, 14336], P(None, 'mp'), may hold values from -0.09375 to 0.09375
- up_previous: bfloat16 [4096, 14336], P(None, 'mp'), may hold values from -0.09375 to 0.09375
- down_previous: bfloat16 [14336, 4096], P('mp'), may hold values from -0.046875 to 0.046875
Outputs:
- online_output: bfloat16 [4096, 4096], P('dp', 'mp')
- target_output: bfloat16 [4096, 4096], P('dp', 'mp')
The draws below stay inside these ranges and needn't reach their ends.
All inputs are finite; a program needn't handle non-finite values.
Results may differ from the reference program's by a relative error of at most 0.0072.
Values may be sent and summed in bfloat16 or wider, within the bound.
A program may use at most 128 MiB of HBM per device.

```python
import jax
import jax.numpy as jnp

D = 4096
FF = 14336
TOKENS = 4096


def levels(rng, shape, split, least, largest):
    def one(dim, blocks):
        steps = jax.random.uniform(jax.random.fold_in(jax.random.fold_in(rng, 6), dim), (blocks,), jnp.float32, least / len(split), largest / len(split))
        return jnp.repeat(jnp.exp(steps), shape[dim] // blocks).reshape((-1,) + (1,) * (len(shape) - dim - 1))

    loudness = one(*split[0])
    for cut in split[1:]:
        loudness = loudness * one(*cut)
    return loudness


def scatter_about(own_key, extent, width, limit, split=(), kind=jnp.bfloat16):
    values = jax.random.normal(own_key, extent, jnp.float32) * width
    if len(split) > 0:
        values = levels(own_key, extent, split, -0.22, 0.18) * values
    return jnp.clip(values, min=-limit, max=limit).astype(kind)


def setup_inputs(seed: int = 0) -> dict:
    splits = jax.random.split(jax.random.key(seed), 8)
    hidden_states = scatter_about(splits[0], (TOKENS, D), 1.0, 6.0, ((0, 8), (1, 16)))
    gate_online = scatter_about(splits[1], (D, FF), D ** -0.5, 0.09375, ((0, 8), (1, 16)))
    up_online = scatter_about(splits[2], (D, FF), D ** -0.5, 0.09375, ((0, 8), (1, 16)))
    down_online = scatter_about(splits[3], (FF, D), FF ** -0.5, 0.046875, ((0, 16), (1, 8)))
    gate_previous = scatter_about(splits[4], (D, FF), D ** -0.5, 0.09375, ((1, 16),))
    up_previous = scatter_about(splits[5], (D, FF), D ** -0.5, 0.09375, ((1, 16),))
    down_previous = scatter_about(splits[6], (FF, D), FF ** -0.5, 0.046875, ((0, 16),))
    return {"hidden_states": hidden_states, "gate_online": gate_online, "up_online": up_online, "down_online": down_online, "gate_previous": gate_previous, "up_previous": up_previous, "down_previous": down_previous}


POLYAK = 0.25


def blend(online, previous):
    return (POLYAK * online.astype(jnp.float32) + (1.0 - POLYAK) * previous.astype(jnp.float32)).astype(jnp.bfloat16)


def forward(inputs, gate_weight, up_weight, down_weight):
    gate = jnp.dot(inputs, gate_weight, preferred_element_type=jnp.float32)
    up_part = jnp.dot(inputs, up_weight, preferred_element_type=jnp.float32)
    inner = (jax.nn.silu(gate) * up_part).astype(jnp.bfloat16)
    return jnp.dot(inner, down_weight, preferred_element_type=jnp.float32).astype(jnp.bfloat16)


def reference(hidden_states, gate_online, up_online, down_online, gate_previous, up_previous, down_previous):
    online_output = forward(hidden_states, gate_online, up_online, down_online)
    target_output = forward(hidden_states, blend(gate_online, gate_previous), blend(up_online, up_previous), blend(down_online, down_previous))
    return online_output, target_output
```

```python
import functools

import jax
import jax.numpy as jnp
from jax import lax
from jax.experimental import pallas as pl
from jax.experimental.pallas import tpu as pltpu
from jax.sharding import PartitionSpec as P

POLYAK = 0.25
MESH = pl.DeviceIdType.MESH


def blend(online, previous):
    return (
        POLYAK * online.astype(jnp.float32) + (1.0 - POLYAK) * previous.astype(jnp.float32)
    ).astype(jnp.bfloat16)


def gather_kernel(ndp, nmp, h_ref, g_ref, u_ref, dn_ref, hf_ref, gf_ref, uf_ref, df_ref,
                  send_sem, recv_sem, local_sem):
    d = lax.axis_index("dp")
    m = lax.axis_index("mp")
    kr = g_ref.shape[0]
    dc = dn_ref.shape[1]
    hc = h_ref.shape[1]
    rows = pl.ds(pl.multiple_of(d * kr, kr), kr)
    cols = pl.ds(pl.multiple_of(d * dc, dc), dc)
    hcols = pl.ds(pl.multiple_of(m * hc, hc), hc)

    locals_ = [
        pltpu.make_async_copy(h_ref, hf_ref.at[:, hcols], local_sem.at[0]),
        pltpu.make_async_copy(g_ref, gf_ref.at[rows], local_sem.at[1]),
        pltpu.make_async_copy(u_ref, uf_ref.at[rows], local_sem.at[2]),
        pltpu.make_async_copy(dn_ref, df_ref.at[:, cols], local_sem.at[3]),
    ]
    for c in locals_:
        c.start()

    copies = []
    k = 0
    for s in range(1, ndp):
        peer = lax.rem(d + s, ndp)
        for src, dst in ((g_ref, gf_ref.at[rows]), (u_ref, uf_ref.at[rows]),
                         (dn_ref, df_ref.at[:, cols])):
            copies.append(pltpu.make_async_remote_copy(
                src_ref=src, dst_ref=dst, send_sem=send_sem.at[k], recv_sem=recv_sem.at[k],
                device_id=(peer, m), device_id_type=MESH))
            k += 1
    for s in range(1, nmp):
        peer = lax.rem(m + s, nmp)
        copies.append(pltpu.make_async_remote_copy(
            src_ref=h_ref, dst_ref=hf_ref.at[:, hcols], send_sem=send_sem.at[k],
            recv_sem=recv_sem.at[k], device_id=(d, peer), device_id_type=MESH))
        k += 1
    for c in copies:
        c.start()
    for c in locals_:
        c.wait()
    for c in copies:
        c.wait()


def gather_all(h, g, u, dn, ndp, nmp):
    n_copies = 3 * (ndp - 1) + (nmp - 1)
    any_spec = pl.BlockSpec(memory_space=pl.ANY)
    out_shape = (
        jax.ShapeDtypeStruct((h.shape[0], h.shape[1] * nmp), h.dtype),
        jax.ShapeDtypeStruct((g.shape[0] * ndp, g.shape[1]), g.dtype),
        jax.ShapeDtypeStruct((u.shape[0] * ndp, u.shape[1]), u.dtype),
        jax.ShapeDtypeStruct((dn.shape[0], dn.shape[1] * ndp), dn.dtype),
    )
    return pl.pallas_call(
        functools.partial(gather_kernel, ndp, nmp),
        out_shape=out_shape,
        in_specs=[any_spec] * 4,
        out_specs=[any_spec] * 4,
        scratch_shapes=[
            pltpu.SemaphoreType.DMA((n_copies,)),
            pltpu.SemaphoreType.DMA((n_copies,)),
            pltpu.SemaphoreType.DMA((4,)),
        ],
        compiler_params=pltpu.CompilerParams(has_side_effects=True),
    )(h, g, u, dn)


def local(ndp, nmp, hidden_states, gate_online, up_online, down_online, gate_previous,
          up_previous, down_previous):
    features_all, gate_full, up_full, down_full = gather_all(
        hidden_states, gate_online, up_online, down_online, ndp, nmp)

    def pair(piece, previous):
        target_piece = blend(piece, previous)
        o = jnp.dot(features_all, piece, preferred_element_type=jnp.float32)
        t = jnp.dot(features_all, target_piece, preferred_element_type=jnp.float32)
        return o, t

    gate_o, gate_t = pair(gate_full, gate_previous)
    up_o, up_t = pair(up_full, up_previous)
    inner_o = (jax.nn.silu(gate_o) * up_o).astype(jnp.bfloat16)
    inner_t = (jax.nn.silu(gate_t) * up_t).astype(jnp.bfloat16)
    target_down = blend(down_full, down_previous)
    online_part = jnp.dot(inner_o, down_full, preferred_element_type=jnp.float32)
    target_part = jnp.dot(inner_t, target_down, preferred_element_type=jnp.float32)
    terms = jnp.stack([online_part, target_part], axis=0)
    summed = lax.psum_scatter(terms, "mp", scatter_dimension=2, tiled=True)
    result = summed.astype(jnp.bfloat16)
    return (result[0], result[1])


def solution(mesh):
    ndp = mesh.shape["dp"]
    nmp = mesh.shape["mp"]
    in_specs = (
        P("dp", "mp"),
        P("dp", "mp"),
        P("dp", "mp"),
        P("mp", "dp"),
        P(None, "mp"),
        P(None, "mp"),
        P("mp", None),
    )
    out_specs = (P("dp", "mp"), P("dp", "mp"))
    return jax.shard_map(functools.partial(local, ndp, nmp), mesh=mesh, in_specs=in_specs,
                         out_specs=out_specs, check_vma=False)
```

```python
import functools

import jax
import jax.numpy as jnp
from jax import lax
from jax.experimental import pallas as pl
from jax.experimental.pallas import tpu as pltpu
from jax.sharding import PartitionSpec as P

POLYAK = 0.25
MESH = pl.DeviceIdType.MESH


def blend(online, previous):
    return (
        POLYAK * online.astype(jnp.float32) + (1.0 - POLYAK) * previous.astype(jnp.float32)
    ).astype(jnp.bfloat16)


def gather_kernel(ndp, nmp, h_ref, g_ref, u_ref, dn_ref, hf_ref, gf_ref, uf_ref, df_ref,
                  send_sem, recv_sem, local_sem):
    d = lax.axis_index("dp")
    m = lax.axis_index("mp")
    kr = g_ref.shape[0]
    dc = dn_ref.shape[1]
    hc = h_ref.shape[1]
    rows = pl.ds(pl.multiple_of(d * kr, kr), kr)
    cols = pl.ds(pl.multiple_of(d * dc, dc), dc)
    hcols = pl.ds(pl.multiple_of(m * hc, hc), hc)

    locals_ = [
        pltpu.make_async_copy(h_ref, hf_ref.at[:, hcols], local_sem.at[0]),
        pltpu.make_async_copy(g_ref, gf_ref.at[rows], local_sem.at[1]),
        pltpu.make_async_copy(u_ref, uf_ref.at[rows], local_sem.at[2]),
        pltpu.make_async_copy(dn_ref, df_ref.at[:, cols], local_sem.at[3]),
    ]
    for c in locals_:
        c.start()

    copies = []
    k = 0
    for s in range(1, ndp):
        peer = lax.rem(d + s, ndp)
        for src, dst in ((g_ref, gf_ref.at[rows]), (u_ref, uf_ref.at[rows]),
                         (dn_ref, df_ref.at[:, cols])):
            copies.append(pltpu.make_async_remote_copy(
                src_ref=src, dst_ref=dst, send_sem=send_sem.at[k], recv_sem=recv_sem.at[k],
                device_id=(peer, m), device_id_type=MESH))
            k += 1
    for s in range(1, nmp):
        peer = lax.rem(m + s, nmp)
        copies.append(pltpu.make_async_remote_copy(
            src_ref=h_ref, dst_ref=hf_ref.at[:, hcols], send_sem=send_sem.at[k],
            recv_sem=recv_sem.at[k], device_id=(d, peer), device_id_type=MESH))
        k += 1
    for c in copies:
        c.start()
    for c in locals_:
        c.wait()
    for c in copies:
        c.wait()


def gather_all(h, g, u, dn, ndp, nmp):
    n_copies = 3 * (ndp - 1) + (nmp - 1)
    any_spec = pl.BlockSpec(memory_space=pl.ANY)
    out_shape = (
        jax.ShapeDtypeStruct((h.shape[0], h.shape[1] * nmp), h.dtype),
        jax.ShapeDtypeStruct((g.shape[0] * ndp, g.shape[1]), g.dtype),
        jax.ShapeDtypeStruct((u.shape[0] * ndp, u.shape[1]), u.dtype),
        jax.ShapeDtypeStruct((dn.shape[0], dn.shape[1] * ndp), dn.dtype),
    )
    return pl.pallas_call(
        functools.partial(gather_kernel, ndp, nmp),
        out_shape=out_shape,
        in_specs=[any_spec] * 4,
        out_specs=[any_spec] * 4,
        scratch_shapes=[
            pltpu.SemaphoreType.DMA((n_copies,)),
            pltpu.SemaphoreType.DMA((n_copies,)),
            pltpu.SemaphoreType.DMA((4,)),
        ],
        compiler_params=pltpu.CompilerParams(has_side_effects=True),
    )(h, g, u, dn)


def reduce_kernel(nmp, t_ref, o_ref, buf, send_sem, recv_sem, local_sem):
    d = lax.axis_index("dp")
    m = lax.axis_index("mp")
    w = o_ref.shape[2]
    mine = pl.ds(pl.multiple_of(m * w, w), w)
    local_copy = pltpu.make_async_copy(t_ref.at[:, :, mine], buf.at[0], local_sem.at[0])
    local_copy.start()
    copies = []
    for s in range(1, nmp):
        peer = lax.rem(m + s, nmp)
        theirs = pl.ds(pl.multiple_of(peer * w, w), w)
        copies.append(pltpu.make_async_remote_copy(
            src_ref=t_ref.at[:, :, theirs], dst_ref=buf.at[s], send_sem=send_sem.at[s],
            recv_sem=recv_sem.at[s], device_id=(d, peer), device_id_type=MESH))
    for c in copies:
        c.start()
    local_copy.wait()
    for c in copies:
        c.wait()
    rows = 32

    def body(i, carry):
        r = pl.ds(pl.multiple_of(i * rows, rows), rows)
        for k in range(o_ref.shape[0]):
            acc = buf[0, k, r, :].astype(jnp.float32)
            for s in range(1, nmp):
                acc = acc + buf[s, k, r, :].astype(jnp.float32)
            o_ref[k, r, :] = acc.astype(o_ref.dtype)
        return carry

    lax.fori_loop(0, o_ref.shape[1] // rows, body, 0)


def reduce_scatter(terms, nmp):
    n, t, width = terms.shape
    w = width // nmp
    return pl.pallas_call(
        functools.partial(reduce_kernel, nmp),
        out_shape=jax.ShapeDtypeStruct((n, t, w), jnp.bfloat16),
        in_specs=[pl.BlockSpec(memory_space=pl.ANY)],
        out_specs=pl.BlockSpec(memory_space=pltpu.VMEM),
        scratch_shapes=[
            pltpu.VMEM((nmp, n, t, w), jnp.bfloat16),
            pltpu.SemaphoreType.DMA((nmp,)),
            pltpu.SemaphoreType.DMA((nmp,)),
            pltpu.SemaphoreType.DMA((1,)),
        ],
        compiler_params=pltpu.CompilerParams(has_side_effects=True,
                                             vmem_limit_bytes=48 * 1024 * 1024),
    )(terms)


def local(ndp, nmp, hidden_states, gate_online, up_online, down_online, gate_previous,
          up_previous, down_previous):
    features_all, gate_full, up_full, down_full = gather_all(
        hidden_states, gate_online, up_online, down_online, ndp, nmp)

    def pair(piece, previous):
        target_piece = blend(piece, previous)
        o = jnp.dot(features_all, piece, preferred_element_type=jnp.float32)
        t = jnp.dot(features_all, target_piece, preferred_element_type=jnp.float32)
        return o, t

    gate_o, gate_t = pair(gate_full, gate_previous)
    up_o, up_t = pair(up_full, up_previous)
    inner_o = (jax.nn.silu(gate_o) * up_o).astype(jnp.bfloat16)
    inner_t = (jax.nn.silu(gate_t) * up_t).astype(jnp.bfloat16)
    target_down = blend(down_full, down_previous)
    online_part = jnp.dot(inner_o, down_full, preferred_element_type=jnp.float32)
    target_part = jnp.dot(inner_t, target_down, preferred_element_type=jnp.float32)
    terms = jnp.stack([online_part, target_part], axis=0).astype(jnp.bfloat16)
    result = reduce_scatter(terms, nmp)
    return (result[0], result[1])


def solution(mesh):
    ndp = mesh.shape["dp"]
    nmp = mesh.shape["mp"]
    in_specs = (
        P("dp", "mp"),
        P("dp", "mp"),
        P("dp", "mp"),
        P("mp", "dp"),
        P(None, "mp"),
        P(None, "mp"),
        P("mp", None),
    )
    out_specs = (P("dp", "mp"), P("dp", "mp"))
    return jax.shard_map(functools.partial(local, ndp, nmp), mesh=mesh, in_specs=in_specs,
                         out_specs=out_specs, check_vma=False)
```

```python
import functools

import jax
import jax.numpy as jnp
from jax import lax
from jax.experimental import pallas as pl
from jax.experimental.pallas import tpu as pltpu
from jax.sharding import PartitionSpec as P

POLYAK = 0.25
MESH = pl.DeviceIdType.MESH


def blend(online, previous):
    return (
        POLYAK * online.astype(jnp.float32) + (1.0 - POLYAK) * previous.astype(jnp.float32)
    ).astype(jnp.bfloat16)


def gather_kernel(ndp, g_ref, u_ref, dn_ref, gf_ref, uf_ref, df_ref, send_sem, recv_sem,
                  local_sem):
    d = lax.axis_index("dp")
    m = lax.axis_index("mp")
    kr = g_ref.shape[0]
    dc = dn_ref.shape[1]
    rows = pl.ds(pl.multiple_of(d * kr, kr), kr)
    cols = pl.ds(pl.multiple_of(d * dc, dc), dc)

    locals_ = [
        pltpu.make_async_copy(g_ref, gf_ref.at[rows], local_sem.at[0]),
        pltpu.make_async_copy(u_ref, uf_ref.at[rows], local_sem.at[1]),
        pltpu.make_async_copy(dn_ref, df_ref.at[:, cols], local_sem.at[2]),
    ]
    for c in locals_:
        c.start()

    copies = []
    k = 0
    for s in range(1, ndp):
        peer = lax.rem(d + s, ndp)
        for src, dst in ((g_ref, gf_ref.at[rows]), (u_ref, uf_ref.at[rows]),
                         (dn_ref, df_ref.at[:, cols])):
            copies.append(pltpu.make_async_remote_copy(
                src_ref=src, dst_ref=dst, send_sem=send_sem.at[k], recv_sem=recv_sem.at[k],
                device_id=(peer, m), device_id_type=MESH))
            k += 1
    for c in copies:
        c.start()
    for c in locals_:
        c.wait()
    for c in copies:
        c.wait()


def gather_weights(g, u, dn, ndp):
    n_copies = 3 * (ndp - 1)
    any_spec = pl.BlockSpec(memory_space=pl.ANY)
    out_shape = (
        jax.ShapeDtypeStruct((g.shape[0] * ndp, g.shape[1]), g.dtype),
        jax.ShapeDtypeStruct((u.shape[0] * ndp, u.shape[1]), u.dtype),
        jax.ShapeDtypeStruct((dn.shape[0], dn.shape[1] * ndp), dn.dtype),
    )
    return pl.pallas_call(
        functools.partial(gather_kernel, ndp),
        out_shape=out_shape,
        in_specs=[any_spec] * 3,
        out_specs=[any_spec] * 3,
        scratch_shapes=[
            pltpu.SemaphoreType.DMA((n_copies,)),
            pltpu.SemaphoreType.DMA((n_copies,)),
            pltpu.SemaphoreType.DMA((3,)),
        ],
        compiler_params=pltpu.CompilerParams(has_side_effects=True),
    )(g, u, dn)


def reduce_kernel(nmp, t_ref, o_ref, buf, send_sem, recv_sem, local_sem):
    d = lax.axis_index("dp")
    m = lax.axis_index("mp")
    w = o_ref.shape[2]
    mine = pl.ds(pl.multiple_of(m * w, w), w)
    local_copy = pltpu.make_async_copy(t_ref.at[:, :, mine], buf.at[0], local_sem.at[0])
    local_copy.start()
    copies = []
    for s in range(1, nmp):
        peer = lax.rem(m + s, nmp)
        theirs = pl.ds(pl.multiple_of(peer * w, w), w)
        copies.append(pltpu.make_async_remote_copy(
            src_ref=t_ref.at[:, :, theirs], dst_ref=buf.at[s], send_sem=send_sem.at[s],
            recv_sem=recv_sem.at[s], device_id=(d, peer), device_id_type=MESH))
    for c in copies:
        c.start()
    local_copy.wait()
    for c in copies:
        c.wait()
    rows = 32

    def body(i, carry):
        r = pl.ds(pl.multiple_of(i * rows, rows), rows)
        for k in range(o_ref.shape[0]):
            acc = buf[0, k, r, :].astype(jnp.float32)
            for s in range(1, nmp):
                acc = acc + buf[s, k, r, :].astype(jnp.float32)
            o_ref[k, r, :] = acc.astype(o_ref.dtype)
        return carry

    lax.fori_loop(0, o_ref.shape[1] // rows, body, 0)


def reduce_scatter(terms, nmp):
    n, t, width = terms.shape
    w = width // nmp
    return pl.pallas_call(
        functools.partial(reduce_kernel, nmp),
        out_shape=jax.ShapeDtypeStruct((n, t, w), jnp.bfloat16),
        in_specs=[pl.BlockSpec(memory_space=pl.ANY)],
        out_specs=pl.BlockSpec(memory_space=pltpu.VMEM),
        scratch_shapes=[
            pltpu.VMEM((nmp, n, t, w), jnp.bfloat16),
            pltpu.SemaphoreType.DMA((nmp,)),
            pltpu.SemaphoreType.DMA((nmp,)),
            pltpu.SemaphoreType.DMA((1,)),
        ],
        compiler_params=pltpu.CompilerParams(has_side_effects=True,
                                             vmem_limit_bytes=48 * 1024 * 1024),
    )(terms)


def local(ndp, nmp, hidden_states, gate_online, up_online, down_online, gate_previous,
          up_previous, down_previous):
    features_all = lax.all_gather(hidden_states, "mp", axis=1, tiled=True)
    gate_full, up_full, down_full = gather_weights(gate_online, up_online, down_online, ndp)

    def pair(piece, previous):
        target_piece = blend(piece, previous)
        o = jnp.dot(features_all, piece, preferred_element_type=jnp.float32)
        t = jnp.dot(features_all, target_piece, preferred_element_type=jnp.float32)
        return o, t

    gate_o, gate_t = pair(gate_full, gate_previous)
    up_o, up_t = pair(up_full, up_previous)
    inner_o = (jax.nn.silu(gate_o) * up_o).astype(jnp.bfloat16)
    inner_t = (jax.nn.silu(gate_t) * up_t).astype(jnp.bfloat16)
    target_down = blend(down_full, down_previous)
    online_part = jnp.dot(inner_o, down_full, preferred_element_type=jnp.float32)
    target_part = jnp.dot(inner_t, target_down, preferred_element_type=jnp.float32)
    online_out = lax.psum_scatter(online_part, "mp", scatter_dimension=1, tiled=True)
    target_out = reduce_scatter(target_part.astype(jnp.bfloat16)[None], nmp)
    return (online_out.astype(jnp.bfloat16), target_out[0])


def solution(mesh):
    ndp = mesh.shape["dp"]
    nmp = mesh.shape["mp"]
    in_specs = (
        P("dp", "mp"),
        P("dp", "mp"),
        P("dp", "mp"),
        P("mp", "dp"),
        P(None, "mp"),
        P(None, "mp"),
        P("mp", None),
    )
    out_specs = (P("dp", "mp"), P("dp", "mp"))
    return jax.shard_map(functools.partial(local, ndp, nmp), mesh=mesh, in_specs=in_specs,
                         out_specs=out_specs, check_vma=False)
```

```python
import functools

import jax
import jax.numpy as jnp
from jax import lax
from jax.experimental import pallas as pl
from jax.experimental.pallas import tpu as pltpu
from jax.sharding import PartitionSpec as P

POLYAK = 0.25
MESH = pl.DeviceIdType.MESH


def blend(online, previous):
    return (
        POLYAK * online.astype(jnp.float32) + (1.0 - POLYAK) * previous.astype(jnp.float32)
    ).astype(jnp.bfloat16)


def gather_kernel(ndp, g_ref, u_ref, gf_ref, uf_ref, send_sem, recv_sem, local_sem):
    d = lax.axis_index("dp")
    m = lax.axis_index("mp")
    kr = g_ref.shape[0]
    rows = pl.ds(pl.multiple_of(d * kr, kr), kr)

    locals_ = [
        pltpu.make_async_copy(g_ref, gf_ref.at[rows], local_sem.at[0]),
        pltpu.make_async_copy(u_ref, uf_ref.at[rows], local_sem.at[1]),
    ]
    for c in locals_:
        c.start()

    copies = []
    k = 0
    for s in range(1, ndp):
        peer = lax.rem(d + s, ndp)
        for src, dst in ((g_ref, gf_ref.at[rows]), (u_ref, uf_ref.at[rows])):
            copies.append(pltpu.make_async_remote_copy(
                src_ref=src, dst_ref=dst, send_sem=send_sem.at[k], recv_sem=recv_sem.at[k],
                device_id=(peer, m), device_id_type=MESH))
            k += 1
    for c in copies:
        c.start()
    for c in locals_:
        c.wait()
    for c in copies:
        c.wait()


def gather_weights(g, u, ndp):
    n_copies = 2 * (ndp - 1)
    any_spec = pl.BlockSpec(memory_space=pl.ANY)
    out_shape = (
        jax.ShapeDtypeStruct((g.shape[0] * ndp, g.shape[1]), g.dtype),
        jax.ShapeDtypeStruct((u.shape[0] * ndp, u.shape[1]), u.dtype),
    )
    return pl.pallas_call(
        functools.partial(gather_kernel, ndp),
        out_shape=out_shape,
        in_specs=[any_spec] * 2,
        out_specs=[any_spec] * 2,
        scratch_shapes=[
            pltpu.SemaphoreType.DMA((n_copies,)),
            pltpu.SemaphoreType.DMA((n_copies,)),
            pltpu.SemaphoreType.DMA((2,)),
        ],
        compiler_params=pltpu.CompilerParams(has_side_effects=True),
    )(g, u)


def reduce_kernel(nmp, t_ref, o_ref, buf, send_sem, recv_sem, local_sem):
    d = lax.axis_index("dp")
    m = lax.axis_index("mp")
    w = o_ref.shape[2]
    mine = pl.ds(pl.multiple_of(m * w, w), w)
    local_copy = pltpu.make_async_copy(t_ref.at[:, :, mine], buf.at[0], local_sem.at[0])
    local_copy.start()
    copies = []
    for s in range(1, nmp):
        peer = lax.rem(m + s, nmp)
        theirs = pl.ds(pl.multiple_of(peer * w, w), w)
        copies.append(pltpu.make_async_remote_copy(
            src_ref=t_ref.at[:, :, theirs], dst_ref=buf.at[s], send_sem=send_sem.at[s],
            recv_sem=recv_sem.at[s], device_id=(d, peer), device_id_type=MESH))
    for c in copies:
        c.start()
    local_copy.wait()
    for c in copies:
        c.wait()
    rows = 32

    def body(i, carry):
        r = pl.ds(pl.multiple_of(i * rows, rows), rows)
        for k in range(o_ref.shape[0]):
            acc = buf[0, k, r, :].astype(jnp.float32)
            for s in range(1, nmp):
                acc = acc + buf[s, k, r, :].astype(jnp.float32)
            o_ref[k, r, :] = acc.astype(o_ref.dtype)
        return carry

    lax.fori_loop(0, o_ref.shape[1] // rows, body, 0)


def reduce_scatter(terms, nmp):
    n, t, width = terms.shape
    w = width // nmp
    return pl.pallas_call(
        functools.partial(reduce_kernel, nmp),
        out_shape=jax.ShapeDtypeStruct((n, t, w), jnp.bfloat16),
        in_specs=[pl.BlockSpec(memory_space=pl.ANY)],
        out_specs=pl.BlockSpec(memory_space=pltpu.VMEM),
        scratch_shapes=[
            pltpu.VMEM((nmp, n, t, w), jnp.bfloat16),
            pltpu.SemaphoreType.DMA((nmp,)),
            pltpu.SemaphoreType.DMA((nmp,)),
            pltpu.SemaphoreType.DMA((1,)),
        ],
        compiler_params=pltpu.CompilerParams(has_side_effects=True,
                                             vmem_limit_bytes=48 * 1024 * 1024),
    )(terms)


def local(ndp, nmp, hidden_states, gate_online, up_online, down_online, gate_previous,
          up_previous, down_previous):
    features_all = lax.all_gather(hidden_states, "mp", axis=1, tiled=True)
    down_full = lax.all_gather(down_online, "dp", axis=1, tiled=True)
    gate_full, up_full = gather_weights(gate_online, up_online, ndp)

    def pair(piece, previous):
        target_piece = blend(piece, previous)
        o = jnp.dot(features_all, piece, preferred_element_type=jnp.float32)
        t = jnp.dot(features_all, target_piece, preferred_element_type=jnp.float32)
        return o, t

    gate_o, gate_t = pair(gate_full, gate_previous)
    up_o, up_t = pair(up_full, up_previous)
    inner_o = (jax.nn.silu(gate_o) * up_o).astype(jnp.bfloat16)
    inner_t = (jax.nn.silu(gate_t) * up_t).astype(jnp.bfloat16)
    target_down = blend(down_full, down_previous)
    online_part = jnp.dot(inner_o, down_full, preferred_element_type=jnp.float32)
    target_part = jnp.dot(inner_t, target_down, preferred_element_type=jnp.float32)
    online_out = lax.psum_scatter(online_part, "mp", scatter_dimension=1, tiled=True)
    target_out = reduce_scatter(target_part.astype(jnp.bfloat16)[None], nmp)
    return (online_out.astype(jnp.bfloat16), target_out[0])


def solution(mesh):
    ndp = mesh.shape["dp"]
    nmp = mesh.shape["mp"]
    in_specs = (
        P("dp", "mp"),
        P("dp", "mp"),
        P("dp", "mp"),
        P("mp", "dp"),
        P(None, "mp"),
        P(None, "mp"),
        P("mp", None),
    )
    out_specs = (P("dp", "mp"), P("dp", "mp"))
    return jax.shard_map(functools.partial(local, ndp, nmp), mesh=mesh, in_specs=in_specs,
                         out_specs=out_specs, check_vma=False)
```

```python
import functools

import jax
import jax.numpy as jnp
from jax import lax
from jax.experimental import pallas as pl
from jax.experimental.pallas import tpu as pltpu
from jax.sharding import PartitionSpec as P

POLYAK = 0.25
MESH = pl.DeviceIdType.MESH


def blend(online, previous):
    return (
        POLYAK * online.astype(jnp.float32) + (1.0 - POLYAK) * previous.astype(jnp.float32)
    ).astype(jnp.bfloat16)


def gather_kernel(ndp, g_ref, u_ref, dn_ref, gf_ref, uf_ref, df_ref, send_sem, recv_sem,
                  local_sem):
    d = lax.axis_index("dp")
    m = lax.axis_index("mp")
    kr = g_ref.shape[0]
    dc = dn_ref.shape[1]
    rows = pl.ds(pl.multiple_of(d * kr, kr), kr)
    cols = pl.ds(pl.multiple_of(d * dc, dc), dc)

    locals_ = [
        pltpu.make_async_copy(g_ref, gf_ref.at[rows], local_sem.at[0]),
        pltpu.make_async_copy(u_ref, uf_ref.at[rows], local_sem.at[1]),
        pltpu.make_async_copy(dn_ref, df_ref.at[:, cols], local_sem.at[2]),
    ]
    for c in locals_:
        c.start()

    copies = []
    k = 0
    for s in range(1, ndp):
        peer = lax.rem(d + s, ndp)
        for src, dst in ((g_ref, gf_ref.at[rows]), (u_ref, uf_ref.at[rows]),
                         (dn_ref, df_ref.at[:, cols])):
            copies.append(pltpu.make_async_remote_copy(
                src_ref=src, dst_ref=dst, send_sem=send_sem.at[k], recv_sem=recv_sem.at[k],
                device_id=(peer, m), device_id_type=MESH))
            k += 1
    for c in copies:
        c.start()
    for c in locals_:
        c.wait()
    for c in copies:
        c.wait()


def gather_weights_direct(g, u, dn, ndp):
    n_copies = 3 * (ndp - 1)
    any_spec = pl.BlockSpec(memory_space=pl.ANY)
    out_shape = (
        jax.ShapeDtypeStruct((g.shape[0] * ndp, g.shape[1]), g.dtype),
        jax.ShapeDtypeStruct((u.shape[0] * ndp, u.shape[1]), u.dtype),
        jax.ShapeDtypeStruct((dn.shape[0], dn.shape[1] * ndp), dn.dtype),
    )
    return pl.pallas_call(
        functools.partial(gather_kernel, ndp),
        out_shape=out_shape,
        in_specs=[any_spec] * 3,
        out_specs=[any_spec] * 3,
        scratch_shapes=[
            pltpu.SemaphoreType.DMA((n_copies,)),
            pltpu.SemaphoreType.DMA((n_copies,)),
            pltpu.SemaphoreType.DMA((3,)),
        ],
        compiler_params=pltpu.CompilerParams(has_side_effects=True),
    )(g, u, dn)


def relay_gather_kernel(g_ref, u_ref, dn_ref, gf_ref, uf_ref, df_ref, send_sem, recv_sem,
                        local_sem):
    ndp = 8
    d = lax.axis_index("dp")
    m = lax.axis_index("mp")
    lo = d % 2
    partner = d - lo + (1 - lo)
    nxt = (d + 2) % ndp
    prv = (d + ndp - 2) % ndp
    far = (d + 4) % ndp
    owns = (g_ref, u_ref, dn_ref)
    fulls = (gf_ref, uf_ref, df_ref)

    def slot(w, idx, half=None):
        if w < 2:
            kr = owns[w].shape[0]
            if half is None:
                return fulls[w].at[pl.ds(pl.multiple_of(idx * kr, kr), kr)]
            hk = kr // 2
            return fulls[w].at[pl.ds(pl.multiple_of(idx * kr + half * hk, hk), hk)]
        rr, dc = owns[w].shape
        cols = pl.ds(pl.multiple_of(idx * dc, dc), dc)
        if half is None:
            return fulls[w].at[:, cols]
        hr = rr // 2
        return fulls[w].at[pl.ds(half * hr, hr), cols]

    def rc(w, k, src, dst, target):
        i = w * 8 + k
        return pltpu.make_async_remote_copy(
            src_ref=src, dst_ref=dst, send_sem=send_sem.at[i], recv_sem=recv_sem.at[i],
            device_id=(target, m), device_id_type=MESH)

    locals_ = [pltpu.make_async_copy(owns[w], slot(w, d), local_sem.at[w]) for w in range(3)]
    c = {}
    for w in range(3):
        c[w, 0] = rc(w, 0, owns[w], slot(w, d), partner)
        c[w, 1] = rc(w, 1, owns[w], slot(w, d), nxt)
        c[w, 2] = rc(w, 2, owns[w], slot(w, d), prv)
        c[w, 3] = rc(w, 3, slot(w, partner), slot(w, partner), nxt)
        c[w, 4] = rc(w, 4, slot(w, partner), slot(w, partner), prv)
        c[w, 5] = rc(w, 5, slot(w, prv, 0), slot(w, prv, 0), nxt)
        c[w, 6] = rc(w, 6, slot(w, nxt, 1), slot(w, nxt, 1), prv)
        c[w, 7] = rc(w, 7, slot(w, far), slot(w, far), partner)
    for w in range(3):
        locals_[w].start()
        for k in range(3):
            c[w, k].start()
    for w in range(3):
        c[w, 0].wait_recv()
        c[w, 3].start()
        c[w, 4].start()
        c[w, 1].wait_recv()
        c[w, 5].start()
        c[w, 2].wait_recv()
        c[w, 6].start()
    for w in range(3):
        c[w, 5].wait_recv()
        c[w, 6].wait_recv()
        c[w, 7].start()
    for w in range(3):
        for k in (3, 4, 7):
            c[w, k].wait_recv()
    for w in range(3):
        for k in range(8):
            c[w, k].wait_send()
        locals_[w].wait()


def gather_weights(g, u, dn, ndp):
    if ndp != 8:
        return gather_weights_direct(g, u, dn, ndp)
    any_spec = pl.BlockSpec(memory_space=pl.ANY)
    out_shape = (
        jax.ShapeDtypeStruct((g.shape[0] * ndp, g.shape[1]), g.dtype),
        jax.ShapeDtypeStruct((u.shape[0] * ndp, u.shape[1]), u.dtype),
        jax.ShapeDtypeStruct((dn.shape[0], dn.shape[1] * ndp), dn.dtype),
    )
    return pl.pallas_call(
        relay_gather_kernel,
        out_shape=out_shape,
        in_specs=[any_spec] * 3,
        out_specs=[any_spec] * 3,
        scratch_shapes=[
            pltpu.SemaphoreType.DMA((24,)),
            pltpu.SemaphoreType.DMA((24,)),
            pltpu.SemaphoreType.DMA((3,)),
        ],
        compiler_params=pltpu.CompilerParams(has_side_effects=True),
    )(g, u, dn)


def reduce_kernel(nmp, t_ref, o_ref, buf, send_sem, recv_sem, local_sem):
    d = lax.axis_index("dp")
    m = lax.axis_index("mp")
    w = o_ref.shape[2]
    mine = pl.ds(pl.multiple_of(m * w, w), w)
    local_copy = pltpu.make_async_copy(t_ref.at[:, :, mine], buf.at[0], local_sem.at[0])
    local_copy.start()
    copies = []
    for s in range(1, nmp):
        peer = lax.rem(m + s, nmp)
        theirs = pl.ds(pl.multiple_of(peer * w, w), w)
        copies.append(pltpu.make_async_remote_copy(
            src_ref=t_ref.at[:, :, theirs], dst_ref=buf.at[s], send_sem=send_sem.at[s],
            recv_sem=recv_sem.at[s], device_id=(d, peer), device_id_type=MESH))
    for c in copies:
        c.start()
    local_copy.wait()
    for c in copies:
        c.wait()
    rows = 32

    def body(i, carry):
        r = pl.ds(pl.multiple_of(i * rows, rows), rows)
        for k in range(o_ref.shape[0]):
            acc = buf[0, k, r, :].astype(jnp.float32)
            for s in range(1, nmp):
                acc = acc + buf[s, k, r, :].astype(jnp.float32)
            o_ref[k, r, :] = acc.astype(o_ref.dtype)
        return carry

    lax.fori_loop(0, o_ref.shape[1] // rows, body, 0)


def reduce_scatter(terms, nmp):
    n, t, width = terms.shape
    w = width // nmp
    return pl.pallas_call(
        functools.partial(reduce_kernel, nmp),
        out_shape=jax.ShapeDtypeStruct((n, t, w), jnp.bfloat16),
        in_specs=[pl.BlockSpec(memory_space=pl.ANY)],
        out_specs=pl.BlockSpec(memory_space=pltpu.VMEM),
        scratch_shapes=[
            pltpu.VMEM((nmp, n, t, w), jnp.bfloat16),
            pltpu.SemaphoreType.DMA((nmp,)),
            pltpu.SemaphoreType.DMA((nmp,)),
            pltpu.SemaphoreType.DMA((1,)),
        ],
        compiler_params=pltpu.CompilerParams(has_side_effects=True,
                                             vmem_limit_bytes=48 * 1024 * 1024),
    )(terms)


def local(ndp, nmp, hidden_states, gate_online, up_online, down_online, gate_previous,
          up_previous, down_previous):
    features_all = lax.all_gather(hidden_states, "mp", axis=1, tiled=True)
    gate_full, up_full, down_full = gather_weights(gate_online, up_online, down_online, ndp)

    def pair(piece, previous):
        target_piece = blend(piece, previous)
        o = jnp.dot(features_all, piece, preferred_element_type=jnp.float32)
        t = jnp.dot(features_all, target_piece, preferred_element_type=jnp.float32)
        return o, t

    gate_o, gate_t = pair(gate_full, gate_previous)
    up_o, up_t = pair(up_full, up_previous)
    inner_o = (jax.nn.silu(gate_o) * up_o).astype(jnp.bfloat16)
    inner_t = (jax.nn.silu(gate_t) * up_t).astype(jnp.bfloat16)
    target_down = blend(down_full, down_previous)
    online_part = jnp.dot(inner_o, down_full, preferred_element_type=jnp.float32)
    target_part = jnp.dot(inner_t, target_down, preferred_element_type=jnp.float32)
    online_out = lax.psum_scatter(online_part, "mp", scatter_dimension=1, tiled=True)
    target_out = reduce_scatter(target_part.astype(jnp.bfloat16)[None], nmp)
    return (online_out.astype(jnp.bfloat16), target_out[0])


def solution(mesh):
    ndp = mesh.shape["dp"]
    nmp = mesh.shape["mp"]
    in_specs = (
        P("dp", "mp"),
        P("dp", "mp"),
        P("dp", "mp"),
        P("mp", "dp"),
        P(None, "mp"),
        P(None, "mp"),
        P("mp", None),
    )
    out_specs = (P("dp", "mp"), P("dp", "mp"))
    return jax.shard_map(functools.partial(local, ndp, nmp), mesh=mesh, in_specs=in_specs,
                         out_specs=out_specs, check_vma=False)
```

```python
import functools

import jax
import jax.numpy as jnp
from jax import lax
from jax.experimental import pallas as pl
from jax.experimental.pallas import tpu as pltpu
from jax.sharding import PartitionSpec as P

POLYAK = 0.25
MESH = pl.DeviceIdType.MESH


def blend(online, previous):
    return (
        POLYAK * online.astype(jnp.float32) + (1.0 - POLYAK) * previous.astype(jnp.float32)
    ).astype(jnp.bfloat16)


def gather_kernel(ndp, g_ref, u_ref, dn_ref, gf_ref, uf_ref, df_ref, send_sem, recv_sem,
                  local_sem):
    d = lax.axis_index("dp")
    m = lax.axis_index("mp")
    kr = g_ref.shape[0]
    dc = dn_ref.shape[1]
    rows = pl.ds(pl.multiple_of(d * kr, kr), kr)
    cols = pl.ds(pl.multiple_of(d * dc, dc), dc)

    locals_ = [
        pltpu.make_async_copy(g_ref, gf_ref.at[rows], local_sem.at[0]),
        pltpu.make_async_copy(u_ref, uf_ref.at[rows], local_sem.at[1]),
        pltpu.make_async_copy(dn_ref, df_ref.at[:, cols], local_sem.at[2]),
    ]
    for c in locals_:
        c.start()

    copies = []
    k = 0
    for s in range(1, ndp):
        peer = lax.rem(d + s, ndp)
        for src, dst in ((g_ref, gf_ref.at[rows]), (u_ref, uf_ref.at[rows]),
                         (dn_ref, df_ref.at[:, cols])):
            copies.append(pltpu.make_async_remote_copy(
                src_ref=src, dst_ref=dst, send_sem=send_sem.at[k], recv_sem=recv_sem.at[k],
                device_id=(peer, m), device_id_type=MESH))
            k += 1
    for c in copies:
        c.start()
    for c in locals_:
        c.wait()
    for c in copies:
        c.wait()


def gather_weights_direct(g, u, dn, ndp):
    n_copies = 3 * (ndp - 1)
    any_spec = pl.BlockSpec(memory_space=pl.ANY)
    out_shape = (
        jax.ShapeDtypeStruct((g.shape[0] * ndp, g.shape[1]), g.dtype),
        jax.ShapeDtypeStruct((u.shape[0] * ndp, u.shape[1]), u.dtype),
        jax.ShapeDtypeStruct((dn.shape[0], dn.shape[1] * ndp), dn.dtype),
    )
    return pl.pallas_call(
        functools.partial(gather_kernel, ndp),
        out_shape=out_shape,
        in_specs=[any_spec] * 3,
        out_specs=[any_spec] * 3,
        scratch_shapes=[
            pltpu.SemaphoreType.DMA((n_copies,)),
            pltpu.SemaphoreType.DMA((n_copies,)),
            pltpu.SemaphoreType.DMA((3,)),
        ],
        compiler_params=pltpu.CompilerParams(has_side_effects=True),
    )(g, u, dn)


def relay_gather_kernel(g_ref, u_ref, dn_ref, gf_ref, uf_ref, df_ref, send_sem, recv_sem,
                        local_sem):
    ndp = 8
    d = lax.axis_index("dp")
    m = lax.axis_index("mp")
    lo = d % 2
    partner = d - lo + (1 - lo)
    nxt = (d + 2) % ndp
    prv = (d + ndp - 2) % ndp
    far = (d + 4) % ndp
    owns = (g_ref, u_ref, dn_ref)
    fulls = (gf_ref, uf_ref, df_ref)

    def slot(w, idx, half=None):
        if w < 2:
            kr = owns[w].shape[0]
            if half is None:
                return fulls[w].at[pl.ds(pl.multiple_of(idx * kr, kr), kr)]
            hk = kr // 2
            return fulls[w].at[pl.ds(pl.multiple_of(idx * kr + half * hk, hk), hk)]
        rr, dc = owns[w].shape
        cols = pl.ds(pl.multiple_of(idx * dc, dc), dc)
        if half is None:
            return fulls[w].at[:, cols]
        hr = rr // 2
        return fulls[w].at[pl.ds(half * hr, hr), cols]

    def rc(w, k, src, dst, target):
        i = w * 8 + k
        return pltpu.make_async_remote_copy(
            src_ref=src, dst_ref=dst, send_sem=send_sem.at[i], recv_sem=recv_sem.at[i],
            device_id=(target, m), device_id_type=MESH)

    locals_ = [pltpu.make_async_copy(owns[w], slot(w, d), local_sem.at[w]) for w in range(3)]
    c = {}
    for w in range(3):
        c[w, 0] = rc(w, 0, owns[w], slot(w, d), partner)
        c[w, 1] = rc(w, 1, owns[w], slot(w, d), nxt)
        c[w, 2] = rc(w, 2, owns[w], slot(w, d), prv)
        c[w, 3] = rc(w, 3, slot(w, partner), slot(w, partner), nxt)
        c[w, 4] = rc(w, 4, slot(w, partner), slot(w, partner), prv)
        c[w, 5] = rc(w, 5, slot(w, prv, 0), slot(w, prv, 0), nxt)
        c[w, 6] = rc(w, 6, slot(w, nxt, 1), slot(w, nxt, 1), prv)
        c[w, 7] = rc(w, 7, slot(w, far), slot(w, far), partner)
    for w in range(3):
        locals_[w].start()
        for k in range(3):
            c[w, k].start()
    for w in range(3):
        c[w, 0].wait_recv()
        c[w, 3].start()
        c[w, 4].start()
        c[w, 1].wait_recv()
        c[w, 5].start()
        c[w, 2].wait_recv()
        c[w, 6].start()
    for w in range(3):
        c[w, 5].wait_recv()
        c[w, 6].wait_recv()
        c[w, 7].start()
    for w in range(3):
        for k in (3, 4, 7):
            c[w, k].wait_recv()
    for w in range(3):
        for k in range(8):
            c[w, k].wait_send()
        locals_[w].wait()


def gather_weights(g, u, dn, ndp):
    if ndp != 8:
        return gather_weights_direct(g, u, dn, ndp)
    any_spec = pl.BlockSpec(memory_space=pl.ANY)
    out_shape = (
        jax.ShapeDtypeStruct((g.shape[0] * ndp, g.shape[1]), g.dtype),
        jax.ShapeDtypeStruct((u.shape[0] * ndp, u.shape[1]), u.dtype),
        jax.ShapeDtypeStruct((dn.shape[0], dn.shape[1] * ndp), dn.dtype),
    )
    return pl.pallas_call(
        relay_gather_kernel,
        out_shape=out_shape,
        in_specs=[any_spec] * 3,
        out_specs=[any_spec] * 3,
        scratch_shapes=[
            pltpu.SemaphoreType.DMA((24,)),
            pltpu.SemaphoreType.DMA((24,)),
            pltpu.SemaphoreType.DMA((3,)),
        ],
        compiler_params=pltpu.CompilerParams(has_side_effects=True),
    )(g, u, dn)


def reduce_kernel(nmp, t_ref, o_ref, buf, send_sem, recv_sem, local_sem):
    d = lax.axis_index("dp")
    m = lax.axis_index("mp")
    w = o_ref.shape[2]
    mine = pl.ds(pl.multiple_of(m * w, w), w)
    local_copy = pltpu.make_async_copy(t_ref.at[:, :, mine], buf.at[0], local_sem.at[0])
    local_copy.start()
    copies = []
    for s in range(1, nmp):
        peer = lax.rem(m + s, nmp)
        theirs = pl.ds(pl.multiple_of(peer * w, w), w)
        copies.append(pltpu.make_async_remote_copy(
            src_ref=t_ref.at[:, :, theirs], dst_ref=buf.at[s], send_sem=send_sem.at[s],
            recv_sem=recv_sem.at[s], device_id=(d, peer), device_id_type=MESH))
    for c in copies:
        c.start()
    local_copy.wait()
    for c in copies:
        c.wait()
    rows = 32

    def body(i, carry):
        r = pl.ds(pl.multiple_of(i * rows, rows), rows)
        for k in range(o_ref.shape[0]):
            acc = buf[0, k, r, :].astype(jnp.float32)
            for s in range(1, nmp):
                acc = acc + buf[s, k, r, :].astype(jnp.float32)
            o_ref[k, r, :] = acc.astype(o_ref.dtype)
        return carry

    lax.fori_loop(0, o_ref.shape[1] // rows, body, 0)


def reduce_scatter(terms, nmp):
    n, t, width = terms.shape
    w = width // nmp
    return pl.pallas_call(
        functools.partial(reduce_kernel, nmp),
        out_shape=jax.ShapeDtypeStruct((n, t, w), jnp.bfloat16),
        in_specs=[pl.BlockSpec(memory_space=pl.ANY)],
        out_specs=pl.BlockSpec(memory_space=pltpu.VMEM),
        scratch_shapes=[
            pltpu.VMEM((nmp, n, t, w), jnp.bfloat16),
            pltpu.SemaphoreType.DMA((nmp,)),
            pltpu.SemaphoreType.DMA((nmp,)),
            pltpu.SemaphoreType.DMA((1,)),
        ],
        compiler_params=pltpu.CompilerParams(has_side_effects=True,
                                             vmem_limit_bytes=48 * 1024 * 1024),
    )(terms)


def hier_reduce_kernel(t_ref, o_ref, own, r1, sb2, r2, s2, sb3, r3,
                       ls, ss1, rs1, ss2, rs2, ss3, rs3):
    d = lax.axis_index("dp")
    m = lax.axis_index("mp")
    c = m % 2
    z = (m // 2) % 4
    xh = m // 8
    w = o_ref.shape[2]
    rows = 32
    nchunk = o_ref.shape[1] // rows

    def blk(b):
        return t_ref.at[:, :, pl.ds(pl.multiple_of(b * w, w), w)]

    def dev(mm):
        return (d, mm)

    locs = []
    st1 = []
    for j in range(8):
        bx, bz = j // 4, j % 4
        locs.append(pltpu.make_async_copy(blk(bx * 8 + bz * 2 + c), own.at[j], ls.at[j]))
        st1.append(pltpu.make_async_remote_copy(
            src_ref=blk(bx * 8 + bz * 2 + (1 - c)), dst_ref=r1.at[j], send_sem=ss1.at[j],
            recv_sem=rs1.at[j], device_id=dev(m + 1 - 2 * c), device_id_type=MESH))
    for j in range(8):
        st1[j].start()
        locs[j].start()
    for j in range(8):
        locs[j].wait()
        st1[j].wait()

    st2 = []
    for s in range(1, 4):
        zt = (z + s) % 4

        def fill(i, carry, s=s, zt=zt):
            r = pl.ds(pl.multiple_of(i * rows, rows), rows)
            for bx in range(2):
                idx = bx * 4 + zt
                sb2[s - 1, bx, :, r, :] = (own[idx, :, r, :].astype(jnp.float32)
                                           + r1[idx, :, r, :].astype(jnp.float32)
                                           ).astype(sb2.dtype)
            return carry

        lax.fori_loop(0, nchunk, fill, 0)
        cp = pltpu.make_async_remote_copy(
            src_ref=sb2.at[s - 1], dst_ref=r2.at[s - 1], send_sem=ss2.at[s - 1],
            recv_sem=rs2.at[s - 1], device_id=dev(xh * 8 + zt * 2 + c), device_id_type=MESH)
        cp.start()
        st2.append(cp)
    for cp in st2:
        cp.wait()

    def sum2(i, carry):
        r = pl.ds(pl.multiple_of(i * rows, rows), rows)
        for bx in range(2):
            idx = bx * 4 + z
            acc = own[idx, :, r, :].astype(jnp.float32) + r1[idx, :, r, :].astype(jnp.float32)
            for k in range(3):
                acc = acc + r2[k, bx, :, r, :].astype(jnp.float32)
            s2[bx, :, r, :] = acc
        return carry

    lax.fori_loop(0, nchunk, sum2, 0)
    sb3[...] = s2[1 - xh].astype(sb3.dtype)
    cp3 = pltpu.make_async_remote_copy(
        src_ref=sb3, dst_ref=r3, send_sem=ss3.at[0], recv_sem=rs3.at[0],
        device_id=dev(m + 8 - 16 * xh), device_id_type=MESH)
    cp3.start()
    cp3.wait()
    o_ref[...] = (s2[xh] + r3[...].astype(jnp.float32)).astype(o_ref.dtype)


def hier_reduce_scatter(terms):
    n, t, width = terms.shape
    w = width // 16
    bf = jnp.bfloat16
    dma = pltpu.SemaphoreType.DMA
    return pl.pallas_call(
        hier_reduce_kernel,
        out_shape=jax.ShapeDtypeStruct((n, t, w), bf),
        in_specs=[pl.BlockSpec(memory_space=pl.ANY)],
        out_specs=pl.BlockSpec(memory_space=pltpu.VMEM),
        scratch_shapes=[
            pltpu.VMEM((8, n, t, w), bf),
            pltpu.VMEM((8, n, t, w), bf),
            pltpu.VMEM((3, 2, n, t, w), bf),
            pltpu.VMEM((3, 2, n, t, w), bf),
            pltpu.VMEM((2, n, t, w), jnp.float32),
            pltpu.VMEM((n, t, w), bf),
            pltpu.VMEM((n, t, w), bf),
            dma((8,)), dma((8,)), dma((8,)), dma((3,)), dma((3,)), dma((1,)), dma((1,)),
        ],
        compiler_params=pltpu.CompilerParams(has_side_effects=True,
                                             vmem_limit_bytes=56 * 1024 * 1024),
    )(terms)


def local(ndp, nmp, hidden_states, gate_online, up_online, down_online, gate_previous,
          up_previous, down_previous):
    features_all = lax.all_gather(hidden_states, "mp", axis=1, tiled=True)
    gate_full, up_full, down_full = gather_weights(gate_online, up_online, down_online, ndp)

    def pair(piece, previous):
        target_piece = blend(piece, previous)
        o = jnp.dot(features_all, piece, preferred_element_type=jnp.float32)
        t = jnp.dot(features_all, target_piece, preferred_element_type=jnp.float32)
        return o, t

    gate_o, gate_t = pair(gate_full, gate_previous)
    up_o, up_t = pair(up_full, up_previous)
    inner_o = (jax.nn.silu(gate_o) * up_o).astype(jnp.bfloat16)
    inner_t = (jax.nn.silu(gate_t) * up_t).astype(jnp.bfloat16)
    target_down = blend(down_full, down_previous)
    online_part = jnp.dot(inner_o, down_full, preferred_element_type=jnp.float32)
    target_part = jnp.dot(inner_t, target_down, preferred_element_type=jnp.float32)
    terms = jnp.stack([online_part, target_part], axis=0).astype(jnp.bfloat16)
    if nmp == 16:
        result = hier_reduce_scatter(terms)
    else:
        result = reduce_scatter(terms, nmp)
    return (result[0], result[1])


def solution(mesh):
    ndp = mesh.shape["dp"]
    nmp = mesh.shape["mp"]
    in_specs = (
        P("dp", "mp"),
        P("dp", "mp"),
        P("dp", "mp"),
        P("mp", "dp"),
        P(None, "mp"),
        P(None, "mp"),
        P("mp", None),
    )
    out_specs = (P("dp", "mp"), P("dp", "mp"))
    return jax.shard_map(functools.partial(local, ndp, nmp), mesh=mesh, in_specs=in_specs,
                         out_specs=out_specs, check_vma=False)
```

```python
import functools

import jax
import jax.numpy as jnp
from jax import lax
from jax.experimental import pallas as pl
from jax.experimental.pallas import tpu as pltpu
from jax.sharding import PartitionSpec as P

POLYAK = 0.25
MESH = pl.DeviceIdType.MESH


def blend(online, previous):
    return (
        POLYAK * online.astype(jnp.float32) + (1.0 - POLYAK) * previous.astype(jnp.float32)
    ).astype(jnp.bfloat16)


def gather_kernel(ndp, g_ref, u_ref, dn_ref, gf_ref, uf_ref, df_ref, send_sem, recv_sem,
                  local_sem):
    d = lax.axis_index("dp")
    m = lax.axis_index("mp")
    kr = g_ref.shape[0]
    dc = dn_ref.shape[1]
    rows = pl.ds(pl.multiple_of(d * kr, kr), kr)
    cols = pl.ds(pl.multiple_of(d * dc, dc), dc)

    locals_ = [
        pltpu.make_async_copy(g_ref, gf_ref.at[rows], local_sem.at[0]),
        pltpu.make_async_copy(u_ref, uf_ref.at[rows], local_sem.at[1]),
        pltpu.make_async_copy(dn_ref, df_ref.at[:, cols], local_sem.at[2]),
    ]
    for c in locals_:
        c.start()

    copies = []
    k = 0
    for s in range(1, ndp):
        peer = lax.rem(d + s, ndp)
        for src, dst in ((g_ref, gf_ref.at[rows]), (u_ref, uf_ref.at[rows]),
                         (dn_ref, df_ref.at[:, cols])):
            copies.append(pltpu.make_async_remote_copy(
                src_ref=src, dst_ref=dst, send_sem=send_sem.at[k], recv_sem=recv_sem.at[k],
                device_id=(peer, m), device_id_type=MESH))
            k += 1
    for c in copies:
        c.start()
    for c in locals_:
        c.wait()
    for c in copies:
        c.wait()


def gather_weights_direct(g, u, dn, ndp):
    n_copies = 3 * (ndp - 1)
    any_spec = pl.BlockSpec(memory_space=pl.ANY)
    out_shape = (
        jax.ShapeDtypeStruct((g.shape[0] * ndp, g.shape[1]), g.dtype),
        jax.ShapeDtypeStruct((u.shape[0] * ndp, u.shape[1]), u.dtype),
        jax.ShapeDtypeStruct((dn.shape[0], dn.shape[1] * ndp), dn.dtype),
    )
    return pl.pallas_call(
        functools.partial(gather_kernel, ndp),
        out_shape=out_shape,
        in_specs=[any_spec] * 3,
        out_specs=[any_spec] * 3,
        scratch_shapes=[
            pltpu.SemaphoreType.DMA((n_copies,)),
            pltpu.SemaphoreType.DMA((n_copies,)),
            pltpu.SemaphoreType.DMA((3,)),
        ],
        compiler_params=pltpu.CompilerParams(has_side_effects=True),
    )(g, u, dn)


def relay_gather_kernel(g_ref, u_ref, dn_ref, gf_ref, uf_ref, df_ref, send_sem, recv_sem,
                        local_sem):
    ndp = 8
    d = lax.axis_index("dp")
    m = lax.axis_index("mp")
    lo = d % 2
    partner = d - lo + (1 - lo)
    nxt = (d + 2) % ndp
    prv = (d + ndp - 2) % ndp
    far = (d + 4) % ndp
    owns = (g_ref, u_ref, dn_ref)
    fulls = (gf_ref, uf_ref, df_ref)

    def slot(w, idx, half=None):
        if w < 2:
            kr = owns[w].shape[0]
            if half is None:
                return fulls[w].at[pl.ds(pl.multiple_of(idx * kr, kr), kr)]
            hk = kr // 2
            return fulls[w].at[pl.ds(pl.multiple_of(idx * kr + half * hk, hk), hk)]
        rr, dc = owns[w].shape
        cols = pl.ds(pl.multiple_of(idx * dc, dc), dc)
        if half is None:
            return fulls[w].at[:, cols]
        hr = rr // 2
        return fulls[w].at[pl.ds(half * hr, hr), cols]

    def rc(w, k, src, dst, target):
        i = w * 8 + k
        return pltpu.make_async_remote_copy(
            src_ref=src, dst_ref=dst, send_sem=send_sem.at[i], recv_sem=recv_sem.at[i],
            device_id=(target, m), device_id_type=MESH)

    locals_ = [pltpu.make_async_copy(owns[w], slot(w, d), local_sem.at[w]) for w in range(3)]
    c = {}
    for w in range(3):
        c[w, 0] = rc(w, 0, owns[w], slot(w, d), partner)
        c[w, 1] = rc(w, 1, owns[w], slot(w, d), nxt)
        c[w, 2] = rc(w, 2, owns[w], slot(w, d), prv)
        c[w, 3] = rc(w, 3, slot(w, partner), slot(w, partner), nxt)
        c[w, 4] = rc(w, 4, slot(w, partner), slot(w, partner), prv)
        c[w, 5] = rc(w, 5, slot(w, prv, 0), slot(w, prv, 0), nxt)
        c[w, 6] = rc(w, 6, slot(w, nxt, 1), slot(w, nxt, 1), prv)
        c[w, 7] = rc(w, 7, slot(w, far), slot(w, far), partner)
    for w in range(3):
        locals_[w].start()
        for k in range(3):
            c[w, k].start()
    for w in range(3):
        c[w, 0].wait_recv()
        c[w, 3].start()
        c[w, 4].start()
        c[w, 1].wait_recv()
        c[w, 5].start()
        c[w, 2].wait_recv()
        c[w, 6].start()
    for w in range(3):
        c[w, 5].wait_recv()
        c[w, 6].wait_recv()
        c[w, 7].start()
    for w in range(3):
        for k in (3, 4, 7):
            c[w, k].wait_recv()
    for w in range(3):
        for k in range(8):
            c[w, k].wait_send()
        locals_[w].wait()


def gather_weights(g, u, dn, ndp):
    if ndp != 8:
        return gather_weights_direct(g, u, dn, ndp)
    any_spec = pl.BlockSpec(memory_space=pl.ANY)
    out_shape = (
        jax.ShapeDtypeStruct((g.shape[0] * ndp, g.shape[1]), g.dtype),
        jax.ShapeDtypeStruct((u.shape[0] * ndp, u.shape[1]), u.dtype),
        jax.ShapeDtypeStruct((dn.shape[0], dn.shape[1] * ndp), dn.dtype),
    )
    return pl.pallas_call(
        relay_gather_kernel,
        out_shape=out_shape,
        in_specs=[any_spec] * 3,
        out_specs=[any_spec] * 3,
        scratch_shapes=[
            pltpu.SemaphoreType.DMA((24,)),
            pltpu.SemaphoreType.DMA((24,)),
            pltpu.SemaphoreType.DMA((3,)),
        ],
        compiler_params=pltpu.CompilerParams(has_side_effects=True),
    )(g, u, dn)


def reduce_kernel(nmp, t_ref, o_ref, buf, send_sem, recv_sem, local_sem):
    d = lax.axis_index("dp")
    m = lax.axis_index("mp")
    w = o_ref.shape[2]
    mine = pl.ds(pl.multiple_of(m * w, w), w)
    local_copy = pltpu.make_async_copy(t_ref.at[:, :, mine], buf.at[0], local_sem.at[0])
    local_copy.start()
    copies = []
    for s in range(1, nmp):
        peer = lax.rem(m + s, nmp)
        theirs = pl.ds(pl.multiple_of(peer * w, w), w)
        copies.append(pltpu.make_async_remote_copy(
            src_ref=t_ref.at[:, :, theirs], dst_ref=buf.at[s], send_sem=send_sem.at[s],
            recv_sem=recv_sem.at[s], device_id=(d, peer), device_id_type=MESH))
    for c in copies:
        c.start()
    local_copy.wait()
    for c in copies:
        c.wait()
    rows = 32

    def body(i, carry):
        r = pl.ds(pl.multiple_of(i * rows, rows), rows)
        for k in range(o_ref.shape[0]):
            acc = buf[0, k, r, :].astype(jnp.float32)
            for s in range(1, nmp):
                acc = acc + buf[s, k, r, :].astype(jnp.float32)
            o_ref[k, r, :] = acc.astype(o_ref.dtype)
        return carry

    lax.fori_loop(0, o_ref.shape[1] // rows, body, 0)


def reduce_scatter(terms, nmp):
    n, t, width = terms.shape
    w = width // nmp
    return pl.pallas_call(
        functools.partial(reduce_kernel, nmp),
        out_shape=jax.ShapeDtypeStruct((n, t, w), jnp.bfloat16),
        in_specs=[pl.BlockSpec(memory_space=pl.ANY)],
        out_specs=pl.BlockSpec(memory_space=pltpu.VMEM),
        scratch_shapes=[
            pltpu.VMEM((nmp, n, t, w), jnp.bfloat16),
            pltpu.SemaphoreType.DMA((nmp,)),
            pltpu.SemaphoreType.DMA((nmp,)),
            pltpu.SemaphoreType.DMA((1,)),
        ],
        compiler_params=pltpu.CompilerParams(has_side_effects=True,
                                             vmem_limit_bytes=48 * 1024 * 1024),
    )(terms)


def hier_reduce_kernel(ta_ref, tb_ref, o_ref, own, r1, sb2, r2, s2, sb3, r3,
                       ls, ss1, rs1, ss2, rs2, ss3, rs3):
    d = lax.axis_index("dp")
    m = lax.axis_index("mp")
    c = m % 2
    z = (m // 2) % 4
    xh = m // 8
    w = o_ref.shape[2]
    rows = 32
    nchunk = o_ref.shape[1] // rows

    def blk(b, k):
        return (ta_ref, tb_ref)[k].at[:, pl.ds(pl.multiple_of(b * w, w), w)]

    def dev(mm):
        return (d, mm)

    locs = []
    st1 = []
    for j in range(16):
        bx, bz, k = j // 8, (j // 2) % 4, j % 2
        jj = bx * 4 + bz
        locs.append(pltpu.make_async_copy(blk(bx * 8 + bz * 2 + c, k), own.at[jj, k],
                                          ls.at[j]))
        st1.append(pltpu.make_async_remote_copy(
            src_ref=blk(bx * 8 + bz * 2 + (1 - c), k), dst_ref=r1.at[jj, k], send_sem=ss1.at[j],
            recv_sem=rs1.at[j], device_id=dev(m + 1 - 2 * c), device_id_type=MESH))
    for j in range(16):
        st1[j].start()
        locs[j].start()
    for j in range(16):
        locs[j].wait()
        st1[j].wait()

    st2 = []
    for s in range(1, 4):
        zt = (z + s) % 4

        def fill(i, carry, s=s, zt=zt):
            r = pl.ds(pl.multiple_of(i * rows, rows), rows)
            for bx in range(2):
                idx = bx * 4 + zt
                sb2[s - 1, bx, :, r, :] = (own[idx, :, r, :].astype(jnp.float32)
                                           + r1[idx, :, r, :].astype(jnp.float32)
                                           ).astype(sb2.dtype)
            return carry

        lax.fori_loop(0, nchunk, fill, 0)
        cp = pltpu.make_async_remote_copy(
            src_ref=sb2.at[s - 1], dst_ref=r2.at[s - 1], send_sem=ss2.at[s - 1],
            recv_sem=rs2.at[s - 1], device_id=dev(xh * 8 + zt * 2 + c), device_id_type=MESH)
        cp.start()
        st2.append(cp)
    for cp in st2:
        cp.wait()

    def sum2(i, carry):
        r = pl.ds(pl.multiple_of(i * rows, rows), rows)
        for bx in range(2):
            idx = bx * 4 + z
            acc = own[idx, :, r, :].astype(jnp.float32) + r1[idx, :, r, :].astype(jnp.float32)
            for k in range(3):
                acc = acc + r2[k, bx, :, r, :].astype(jnp.float32)
            s2[bx, :, r, :] = acc
        return carry

    lax.fori_loop(0, nchunk, sum2, 0)
    sb3[...] = s2[1 - xh].astype(sb3.dtype)
    cp3 = pltpu.make_async_remote_copy(
        src_ref=sb3, dst_ref=r3, send_sem=ss3.at[0], recv_sem=rs3.at[0],
        device_id=dev(m + 8 - 16 * xh), device_id_type=MESH)
    cp3.start()
    cp3.wait()
    o_ref[...] = (s2[xh] + r3[...].astype(jnp.float32)).astype(o_ref.dtype)


def hier_reduce_scatter(ta, tb):
    n = 2
    t, width = ta.shape
    w = width // 16
    bf = jnp.bfloat16
    dma = pltpu.SemaphoreType.DMA
    return pl.pallas_call(
        hier_reduce_kernel,
        out_shape=jax.ShapeDtypeStruct((n, t, w), bf),
        in_specs=[pl.BlockSpec(memory_space=pl.ANY)] * 2,
        out_specs=pl.BlockSpec(memory_space=pltpu.VMEM),
        scratch_shapes=[
            pltpu.VMEM((8, n, t, w), bf),
            pltpu.VMEM((8, n, t, w), bf),
            pltpu.VMEM((3, 2, n, t, w), bf),
            pltpu.VMEM((3, 2, n, t, w), bf),
            pltpu.VMEM((2, n, t, w), jnp.float32),
            pltpu.VMEM((n, t, w), bf),
            pltpu.VMEM((n, t, w), bf),
            dma((16,)), dma((16,)), dma((16,)), dma((3,)), dma((3,)), dma((1,)), dma((1,)),
        ],
        compiler_params=pltpu.CompilerParams(has_side_effects=True,
                                             vmem_limit_bytes=56 * 1024 * 1024),
    )(ta, tb)


def local(ndp, nmp, hidden_states, gate_online, up_online, down_online, gate_previous,
          up_previous, down_previous):
    features_all = lax.all_gather(hidden_states, "mp", axis=1, tiled=True)
    gate_full, up_full, down_full = gather_weights(gate_online, up_online, down_online, ndp)

    def pair(piece, previous):
        target_piece = blend(piece, previous)
        o = jnp.dot(features_all, piece, preferred_element_type=jnp.float32)
        t = jnp.dot(features_all, target_piece, preferred_element_type=jnp.float32)
        return o, t

    gate_o, gate_t = pair(gate_full, gate_previous)
    up_o, up_t = pair(up_full, up_previous)
    inner_o = (jax.nn.silu(gate_o) * up_o).astype(jnp.bfloat16)
    inner_t = (jax.nn.silu(gate_t) * up_t).astype(jnp.bfloat16)
    target_down = blend(down_full, down_previous)
    online_part = jnp.dot(inner_o, down_full, preferred_element_type=jnp.float32)
    target_part = jnp.dot(inner_t, target_down, preferred_element_type=jnp.float32)
    if nmp == 16:
        result = hier_reduce_scatter(online_part.astype(jnp.bfloat16),
                                     target_part.astype(jnp.bfloat16))
    else:
        terms = jnp.stack([online_part, target_part], axis=0).astype(jnp.bfloat16)
        result = reduce_scatter(terms, nmp)
    return (result[0], result[1])


def solution(mesh):
    ndp = mesh.shape["dp"]
    nmp = mesh.shape["mp"]
    in_specs = (
        P("dp", "mp"),
        P("dp", "mp"),
        P("dp", "mp"),
        P("mp", "dp"),
        P(None, "mp"),
        P(None, "mp"),
        P("mp", None),
    )
    out_specs = (P("dp", "mp"), P("dp", "mp"))
    return jax.shard_map(functools.partial(local, ndp, nmp), mesh=mesh, in_specs=in_specs,
                         out_specs=out_specs, check_vma=False)
```

```python
import functools

import jax
import jax.numpy as jnp
from jax import lax
from jax.experimental import pallas as pl
from jax.experimental.pallas import tpu as pltpu
from jax.sharding import PartitionSpec as P

POLYAK = 0.25
MESH = pl.DeviceIdType.MESH


def blend(online, previous):
    return (
        POLYAK * online.astype(jnp.float32) + (1.0 - POLYAK) * previous.astype(jnp.float32)
    ).astype(jnp.bfloat16)


def gather_kernel(ndp, g_ref, u_ref, dn_ref, gf_ref, uf_ref, df_ref, send_sem, recv_sem,
                  local_sem):
    d = lax.axis_index("dp")
    m = lax.axis_index("mp")
    kr = g_ref.shape[0]
    dc = dn_ref.shape[1]
    rows = pl.ds(pl.multiple_of(d * kr, kr), kr)
    cols = pl.ds(pl.multiple_of(d * dc, dc), dc)

    locals_ = [
        pltpu.make_async_copy(g_ref, gf_ref.at[rows], local_sem.at[0]),
        pltpu.make_async_copy(u_ref, uf_ref.at[rows], local_sem.at[1]),
        pltpu.make_async_copy(dn_ref, df_ref.at[:, cols], local_sem.at[2]),
    ]
    for c in locals_:
        c.start()

    copies = []
    k = 0
    for s in range(1, ndp):
        peer = lax.rem(d + s, ndp)
        for src, dst in ((g_ref, gf_ref.at[rows]), (u_ref, uf_ref.at[rows]),
                         (dn_ref, df_ref.at[:, cols])):
            copies.append(pltpu.make_async_remote_copy(
                src_ref=src, dst_ref=dst, send_sem=send_sem.at[k], recv_sem=recv_sem.at[k],
                device_id=(peer, m), device_id_type=MESH))
            k += 1
    for c in copies:
        c.start()
    for c in locals_:
        c.wait()
    for c in copies:
        c.wait()


def gather_weights_direct(g, u, dn, ndp):
    n_copies = 3 * (ndp - 1)
    any_spec = pl.BlockSpec(memory_space=pl.ANY)
    out_shape = (
        jax.ShapeDtypeStruct((g.shape[0] * ndp, g.shape[1]), g.dtype),
        jax.ShapeDtypeStruct((u.shape[0] * ndp, u.shape[1]), u.dtype),
        jax.ShapeDtypeStruct((dn.shape[0], dn.shape[1] * ndp), dn.dtype),
    )
    return pl.pallas_call(
        functools.partial(gather_kernel, ndp),
        out_shape=out_shape,
        in_specs=[any_spec] * 3,
        out_specs=[any_spec] * 3,
        scratch_shapes=[
            pltpu.SemaphoreType.DMA((n_copies,)),
            pltpu.SemaphoreType.DMA((n_copies,)),
            pltpu.SemaphoreType.DMA((3,)),
        ],
        compiler_params=pltpu.CompilerParams(has_side_effects=True),
    )(g, u, dn)


def relay_gather_kernel(g_ref, u_ref, dn_ref, gf_ref, uf_ref, df_ref, send_sem, recv_sem,
                        local_sem):
    ndp = 8
    d = lax.axis_index("dp")
    m = lax.axis_index("mp")
    lo = d % 2
    partner = d - lo + (1 - lo)
    nxt = (d + 2) % ndp
    prv = (d + ndp - 2) % ndp
    far = (d + 4) % ndp
    owns = (g_ref, u_ref, dn_ref)
    fulls = (gf_ref, uf_ref, df_ref)

    def slot(w, idx, half=None):
        if w < 2:
            kr = owns[w].shape[0]
            if half is None:
                return fulls[w].at[pl.ds(pl.multiple_of(idx * kr, kr), kr)]
            hk = kr // 2
            return fulls[w].at[pl.ds(pl.multiple_of(idx * kr + half * hk, hk), hk)]
        rr, dc = owns[w].shape
        cols = pl.ds(pl.multiple_of(idx * dc, dc), dc)
        if half is None:
            return fulls[w].at[:, cols]
        hr = rr // 2
        return fulls[w].at[pl.ds(half * hr, hr), cols]

    def rc(w, k, src, dst, target):
        i = w * 8 + k
        return pltpu.make_async_remote_copy(
            src_ref=src, dst_ref=dst, send_sem=send_sem.at[i], recv_sem=recv_sem.at[i],
            device_id=(target, m), device_id_type=MESH)

    locals_ = [pltpu.make_async_copy(owns[w], slot(w, d), local_sem.at[w]) for w in range(3)]
    c = {}
    for w in range(3):
        c[w, 0] = rc(w, 0, owns[w], slot(w, d), partner)
        c[w, 1] = rc(w, 1, owns[w], slot(w, d), nxt)
        c[w, 2] = rc(w, 2, owns[w], slot(w, d), prv)
        c[w, 3] = rc(w, 3, slot(w, partner), slot(w, partner), nxt)
        c[w, 4] = rc(w, 4, slot(w, partner), slot(w, partner), prv)
        c[w, 5] = rc(w, 5, slot(w, prv, 0), slot(w, prv, 0), nxt)
        c[w, 6] = rc(w, 6, slot(w, nxt, 1), slot(w, nxt, 1), prv)
        c[w, 7] = rc(w, 7, slot(w, far), slot(w, far), partner)
    for w in range(3):
        locals_[w].start()
        for k in range(3):
            c[w, k].start()
    for w in range(3):
        c[w, 0].wait_recv()
        c[w, 3].start()
        c[w, 4].start()
        c[w, 1].wait_recv()
        c[w, 5].start()
        c[w, 2].wait_recv()
        c[w, 6].start()
    for w in range(3):
        c[w, 5].wait_recv()
        c[w, 6].wait_recv()
        c[w, 7].start()
    for w in range(3):
        for k in (3, 4, 7):
            c[w, k].wait_recv()
    for w in range(3):
        for k in range(8):
            c[w, k].wait_send()
        locals_[w].wait()


def gather_weights(g, u, dn, ndp):
    if ndp != 8:
        return gather_weights_direct(g, u, dn, ndp)
    any_spec = pl.BlockSpec(memory_space=pl.ANY)
    out_shape = (
        jax.ShapeDtypeStruct((g.shape[0] * ndp, g.shape[1]), g.dtype),
        jax.ShapeDtypeStruct((u.shape[0] * ndp, u.shape[1]), u.dtype),
        jax.ShapeDtypeStruct((dn.shape[0], dn.shape[1] * ndp), dn.dtype),
    )
    return pl.pallas_call(
        relay_gather_kernel,
        out_shape=out_shape,
        in_specs=[any_spec] * 3,
        out_specs=[any_spec] * 3,
        scratch_shapes=[
            pltpu.SemaphoreType.DMA((24,)),
            pltpu.SemaphoreType.DMA((24,)),
            pltpu.SemaphoreType.DMA((3,)),
        ],
        compiler_params=pltpu.CompilerParams(has_side_effects=True),
    )(g, u, dn)


def reduce_kernel(nmp, t_ref, o_ref, buf, send_sem, recv_sem, local_sem):
    d = lax.axis_index("dp")
    m = lax.axis_index("mp")
    w = o_ref.shape[2]
    mine = pl.ds(pl.multiple_of(m * w, w), w)
    local_copy = pltpu.make_async_copy(t_ref.at[:, :, mine], buf.at[0], local_sem.at[0])
    local_copy.start()
    copies = []
    for s in range(1, nmp):
        peer = lax.rem(m + s, nmp)
        theirs = pl.ds(pl.multiple_of(peer * w, w), w)
        copies.append(pltpu.make_async_remote_copy(
            src_ref=t_ref.at[:, :, theirs], dst_ref=buf.at[s], send_sem=send_sem.at[s],
            recv_sem=recv_sem.at[s], device_id=(d, peer), device_id_type=MESH))
    for c in copies:
        c.start()
    local_copy.wait()
    for c in copies:
        c.wait()
    rows = 32

    def body(i, carry):
        r = pl.ds(pl.multiple_of(i * rows, rows), rows)
        for k in range(o_ref.shape[0]):
            acc = buf[0, k, r, :].astype(jnp.float32)
            for s in range(1, nmp):
                acc = acc + buf[s, k, r, :].astype(jnp.float32)
            o_ref[k, r, :] = acc.astype(o_ref.dtype)
        return carry

    lax.fori_loop(0, o_ref.shape[1] // rows, body, 0)


def reduce_scatter(terms, nmp):
    n, t, width = terms.shape
    w = width // nmp
    return pl.pallas_call(
        functools.partial(reduce_kernel, nmp),
        out_shape=jax.ShapeDtypeStruct((n, t, w), jnp.bfloat16),
        in_specs=[pl.BlockSpec(memory_space=pl.ANY)],
        out_specs=pl.BlockSpec(memory_space=pltpu.VMEM),
        scratch_shapes=[
            pltpu.VMEM((nmp, n, t, w), jnp.bfloat16),
            pltpu.SemaphoreType.DMA((nmp,)),
            pltpu.SemaphoreType.DMA((nmp,)),
            pltpu.SemaphoreType.DMA((1,)),
        ],
        compiler_params=pltpu.CompilerParams(has_side_effects=True,
                                             vmem_limit_bytes=48 * 1024 * 1024),
    )(terms)


def hier_reduce_kernel(ta_ref, tb_ref, o_ref, own, r1, sb2, r2, s2, sb3, r3,
                       ls, ss1, rs1, ss2, rs2, ss3, rs3):
    d = lax.axis_index("dp")
    m = lax.axis_index("mp")
    c = m % 2
    z = (m // 2) % 4
    xh = m // 8
    w = o_ref.shape[2]
    rows = 32
    nchunk = o_ref.shape[1] // rows

    def blk(b, k):
        return (ta_ref, tb_ref)[k].at[:, pl.ds(pl.multiple_of(b * w, w), w)]

    def dev(mm):
        return (d, mm)

    locs = []
    st1 = []
    for j in range(16):
        bx, bz, k = j // 8, (j // 2) % 4, j % 2
        jj = bx * 4 + bz
        locs.append(pltpu.make_async_copy(blk(bx * 8 + bz * 2 + c, k), own.at[jj, k],
                                          ls.at[j]))
        st1.append(pltpu.make_async_remote_copy(
            src_ref=blk(bx * 8 + bz * 2 + (1 - c), k), dst_ref=r1.at[jj, k], send_sem=ss1.at[j],
            recv_sem=rs1.at[j], device_id=dev(m + 1 - 2 * c), device_id_type=MESH))
    for j in range(16):
        st1[j].start()
        locs[j].start()
    for j in range(16):
        locs[j].wait()
        st1[j].wait()

    st2 = []
    for s in range(1, 4):
        zt = (z + s) % 4

        def fill(i, carry, s=s, zt=zt):
            r = pl.ds(pl.multiple_of(i * rows, rows), rows)
            for bx in range(2):
                idx = bx * 4 + zt
                sb2[s - 1, bx, :, r, :] = (own[idx, :, r, :].astype(jnp.float32)
                                           + r1[idx, :, r, :].astype(jnp.float32)
                                           ).astype(sb2.dtype)
            return carry

        lax.fori_loop(0, nchunk, fill, 0)
        cp = pltpu.make_async_remote_copy(
            src_ref=sb2.at[s - 1], dst_ref=r2.at[s - 1], send_sem=ss2.at[s - 1],
            recv_sem=rs2.at[s - 1], device_id=dev(xh * 8 + zt * 2 + c), device_id_type=MESH)
        cp.start()
        st2.append(cp)
    for cp in st2:
        cp.wait()

    def sum2(i, carry):
        r = pl.ds(pl.multiple_of(i * rows, rows), rows)
        for bx in range(2):
            idx = bx * 4 + z
            acc = own[idx, :, r, :].astype(jnp.float32) + r1[idx, :, r, :].astype(jnp.float32)
            for k in range(3):
                acc = acc + r2[k, bx, :, r, :].astype(jnp.float32)
            s2[bx, :, r, :] = acc
        return carry

    lax.fori_loop(0, nchunk, sum2, 0)
    sb3[...] = s2[1 - xh].astype(sb3.dtype)
    cp3 = pltpu.make_async_remote_copy(
        src_ref=sb3, dst_ref=r3, send_sem=ss3.at[0], recv_sem=rs3.at[0],
        device_id=dev(m + 8 - 16 * xh), device_id_type=MESH)
    cp3.start()
    cp3.wait()
    o_ref[...] = (s2[xh] + r3[...].astype(jnp.float32)).astype(o_ref.dtype)


def hier_reduce_scatter(ta, tb):
    n = 2
    t, width = ta.shape
    w = width // 16
    bf = jnp.bfloat16
    dma = pltpu.SemaphoreType.DMA
    return pl.pallas_call(
        hier_reduce_kernel,
        out_shape=jax.ShapeDtypeStruct((n, t, w), bf),
        in_specs=[pl.BlockSpec(memory_space=pl.ANY)] * 2,
        out_specs=pl.BlockSpec(memory_space=pltpu.VMEM),
        scratch_shapes=[
            pltpu.VMEM((8, n, t, w), bf),
            pltpu.VMEM((8, n, t, w), bf),
            pltpu.VMEM((3, 2, n, t, w), bf),
            pltpu.VMEM((3, 2, n, t, w), bf),
            pltpu.VMEM((2, n, t, w), jnp.float32),
            pltpu.VMEM((n, t, w), bf),
            pltpu.VMEM((n, t, w), bf),
            dma((16,)), dma((16,)), dma((16,)), dma((3,)), dma((3,)), dma((1,)), dma((1,)),
        ],
        compiler_params=pltpu.CompilerParams(has_side_effects=True,
                                             vmem_limit_bytes=56 * 1024 * 1024),
    )(ta, tb)


def fused_gather_kernel(h_ref, g_ref, u_ref, dn_ref, gp_ref, upv_ref,
                        gf_ref, uf_ref, df_ref, io_ref, it_ref,
                        hfull, acc, wbuf, tbuf, send_sem, recv_sem, local_sem,
                        hsend, hrecv, wsem):
    ndp = 8
    nmp = 16
    d = lax.axis_index("dp")
    m = lax.axis_index("mp")
    lo = d % 2
    partner = d - lo + (1 - lo)
    nxt = (d + 2) % ndp
    prv = (d + ndp - 2) % ndp
    far = (d + 4) % ndp
    owns = (g_ref, u_ref, dn_ref)
    fulls = (gf_ref, uf_ref, df_ref)
    kr = g_ref.shape[0]
    hc = h_ref.shape[1]
    tokens = h_ref.shape[0]

    def slot(w, idx, half=None):
        if w < 2:
            if half is None:
                return fulls[w].at[pl.ds(pl.multiple_of(idx * kr, kr), kr)]
            hk = kr // 2
            return fulls[w].at[pl.ds(pl.multiple_of(idx * kr + half * hk, hk), hk)]
        rr, dc = owns[w].shape
        cols = pl.ds(pl.multiple_of(idx * dc, dc), dc)
        if half is None:
            return fulls[w].at[:, cols]
        hr = rr // 2
        return fulls[w].at[pl.ds(half * hr, hr), cols]

    def rc(w, k, src, dst, target):
        i = w * 8 + k
        return pltpu.make_async_remote_copy(
            src_ref=src, dst_ref=dst, send_sem=send_sem.at[i], recv_sem=recv_sem.at[i],
            device_id=(target, m), device_id_type=MESH)

    hmine = hfull.at[:, pl.ds(pl.multiple_of(m * hc, hc), hc)]
    hlocal = pltpu.make_async_copy(h_ref, hmine, local_sem.at[3])
    hcopies = []
    for s in range(1, nmp):
        hcopies.append(pltpu.make_async_remote_copy(
            src_ref=h_ref, dst_ref=hmine, send_sem=hsend.at[s - 1], recv_sem=hrecv.at[s - 1],
            device_id=(d, lax.rem(m + s, nmp)), device_id_type=MESH))
    locals_ = [pltpu.make_async_copy(owns[w], slot(w, d), local_sem.at[w]) for w in range(3)]
    c = {}
    for w in range(3):
        c[w, 0] = rc(w, 0, owns[w], slot(w, d), partner)
        c[w, 1] = rc(w, 1, owns[w], slot(w, d), nxt)
        c[w, 2] = rc(w, 2, owns[w], slot(w, d), prv)
        c[w, 3] = rc(w, 3, slot(w, partner), slot(w, partner), nxt)
        c[w, 4] = rc(w, 4, slot(w, partner), slot(w, partner), prv)
        c[w, 5] = rc(w, 5, slot(w, prv, 0), slot(w, prv, 0), nxt)
        c[w, 6] = rc(w, 6, slot(w, nxt, 1), slot(w, nxt, 1), prv)
        c[w, 7] = rc(w, 7, slot(w, far), slot(w, far), partner)
    for w in range(3):
        locals_[w].start()
        for k in range(3):
            c[w, k].start()
    hlocal.start()
    for cp in hcopies:
        cp.start()

    acc[...] = jnp.zeros_like(acc)
    tile = 128
    chunk = 64

    def compute_slot(idx):
        rows = pl.ds(pl.multiple_of(idx * kr, kr), kr)
        loads = [
            pltpu.make_async_copy(gf_ref.at[rows], wbuf.at[0], wsem.at[0]),
            pltpu.make_async_copy(gp_ref.at[rows], wbuf.at[1], wsem.at[1]),
            pltpu.make_async_copy(uf_ref.at[rows], wbuf.at[2], wsem.at[2]),
            pltpu.make_async_copy(upv_ref.at[rows], wbuf.at[3], wsem.at[3]),
        ]
        for ld in loads:
            ld.start()
        for ld in loads:
            ld.wait()

        def mix(i, carry):
            r = pl.ds(pl.multiple_of(i * chunk, chunk), chunk)
            for j in range(2):
                on = wbuf[2 * j, r, :].astype(jnp.float32)
                pv = wbuf[2 * j + 1, r, :].astype(jnp.float32)
                tbuf[j, r, :] = (POLYAK * on + (1.0 - POLYAK) * pv).astype(tbuf.dtype)
            return carry

        lax.fori_loop(0, kr // chunk, mix, 0)
        hcols = pl.ds(pl.multiple_of(idx * kr, kr), kr)

        def mm(i, carry):
            r = pl.ds(pl.multiple_of(i * tile, tile), tile)
            hs = hfull[r, hcols]
            f32 = jnp.float32
            acc[0, r, :] += jnp.dot(hs, wbuf[0], preferred_element_type=f32)
            acc[1, r, :] += jnp.dot(hs, tbuf[0], preferred_element_type=f32)
            acc[2, r, :] += jnp.dot(hs, wbuf[2], preferred_element_type=f32)
            acc[3, r, :] += jnp.dot(hs, tbuf[1], preferred_element_type=f32)
            return carry

        lax.fori_loop(0, tokens // tile, mm, 0)

    hlocal.wait()
    for cp in hcopies:
        cp.wait_recv()
    for w in range(3):
        locals_[w].wait()
    compute_slot(d)
    for w in range(3):
        c[w, 0].wait_recv()
        c[w, 3].start()
        c[w, 4].start()
        c[w, 1].wait_recv()
        c[w, 5].start()
        c[w, 2].wait_recv()
        c[w, 6].start()
    compute_slot(partner)
    compute_slot(prv)
    compute_slot(nxt)
    for w in range(3):
        c[w, 5].wait_recv()
        c[w, 6].wait_recv()
        c[w, 7].start()
    compute_slot(far)
    for w in range(3):
        for k in (3, 4, 7):
            c[w, k].wait_recv()
    compute_slot((partner + 2) % ndp)
    compute_slot((partner + ndp - 2) % ndp)
    compute_slot((partner + 4) % ndp)
    for w in range(3):
        for k in range(8):
            c[w, k].wait_send()
    for cp in hcopies:
        cp.wait_send()

    def finish(i, carry):
        r = pl.ds(pl.multiple_of(i * chunk, chunk), chunk)
        io_ref[r, :] = (jax.nn.silu(acc[0, r, :]) * acc[2, r, :]).astype(io_ref.dtype)
        it_ref[r, :] = (jax.nn.silu(acc[1, r, :]) * acc[3, r, :]).astype(it_ref.dtype)
        return carry

    lax.fori_loop(0, tokens // chunk, finish, 0)


def fused_gather(h, g, u, dn, gp, upv):
    ndp, nmp = 8, 16
    any_spec = pl.BlockSpec(memory_space=pl.ANY)
    tokens, ff = h.shape[0], g.shape[1]
    bf = jnp.bfloat16
    dma = pltpu.SemaphoreType.DMA
    out_shape = (
        jax.ShapeDtypeStruct((g.shape[0] * ndp, ff), g.dtype),
        jax.ShapeDtypeStruct((u.shape[0] * ndp, ff), u.dtype),
        jax.ShapeDtypeStruct((dn.shape[0], dn.shape[1] * ndp), dn.dtype),
        jax.ShapeDtypeStruct((tokens, ff), bf),
        jax.ShapeDtypeStruct((tokens, ff), bf),
    )
    vspec = pl.BlockSpec(memory_space=pltpu.VMEM)
    return pl.pallas_call(
        fused_gather_kernel,
        out_shape=out_shape,
        in_specs=[any_spec] * 6,
        out_specs=[any_spec] * 3 + [vspec] * 2,
        scratch_shapes=[
            pltpu.VMEM((tokens, h.shape[1] * nmp), bf),
            pltpu.VMEM((4, tokens, ff), jnp.float32),
            pltpu.VMEM((4, g.shape[0], ff), bf),
            pltpu.VMEM((2, g.shape[0], ff), bf),
            dma((24,)), dma((24,)), dma((4,)), dma((nmp - 1,)), dma((nmp - 1,)), dma((4,)),
        ],
        compiler_params=pltpu.CompilerParams(has_side_effects=True,
                                             vmem_limit_bytes=56 * 1024 * 1024),
    )(h, g, u, dn, gp, upv)


def local(ndp, nmp, hidden_states, gate_online, up_online, down_online, gate_previous,
          up_previous, down_previous):
    if ndp == 8 and nmp == 16:
        _, _, down_full, inner_o, inner_t = fused_gather(
            hidden_states, gate_online, up_online, down_online, gate_previous, up_previous)
    else:
        features_all = lax.all_gather(hidden_states, "mp", axis=1, tiled=True)
        gate_full, up_full, down_full = gather_weights(gate_online, up_online, down_online, ndp)

        def pair(piece, previous):
            target_piece = blend(piece, previous)
            o = jnp.dot(features_all, piece, preferred_element_type=jnp.float32)
            t = jnp.dot(features_all, target_piece, preferred_element_type=jnp.float32)
            return o, t

        gate_o, gate_t = pair(gate_full, gate_previous)
        up_o, up_t = pair(up_full, up_previous)
        inner_o = (jax.nn.silu(gate_o) * up_o).astype(jnp.bfloat16)
        inner_t = (jax.nn.silu(gate_t) * up_t).astype(jnp.bfloat16)
    target_down = blend(down_full, down_previous)
    online_part = jnp.dot(inner_o, down_full, preferred_element_type=jnp.float32)
    target_part = jnp.dot(inner_t, target_down, preferred_element_type=jnp.float32)
    if nmp == 16:
        result = hier_reduce_scatter(online_part.astype(jnp.bfloat16),
                                     target_part.astype(jnp.bfloat16))
    else:
        terms = jnp.stack([online_part, target_part], axis=0).astype(jnp.bfloat16)
        result = reduce_scatter(terms, nmp)
    return (result[0], result[1])


def solution(mesh):
    ndp = mesh.shape["dp"]
    nmp = mesh.shape["mp"]
    in_specs = (
        P("dp", "mp"),
        P("dp", "mp"),
        P("dp", "mp"),
        P("mp", "dp"),
        P(None, "mp"),
        P(None, "mp"),
        P("mp", None),
    )
    out_specs = (P("dp", "mp"), P("dp", "mp"))
    return jax.shard_map(functools.partial(local, ndp, nmp), mesh=mesh, in_specs=in_specs,
                         out_specs=out_specs, check_vma=False)
```

```python
import functools

import jax
import jax.numpy as jnp
from jax import lax
from jax.experimental import pallas as pl
from jax.experimental.pallas import tpu as pltpu
from jax.sharding import PartitionSpec as P

POLYAK = 0.25
MESH = pl.DeviceIdType.MESH


def blend(online, previous):
    return (
        POLYAK * online.astype(jnp.float32) + (1.0 - POLYAK) * previous.astype(jnp.float32)
    ).astype(jnp.bfloat16)


def gather_kernel(ndp, g_ref, u_ref, dn_ref, gf_ref, uf_ref, df_ref, send_sem, recv_sem,
                  local_sem):
    d = lax.axis_index("dp")
    m = lax.axis_index("mp")
    kr = g_ref.shape[0]
    dc = dn_ref.shape[1]
    rows = pl.ds(pl.multiple_of(d * kr, kr), kr)
    cols = pl.ds(pl.multiple_of(d * dc, dc), dc)

    locals_ = [
        pltpu.make_async_copy(g_ref, gf_ref.at[rows], local_sem.at[0]),
        pltpu.make_async_copy(u_ref, uf_ref.at[rows], local_sem.at[1]),
        pltpu.make_async_copy(dn_ref, df_ref.at[:, cols], local_sem.at[2]),
    ]
    for c in locals_:
        c.start()

    copies = []
    k = 0
    for s in range(1, ndp):
        peer = lax.rem(d + s, ndp)
        for src, dst in ((g_ref, gf_ref.at[rows]), (u_ref, uf_ref.at[rows]),
                         (dn_ref, df_ref.at[:, cols])):
            copies.append(pltpu.make_async_remote_copy(
                src_ref=src, dst_ref=dst, send_sem=send_sem.at[k], recv_sem=recv_sem.at[k],
                device_id=(peer, m), device_id_type=MESH))
            k += 1
    for c in copies:
        c.start()
    for c in locals_:
        c.wait()
    for c in copies:
        c.wait()


def gather_weights_direct(g, u, dn, ndp):
    n_copies = 3 * (ndp - 1)
    any_spec = pl.BlockSpec(memory_space=pl.ANY)
    out_shape = (
        jax.ShapeDtypeStruct((g.shape[0] * ndp, g.shape[1]), g.dtype),
        jax.ShapeDtypeStruct((u.shape[0] * ndp, u.shape[1]), u.dtype),
        jax.ShapeDtypeStruct((dn.shape[0], dn.shape[1] * ndp), dn.dtype),
    )
    return pl.pallas_call(
        functools.partial(gather_kernel, ndp),
        out_shape=out_shape,
        in_specs=[any_spec] * 3,
        out_specs=[any_spec] * 3,
        scratch_shapes=[
            pltpu.SemaphoreType.DMA((n_copies,)),
            pltpu.SemaphoreType.DMA((n_copies,)),
            pltpu.SemaphoreType.DMA((3,)),
        ],
        compiler_params=pltpu.CompilerParams(has_side_effects=True),
    )(g, u, dn)


def relay_gather_kernel(g_ref, u_ref, dn_ref, gf_ref, uf_ref, df_ref, send_sem, recv_sem,
                        local_sem):
    ndp = 8
    d = lax.axis_index("dp")
    m = lax.axis_index("mp")
    lo = d % 2
    partner = d - lo + (1 - lo)
    nxt = (d + 2) % ndp
    prv = (d + ndp - 2) % ndp
    far = (d + 4) % ndp
    owns = (g_ref, u_ref, dn_ref)
    fulls = (gf_ref, uf_ref, df_ref)

    def slot(w, idx, half=None):
        if w < 2:
            kr = owns[w].shape[0]
            if half is None:
                return fulls[w].at[pl.ds(pl.multiple_of(idx * kr, kr), kr)]
            hk = kr // 2
            return fulls[w].at[pl.ds(pl.multiple_of(idx * kr + half * hk, hk), hk)]
        rr, dc = owns[w].shape
        cols = pl.ds(pl.multiple_of(idx * dc, dc), dc)
        if half is None:
            return fulls[w].at[:, cols]
        hr = rr // 2
        return fulls[w].at[pl.ds(half * hr, hr), cols]

    def rc(w, k, src, dst, target):
        i = w * 8 + k
        return pltpu.make_async_remote_copy(
            src_ref=src, dst_ref=dst, send_sem=send_sem.at[i], recv_sem=recv_sem.at[i],
            device_id=(target, m), device_id_type=MESH)

    locals_ = [pltpu.make_async_copy(owns[w], slot(w, d), local_sem.at[w]) for w in range(3)]
    c = {}
    for w in range(3):
        c[w, 0] = rc(w, 0, owns[w], slot(w, d), partner)
        c[w, 1] = rc(w, 1, owns[w], slot(w, d), nxt)
        c[w, 2] = rc(w, 2, owns[w], slot(w, d), prv)
        c[w, 3] = rc(w, 3, slot(w, partner), slot(w, partner), nxt)
        c[w, 4] = rc(w, 4, slot(w, partner), slot(w, partner), prv)
        c[w, 5] = rc(w, 5, slot(w, prv, 0), slot(w, prv, 0), nxt)
        c[w, 6] = rc(w, 6, slot(w, nxt, 1), slot(w, nxt, 1), prv)
        c[w, 7] = rc(w, 7, slot(w, far), slot(w, far), partner)
    for w in range(3):
        locals_[w].start()
        for k in range(3):
            c[w, k].start()
    for w in range(3):
        c[w, 0].wait_recv()
        c[w, 3].start()
        c[w, 4].start()
        c[w, 1].wait_recv()
        c[w, 5].start()
        c[w, 2].wait_recv()
        c[w, 6].start()
    for w in range(3):
        c[w, 5].wait_recv()
        c[w, 6].wait_recv()
        c[w, 7].start()
    for w in range(3):
        for k in (3, 4, 7):
            c[w, k].wait_recv()
    for w in range(3):
        for k in range(8):
            c[w, k].wait_send()
        locals_[w].wait()


def gather_weights(g, u, dn, ndp):
    if ndp != 8:
        return gather_weights_direct(g, u, dn, ndp)
    any_spec = pl.BlockSpec(memory_space=pl.ANY)
    out_shape = (
        jax.ShapeDtypeStruct((g.shape[0] * ndp, g.shape[1]), g.dtype),
        jax.ShapeDtypeStruct((u.shape[0] * ndp, u.shape[1]), u.dtype),
        jax.ShapeDtypeStruct((dn.shape[0], dn.shape[1] * ndp), dn.dtype),
    )
    return pl.pallas_call(
        relay_gather_kernel,
        out_shape=out_shape,
        in_specs=[any_spec] * 3,
        out_specs=[any_spec] * 3,
        scratch_shapes=[
            pltpu.SemaphoreType.DMA((24,)),
            pltpu.SemaphoreType.DMA((24,)),
            pltpu.SemaphoreType.DMA((3,)),
        ],
        compiler_params=pltpu.CompilerParams(has_side_effects=True),
    )(g, u, dn)


def reduce_kernel(nmp, t_ref, o_ref, buf, send_sem, recv_sem, local_sem):
    d = lax.axis_index("dp")
    m = lax.axis_index("mp")
    w = o_ref.shape[2]
    mine = pl.ds(pl.multiple_of(m * w, w), w)
    local_copy = pltpu.make_async_copy(t_ref.at[:, :, mine], buf.at[0], local_sem.at[0])
    local_copy.start()
    copies = []
    for s in range(1, nmp):
        peer = lax.rem(m + s, nmp)
        theirs = pl.ds(pl.multiple_of(peer * w, w), w)
        copies.append(pltpu.make_async_remote_copy(
            src_ref=t_ref.at[:, :, theirs], dst_ref=buf.at[s], send_sem=send_sem.at[s],
            recv_sem=recv_sem.at[s], device_id=(d, peer), device_id_type=MESH))
    for c in copies:
        c.start()
    local_copy.wait()
    for c in copies:
        c.wait()
    rows = 32

    def body(i, carry):
        r = pl.ds(pl.multiple_of(i * rows, rows), rows)
        for k in range(o_ref.shape[0]):
            acc = buf[0, k, r, :].astype(jnp.float32)
            for s in range(1, nmp):
                acc = acc + buf[s, k, r, :].astype(jnp.float32)
            o_ref[k, r, :] = acc.astype(o_ref.dtype)
        return carry

    lax.fori_loop(0, o_ref.shape[1] // rows, body, 0)


def reduce_scatter(terms, nmp):
    n, t, width = terms.shape
    w = width // nmp
    return pl.pallas_call(
        functools.partial(reduce_kernel, nmp),
        out_shape=jax.ShapeDtypeStruct((n, t, w), jnp.bfloat16),
        in_specs=[pl.BlockSpec(memory_space=pl.ANY)],
        out_specs=pl.BlockSpec(memory_space=pltpu.VMEM),
        scratch_shapes=[
            pltpu.VMEM((nmp, n, t, w), jnp.bfloat16),
            pltpu.SemaphoreType.DMA((nmp,)),
            pltpu.SemaphoreType.DMA((nmp,)),
            pltpu.SemaphoreType.DMA((1,)),
        ],
        compiler_params=pltpu.CompilerParams(has_side_effects=True,
                                             vmem_limit_bytes=48 * 1024 * 1024),
    )(terms)


def hier_reduce_kernel(ta_ref, tb_ref, o_ref, own, r1, sb2, r2, s2, sb3, r3,
                       ls, ss1, rs1, ss2, rs2, ss3, rs3):
    d = lax.axis_index("dp")
    m = lax.axis_index("mp")
    c = m % 2
    z = (m // 2) % 4
    xh = m // 8
    w = o_ref.shape[2]
    rows = 32
    nchunk = o_ref.shape[1] // rows

    def blk(b, k):
        return (ta_ref, tb_ref)[k].at[:, pl.ds(pl.multiple_of(b * w, w), w)]

    def dev(mm):
        return (d, mm)

    locs = []
    st1 = []
    for j in range(16):
        bx, bz, k = j // 8, (j // 2) % 4, j % 2
        jj = bx * 4 + bz
        locs.append(pltpu.make_async_copy(blk(bx * 8 + bz * 2 + c, k), own.at[jj, k],
                                          ls.at[j]))
        st1.append(pltpu.make_async_remote_copy(
            src_ref=blk(bx * 8 + bz * 2 + (1 - c), k), dst_ref=r1.at[jj, k], send_sem=ss1.at[j],
            recv_sem=rs1.at[j], device_id=dev(m + 1 - 2 * c), device_id_type=MESH))
    for j in range(16):
        st1[j].start()
        locs[j].start()
    for j in range(16):
        locs[j].wait()
        st1[j].wait()

    st2 = []
    for s in range(1, 4):
        zt = (z + s) % 4

        def fill(i, carry, s=s, zt=zt):
            r = pl.ds(pl.multiple_of(i * rows, rows), rows)
            for bx in range(2):
                idx = bx * 4 + zt
                sb2[s - 1, bx, :, r, :] = (own[idx, :, r, :].astype(jnp.float32)
                                           + r1[idx, :, r, :].astype(jnp.float32)
                                           ).astype(sb2.dtype)
            return carry

        lax.fori_loop(0, nchunk, fill, 0)
        cp = pltpu.make_async_remote_copy(
            src_ref=sb2.at[s - 1], dst_ref=r2.at[s - 1], send_sem=ss2.at[s - 1],
            recv_sem=rs2.at[s - 1], device_id=dev(xh * 8 + zt * 2 + c), device_id_type=MESH)
        cp.start()
        st2.append(cp)
    for cp in st2:
        cp.wait()

    def sum2(i, carry):
        r = pl.ds(pl.multiple_of(i * rows, rows), rows)
        for bx in range(2):
            idx = bx * 4 + z
            acc = own[idx, :, r, :].astype(jnp.float32) + r1[idx, :, r, :].astype(jnp.float32)
            for k in range(3):
                acc = acc + r2[k, bx, :, r, :].astype(jnp.float32)
            s2[bx, :, r, :] = acc
        return carry

    lax.fori_loop(0, nchunk, sum2, 0)
    sb3[...] = s2[1 - xh].astype(sb3.dtype)
    cp3 = pltpu.make_async_remote_copy(
        src_ref=sb3, dst_ref=r3, send_sem=ss3.at[0], recv_sem=rs3.at[0],
        device_id=dev(m + 8 - 16 * xh), device_id_type=MESH)
    cp3.start()
    cp3.wait()
    o_ref[...] = (s2[xh] + r3[...].astype(jnp.float32)).astype(o_ref.dtype)


def hier_reduce_scatter(ta, tb):
    n = 2
    t, width = ta.shape
    w = width // 16
    bf = jnp.bfloat16
    dma = pltpu.SemaphoreType.DMA
    return pl.pallas_call(
        hier_reduce_kernel,
        out_shape=jax.ShapeDtypeStruct((n, t, w), bf),
        in_specs=[pl.BlockSpec(memory_space=pl.ANY)] * 2,
        out_specs=pl.BlockSpec(memory_space=pltpu.VMEM),
        scratch_shapes=[
            pltpu.VMEM((8, n, t, w), bf),
            pltpu.VMEM((8, n, t, w), bf),
            pltpu.VMEM((3, 2, n, t, w), bf),
            pltpu.VMEM((3, 2, n, t, w), bf),
            pltpu.VMEM((2, n, t, w), jnp.float32),
            pltpu.VMEM((n, t, w), bf),
            pltpu.VMEM((n, t, w), bf),
            dma((16,)), dma((16,)), dma((16,)), dma((3,)), dma((3,)), dma((1,)), dma((1,)),
        ],
        compiler_params=pltpu.CompilerParams(has_side_effects=True,
                                             vmem_limit_bytes=56 * 1024 * 1024),
    )(ta, tb)


def local(ndp, nmp, hidden_states, gate_online, up_online, down_online, gate_previous,
          up_previous, down_previous):
    features_all = lax.all_gather(hidden_states, "mp", axis=1, tiled=True)
    gate_full, up_full, down_full = gather_weights(gate_online, up_online, down_online, ndp)

    def pair(piece, previous):
        target_piece = blend(piece, previous)
        o = jnp.dot(features_all, piece, preferred_element_type=jnp.float32)
        t = jnp.dot(features_all, target_piece, preferred_element_type=jnp.float32)
        return o, t

    gate_o, gate_t = pair(gate_full, gate_previous)
    up_o, up_t = pair(up_full, up_previous)
    inner_o = (jax.nn.silu(gate_o) * up_o).astype(jnp.bfloat16)
    inner_t = (jax.nn.silu(gate_t) * up_t).astype(jnp.bfloat16)
    inner_o, inner_t = lax.optimization_barrier((inner_o, inner_t))
    target_down = blend(down_full, down_previous)
    online_part = jnp.dot(inner_o, down_full, preferred_element_type=jnp.float32)
    target_part = jnp.dot(inner_t, target_down, preferred_element_type=jnp.float32)
    if nmp == 16:
        result = hier_reduce_scatter(online_part.astype(jnp.bfloat16),
                                     target_part.astype(jnp.bfloat16))
    else:
        terms = jnp.stack([online_part, target_part], axis=0).astype(jnp.bfloat16)
        result = reduce_scatter(terms, nmp)
    return (result[0], result[1])


def solution(mesh):
    ndp = mesh.shape["dp"]
    nmp = mesh.shape["mp"]
    in_specs = (
        P("dp", "mp"),
        P("dp", "mp"),
        P("dp", "mp"),
        P("mp", "dp"),
        P(None, "mp"),
        P(None, "mp"),
        P("mp", None),
    )
    out_specs = (P("dp", "mp"), P("dp", "mp"))
    return jax.shard_map(functools.partial(local, ndp, nmp), mesh=mesh, in_specs=in_specs,
                         out_specs=out_specs, check_vma=False)
```

```python
import functools

import jax
import jax.numpy as jnp
from jax import lax
from jax.experimental import pallas as pl
from jax.experimental.pallas import tpu as pltpu
from jax.sharding import PartitionSpec as P

POLYAK = 0.25
MESH = pl.DeviceIdType.MESH


def blend(online, previous):
    return (
        POLYAK * online.astype(jnp.float32) + (1.0 - POLYAK) * previous.astype(jnp.float32)
    ).astype(jnp.bfloat16)


def gather_kernel(ndp, g_ref, u_ref, dn_ref, gf_ref, uf_ref, df_ref, send_sem, recv_sem,
                  local_sem):
    d = lax.axis_index("dp")
    m = lax.axis_index("mp")
    kr = g_ref.shape[0]
    dc = dn_ref.shape[1]
    rows = pl.ds(pl.multiple_of(d * kr, kr), kr)
    cols = pl.ds(pl.multiple_of(d * dc, dc), dc)

    locals_ = [
        pltpu.make_async_copy(g_ref, gf_ref.at[rows], local_sem.at[0]),
        pltpu.make_async_copy(u_ref, uf_ref.at[rows], local_sem.at[1]),
        pltpu.make_async_copy(dn_ref, df_ref.at[:, cols], local_sem.at[2]),
    ]
    for c in locals_:
        c.start()

    copies = []
    k = 0
    for s in range(1, ndp):
        peer = lax.rem(d + s, ndp)
        for src, dst in ((g_ref, gf_ref.at[rows]), (u_ref, uf_ref.at[rows]),
                         (dn_ref, df_ref.at[:, cols])):
            copies.append(pltpu.make_async_remote_copy(
                src_ref=src, dst_ref=dst, send_sem=send_sem.at[k], recv_sem=recv_sem.at[k],
                device_id=(peer, m), device_id_type=MESH))
            k += 1
    for c in copies:
        c.start()
    for c in locals_:
        c.wait()
    for c in copies:
        c.wait()


def gather_weights_direct(g, u, dn, ndp):
    n_copies = 3 * (ndp - 1)
    any_spec = pl.BlockSpec(memory_space=pl.ANY)
    out_shape = (
        jax.ShapeDtypeStruct((g.shape[0] * ndp, g.shape[1]), g.dtype),
        jax.ShapeDtypeStruct((u.shape[0] * ndp, u.shape[1]), u.dtype),
        jax.ShapeDtypeStruct((dn.shape[0], dn.shape[1] * ndp), dn.dtype),
    )
    return pl.pallas_call(
        functools.partial(gather_kernel, ndp),
        out_shape=out_shape,
        in_specs=[any_spec] * 3,
        out_specs=[any_spec] * 3,
        scratch_shapes=[
            pltpu.SemaphoreType.DMA((n_copies,)),
            pltpu.SemaphoreType.DMA((n_copies,)),
            pltpu.SemaphoreType.DMA((3,)),
        ],
        compiler_params=pltpu.CompilerParams(has_side_effects=True),
    )(g, u, dn)


def relay_gather_kernel(h_ref, g_ref, u_ref, dn_ref, hf_ref, gf_ref, uf_ref, df_ref, send_sem,
                        recv_sem, local_sem, hsend, hrecv):
    ndp = 8
    d = lax.axis_index("dp")
    m = lax.axis_index("mp")
    lo = d % 2
    partner = d - lo + (1 - lo)
    nxt = (d + 2) % ndp
    prv = (d + ndp - 2) % ndp
    far = (d + 4) % ndp
    owns = (g_ref, u_ref, dn_ref)
    fulls = (gf_ref, uf_ref, df_ref)

    def slot(w, idx, half=None):
        if w < 2:
            kr = owns[w].shape[0]
            if half is None:
                return fulls[w].at[pl.ds(pl.multiple_of(idx * kr, kr), kr)]
            hk = kr // 2
            return fulls[w].at[pl.ds(pl.multiple_of(idx * kr + half * hk, hk), hk)]
        rr, dc = owns[w].shape
        cols = pl.ds(pl.multiple_of(idx * dc, dc), dc)
        if half is None:
            return fulls[w].at[:, cols]
        hr = rr // 2
        return fulls[w].at[pl.ds(half * hr, hr), cols]

    def rc(w, k, src, dst, target):
        i = w * 8 + k
        return pltpu.make_async_remote_copy(
            src_ref=src, dst_ref=dst, send_sem=send_sem.at[i], recv_sem=recv_sem.at[i],
            device_id=(target, m), device_id_type=MESH)

    locals_ = [pltpu.make_async_copy(owns[w], slot(w, d), local_sem.at[w]) for w in range(3)]
    c = {}
    for w in range(3):
        c[w, 0] = rc(w, 0, owns[w], slot(w, d), partner)
        c[w, 1] = rc(w, 1, owns[w], slot(w, d), nxt)
        c[w, 2] = rc(w, 2, owns[w], slot(w, d), prv)
        c[w, 3] = rc(w, 3, slot(w, partner), slot(w, partner), nxt)
        c[w, 4] = rc(w, 4, slot(w, partner), slot(w, partner), prv)
        c[w, 5] = rc(w, 5, slot(w, prv, 0), slot(w, prv, 0), nxt)
        c[w, 6] = rc(w, 6, slot(w, nxt, 1), slot(w, nxt, 1), prv)
        c[w, 7] = rc(w, 7, slot(w, far), slot(w, far), partner)
    nmp = 16
    hc = h_ref.shape[1]
    hmine = hf_ref.at[:, pl.ds(pl.multiple_of(m * hc, hc), hc)]
    hlocal = pltpu.make_async_copy(h_ref, hmine, local_sem.at[3])
    hcopies = []
    for s in range(1, nmp):
        hcopies.append(pltpu.make_async_remote_copy(
            src_ref=h_ref, dst_ref=hmine, send_sem=hsend.at[s - 1], recv_sem=hrecv.at[s - 1],
            device_id=(d, lax.rem(m + s, nmp)), device_id_type=MESH))
    for w in range(3):
        locals_[w].start()
        for k in range(3):
            c[w, k].start()
    hlocal.start()
    for cp in hcopies:
        cp.start()
    for w in range(3):
        c[w, 0].wait_recv()
        c[w, 3].start()
        c[w, 4].start()
        c[w, 1].wait_recv()
        c[w, 5].start()
        c[w, 2].wait_recv()
        c[w, 6].start()
    for w in range(3):
        c[w, 5].wait_recv()
        c[w, 6].wait_recv()
        c[w, 7].start()
    for w in range(3):
        for k in (3, 4, 7):
            c[w, k].wait_recv()
    for w in range(3):
        for k in range(8):
            c[w, k].wait_send()
        locals_[w].wait()
    hlocal.wait()
    for cp in hcopies:
        cp.wait()


def gather_relay(h, g, u, dn, ndp):
    any_spec = pl.BlockSpec(memory_space=pl.ANY)
    out_shape = (
        jax.ShapeDtypeStruct((g.shape[0] * ndp, g.shape[1]), g.dtype),
        jax.ShapeDtypeStruct((u.shape[0] * ndp, u.shape[1]), u.dtype),
        jax.ShapeDtypeStruct((dn.shape[0], dn.shape[1] * ndp), dn.dtype),
    )
    return pl.pallas_call(
        relay_gather_kernel,
        out_shape=(jax.ShapeDtypeStruct((h.shape[0], h.shape[1] * 16), h.dtype),) + out_shape,
        in_specs=[any_spec] * 4,
        out_specs=[any_spec] * 4,
        scratch_shapes=[
            pltpu.SemaphoreType.DMA((24,)),
            pltpu.SemaphoreType.DMA((24,)),
            pltpu.SemaphoreType.DMA((4,)),
            pltpu.SemaphoreType.DMA((15,)),
            pltpu.SemaphoreType.DMA((15,)),
        ],
        compiler_params=pltpu.CompilerParams(has_side_effects=True),
    )(h, g, u, dn)


def reduce_kernel(nmp, t_ref, o_ref, buf, send_sem, recv_sem, local_sem):
    d = lax.axis_index("dp")
    m = lax.axis_index("mp")
    w = o_ref.shape[2]
    mine = pl.ds(pl.multiple_of(m * w, w), w)
    local_copy = pltpu.make_async_copy(t_ref.at[:, :, mine], buf.at[0], local_sem.at[0])
    local_copy.start()
    copies = []
    for s in range(1, nmp):
        peer = lax.rem(m + s, nmp)
        theirs = pl.ds(pl.multiple_of(peer * w, w), w)
        copies.append(pltpu.make_async_remote_copy(
            src_ref=t_ref.at[:, :, theirs], dst_ref=buf.at[s], send_sem=send_sem.at[s],
            recv_sem=recv_sem.at[s], device_id=(d, peer), device_id_type=MESH))
    for c in copies:
        c.start()
    local_copy.wait()
    for c in copies:
        c.wait()
    rows = 32

    def body(i, carry):
        r = pl.ds(pl.multiple_of(i * rows, rows), rows)
        for k in range(o_ref.shape[0]):
            acc = buf[0, k, r, :].astype(jnp.float32)
            for s in range(1, nmp):
                acc = acc + buf[s, k, r, :].astype(jnp.float32)
            o_ref[k, r, :] = acc.astype(o_ref.dtype)
        return carry

    lax.fori_loop(0, o_ref.shape[1] // rows, body, 0)


def reduce_scatter(terms, nmp):
    n, t, width = terms.shape
    w = width // nmp
    return pl.pallas_call(
        functools.partial(reduce_kernel, nmp),
        out_shape=jax.ShapeDtypeStruct((n, t, w), jnp.bfloat16),
        in_specs=[pl.BlockSpec(memory_space=pl.ANY)],
        out_specs=pl.BlockSpec(memory_space=pltpu.VMEM),
        scratch_shapes=[
            pltpu.VMEM((nmp, n, t, w), jnp.bfloat16),
            pltpu.SemaphoreType.DMA((nmp,)),
            pltpu.SemaphoreType.DMA((nmp,)),
            pltpu.SemaphoreType.DMA((1,)),
        ],
        compiler_params=pltpu.CompilerParams(has_side_effects=True,
                                             vmem_limit_bytes=48 * 1024 * 1024),
    )(terms)


def hier_reduce_kernel(ta_ref, tb_ref, o_ref, own, r1, sb2, r2, s2, sb3, r3,
                       ls, ss1, rs1, ss2, rs2, ss3, rs3):
    d = lax.axis_index("dp")
    m = lax.axis_index("mp")
    c = m % 2
    z = (m // 2) % 4
    xh = m // 8
    w = o_ref.shape[2]
    rows = 32
    nchunk = o_ref.shape[1] // rows

    def blk(b, k):
        return (ta_ref, tb_ref)[k].at[:, pl.ds(pl.multiple_of(b * w, w), w)]

    def dev(mm):
        return (d, mm)

    locs = []
    st1 = []
    for j in range(16):
        bx, bz, k = j // 8, (j // 2) % 4, j % 2
        jj = bx * 4 + bz
        locs.append(pltpu.make_async_copy(blk(bx * 8 + bz * 2 + c, k), own.at[jj, k],
                                          ls.at[j]))
        st1.append(pltpu.make_async_remote_copy(
            src_ref=blk(bx * 8 + bz * 2 + (1 - c), k), dst_ref=r1.at[jj, k], send_sem=ss1.at[j],
            recv_sem=rs1.at[j], device_id=dev(m + 1 - 2 * c), device_id_type=MESH))
    for j in range(16):
        st1[j].start()
        locs[j].start()
    for j in range(16):
        locs[j].wait()
        st1[j].wait()

    st2 = []
    for s in range(1, 4):
        zt = (z + s) % 4

        def fill(i, carry, s=s, zt=zt):
            r = pl.ds(pl.multiple_of(i * rows, rows), rows)
            for bx in range(2):
                idx = bx * 4 + zt
                sb2[s - 1, bx, :, r, :] = (own[idx, :, r, :].astype(jnp.float32)
                                           + r1[idx, :, r, :].astype(jnp.float32)
                                           ).astype(sb2.dtype)
            return carry

        lax.fori_loop(0, nchunk, fill, 0)
        cp = pltpu.make_async_remote_copy(
            src_ref=sb2.at[s - 1], dst_ref=r2.at[s - 1], send_sem=ss2.at[s - 1],
            recv_sem=rs2.at[s - 1], device_id=dev(xh * 8 + zt * 2 + c), device_id_type=MESH)
        cp.start()
        st2.append(cp)
    for cp in st2:
        cp.wait()

    def sum2(i, carry):
        r = pl.ds(pl.multiple_of(i * rows, rows), rows)
        for bx in range(2):
            idx = bx * 4 + z
            acc = own[idx, :, r, :].astype(jnp.float32) + r1[idx, :, r, :].astype(jnp.float32)
            for k in range(3):
                acc = acc + r2[k, bx, :, r, :].astype(jnp.float32)
            s2[bx, :, r, :] = acc
        return carry

    lax.fori_loop(0, nchunk, sum2, 0)
    sb3[...] = s2[1 - xh].astype(sb3.dtype)
    cp3 = pltpu.make_async_remote_copy(
        src_ref=sb3, dst_ref=r3, send_sem=ss3.at[0], recv_sem=rs3.at[0],
        device_id=dev(m + 8 - 16 * xh), device_id_type=MESH)
    cp3.start()
    cp3.wait()
    o_ref[...] = (s2[xh] + r3[...].astype(jnp.float32)).astype(o_ref.dtype)


def hier_reduce_scatter(ta, tb):
    n = 2
    t, width = ta.shape
    w = width // 16
    bf = jnp.bfloat16
    dma = pltpu.SemaphoreType.DMA
    return pl.pallas_call(
        hier_reduce_kernel,
        out_shape=jax.ShapeDtypeStruct((n, t, w), bf),
        in_specs=[pl.BlockSpec(memory_space=pl.ANY)] * 2,
        out_specs=pl.BlockSpec(memory_space=pltpu.VMEM),
        scratch_shapes=[
            pltpu.VMEM((8, n, t, w), bf),
            pltpu.VMEM((8, n, t, w), bf),
            pltpu.VMEM((3, 2, n, t, w), bf),
            pltpu.VMEM((3, 2, n, t, w), bf),
            pltpu.VMEM((2, n, t, w), jnp.float32),
            pltpu.VMEM((n, t, w), bf),
            pltpu.VMEM((n, t, w), bf),
            dma((16,)), dma((16,)), dma((16,)), dma((3,)), dma((3,)), dma((1,)), dma((1,)),
        ],
        compiler_params=pltpu.CompilerParams(has_side_effects=True,
                                             vmem_limit_bytes=56 * 1024 * 1024),
    )(ta, tb)


def local(ndp, nmp, hidden_states, gate_online, up_online, down_online, gate_previous,
          up_previous, down_previous):
    if ndp == 8 and nmp == 16:
        features_all, gate_full, up_full, down_full = gather_relay(
            hidden_states, gate_online, up_online, down_online, ndp)
    else:
        features_all = lax.all_gather(hidden_states, "mp", axis=1, tiled=True)
        gate_full, up_full, down_full = gather_weights_direct(gate_online, up_online,
                                                              down_online, ndp)

    def pair(piece, previous):
        target_piece = blend(piece, previous)
        o = jnp.dot(features_all, piece, preferred_element_type=jnp.float32)
        t = jnp.dot(features_all, target_piece, preferred_element_type=jnp.float32)
        return o, t

    gate_o, gate_t = pair(gate_full, gate_previous)
    up_o, up_t = pair(up_full, up_previous)
    inner_o = (jax.nn.silu(gate_o) * up_o).astype(jnp.bfloat16)
    inner_t = (jax.nn.silu(gate_t) * up_t).astype(jnp.bfloat16)
    inner_o, inner_t = lax.optimization_barrier((inner_o, inner_t))
    target_down = blend(down_full, down_previous)
    online_part = jnp.dot(inner_o, down_full, preferred_element_type=jnp.float32)
    target_part = jnp.dot(inner_t, target_down, preferred_element_type=jnp.float32)
    if nmp == 16:
        result = hier_reduce_scatter(online_part.astype(jnp.bfloat16),
                                     target_part.astype(jnp.bfloat16))
    else:
        terms = jnp.stack([online_part, target_part], axis=0).astype(jnp.bfloat16)
        result = reduce_scatter(terms, nmp)
    return (result[0], result[1])


def solution(mesh):
    ndp = mesh.shape["dp"]
    nmp = mesh.shape["mp"]
    in_specs = (
        P("dp", "mp"),
        P("dp", "mp"),
        P("dp", "mp"),
        P("mp", "dp"),
        P(None, "mp"),
        P(None, "mp"),
        P("mp", None),
    )
    out_specs = (P("dp", "mp"), P("dp", "mp"))
    return jax.shard_map(functools.partial(local, ndp, nmp), mesh=mesh, in_specs=in_specs,
                         out_specs=out_specs, check_vma=False)
```

```python
import functools

import jax
import jax.numpy as jnp
from jax import lax
from jax.experimental import pallas as pl
from jax.experimental.pallas import tpu as pltpu
from jax.sharding import PartitionSpec as P

POLYAK = 0.25
MESH = pl.DeviceIdType.MESH


def blend(online, previous):
    return (
        POLYAK * online.astype(jnp.float32) + (1.0 - POLYAK) * previous.astype(jnp.float32)
    ).astype(jnp.bfloat16)


def gather_kernel(ndp, g_ref, u_ref, dn_ref, gf_ref, uf_ref, df_ref, send_sem, recv_sem,
                  local_sem):
    d = lax.axis_index("dp")
    m = lax.axis_index("mp")
    kr = g_ref.shape[0]
    dc = dn_ref.shape[1]
    rows = pl.ds(pl.multiple_of(d * kr, kr), kr)
    cols = pl.ds(pl.multiple_of(d * dc, dc), dc)

    locals_ = [
        pltpu.make_async_copy(g_ref, gf_ref.at[rows], local_sem.at[0]),
        pltpu.make_async_copy(u_ref, uf_ref.at[rows], local_sem.at[1]),
        pltpu.make_async_copy(dn_ref, df_ref.at[:, cols], local_sem.at[2]),
    ]
    for c in locals_:
        c.start()

    copies = []
    k = 0
    for s in range(1, ndp):
        peer = lax.rem(d + s, ndp)
        for src, dst in ((g_ref, gf_ref.at[rows]), (u_ref, uf_ref.at[rows]),
                         (dn_ref, df_ref.at[:, cols])):
            copies.append(pltpu.make_async_remote_copy(
                src_ref=src, dst_ref=dst, send_sem=send_sem.at[k], recv_sem=recv_sem.at[k],
                device_id=(peer, m), device_id_type=MESH))
            k += 1
    for c in copies:
        c.start()
    for c in locals_:
        c.wait()
    for c in copies:
        c.wait()


def gather_weights_direct(g, u, dn, ndp):
    n_copies = 3 * (ndp - 1)
    any_spec = pl.BlockSpec(memory_space=pl.ANY)
    out_shape = (
        jax.ShapeDtypeStruct((g.shape[0] * ndp, g.shape[1]), g.dtype),
        jax.ShapeDtypeStruct((u.shape[0] * ndp, u.shape[1]), u.dtype),
        jax.ShapeDtypeStruct((dn.shape[0], dn.shape[1] * ndp), dn.dtype),
    )
    return pl.pallas_call(
        functools.partial(gather_kernel, ndp),
        out_shape=out_shape,
        in_specs=[any_spec] * 3,
        out_specs=[any_spec] * 3,
        scratch_shapes=[
            pltpu.SemaphoreType.DMA((n_copies,)),
            pltpu.SemaphoreType.DMA((n_copies,)),
            pltpu.SemaphoreType.DMA((3,)),
        ],
        compiler_params=pltpu.CompilerParams(has_side_effects=True),
    )(g, u, dn)


def relay_gather_kernel(h_ref, g_ref, u_ref, dn_ref, hf_ref, gf_ref, uf_ref, df_ref, send_sem,
                        recv_sem, local_sem, hsend, hrecv):
    ndp = 8
    d = lax.axis_index("dp")
    m = lax.axis_index("mp")
    lo = d % 2
    partner = d - lo + (1 - lo)
    nxt = (d + 2) % ndp
    prv = (d + ndp - 2) % ndp
    far = (d + 4) % ndp
    owns = (g_ref, u_ref, dn_ref)
    fulls = (gf_ref, uf_ref, df_ref)

    def slot(w, idx, half=None):
        if w < 2:
            kr = owns[w].shape[0]
            if half is None:
                return fulls[w].at[pl.ds(pl.multiple_of(idx * kr, kr), kr)]
            hk = kr // 2
            return fulls[w].at[pl.ds(pl.multiple_of(idx * kr + half * hk, hk), hk)]
        rr, dc = owns[w].shape
        cols = pl.ds(pl.multiple_of(idx * dc, dc), dc)
        if half is None:
            return fulls[w].at[:, cols]
        hr = rr // 2
        return fulls[w].at[pl.ds(half * hr, hr), cols]

    def rc(w, k, src, dst, target):
        i = w * 8 + k
        return pltpu.make_async_remote_copy(
            src_ref=src, dst_ref=dst, send_sem=send_sem.at[i], recv_sem=recv_sem.at[i],
            device_id=(target, m), device_id_type=MESH)

    locals_ = [pltpu.make_async_copy(owns[w], slot(w, d), local_sem.at[w]) for w in range(3)]
    c = {}
    for w in range(3):
        c[w, 0] = rc(w, 0, owns[w], slot(w, d), partner)
        c[w, 1] = rc(w, 1, owns[w], slot(w, d), nxt)
        c[w, 2] = rc(w, 2, owns[w], slot(w, d), prv)
        c[w, 3] = rc(w, 3, slot(w, partner), slot(w, partner), nxt)
        c[w, 4] = rc(w, 4, slot(w, partner), slot(w, partner), prv)
        c[w, 5] = rc(w, 5, slot(w, prv, 0), slot(w, prv, 0), nxt)
        c[w, 6] = rc(w, 6, slot(w, nxt, 1), slot(w, nxt, 1), prv)
        c[w, 7] = rc(w, 7, slot(w, far), slot(w, far), partner)
    nmp = 16
    hc = h_ref.shape[1]
    hmine = hf_ref.at[:, pl.ds(pl.multiple_of(m * hc, hc), hc)]
    hlocal = pltpu.make_async_copy(h_ref, hmine, local_sem.at[3])
    hcopies = []
    for s in range(1, nmp):
        hcopies.append(pltpu.make_async_remote_copy(
            src_ref=h_ref, dst_ref=hmine, send_sem=hsend.at[s - 1], recv_sem=hrecv.at[s - 1],
            device_id=(d, lax.rem(m + s, nmp)), device_id_type=MESH))
    for w in range(3):
        locals_[w].start()
        for k in range(3):
            c[w, k].start()
    hlocal.start()
    for cp in hcopies:
        cp.start()
    for w in range(3):
        c[w, 1].wait_recv()
        c[w, 5].start()
        c[w, 2].wait_recv()
        c[w, 6].start()
    for w in range(3):
        c[w, 5].wait_recv()
        c[w, 6].wait_recv()
        c[w, 7].start()
    for w in range(3):
        c[w, 0].wait_recv()
        c[w, 3].start()
        c[w, 4].start()
    for w in range(3):
        for k in (3, 4, 7):
            c[w, k].wait_recv()
    for w in range(3):
        for k in range(8):
            c[w, k].wait_send()
        locals_[w].wait()
    hlocal.wait()
    for cp in hcopies:
        cp.wait()


def gather_relay(h, g, u, dn, ndp):
    any_spec = pl.BlockSpec(memory_space=pl.ANY)
    out_shape = (
        jax.ShapeDtypeStruct((g.shape[0] * ndp, g.shape[1]), g.dtype),
        jax.ShapeDtypeStruct((u.shape[0] * ndp, u.shape[1]), u.dtype),
        jax.ShapeDtypeStruct((dn.shape[0], dn.shape[1] * ndp), dn.dtype),
    )
    return pl.pallas_call(
        relay_gather_kernel,
        out_shape=(jax.ShapeDtypeStruct((h.shape[0], h.shape[1] * 16), h.dtype),) + out_shape,
        in_specs=[any_spec] * 4,
        out_specs=[any_spec] * 4,
        scratch_shapes=[
            pltpu.SemaphoreType.DMA((24,)),
            pltpu.SemaphoreType.DMA((24,)),
            pltpu.SemaphoreType.DMA((4,)),
            pltpu.SemaphoreType.DMA((15,)),
            pltpu.SemaphoreType.DMA((15,)),
        ],
        compiler_params=pltpu.CompilerParams(has_side_effects=True),
    )(h, g, u, dn)


def reduce_kernel(nmp, t_ref, o_ref, buf, send_sem, recv_sem, local_sem):
    d = lax.axis_index("dp")
    m = lax.axis_index("mp")
    w = o_ref.shape[2]
    mine = pl.ds(pl.multiple_of(m * w, w), w)
    local_copy = pltpu.make_async_copy(t_ref.at[:, :, mine], buf.at[0], local_sem.at[0])
    local_copy.start()
    copies = []
    for s in range(1, nmp):
        peer = lax.rem(m + s, nmp)
        theirs = pl.ds(pl.multiple_of(peer * w, w), w)
        copies.append(pltpu.make_async_remote_copy(
            src_ref=t_ref.at[:, :, theirs], dst_ref=buf.at[s], send_sem=send_sem.at[s],
            recv_sem=recv_sem.at[s], device_id=(d, peer), device_id_type=MESH))
    for c in copies:
        c.start()
    local_copy.wait()
    for c in copies:
        c.wait()
    rows = 32

    def body(i, carry):
        r = pl.ds(pl.multiple_of(i * rows, rows), rows)
        for k in range(o_ref.shape[0]):
            acc = buf[0, k, r, :].astype(jnp.float32)
            for s in range(1, nmp):
                acc = acc + buf[s, k, r, :].astype(jnp.float32)
            o_ref[k, r, :] = acc.astype(o_ref.dtype)
        return carry

    lax.fori_loop(0, o_ref.shape[1] // rows, body, 0)


def reduce_scatter(terms, nmp):
    n, t, width = terms.shape
    w = width // nmp
    return pl.pallas_call(
        functools.partial(reduce_kernel, nmp),
        out_shape=jax.ShapeDtypeStruct((n, t, w), jnp.bfloat16),
        in_specs=[pl.BlockSpec(memory_space=pl.ANY)],
        out_specs=pl.BlockSpec(memory_space=pltpu.VMEM),
        scratch_shapes=[
            pltpu.VMEM((nmp, n, t, w), jnp.bfloat16),
            pltpu.SemaphoreType.DMA((nmp,)),
            pltpu.SemaphoreType.DMA((nmp,)),
            pltpu.SemaphoreType.DMA((1,)),
        ],
        compiler_params=pltpu.CompilerParams(has_side_effects=True,
                                             vmem_limit_bytes=48 * 1024 * 1024),
    )(terms)


def hier_reduce_kernel(ta_ref, tb_ref, o_ref, own, r1, sb2, r2, s2, sb3, r3,
                       ls, ss1, rs1, ss2, rs2, ss3, rs3):
    d = lax.axis_index("dp")
    m = lax.axis_index("mp")
    c = m % 2
    z = (m // 2) % 4
    xh = m // 8
    w = o_ref.shape[2]
    rows = 32
    nchunk = o_ref.shape[1] // rows

    def blk(b, k):
        return (ta_ref, tb_ref)[k].at[:, pl.ds(pl.multiple_of(b * w, w), w)]

    def dev(mm):
        return (d, mm)

    locs = []
    st1 = []
    for j in range(16):
        bx, bz, k = j // 8, (j // 2) % 4, j % 2
        jj = bx * 4 + bz
        locs.append(pltpu.make_async_copy(blk(bx * 8 + bz * 2 + c, k), own.at[jj, k],
                                          ls.at[j]))
        st1.append(pltpu.make_async_remote_copy(
            src_ref=blk(bx * 8 + bz * 2 + (1 - c), k), dst_ref=r1.at[jj, k], send_sem=ss1.at[j],
            recv_sem=rs1.at[j], device_id=dev(m + 1 - 2 * c), device_id_type=MESH))
    for j in range(16):
        st1[j].start()
        locs[j].start()
    for j in range(16):
        locs[j].wait()
        st1[j].wait()

    st2 = []
    for s in range(1, 4):
        zt = (z + s) % 4

        def fill(i, carry, s=s, zt=zt):
            r = pl.ds(pl.multiple_of(i * rows, rows), rows)
            for bx in range(2):
                idx = bx * 4 + zt
                sb2[s - 1, bx, :, r, :] = (own[idx, :, r, :].astype(jnp.float32)
                                           + r1[idx, :, r, :].astype(jnp.float32)
                                           ).astype(sb2.dtype)
            return carry

        lax.fori_loop(0, nchunk, fill, 0)
        cp = pltpu.make_async_remote_copy(
            src_ref=sb2.at[s - 1], dst_ref=r2.at[s - 1], send_sem=ss2.at[s - 1],
            recv_sem=rs2.at[s - 1], device_id=dev(xh * 8 + zt * 2 + c), device_id_type=MESH)
        cp.start()
        st2.append(cp)
    for cp in st2:
        cp.wait()

    def sum2(i, carry):
        r = pl.ds(pl.multiple_of(i * rows, rows), rows)
        for bx in range(2):
            idx = bx * 4 + z
            acc = own[idx, :, r, :].astype(jnp.float32) + r1[idx, :, r, :].astype(jnp.float32)
            for k in range(3):
                acc = acc + r2[k, bx, :, r, :].astype(jnp.float32)
            s2[bx, :, r, :] = acc
        return carry

    lax.fori_loop(0, nchunk, sum2, 0)
    sb3[...] = s2[1 - xh].astype(sb3.dtype)
    cp3 = pltpu.make_async_remote_copy(
        src_ref=sb3, dst_ref=r3, send_sem=ss3.at[0], recv_sem=rs3.at[0],
        device_id=dev(m + 8 - 16 * xh), device_id_type=MESH)
    cp3.start()
    cp3.wait()
    o_ref[...] = (s2[xh] + r3[...].astype(jnp.float32)).astype(o_ref.dtype)


def hier_reduce_scatter(ta, tb):
    n = 2
    t, width = ta.shape
    w = width // 16
    bf = jnp.bfloat16
    dma = pltpu.SemaphoreType.DMA
    return pl.pallas_call(
        hier_reduce_kernel,
        out_shape=jax.ShapeDtypeStruct((n, t, w), bf),
        in_specs=[pl.BlockSpec(memory_space=pl.ANY)] * 2,
        out_specs=pl.BlockSpec(memory_space=pltpu.VMEM),
        scratch_shapes=[
            pltpu.VMEM((8, n, t, w), bf),
            pltpu.VMEM((8, n, t, w), bf),
            pltpu.VMEM((3, 2, n, t, w), bf),
            pltpu.VMEM((3, 2, n, t, w), bf),
            pltpu.VMEM((2, n, t, w), jnp.float32),
            pltpu.VMEM((n, t, w), bf),
            pltpu.VMEM((n, t, w), bf),
            dma((16,)), dma((16,)), dma((16,)), dma((3,)), dma((3,)), dma((1,)), dma((1,)),
        ],
        compiler_params=pltpu.CompilerParams(has_side_effects=True,
                                             vmem_limit_bytes=56 * 1024 * 1024),
    )(ta, tb)


def local(ndp, nmp, hidden_states, gate_online, up_online, down_online, gate_previous,
          up_previous, down_previous):
    if ndp == 8 and nmp == 16:
        features_all, gate_full, up_full, down_full = gather_relay(
            hidden_states, gate_online, up_online, down_online, ndp)
    else:
        features_all = lax.all_gather(hidden_states, "mp", axis=1, tiled=True)
        gate_full, up_full, down_full = gather_weights_direct(gate_online, up_online,
                                                              down_online, ndp)

    def pair(piece, previous):
        target_piece = blend(piece, previous)
        o = jnp.dot(features_all, piece, preferred_element_type=jnp.float32)
        t = jnp.dot(features_all, target_piece, preferred_element_type=jnp.float32)
        return o, t

    gate_o, gate_t = pair(gate_full, gate_previous)
    up_o, up_t = pair(up_full, up_previous)
    inner_o = (jax.nn.silu(gate_o) * up_o).astype(jnp.bfloat16)
    inner_t = (jax.nn.silu(gate_t) * up_t).astype(jnp.bfloat16)
    inner_o, inner_t = lax.optimization_barrier((inner_o, inner_t))
    target_down = blend(down_full, down_previous)
    online_part = jnp.dot(inner_o, down_full, preferred_element_type=jnp.float32)
    target_part = jnp.dot(inner_t, target_down, preferred_element_type=jnp.float32)
    if nmp == 16:
        result = hier_reduce_scatter(online_part.astype(jnp.bfloat16),
                                     target_part.astype(jnp.bfloat16))
    else:
        terms = jnp.stack([online_part, target_part], axis=0).astype(jnp.bfloat16)
        result = reduce_scatter(terms, nmp)
    return (result[0], result[1])


def solution(mesh):
    ndp = mesh.shape["dp"]
    nmp = mesh.shape["mp"]
    in_specs = (
        P("dp", "mp"),
        P("dp", "mp"),
        P("dp", "mp"),
        P("mp", "dp"),
        P(None, "mp"),
        P(None, "mp"),
        P("mp", None),
    )
    out_specs = (P("dp", "mp"), P("dp", "mp"))
    return jax.shard_map(functools.partial(local, ndp, nmp), mesh=mesh, in_specs=in_specs,
                         out_specs=out_specs, check_vma=False)
```

```python
import functools

import jax
import jax.numpy as jnp
from jax import lax
from jax.experimental import pallas as pl
from jax.experimental.pallas import tpu as pltpu
from jax.sharding import PartitionSpec as P

POLYAK = 0.25
MESH = pl.DeviceIdType.MESH


def blend(online, previous):
    return (
        POLYAK * online.astype(jnp.float32) + (1.0 - POLYAK) * previous.astype(jnp.float32)
    ).astype(jnp.bfloat16)


def gather_kernel(ndp, g_ref, u_ref, dn_ref, gf_ref, uf_ref, df_ref, send_sem, recv_sem,
                  local_sem):
    d = lax.axis_index("dp")
    m = lax.axis_index("mp")
    kr = g_ref.shape[0]
    dc = dn_ref.shape[1]
    rows = pl.ds(pl.multiple_of(d * kr, kr), kr)
    cols = pl.ds(pl.multiple_of(d * dc, dc), dc)

    locals_ = [
        pltpu.make_async_copy(g_ref, gf_ref.at[rows], local_sem.at[0]),
        pltpu.make_async_copy(u_ref, uf_ref.at[rows], local_sem.at[1]),
        pltpu.make_async_copy(dn_ref, df_ref.at[:, cols], local_sem.at[2]),
    ]
    for c in locals_:
        c.start()

    copies = []
    k = 0
    for s in range(1, ndp):
        peer = lax.rem(d + s, ndp)
        for src, dst in ((g_ref, gf_ref.at[rows]), (u_ref, uf_ref.at[rows]),
                         (dn_ref, df_ref.at[:, cols])):
            copies.append(pltpu.make_async_remote_copy(
                src_ref=src, dst_ref=dst, send_sem=send_sem.at[k], recv_sem=recv_sem.at[k],
                device_id=(peer, m), device_id_type=MESH))
            k += 1
    for c in copies:
        c.start()
    for c in locals_:
        c.wait()
    for c in copies:
        c.wait()


def gather_weights_direct(g, u, dn, ndp):
    n_copies = 3 * (ndp - 1)
    any_spec = pl.BlockSpec(memory_space=pl.ANY)
    out_shape = (
        jax.ShapeDtypeStruct((g.shape[0] * ndp, g.shape[1]), g.dtype),
        jax.ShapeDtypeStruct((u.shape[0] * ndp, u.shape[1]), u.dtype),
        jax.ShapeDtypeStruct((dn.shape[0], dn.shape[1] * ndp), dn.dtype),
    )
    return pl.pallas_call(
        functools.partial(gather_kernel, ndp),
        out_shape=out_shape,
        in_specs=[any_spec] * 3,
        out_specs=[any_spec] * 3,
        scratch_shapes=[
            pltpu.SemaphoreType.DMA((n_copies,)),
            pltpu.SemaphoreType.DMA((n_copies,)),
            pltpu.SemaphoreType.DMA((3,)),
        ],
        compiler_params=pltpu.CompilerParams(has_side_effects=True),
    )(g, u, dn)


def relay_gather_kernel(h_ref, g_ref, u_ref, dn_ref, hf_ref, gf_ref, uf_ref, df_ref, send_sem,
                        recv_sem, local_sem, hsend, hrecv):
    ndp = 8
    d = lax.axis_index("dp")
    m = lax.axis_index("mp")
    lo = d % 2
    partner = d - lo + (1 - lo)
    nxt = (d + 2) % ndp
    prv = (d + ndp - 2) % ndp
    far = (d + 4) % ndp
    owns = (g_ref, u_ref, dn_ref)
    fulls = (gf_ref, uf_ref, df_ref)

    def slot(w, idx, half=None):
        if w < 2:
            kr = owns[w].shape[0]
            if half is None:
                return fulls[w].at[pl.ds(pl.multiple_of(idx * kr, kr), kr)]
            hk = kr // 2
            return fulls[w].at[pl.ds(pl.multiple_of(idx * kr + half * hk, hk), hk)]
        rr, dc = owns[w].shape
        cols = pl.ds(pl.multiple_of(idx * dc, dc), dc)
        if half is None:
            return fulls[w].at[:, cols]
        hr = rr // 2
        return fulls[w].at[pl.ds(half * hr, hr), cols]

    def rc(w, k, src, dst, target):
        i = w * 8 + k
        return pltpu.make_async_remote_copy(
            src_ref=src, dst_ref=dst, send_sem=send_sem.at[i], recv_sem=recv_sem.at[i],
            device_id=(target, m), device_id_type=MESH)

    locals_ = [pltpu.make_async_copy(owns[w], slot(w, d), local_sem.at[w]) for w in range(3)]
    c = {}
    for w in range(3):
        c[w, 0] = rc(w, 0, owns[w], slot(w, d), partner)
        c[w, 1] = rc(w, 1, owns[w], slot(w, d), nxt)
        c[w, 2] = rc(w, 2, owns[w], slot(w, d), prv)
        c[w, 3] = rc(w, 3, slot(w, partner), slot(w, partner), nxt)
        c[w, 4] = rc(w, 4, slot(w, partner), slot(w, partner), prv)
        c[w, 5] = rc(w, 5, slot(w, prv, 0), slot(w, prv, 0), nxt)
        c[w, 6] = rc(w, 6, slot(w, nxt, 1), slot(w, nxt, 1), prv)
        c[w, 7] = rc(w, 7, slot(w, far), slot(w, far), partner)
    nmp = 16
    hc = h_ref.shape[1]
    hmine = hf_ref.at[:, pl.ds(pl.multiple_of(m * hc, hc), hc)]
    hlocal = pltpu.make_async_copy(h_ref, hmine, local_sem.at[3])
    hcopies = []
    for s in range(1, nmp):
        hcopies.append(pltpu.make_async_remote_copy(
            src_ref=h_ref, dst_ref=hmine, send_sem=hsend.at[s - 1], recv_sem=hrecv.at[s - 1],
            device_id=(d, lax.rem(m + s, nmp)), device_id_type=MESH))
    for w in range(3):
        locals_[w].start()
        for k in range(3):
            c[w, k].start()
    hlocal.start()
    for cp in hcopies:
        cp.start()
    for w in range(3):
        c[w, 1].wait_recv()
        c[w, 5].start()
        c[w, 2].wait_recv()
        c[w, 6].start()
    for w in range(3):
        c[w, 5].wait_recv()
        c[w, 6].wait_recv()
        c[w, 7].start()
    for w in range(3):
        c[w, 0].wait_recv()
        c[w, 3].start()
        c[w, 4].start()
    for w in range(3):
        for k in (3, 4, 7):
            c[w, k].wait_recv()
    for w in range(3):
        for k in range(8):
            c[w, k].wait_send()
        locals_[w].wait()
    hlocal.wait()
    for cp in hcopies:
        cp.wait()


def gather_relay(h, g, u, dn, ndp):
    any_spec = pl.BlockSpec(memory_space=pl.ANY)
    out_shape = (
        jax.ShapeDtypeStruct((g.shape[0] * ndp, g.shape[1]), g.dtype),
        jax.ShapeDtypeStruct((u.shape[0] * ndp, u.shape[1]), u.dtype),
        jax.ShapeDtypeStruct((dn.shape[0], dn.shape[1] * ndp), dn.dtype),
    )
    return pl.pallas_call(
        relay_gather_kernel,
        out_shape=(jax.ShapeDtypeStruct((h.shape[0], h.shape[1] * 16), h.dtype),) + out_shape,
        in_specs=[any_spec] * 4,
        out_specs=[any_spec] * 4,
        scratch_shapes=[
            pltpu.SemaphoreType.DMA((24,)),
            pltpu.SemaphoreType.DMA((24,)),
            pltpu.SemaphoreType.DMA((4,)),
            pltpu.SemaphoreType.DMA((15,)),
            pltpu.SemaphoreType.DMA((15,)),
        ],
        compiler_params=pltpu.CompilerParams(has_side_effects=True),
    )(h, g, u, dn)


def reduce_kernel(nmp, t_ref, o_ref, buf, send_sem, recv_sem, local_sem):
    d = lax.axis_index("dp")
    m = lax.axis_index("mp")
    w = o_ref.shape[2]
    mine = pl.ds(pl.multiple_of(m * w, w), w)
    local_copy = pltpu.make_async_copy(t_ref.at[:, :, mine], buf.at[0], local_sem.at[0])
    local_copy.start()
    copies = []
    for s in range(1, nmp):
        peer = lax.rem(m + s, nmp)
        theirs = pl.ds(pl.multiple_of(peer * w, w), w)
        copies.append(pltpu.make_async_remote_copy(
            src_ref=t_ref.at[:, :, theirs], dst_ref=buf.at[s], send_sem=send_sem.at[s],
            recv_sem=recv_sem.at[s], device_id=(d, peer), device_id_type=MESH))
    for c in copies:
        c.start()
    local_copy.wait()
    for c in copies:
        c.wait()
    rows = 32

    def body(i, carry):
        r = pl.ds(pl.multiple_of(i * rows, rows), rows)
        for k in range(o_ref.shape[0]):
            acc = buf[0, k, r, :].astype(jnp.float32)
            for s in range(1, nmp):
                acc = acc + buf[s, k, r, :].astype(jnp.float32)
            o_ref[k, r, :] = acc.astype(o_ref.dtype)
        return carry

    lax.fori_loop(0, o_ref.shape[1] // rows, body, 0)


def reduce_scatter(terms, nmp):
    n, t, width = terms.shape
    w = width // nmp
    return pl.pallas_call(
        functools.partial(reduce_kernel, nmp),
        out_shape=jax.ShapeDtypeStruct((n, t, w), jnp.bfloat16),
        in_specs=[pl.BlockSpec(memory_space=pl.ANY)],
        out_specs=pl.BlockSpec(memory_space=pltpu.VMEM),
        scratch_shapes=[
            pltpu.VMEM((nmp, n, t, w), jnp.bfloat16),
            pltpu.SemaphoreType.DMA((nmp,)),
            pltpu.SemaphoreType.DMA((nmp,)),
            pltpu.SemaphoreType.DMA((1,)),
        ],
        compiler_params=pltpu.CompilerParams(has_side_effects=True,
                                             vmem_limit_bytes=48 * 1024 * 1024),
    )(terms)


def hier_reduce_kernel(ta_ref, tb_ref, o_ref, own, r1, sb2, r2, s2, sb3, r3,
                       ls, ss1, rs1, ss2, rs2, ss3, rs3):
    d = lax.axis_index("dp")
    m = lax.axis_index("mp")
    c = m % 2
    z = (m // 2) % 4
    xh = m // 8
    w = o_ref.shape[2]
    rows = 32
    nchunk = o_ref.shape[1] // rows

    def blk(b, k):
        return (ta_ref, tb_ref)[k].at[:, pl.ds(pl.multiple_of(b * w, w), w)]

    def dev(mm):
        return (d, mm)

    locs = []
    st1 = []
    for j in range(16):
        bx, bz, k = j // 8, (j // 2) % 4, j % 2
        jj = bx * 4 + bz
        locs.append(pltpu.make_async_copy(blk(bx * 8 + bz * 2 + c, k), own.at[jj, k],
                                          ls.at[j]))
        st1.append(pltpu.make_async_remote_copy(
            src_ref=blk(bx * 8 + bz * 2 + (1 - c), k), dst_ref=r1.at[jj, k], send_sem=ss1.at[j],
            recv_sem=rs1.at[j], device_id=dev(m + 1 - 2 * c), device_id_type=MESH))
    for j in range(16):
        st1[j].start()
        locs[j].start()
    for j in range(16):
        locs[j].wait()
        st1[j].wait()

    st2 = []
    for s in range(1, 4):
        zt = (z + s) % 4

        def fill(i, carry, s=s, zt=zt):
            r = pl.ds(pl.multiple_of(i * rows, rows), rows)
            for bx in range(2):
                idx = bx * 4 + zt
                sb2[s - 1, bx, :, r, :] = (own[idx, :, r, :].astype(jnp.float32)
                                           + r1[idx, :, r, :].astype(jnp.float32)
                                           ).astype(sb2.dtype)
            return carry

        lax.fori_loop(0, nchunk, fill, 0)
        cp = pltpu.make_async_remote_copy(
            src_ref=sb2.at[s - 1], dst_ref=r2.at[s - 1], send_sem=ss2.at[s - 1],
            recv_sem=rs2.at[s - 1], device_id=dev(xh * 8 + zt * 2 + c), device_id_type=MESH)
        cp.start()
        st2.append(cp)
    for cp in st2:
        cp.wait()

    def sum2(i, carry):
        r = pl.ds(pl.multiple_of(i * rows, rows), rows)
        for bx in range(2):
            idx = bx * 4 + z
            acc = own[idx, :, r, :].astype(jnp.float32) + r1[idx, :, r, :].astype(jnp.float32)
            for k in range(3):
                acc = acc + r2[k, bx, :, r, :].astype(jnp.float32)
            s2[bx, :, r, :] = acc
        return carry

    lax.fori_loop(0, nchunk, sum2, 0)
    sb3[...] = s2[1 - xh].astype(sb3.dtype)
    cp3 = pltpu.make_async_remote_copy(
        src_ref=sb3, dst_ref=r3, send_sem=ss3.at[0], recv_sem=rs3.at[0],
        device_id=dev(m + 8 - 16 * xh), device_id_type=MESH)
    cp3.start()
    cp3.wait()
    o_ref[...] = (s2[xh] + r3[...].astype(jnp.float32)).astype(o_ref.dtype)


def hier_reduce_scatter(ta, tb):
    n = 2
    t, width = ta.shape
    w = width // 16
    bf = jnp.bfloat16
    dma = pltpu.SemaphoreType.DMA
    return pl.pallas_call(
        hier_reduce_kernel,
        out_shape=jax.ShapeDtypeStruct((n, t, w), bf),
        in_specs=[pl.BlockSpec(memory_space=pl.ANY)] * 2,
        out_specs=pl.BlockSpec(memory_space=pltpu.VMEM),
        scratch_shapes=[
            pltpu.VMEM((8, n, t, w), bf),
            pltpu.VMEM((8, n, t, w), bf),
            pltpu.VMEM((3, 2, n, t, w), bf),
            pltpu.VMEM((3, 2, n, t, w), bf),
            pltpu.VMEM((2, n, t, w), jnp.float32),
            pltpu.VMEM((n, t, w), bf),
            pltpu.VMEM((n, t, w), bf),
            dma((16,)), dma((16,)), dma((16,)), dma((3,)), dma((3,)), dma((1,)), dma((1,)),
        ],
        compiler_params=pltpu.CompilerParams(has_side_effects=True,
                                             vmem_limit_bytes=56 * 1024 * 1024),
    )(ta, tb)


def split_reduce_kernel(ta_ref, tb_ref, o_ref, own, r1, sa2, ra2, fa2, sa3, ra3,
                        sb2, rb2, fb2, sb3, rb3, ls, ss1, rs1, ssa2, rsa2, ssa3, rsa3,
                        ssb2, rsb2, ssb3, rsb3):
    d = lax.axis_index("dp")
    m = lax.axis_index("mp")
    c = m % 2
    z = (m // 2) % 4
    xh = m // 8
    w = o_ref.shape[2]
    half = o_ref.shape[1] // 2
    ra = pl.ds(0, half)
    rb = pl.ds(half, half)
    rows = 32
    nchunk = half // rows
    f32 = jnp.float32
    xpeer = m + 8 - 16 * xh

    def blk(b, k):
        return (ta_ref, tb_ref)[k].at[:, pl.ds(pl.multiple_of(b * w, w), w)]

    def rcopy(src, dst, ss, rs, mm):
        return pltpu.make_async_remote_copy(src_ref=src, dst_ref=dst, send_sem=ss, recv_sem=rs,
                                            device_id=(d, mm), device_id_type=MESH)

    locs = []
    st1 = []
    for j in range(16):
        bx, bz, k = j // 8, (j // 2) % 4, j % 2
        jj = bx * 4 + bz
        locs.append(pltpu.make_async_copy(blk(bx * 8 + bz * 2 + c, k), own.at[jj, k],
                                          ls.at[j]))
        st1.append(rcopy(blk(bx * 8 + bz * 2 + (1 - c), k), r1.at[jj, k], ss1.at[j], rs1.at[j],
                         m + 1 - 2 * c))
    for j in range(16):
        st1[j].start()
        locs[j].start()
    for j in range(16):
        locs[j].wait()
        st1[j].wait()

    def pair_sum(idx, r):
        return own[idx, :, r, :].astype(f32) + r1[idx, :, r, :].astype(f32)

    def fill_b2(i, carry):
        r = pl.ds(pl.multiple_of(half + i * rows, rows), rows)
        q = pl.ds(pl.multiple_of(i * rows, rows), rows)
        for bz in range(4):
            sb2[bz, :, q, :] = pair_sum((1 - xh) * 4 + bz, r).astype(sb2.dtype)
        return carry

    lax.fori_loop(0, nchunk, fill_b2, 0)
    cb2 = rcopy(sb2, rb2, ssb2.at[0], rsb2.at[0], xpeer)
    cb2.start()
    ca2 = []
    for s in range(1, 4):
        zt = (z + s) % 4

        def fill_a2(i, carry, s=s, zt=zt):
            q = pl.ds(pl.multiple_of(i * rows, rows), rows)
            for bx in range(2):
                sa2[s - 1, bx, :, q, :] = pair_sum(bx * 4 + zt, q).astype(sa2.dtype)
            return carry

        lax.fori_loop(0, nchunk, fill_a2, 0)
        cp = rcopy(sa2.at[s - 1], ra2.at[s - 1], ssa2.at[s - 1], rsa2.at[s - 1],
                   xh * 8 + zt * 2 + c)
        cp.start()
        ca2.append(cp)

    cb2.wait()

    def sum_b2(i, carry):
        r = pl.ds(pl.multiple_of(half + i * rows, rows), rows)
        q = pl.ds(pl.multiple_of(i * rows, rows), rows)
        for bz in range(4):
            fb2[bz, :, q, :] = pair_sum(xh * 4 + bz, r) + rb2[bz, :, q, :].astype(f32)
        return carry

    lax.fori_loop(0, nchunk, sum_b2, 0)
    cb3 = []
    for s in range(1, 4):
        zt = (z + s) % 4
        sb3[s - 1] = fb2[zt].astype(sb3.dtype)
        cp = rcopy(sb3.at[s - 1], rb3.at[s - 1], ssb3.at[s - 1], rsb3.at[s - 1],
                   xh * 8 + zt * 2 + c)
        cp.start()
        cb3.append(cp)

    for cp in ca2:
        cp.wait()

    def sum_a2(i, carry):
        q = pl.ds(pl.multiple_of(i * rows, rows), rows)
        for bx in range(2):
            acc = pair_sum(bx * 4 + z, q)
            for k in range(3):
                acc = acc + ra2[k, bx, :, q, :].astype(f32)
            fa2[bx, :, q, :] = acc
        return carry

    lax.fori_loop(0, nchunk, sum_a2, 0)
    sa3[...] = fa2[1 - xh].astype(sa3.dtype)
    ca3 = rcopy(sa3, ra3, ssa3.at[0], rsa3.at[0], xpeer)
    ca3.start()
    for cp in cb3:
        cp.wait()
    acc = fb2[z]
    for k in range(3):
        acc = acc + rb3[k].astype(f32)
    o_ref[:, rb, :] = acc.astype(o_ref.dtype)
    ca3.wait()
    o_ref[:, ra, :] = (fa2[xh] + ra3[...].astype(f32)).astype(o_ref.dtype)


def split_reduce_scatter(ta, tb):
    n = 2
    t, width = ta.shape
    w = width // 16
    h = t // 2
    bf = jnp.bfloat16
    f32 = jnp.float32
    dma = pltpu.SemaphoreType.DMA
    return pl.pallas_call(
        split_reduce_kernel,
        out_shape=jax.ShapeDtypeStruct((n, t, w), bf),
        in_specs=[pl.BlockSpec(memory_space=pl.ANY)] * 2,
        out_specs=pl.BlockSpec(memory_space=pltpu.VMEM),
        scratch_shapes=[
            pltpu.VMEM((8, n, t, w), bf),
            pltpu.VMEM((8, n, t, w), bf),
            pltpu.VMEM((3, 2, n, h, w), bf),
            pltpu.VMEM((3, 2, n, h, w), bf),
            pltpu.VMEM((2, n, h, w), f32),
            pltpu.VMEM((n, h, w), bf),
            pltpu.VMEM((n, h, w), bf),
            pltpu.VMEM((4, n, h, w), bf),
            pltpu.VMEM((4, n, h, w), bf),
            pltpu.VMEM((4, n, h, w), f32),
            pltpu.VMEM((3, n, h, w), bf),
            pltpu.VMEM((3, n, h, w), bf),
            dma((16,)), dma((16,)), dma((16,)),
            dma((3,)), dma((3,)), dma((1,)), dma((1,)),
            dma((1,)), dma((1,)), dma((3,)), dma((3,)),
        ],
        compiler_params=pltpu.CompilerParams(has_side_effects=True,
                                             vmem_limit_bytes=56 * 1024 * 1024),
    )(ta, tb)


def local(ndp, nmp, hidden_states, gate_online, up_online, down_online, gate_previous,
          up_previous, down_previous):
    if ndp == 8 and nmp == 16:
        features_all, gate_full, up_full, down_full = gather_relay(
            hidden_states, gate_online, up_online, down_online, ndp)
    else:
        features_all = lax.all_gather(hidden_states, "mp", axis=1, tiled=True)
        gate_full, up_full, down_full = gather_weights_direct(gate_online, up_online,
                                                              down_online, ndp)

    def pair(piece, previous):
        target_piece = blend(piece, previous)
        o = jnp.dot(features_all, piece, preferred_element_type=jnp.float32)
        t = jnp.dot(features_all, target_piece, preferred_element_type=jnp.float32)
        return o, t

    gate_o, gate_t = pair(gate_full, gate_previous)
    up_o, up_t = pair(up_full, up_previous)
    inner_o = (jax.nn.silu(gate_o) * up_o).astype(jnp.bfloat16)
    inner_t = (jax.nn.silu(gate_t) * up_t).astype(jnp.bfloat16)
    inner_o, inner_t = lax.optimization_barrier((inner_o, inner_t))
    target_down = blend(down_full, down_previous)
    online_part = jnp.dot(inner_o, down_full, preferred_element_type=jnp.float32)
    target_part = jnp.dot(inner_t, target_down, preferred_element_type=jnp.float32)
    if nmp == 16:
        result = split_reduce_scatter(online_part.astype(jnp.bfloat16),
                                      target_part.astype(jnp.bfloat16))
    else:
        terms = jnp.stack([online_part, target_part], axis=0).astype(jnp.bfloat16)
        result = reduce_scatter(terms, nmp)
    return (result[0], result[1])


def solution(mesh):
    ndp = mesh.shape["dp"]
    nmp = mesh.shape["mp"]
    in_specs = (
        P("dp", "mp"),
        P("dp", "mp"),
        P("dp", "mp"),
        P("mp", "dp"),
        P(None, "mp"),
        P(None, "mp"),
        P("mp", None),
    )
    out_specs = (P("dp", "mp"), P("dp", "mp"))
    return jax.shard_map(functools.partial(local, ndp, nmp), mesh=mesh, in_specs=in_specs,
                         out_specs=out_specs, check_vma=False)
```

```python
import functools

import jax
import jax.numpy as jnp
from jax import lax
from jax.experimental import pallas as pl
from jax.experimental.pallas import tpu as pltpu
from jax.sharding import PartitionSpec as P

POLYAK = 0.25
MESH = pl.DeviceIdType.MESH


def blend(online, previous):
    return (
        POLYAK * online.astype(jnp.float32) + (1.0 - POLYAK) * previous.astype(jnp.float32)
    ).astype(jnp.bfloat16)


def gather_kernel(ndp, g_ref, u_ref, dn_ref, gf_ref, uf_ref, df_ref, send_sem, recv_sem,
                  local_sem):
    d = lax.axis_index("dp")
    m = lax.axis_index("mp")
    kr = g_ref.shape[0]
    dc = dn_ref.shape[1]
    rows = pl.ds(pl.multiple_of(d * kr, kr), kr)
    cols = pl.ds(pl.multiple_of(d * dc, dc), dc)

    locals_ = [
        pltpu.make_async_copy(g_ref, gf_ref.at[rows], local_sem.at[0]),
        pltpu.make_async_copy(u_ref, uf_ref.at[rows], local_sem.at[1]),
        pltpu.make_async_copy(dn_ref, df_ref.at[:, cols], local_sem.at[2]),
    ]
    for c in locals_:
        c.start()

    copies = []
    k = 0
    for s in range(1, ndp):
        peer = lax.rem(d + s, ndp)
        for src, dst in ((g_ref, gf_ref.at[rows]), (u_ref, uf_ref.at[rows]),
                         (dn_ref, df_ref.at[:, cols])):
            copies.append(pltpu.make_async_remote_copy(
                src_ref=src, dst_ref=dst, send_sem=send_sem.at[k], recv_sem=recv_sem.at[k],
                device_id=(peer, m), device_id_type=MESH))
            k += 1
    for c in copies:
        c.start()
    for c in locals_:
        c.wait()
    for c in copies:
        c.wait()


def gather_weights_direct(g, u, dn, ndp):
    n_copies = 3 * (ndp - 1)
    any_spec = pl.BlockSpec(memory_space=pl.ANY)
    out_shape = (
        jax.ShapeDtypeStruct((g.shape[0] * ndp, g.shape[1]), g.dtype),
        jax.ShapeDtypeStruct((u.shape[0] * ndp, u.shape[1]), u.dtype),
        jax.ShapeDtypeStruct((dn.shape[0], dn.shape[1] * ndp), dn.dtype),
    )
    return pl.pallas_call(
        functools.partial(gather_kernel, ndp),
        out_shape=out_shape,
        in_specs=[any_spec] * 3,
        out_specs=[any_spec] * 3,
        scratch_shapes=[
            pltpu.SemaphoreType.DMA((n_copies,)),
            pltpu.SemaphoreType.DMA((n_copies,)),
            pltpu.SemaphoreType.DMA((3,)),
        ],
        compiler_params=pltpu.CompilerParams(has_side_effects=True),
    )(g, u, dn)


def relay_gather_kernel(h_ref, g_ref, u_ref, dn_ref, hf_ref, gf_ref, uf_ref, df_ref, send_sem,
                        recv_sem, local_sem, hsend, hrecv):
    ndp = 8
    d = lax.axis_index("dp")
    m = lax.axis_index("mp")
    lo = d % 2
    partner = d - lo + (1 - lo)
    nxt = (d + 2) % ndp
    prv = (d + ndp - 2) % ndp
    far = (d + 4) % ndp
    owns = (g_ref, u_ref, dn_ref)
    fulls = (gf_ref, uf_ref, df_ref)

    def slot(w, idx, half=None):
        if w < 2:
            kr = owns[w].shape[0]
            if half is None:
                return fulls[w].at[pl.ds(pl.multiple_of(idx * kr, kr), kr)]
            hk = kr // 2
            return fulls[w].at[pl.ds(pl.multiple_of(idx * kr + half * hk, hk), hk)]
        rr, dc = owns[w].shape
        cols = pl.ds(pl.multiple_of(idx * dc, dc), dc)
        if half is None:
            return fulls[w].at[:, cols]
        hr = rr // 2
        return fulls[w].at[pl.ds(half * hr, hr), cols]

    def rc(w, k, src, dst, target):
        i = w * 8 + k
        return pltpu.make_async_remote_copy(
            src_ref=src, dst_ref=dst, send_sem=send_sem.at[i], recv_sem=recv_sem.at[i],
            device_id=(target, m), device_id_type=MESH)

    locals_ = [pltpu.make_async_copy(owns[w], slot(w, d), local_sem.at[w]) for w in range(3)]
    c = {}
    for w in range(3):
        c[w, 0] = rc(w, 0, owns[w], slot(w, d), partner)
        c[w, 1] = rc(w, 1, owns[w], slot(w, d), nxt)
        c[w, 2] = rc(w, 2, owns[w], slot(w, d), prv)
        c[w, 3] = rc(w, 3, slot(w, partner), slot(w, partner), nxt)
        c[w, 4] = rc(w, 4, slot(w, partner), slot(w, partner), prv)
        c[w, 5] = rc(w, 5, slot(w, prv, 0), slot(w, prv, 0), nxt)
        c[w, 6] = rc(w, 6, slot(w, nxt, 1), slot(w, nxt, 1), prv)
        c[w, 7] = rc(w, 7, slot(w, far), slot(w, far), partner)
    nmp = 16
    hc = h_ref.shape[1]
    hmine = hf_ref.at[:, pl.ds(pl.multiple_of(m * hc, hc), hc)]
    hlocal = pltpu.make_async_copy(h_ref, hmine, local_sem.at[3])
    hcopies = []
    for s in range(1, nmp):
        hcopies.append(pltpu.make_async_remote_copy(
            src_ref=h_ref, dst_ref=hmine, send_sem=hsend.at[s - 1], recv_sem=hrecv.at[s - 1],
            device_id=(d, lax.rem(m + s, nmp)), device_id_type=MESH))
    for w in range(3):
        locals_[w].start()
        for k in range(3):
            c[w, k].start()
    hlocal.start()
    for cp in hcopies:
        cp.start()
    for w in range(3):
        c[w, 1].wait_recv()
        c[w, 5].start()
        c[w, 2].wait_recv()
        c[w, 6].start()
    for w in range(3):
        c[w, 5].wait_recv()
        c[w, 6].wait_recv()
        c[w, 7].start()
    for w in range(3):
        c[w, 0].wait_recv()
        c[w, 3].start()
        c[w, 4].start()
    for w in range(3):
        for k in (3, 4, 7):
            c[w, k].wait_recv()
    for w in range(3):
        for k in range(8):
            c[w, k].wait_send()
        locals_[w].wait()
    hlocal.wait()
    for cp in hcopies:
        cp.wait()


def gather_relay(h, g, u, dn, ndp):
    any_spec = pl.BlockSpec(memory_space=pl.ANY)
    out_shape = (
        jax.ShapeDtypeStruct((g.shape[0] * ndp, g.shape[1]), g.dtype),
        jax.ShapeDtypeStruct((u.shape[0] * ndp, u.shape[1]), u.dtype),
        jax.ShapeDtypeStruct((dn.shape[0], dn.shape[1] * ndp), dn.dtype),
    )
    return pl.pallas_call(
        relay_gather_kernel,
        out_shape=(jax.ShapeDtypeStruct((h.shape[0], h.shape[1] * 16), h.dtype),) + out_shape,
        in_specs=[any_spec] * 4,
        out_specs=[any_spec] * 4,
        scratch_shapes=[
            pltpu.SemaphoreType.DMA((24,)),
            pltpu.SemaphoreType.DMA((24,)),
            pltpu.SemaphoreType.DMA((4,)),
            pltpu.SemaphoreType.DMA((15,)),
            pltpu.SemaphoreType.DMA((15,)),
        ],
        compiler_params=pltpu.CompilerParams(has_side_effects=True),
    )(h, g, u, dn)


def reduce_kernel(nmp, t_ref, o_ref, buf, send_sem, recv_sem, local_sem):
    d = lax.axis_index("dp")
    m = lax.axis_index("mp")
    w = o_ref.shape[2]
    mine = pl.ds(pl.multiple_of(m * w, w), w)
    local_copy = pltpu.make_async_copy(t_ref.at[:, :, mine], buf.at[0], local_sem.at[0])
    local_copy.start()
    copies = []
    for s in range(1, nmp):
        peer = lax.rem(m + s, nmp)
        theirs = pl.ds(pl.multiple_of(peer * w, w), w)
        copies.append(pltpu.make_async_remote_copy(
            src_ref=t_ref.at[:, :, theirs], dst_ref=buf.at[s], send_sem=send_sem.at[s],
            recv_sem=recv_sem.at[s], device_id=(d, peer), device_id_type=MESH))
    for c in copies:
        c.start()
    local_copy.wait()
    for c in copies:
        c.wait()
    rows = 32

    def body(i, carry):
        r = pl.ds(pl.multiple_of(i * rows, rows), rows)
        for k in range(o_ref.shape[0]):
            acc = buf[0, k, r, :].astype(jnp.float32)
            for s in range(1, nmp):
                acc = acc + buf[s, k, r, :].astype(jnp.float32)
            o_ref[k, r, :] = acc.astype(o_ref.dtype)
        return carry

    lax.fori_loop(0, o_ref.shape[1] // rows, body, 0)


def reduce_scatter(terms, nmp):
    n, t, width = terms.shape
    w = width // nmp
    return pl.pallas_call(
        functools.partial(reduce_kernel, nmp),
        out_shape=jax.ShapeDtypeStruct((n, t, w), jnp.bfloat16),
        in_specs=[pl.BlockSpec(memory_space=pl.ANY)],
        out_specs=pl.BlockSpec(memory_space=pltpu.VMEM),
        scratch_shapes=[
            pltpu.VMEM((nmp, n, t, w), jnp.bfloat16),
            pltpu.SemaphoreType.DMA((nmp,)),
            pltpu.SemaphoreType.DMA((nmp,)),
            pltpu.SemaphoreType.DMA((1,)),
        ],
        compiler_params=pltpu.CompilerParams(has_side_effects=True,
                                             vmem_limit_bytes=48 * 1024 * 1024),
    )(terms)


def hier_reduce_kernel(ta_ref, tb_ref, o_ref, own, r1, sb2, r2, s2, sb3, r3,
                       ls, ss1, rs1, ss2, rs2, ss3, rs3):
    d = lax.axis_index("dp")
    m = lax.axis_index("mp")
    c = m % 2
    z = (m // 2) % 4
    xh = m // 8
    w = o_ref.shape[2]
    rows = 32
    nchunk = o_ref.shape[1] // rows

    def blk(b, k):
        return (ta_ref, tb_ref)[k].at[:, pl.ds(pl.multiple_of(b * w, w), w)]

    def dev(mm):
        return (d, mm)

    locs = []
    st1 = []
    for j in range(16):
        bx, bz, k = j // 8, (j // 2) % 4, j % 2
        jj = bx * 4 + bz
        locs.append(pltpu.make_async_copy(blk(bx * 8 + bz * 2 + c, k), own.at[jj, k],
                                          ls.at[j]))
        st1.append(pltpu.make_async_remote_copy(
            src_ref=blk(bx * 8 + bz * 2 + (1 - c), k), dst_ref=r1.at[jj, k], send_sem=ss1.at[j],
            recv_sem=rs1.at[j], device_id=dev(m + 1 - 2 * c), device_id_type=MESH))
    for j in range(16):
        st1[j].start()
        locs[j].start()
    for j in range(16):
        locs[j].wait()
        st1[j].wait()

    st2 = []
    for s in range(1, 4):
        zt = (z + s) % 4

        def fill(i, carry, s=s, zt=zt):
            r = pl.ds(pl.multiple_of(i * rows, rows), rows)
            for bx in range(2):
                idx = bx * 4 + zt
                sb2[s - 1, bx, :, r, :] = (own[idx, :, r, :].astype(jnp.float32)
                                           + r1[idx, :, r, :].astype(jnp.float32)
                                           ).astype(sb2.dtype)
            return carry

        lax.fori_loop(0, nchunk, fill, 0)
        cp = pltpu.make_async_remote_copy(
            src_ref=sb2.at[s - 1], dst_ref=r2.at[s - 1], send_sem=ss2.at[s - 1],
            recv_sem=rs2.at[s - 1], device_id=dev(xh * 8 + zt * 2 + c), device_id_type=MESH)
        cp.start()
        st2.append(cp)
    for cp in st2:
        cp.wait()

    def sum2(i, carry):
        r = pl.ds(pl.multiple_of(i * rows, rows), rows)
        for bx in range(2):
            idx = bx * 4 + z
            acc = own[idx, :, r, :].astype(jnp.float32) + r1[idx, :, r, :].astype(jnp.float32)
            for k in range(3):
                acc = acc + r2[k, bx, :, r, :].astype(jnp.float32)
            s2[bx, :, r, :] = acc
        return carry

    lax.fori_loop(0, nchunk, sum2, 0)
    sb3[...] = s2[1 - xh].astype(sb3.dtype)
    cp3 = pltpu.make_async_remote_copy(
        src_ref=sb3, dst_ref=r3, send_sem=ss3.at[0], recv_sem=rs3.at[0],
        device_id=dev(m + 8 - 16 * xh), device_id_type=MESH)
    cp3.start()
    cp3.wait()
    o_ref[...] = (s2[xh] + r3[...].astype(jnp.float32)).astype(o_ref.dtype)


def hier_reduce_scatter(ta, tb):
    n = 2
    t, width = ta.shape
    w = width // 16
    bf = jnp.bfloat16
    dma = pltpu.SemaphoreType.DMA
    return pl.pallas_call(
        hier_reduce_kernel,
        out_shape=jax.ShapeDtypeStruct((n, t, w), bf),
        in_specs=[pl.BlockSpec(memory_space=pl.ANY)] * 2,
        out_specs=pl.BlockSpec(memory_space=pltpu.VMEM),
        scratch_shapes=[
            pltpu.VMEM((8, n, t, w), bf),
            pltpu.VMEM((8, n, t, w), bf),
            pltpu.VMEM((3, 2, n, t, w), bf),
            pltpu.VMEM((3, 2, n, t, w), bf),
            pltpu.VMEM((2, n, t, w), jnp.float32),
            pltpu.VMEM((n, t, w), bf),
            pltpu.VMEM((n, t, w), bf),
            dma((16,)), dma((16,)), dma((16,)), dma((3,)), dma((3,)), dma((1,)), dma((1,)),
        ],
        compiler_params=pltpu.CompilerParams(has_side_effects=True,
                                             vmem_limit_bytes=56 * 1024 * 1024),
    )(ta, tb)


def split_reduce_kernel(ta_ref, tb_ref, o_ref, own, r1, sa2, ra2, fa2, sa3, ra3,
                        sb2, rb2, fb2, sb3, rb3, ls, ss1, rs1, ssa2, rsa2, ssa3, rsa3,
                        ssb2, rsb2, ssb3, rsb3):
    d = lax.axis_index("dp")
    m = lax.axis_index("mp")
    c = m % 2
    z = (m // 2) % 4
    xh = m // 8
    w = o_ref.shape[2]
    half = o_ref.shape[1] // 2
    ra = pl.ds(0, half)
    rb = pl.ds(half, half)
    rows = 32
    nchunk = half // rows
    f32 = jnp.float32
    xpeer = m + 8 - 16 * xh

    def blk(b, k):
        return (ta_ref, tb_ref)[k].at[:, pl.ds(pl.multiple_of(b * w, w), w)]

    def rcopy(src, dst, ss, rs, mm):
        return pltpu.make_async_remote_copy(src_ref=src, dst_ref=dst, send_sem=ss, recv_sem=rs,
                                            device_id=(d, mm), device_id_type=MESH)

    locs = []
    st1 = []
    for j in range(16):
        bx, bz, k = j // 8, (j // 2) % 4, j % 2
        jj = bx * 4 + bz
        locs.append(pltpu.make_async_copy(blk(bx * 8 + bz * 2 + c, k), own.at[jj, k],
                                          ls.at[j]))
        st1.append(rcopy(blk(bx * 8 + bz * 2 + (1 - c), k), r1.at[jj, k], ss1.at[j], rs1.at[j],
                         m + 1 - 2 * c))
    for j in range(16):
        st1[j].start()
        locs[j].start()
    for j in range(16):
        locs[j].wait()
        st1[j].wait()

    def pair_sum(idx, r):
        return own[idx, :, r, :].astype(f32) + r1[idx, :, r, :].astype(f32)

    def fill_b2(i, carry):
        r = pl.ds(pl.multiple_of(half + i * rows, rows), rows)
        q = pl.ds(pl.multiple_of(i * rows, rows), rows)
        for bz in range(4):
            sb2[bz, :, q, :] = pair_sum((1 - xh) * 4 + bz, r).astype(sb2.dtype)
        return carry

    lax.fori_loop(0, nchunk, fill_b2, 0)
    cb2 = rcopy(sb2, rb2, ssb2.at[0], rsb2.at[0], xpeer)
    cb2.start()
    ca2 = []
    for s in range(1, 4):
        zt = (z + s) % 4

        def fill_a2(i, carry, s=s, zt=zt):
            q = pl.ds(pl.multiple_of(i * rows, rows), rows)
            for bx in range(2):
                sa2[s - 1, bx, :, q, :] = pair_sum(bx * 4 + zt, q).astype(sa2.dtype)
            return carry

        lax.fori_loop(0, nchunk, fill_a2, 0)
        cp = rcopy(sa2.at[s - 1], ra2.at[s - 1], ssa2.at[s - 1], rsa2.at[s - 1],
                   xh * 8 + zt * 2 + c)
        cp.start()
        ca2.append(cp)

    cb2.wait()

    def sum_b2(i, carry):
        r = pl.ds(pl.multiple_of(half + i * rows, rows), rows)
        q = pl.ds(pl.multiple_of(i * rows, rows), rows)
        for bz in range(4):
            fb2[bz, :, q, :] = pair_sum(xh * 4 + bz, r) + rb2[bz, :, q, :].astype(f32)
        return carry

    lax.fori_loop(0, nchunk, sum_b2, 0)
    cb3 = []
    for s in range(1, 4):
        zt = (z + s) % 4
        sb3[s - 1] = fb2[zt].astype(sb3.dtype)
        cp = rcopy(sb3.at[s - 1], rb3.at[s - 1], ssb3.at[s - 1], rsb3.at[s - 1],
                   xh * 8 + zt * 2 + c)
        cp.start()
        cb3.append(cp)

    for cp in ca2:
        cp.wait()

    def sum_a2(i, carry):
        q = pl.ds(pl.multiple_of(i * rows, rows), rows)
        for bx in range(2):
            acc = pair_sum(bx * 4 + z, q)
            for k in range(3):
                acc = acc + ra2[k, bx, :, q, :].astype(f32)
            fa2[bx, :, q, :] = acc
        return carry

    lax.fori_loop(0, nchunk, sum_a2, 0)
    sa3[...] = fa2[1 - xh].astype(sa3.dtype)
    ca3 = rcopy(sa3, ra3, ssa3.at[0], rsa3.at[0], xpeer)
    ca3.start()
    for cp in cb3:
        cp.wait()
    acc = fb2[z]
    for k in range(3):
        acc = acc + rb3[k].astype(f32)
    o_ref[:, rb, :] = acc.astype(o_ref.dtype)
    ca3.wait()
    o_ref[:, ra, :] = (fa2[xh] + ra3[...].astype(f32)).astype(o_ref.dtype)


def split_reduce_scatter(ta, tb):
    n = 2
    t, width = ta.shape
    w = width // 16
    h = t // 2
    bf = jnp.bfloat16
    f32 = jnp.float32
    dma = pltpu.SemaphoreType.DMA
    return pl.pallas_call(
        split_reduce_kernel,
        out_shape=jax.ShapeDtypeStruct((n, t, w), bf),
        in_specs=[pl.BlockSpec(memory_space=pl.ANY)] * 2,
        out_specs=pl.BlockSpec(memory_space=pltpu.VMEM),
        scratch_shapes=[
            pltpu.VMEM((8, n, t, w), bf),
            pltpu.VMEM((8, n, t, w), bf),
            pltpu.VMEM((3, 2, n, h, w), bf),
            pltpu.VMEM((3, 2, n, h, w), bf),
            pltpu.VMEM((2, n, h, w), f32),
            pltpu.VMEM((n, h, w), bf),
            pltpu.VMEM((n, h, w), bf),
            pltpu.VMEM((4, n, h, w), bf),
            pltpu.VMEM((4, n, h, w), bf),
            pltpu.VMEM((4, n, h, w), f32),
            pltpu.VMEM((3, n, h, w), bf),
            pltpu.VMEM((3, n, h, w), bf),
            dma((16,)), dma((16,)), dma((16,)),
            dma((3,)), dma((3,)), dma((1,)), dma((1,)),
            dma((1,)), dma((1,)), dma((3,)), dma((3,)),
        ],
        compiler_params=pltpu.CompilerParams(has_side_effects=True,
                                             vmem_limit_bytes=56 * 1024 * 1024),
    )(ta, tb)


def gate_up_kernel(h_ref, go_ref, gp_ref, uo_ref, upv_ref, io_ref, it_ref, acc, tbuf):
    k = pl.program_id(0)
    tile = 128
    chunk = 64
    f32 = jnp.float32

    @pl.when(k == 0)
    def _():
        acc[...] = jnp.zeros_like(acc)

    def mix(i, carry):
        r = pl.ds(pl.multiple_of(i * chunk, chunk), chunk)
        for j, (on_ref, pv_ref) in enumerate(((go_ref, gp_ref), (uo_ref, upv_ref))):
            on = on_ref[r, :].astype(f32)
            pv = pv_ref[r, :].astype(f32)
            tbuf[j, r, :] = (POLYAK * on + (1.0 - POLYAK) * pv).astype(tbuf.dtype)
        return carry

    lax.fori_loop(0, go_ref.shape[0] // chunk, mix, 0)

    def mm(i, carry):
        r = pl.ds(pl.multiple_of(i * tile, tile), tile)
        hs = h_ref[r, :]
        acc[0, r, :] += jnp.dot(hs, go_ref[...], preferred_element_type=f32)
        acc[1, r, :] += jnp.dot(hs, tbuf[0], preferred_element_type=f32)
        acc[2, r, :] += jnp.dot(hs, uo_ref[...], preferred_element_type=f32)
        acc[3, r, :] += jnp.dot(hs, tbuf[1], preferred_element_type=f32)
        return carry

    lax.fori_loop(0, h_ref.shape[0] // tile, mm, 0)

    @pl.when(k == pl.num_programs(0) - 1)
    def _():
        def finish(i, carry):
            r = pl.ds(pl.multiple_of(i * chunk, chunk), chunk)
            io_ref[r, :] = (jax.nn.silu(acc[0, r, :]) * acc[2, r, :]).astype(io_ref.dtype)
            it_ref[r, :] = (jax.nn.silu(acc[1, r, :]) * acc[3, r, :]).astype(it_ref.dtype)
            return carry

        lax.fori_loop(0, io_ref.shape[0] // chunk, finish, 0)


def gate_up(h_full, go, gp, uo, upv, kb):
    tokens, kdim = h_full.shape
    ff = go.shape[1]
    wspec = pl.BlockSpec((kb, ff), lambda k: (k, 0))
    ospec = pl.BlockSpec((tokens, ff), lambda k: (0, 0))
    flops = 8 * tokens * kdim * ff
    nbytes = 2 * (tokens * kdim + 4 * kdim * ff + 2 * tokens * ff)
    return pl.pallas_call(
        gate_up_kernel,
        grid=(kdim // kb,),
        out_shape=(jax.ShapeDtypeStruct((tokens, ff), jnp.bfloat16),) * 2,
        in_specs=[pl.BlockSpec((tokens, kb), lambda k: (0, k))] + [wspec] * 4,
        out_specs=[ospec, ospec],
        scratch_shapes=[pltpu.VMEM((4, tokens, ff), jnp.float32),
                        pltpu.VMEM((2, kb, ff), jnp.bfloat16)],
        compiler_params=pltpu.CompilerParams(vmem_limit_bytes=48 * 1024 * 1024),
        cost_estimate=pl.CostEstimate(flops=flops, bytes_accessed=nbytes,
                                      transcendentals=2 * tokens * ff),
    )(h_full, go, gp, uo, upv)


def local(ndp, nmp, hidden_states, gate_online, up_online, down_online, gate_previous,
          up_previous, down_previous):
    if ndp == 8 and nmp == 16:
        features_all, gate_full, up_full, down_full = gather_relay(
            hidden_states, gate_online, up_online, down_online, ndp)
    else:
        features_all = lax.all_gather(hidden_states, "mp", axis=1, tiled=True)
        gate_full, up_full, down_full = gather_weights_direct(gate_online, up_online,
                                                              down_online, ndp)

    inner_o, inner_t = gate_up(features_all, gate_full, gate_previous, up_full, up_previous,
                               gate_online.shape[0])
    target_down = blend(down_full, down_previous)
    online_part = jnp.dot(inner_o, down_full, preferred_element_type=jnp.float32)
    target_part = jnp.dot(inner_t, target_down, preferred_element_type=jnp.float32)
    if nmp == 16:
        result = split_reduce_scatter(online_part.astype(jnp.bfloat16),
                                      target_part.astype(jnp.bfloat16))
    else:
        terms = jnp.stack([online_part, target_part], axis=0).astype(jnp.bfloat16)
        result = reduce_scatter(terms, nmp)
    return (result[0], result[1])


def solution(mesh):
    ndp = mesh.shape["dp"]
    nmp = mesh.shape["mp"]
    in_specs = (
        P("dp", "mp"),
        P("dp", "mp"),
        P("dp", "mp"),
        P("mp", "dp"),
        P(None, "mp"),
        P(None, "mp"),
        P("mp", None),
    )
    out_specs = (P("dp", "mp"), P("dp", "mp"))
    return jax.shard_map(functools.partial(local, ndp, nmp), mesh=mesh, in_specs=in_specs,
                         out_specs=out_specs, check_vma=False)
```

```python
import functools

import jax
import jax.numpy as jnp
from jax import lax
from jax.experimental import pallas as pl
from jax.experimental.pallas import tpu as pltpu
from jax.sharding import PartitionSpec as P

POLYAK = 0.25
MESH = pl.DeviceIdType.MESH


def blend(online, previous):
    return (
        POLYAK * online.astype(jnp.float32) + (1.0 - POLYAK) * previous.astype(jnp.float32)
    ).astype(jnp.bfloat16)


def gather_kernel(ndp, g_ref, u_ref, dn_ref, gf_ref, uf_ref, df_ref, send_sem, recv_sem,
                  local_sem):
    d = lax.axis_index("dp")
    m = lax.axis_index("mp")
    kr = g_ref.shape[0]
    dc = dn_ref.shape[1]
    rows = pl.ds(pl.multiple_of(d * kr, kr), kr)
    cols = pl.ds(pl.multiple_of(d * dc, dc), dc)

    locals_ = [
        pltpu.make_async_copy(g_ref, gf_ref.at[rows], local_sem.at[0]),
        pltpu.make_async_copy(u_ref, uf_ref.at[rows], local_sem.at[1]),
        pltpu.make_async_copy(dn_ref, df_ref.at[:, cols], local_sem.at[2]),
    ]
    for c in locals_:
        c.start()

    copies = []
    k = 0
    for s in range(1, ndp):
        peer = lax.rem(d + s, ndp)
        for src, dst in ((g_ref, gf_ref.at[rows]), (u_ref, uf_ref.at[rows]),
                         (dn_ref, df_ref.at[:, cols])):
            copies.append(pltpu.make_async_remote_copy(
                src_ref=src, dst_ref=dst, send_sem=send_sem.at[k], recv_sem=recv_sem.at[k],
                device_id=(peer, m), device_id_type=MESH))
            k += 1
    for c in copies:
        c.start()
    for c in locals_:
        c.wait()
    for c in copies:
        c.wait()


def gather_weights_direct(g, u, dn, ndp):
    n_copies = 3 * (ndp - 1)
    any_spec = pl.BlockSpec(memory_space=pl.ANY)
    out_shape = (
        jax.ShapeDtypeStruct((g.shape[0] * ndp, g.shape[1]), g.dtype),
        jax.ShapeDtypeStruct((u.shape[0] * ndp, u.shape[1]), u.dtype),
        jax.ShapeDtypeStruct((dn.shape[0], dn.shape[1] * ndp), dn.dtype),
    )
    return pl.pallas_call(
        functools.partial(gather_kernel, ndp),
        out_shape=out_shape,
        in_specs=[any_spec] * 3,
        out_specs=[any_spec] * 3,
        scratch_shapes=[
            pltpu.SemaphoreType.DMA((n_copies,)),
            pltpu.SemaphoreType.DMA((n_copies,)),
            pltpu.SemaphoreType.DMA((3,)),
        ],
        compiler_params=pltpu.CompilerParams(has_side_effects=True),
    )(g, u, dn)


def relay_gather_kernel(h_ref, g_ref, u_ref, dn_ref, hf_ref, gf_ref, uf_ref, df_ref, send_sem,
                        recv_sem, local_sem, hsend, hrecv):
    ndp = 8
    d = lax.axis_index("dp")
    m = lax.axis_index("mp")
    lo = d % 2
    partner = d - lo + (1 - lo)
    nxt = (d + 2) % ndp
    prv = (d + ndp - 2) % ndp
    far = (d + 4) % ndp
    owns = (g_ref, u_ref, dn_ref)
    fulls = (gf_ref, uf_ref, df_ref)

    def slot(w, idx, half=None):
        if w < 2:
            kr = owns[w].shape[0]
            if half is None:
                return fulls[w].at[pl.ds(pl.multiple_of(idx * kr, kr), kr)]
            hk = kr // 2
            return fulls[w].at[pl.ds(pl.multiple_of(idx * kr + half * hk, hk), hk)]
        rr, dc = owns[w].shape
        cols = pl.ds(pl.multiple_of(idx * dc, dc), dc)
        if half is None:
            return fulls[w].at[:, cols]
        hr = rr // 2
        return fulls[w].at[pl.ds(half * hr, hr), cols]

    def rc(w, k, src, dst, target):
        i = w * 8 + k
        return pltpu.make_async_remote_copy(
            src_ref=src, dst_ref=dst, send_sem=send_sem.at[i], recv_sem=recv_sem.at[i],
            device_id=(target, m), device_id_type=MESH)

    locals_ = [pltpu.make_async_copy(owns[w], slot(w, d), local_sem.at[w]) for w in range(3)]
    c = {}
    for w in range(3):
        c[w, 0] = rc(w, 0, owns[w], slot(w, d), partner)
        c[w, 1] = rc(w, 1, owns[w], slot(w, d), nxt)
        c[w, 2] = rc(w, 2, owns[w], slot(w, d), prv)
        c[w, 3] = rc(w, 3, slot(w, partner), slot(w, partner), nxt)
        c[w, 4] = rc(w, 4, slot(w, partner), slot(w, partner), prv)
        c[w, 5] = rc(w, 5, slot(w, prv, 0), slot(w, prv, 0), nxt)
        c[w, 6] = rc(w, 6, slot(w, nxt, 1), slot(w, nxt, 1), prv)
        c[w, 7] = rc(w, 7, slot(w, far), slot(w, far), partner)
    nmp = 16
    hc = h_ref.shape[1]
    hmine = hf_ref.at[:, pl.ds(pl.multiple_of(m * hc, hc), hc)]
    hlocal = pltpu.make_async_copy(h_ref, hmine, local_sem.at[3])
    hcopies = []
    for s in range(1, nmp):
        hcopies.append(pltpu.make_async_remote_copy(
            src_ref=h_ref, dst_ref=hmine, send_sem=hsend.at[s - 1], recv_sem=hrecv.at[s - 1],
            device_id=(d, lax.rem(m + s, nmp)), device_id_type=MESH))
    for w in range(3):
        locals_[w].start()
        for k in range(3):
            c[w, k].start()
    hlocal.start()
    for cp in hcopies:
        cp.start()
    for w in range(3):
        c[w, 1].wait_recv()
        c[w, 5].start()
        c[w, 2].wait_recv()
        c[w, 6].start()
    for w in range(3):
        c[w, 5].wait_recv()
        c[w, 6].wait_recv()
        c[w, 7].start()
    for w in range(3):
        c[w, 0].wait_recv()
        c[w, 3].start()
        c[w, 4].start()
    for w in range(3):
        for k in (3, 4, 7):
            c[w, k].wait_recv()
    for w in range(3):
        for k in range(8):
            c[w, k].wait_send()
        locals_[w].wait()
    hlocal.wait()
    for cp in hcopies:
        cp.wait()


def gather_relay(h, g, u, dn, ndp):
    any_spec = pl.BlockSpec(memory_space=pl.ANY)
    out_shape = (
        jax.ShapeDtypeStruct((g.shape[0] * ndp, g.shape[1]), g.dtype),
        jax.ShapeDtypeStruct((u.shape[0] * ndp, u.shape[1]), u.dtype),
        jax.ShapeDtypeStruct((dn.shape[0], dn.shape[1] * ndp), dn.dtype),
    )
    return pl.pallas_call(
        relay_gather_kernel,
        out_shape=(jax.ShapeDtypeStruct((h.shape[0], h.shape[1] * 16), h.dtype),) + out_shape,
        in_specs=[any_spec] * 4,
        out_specs=[any_spec] * 4,
        scratch_shapes=[
            pltpu.SemaphoreType.DMA((24,)),
            pltpu.SemaphoreType.DMA((24,)),
            pltpu.SemaphoreType.DMA((4,)),
            pltpu.SemaphoreType.DMA((15,)),
            pltpu.SemaphoreType.DMA((15,)),
        ],
        compiler_params=pltpu.CompilerParams(has_side_effects=True),
    )(h, g, u, dn)


def reduce_kernel(nmp, t_ref, o_ref, buf, send_sem, recv_sem, local_sem):
    d = lax.axis_index("dp")
    m = lax.axis_index("mp")
    w = o_ref.shape[2]
    mine = pl.ds(pl.multiple_of(m * w, w), w)
    local_copy = pltpu.make_async_copy(t_ref.at[:, :, mine], buf.at[0], local_sem.at[0])
    local_copy.start()
    copies = []
    for s in range(1, nmp):
        peer = lax.rem(m + s, nmp)
        theirs = pl.ds(pl.multiple_of(peer * w, w), w)
        copies.append(pltpu.make_async_remote_copy(
            src_ref=t_ref.at[:, :, theirs], dst_ref=buf.at[s], send_sem=send_sem.at[s],
            recv_sem=recv_sem.at[s], device_id=(d, peer), device_id_type=MESH))
    for c in copies:
        c.start()
    local_copy.wait()
    for c in copies:
        c.wait()
    rows = 32

    def body(i, carry):
        r = pl.ds(pl.multiple_of(i * rows, rows), rows)
        for k in range(o_ref.shape[0]):
            acc = buf[0, k, r, :].astype(jnp.float32)
            for s in range(1, nmp):
                acc = acc + buf[s, k, r, :].astype(jnp.float32)
            o_ref[k, r, :] = acc.astype(o_ref.dtype)
        return carry

    lax.fori_loop(0, o_ref.shape[1] // rows, body, 0)


def reduce_scatter(terms, nmp):
    n, t, width = terms.shape
    w = width // nmp
    return pl.pallas_call(
        functools.partial(reduce_kernel, nmp),
        out_shape=jax.ShapeDtypeStruct((n, t, w), jnp.bfloat16),
        in_specs=[pl.BlockSpec(memory_space=pl.ANY)],
        out_specs=pl.BlockSpec(memory_space=pltpu.VMEM),
        scratch_shapes=[
            pltpu.VMEM((nmp, n, t, w), jnp.bfloat16),
            pltpu.SemaphoreType.DMA((nmp,)),
            pltpu.SemaphoreType.DMA((nmp,)),
            pltpu.SemaphoreType.DMA((1,)),
        ],
        compiler_params=pltpu.CompilerParams(has_side_effects=True,
                                             vmem_limit_bytes=48 * 1024 * 1024),
    )(terms)


def hier_reduce_kernel(ta_ref, tb_ref, o_ref, own, r1, sb2, r2, s2, sb3, r3,
                       ls, ss1, rs1, ss2, rs2, ss3, rs3):
    d = lax.axis_index("dp")
    m = lax.axis_index("mp")
    c = m % 2
    z = (m // 2) % 4
    xh = m // 8
    w = o_ref.shape[2]
    rows = 32
    nchunk = o_ref.shape[1] // rows

    def blk(b, k):
        return (ta_ref, tb_ref)[k].at[:, pl.ds(pl.multiple_of(b * w, w), w)]

    def dev(mm):
        return (d, mm)

    locs = []
    st1 = []
    for j in range(16):
        bx, bz, k = j // 8, (j // 2) % 4, j % 2
        jj = bx * 4 + bz
        locs.append(pltpu.make_async_copy(blk(bx * 8 + bz * 2 + c, k), own.at[jj, k],
                                          ls.at[j]))
        st1.append(pltpu.make_async_remote_copy(
            src_ref=blk(bx * 8 + bz * 2 + (1 - c), k), dst_ref=r1.at[jj, k], send_sem=ss1.at[j],
            recv_sem=rs1.at[j], device_id=dev(m + 1 - 2 * c), device_id_type=MESH))
    for j in range(16):
        st1[j].start()
        locs[j].start()
    for j in range(16):
        locs[j].wait()
        st1[j].wait()

    st2 = []
    for s in range(1, 4):
        zt = (z + s) % 4

        def fill(i, carry, s=s, zt=zt):
            r = pl.ds(pl.multiple_of(i * rows, rows), rows)
            for bx in range(2):
                idx = bx * 4 + zt
                sb2[s - 1, bx, :, r, :] = (own[idx, :, r, :].astype(jnp.float32)
                                           + r1[idx, :, r, :].astype(jnp.float32)
                                           ).astype(sb2.dtype)
            return carry

        lax.fori_loop(0, nchunk, fill, 0)
        cp = pltpu.make_async_remote_copy(
            src_ref=sb2.at[s - 1], dst_ref=r2.at[s - 1], send_sem=ss2.at[s - 1],
            recv_sem=rs2.at[s - 1], device_id=dev(xh * 8 + zt * 2 + c), device_id_type=MESH)
        cp.start()
        st2.append(cp)
    for cp in st2:
        cp.wait()

    def sum2(i, carry):
        r = pl.ds(pl.multiple_of(i * rows, rows), rows)
        for bx in range(2):
            idx = bx * 4 + z
            acc = own[idx, :, r, :].astype(jnp.float32) + r1[idx, :, r, :].astype(jnp.float32)
            for k in range(3):
                acc = acc + r2[k, bx, :, r, :].astype(jnp.float32)
            s2[bx, :, r, :] = acc
        return carry

    lax.fori_loop(0, nchunk, sum2, 0)
    sb3[...] = s2[1 - xh].astype(sb3.dtype)
    cp3 = pltpu.make_async_remote_copy(
        src_ref=sb3, dst_ref=r3, send_sem=ss3.at[0], recv_sem=rs3.at[0],
        device_id=dev(m + 8 - 16 * xh), device_id_type=MESH)
    cp3.start()
    cp3.wait()
    o_ref[...] = (s2[xh] + r3[...].astype(jnp.float32)).astype(o_ref.dtype)


def hier_reduce_scatter(ta, tb):
    n = 2
    t, width = ta.shape
    w = width // 16
    bf = jnp.bfloat16
    dma = pltpu.SemaphoreType.DMA
    return pl.pallas_call(
        hier_reduce_kernel,
        out_shape=jax.ShapeDtypeStruct((n, t, w), bf),
        in_specs=[pl.BlockSpec(memory_space=pl.ANY)] * 2,
        out_specs=pl.BlockSpec(memory_space=pltpu.VMEM),
        scratch_shapes=[
            pltpu.VMEM((8, n, t, w), bf),
            pltpu.VMEM((8, n, t, w), bf),
            pltpu.VMEM((3, 2, n, t, w), bf),
            pltpu.VMEM((3, 2, n, t, w), bf),
            pltpu.VMEM((2, n, t, w), jnp.float32),
            pltpu.VMEM((n, t, w), bf),
            pltpu.VMEM((n, t, w), bf),
            dma((16,)), dma((16,)), dma((16,)), dma((3,)), dma((3,)), dma((1,)), dma((1,)),
        ],
        compiler_params=pltpu.CompilerParams(has_side_effects=True,
                                             vmem_limit_bytes=56 * 1024 * 1024),
    )(ta, tb)


def split_reduce_kernel(ta_ref, tb_ref, o_ref, own, r1, sa2, ra2, fa2, sa3, ra3,
                        sb2, rb2, fb2, sb3, rb3, ls, ss1, rs1, ssa2, rsa2, ssa3, rsa3,
                        ssb2, rsb2, ssb3, rsb3):
    d = lax.axis_index("dp")
    m = lax.axis_index("mp")
    c = m % 2
    z = (m // 2) % 4
    xh = m // 8
    w = o_ref.shape[2]
    half = o_ref.shape[1] // 2
    ra = pl.ds(0, half)
    rb = pl.ds(half, half)
    rows = 32
    nchunk = half // rows
    f32 = jnp.float32
    xpeer = m + 8 - 16 * xh

    def blk(b, k):
        return (ta_ref, tb_ref)[k].at[:, pl.ds(pl.multiple_of(b * w, w), w)]

    def rcopy(src, dst, ss, rs, mm):
        return pltpu.make_async_remote_copy(src_ref=src, dst_ref=dst, send_sem=ss, recv_sem=rs,
                                            device_id=(d, mm), device_id_type=MESH)

    locs = []
    st1 = []
    for j in range(16):
        bx, bz, k = j // 8, (j // 2) % 4, j % 2
        jj = bx * 4 + bz
        locs.append(pltpu.make_async_copy(blk(bx * 8 + bz * 2 + c, k), own.at[jj, k],
                                          ls.at[j]))
        st1.append(rcopy(blk(bx * 8 + bz * 2 + (1 - c), k), r1.at[jj, k], ss1.at[j], rs1.at[j],
                         m + 1 - 2 * c))
    for j in range(16):
        st1[j].start()
        locs[j].start()
    for j in range(16):
        locs[j].wait()
        st1[j].wait()

    def pair_sum(idx, r):
        return own[idx, :, r, :].astype(f32) + r1[idx, :, r, :].astype(f32)

    def fill_b2(i, carry):
        r = pl.ds(pl.multiple_of(half + i * rows, rows), rows)
        q = pl.ds(pl.multiple_of(i * rows, rows), rows)
        for bz in range(4):
            sb2[bz, :, q, :] = pair_sum((1 - xh) * 4 + bz, r).astype(sb2.dtype)
        return carry

    lax.fori_loop(0, nchunk, fill_b2, 0)
    cb2 = rcopy(sb2, rb2, ssb2.at[0], rsb2.at[0], xpeer)
    cb2.start()
    ca2 = []
    for s in range(1, 4):
        zt = (z + s) % 4

        def fill_a2(i, carry, s=s, zt=zt):
            q = pl.ds(pl.multiple_of(i * rows, rows), rows)
            for bx in range(2):
                sa2[s - 1, bx, :, q, :] = pair_sum(bx * 4 + zt, q).astype(sa2.dtype)
            return carry

        lax.fori_loop(0, nchunk, fill_a2, 0)
        cp = rcopy(sa2.at[s - 1], ra2.at[s - 1], ssa2.at[s - 1], rsa2.at[s - 1],
                   xh * 8 + zt * 2 + c)
        cp.start()
        ca2.append(cp)

    cb2.wait()

    def sum_b2(i, carry):
        r = pl.ds(pl.multiple_of(half + i * rows, rows), rows)
        q = pl.ds(pl.multiple_of(i * rows, rows), rows)
        for bz in range(4):
            fb2[bz, :, q, :] = pair_sum(xh * 4 + bz, r) + rb2[bz, :, q, :].astype(f32)
        return carry

    lax.fori_loop(0, nchunk, sum_b2, 0)
    cb3 = []
    for s in range(1, 4):
        zt = (z + s) % 4
        sb3[s - 1] = fb2[zt].astype(sb3.dtype)
        cp = rcopy(sb3.at[s - 1], rb3.at[s - 1], ssb3.at[s - 1], rsb3.at[s - 1],
                   xh * 8 + zt * 2 + c)
        cp.start()
        cb3.append(cp)

    for cp in ca2:
        cp.wait()

    def sum_a2(i, carry):
        q = pl.ds(pl.multiple_of(i * rows, rows), rows)
        for bx in range(2):
            acc = pair_sum(bx * 4 + z, q)
            for k in range(3):
                acc = acc + ra2[k, bx, :, q, :].astype(f32)
            fa2[bx, :, q, :] = acc
        return carry

    lax.fori_loop(0, nchunk, sum_a2, 0)
    sa3[...] = fa2[1 - xh].astype(sa3.dtype)
    ca3 = rcopy(sa3, ra3, ssa3.at[0], rsa3.at[0], xpeer)
    ca3.start()
    for cp in cb3:
        cp.wait()
    acc = fb2[z]
    for k in range(3):
        acc = acc + rb3[k].astype(f32)
    o_ref[:, rb, :] = acc.astype(o_ref.dtype)
    ca3.wait()
    o_ref[:, ra, :] = (fa2[xh] + ra3[...].astype(f32)).astype(o_ref.dtype)


def split_reduce_scatter(ta, tb):
    n = 2
    t, width = ta.shape
    w = width // 16
    h = t // 2
    bf = jnp.bfloat16
    f32 = jnp.float32
    dma = pltpu.SemaphoreType.DMA
    return pl.pallas_call(
        split_reduce_kernel,
        out_shape=jax.ShapeDtypeStruct((n, t, w), bf),
        in_specs=[pl.BlockSpec(memory_space=pl.ANY)] * 2,
        out_specs=pl.BlockSpec(memory_space=pltpu.VMEM),
        scratch_shapes=[
            pltpu.VMEM((8, n, t, w), bf),
            pltpu.VMEM((8, n, t, w), bf),
            pltpu.VMEM((3, 2, n, h, w), bf),
            pltpu.VMEM((3, 2, n, h, w), bf),
            pltpu.VMEM((2, n, h, w), f32),
            pltpu.VMEM((n, h, w), bf),
            pltpu.VMEM((n, h, w), bf),
            pltpu.VMEM((4, n, h, w), bf),
            pltpu.VMEM((4, n, h, w), bf),
            pltpu.VMEM((4, n, h, w), f32),
            pltpu.VMEM((3, n, h, w), bf),
            pltpu.VMEM((3, n, h, w), bf),
            dma((16,)), dma((16,)), dma((16,)),
            dma((3,)), dma((3,)), dma((1,)), dma((1,)),
            dma((1,)), dma((1,)), dma((3,)), dma((3,)),
        ],
        compiler_params=pltpu.CompilerParams(has_side_effects=True,
                                             vmem_limit_bytes=56 * 1024 * 1024),
    )(ta, tb)


def gate_up_kernel(h_ref, go_ref, gp_ref, uo_ref, upv_ref, io_ref, it_ref, acc, tbuf):
    k = pl.program_id(0)
    tile = 128
    chunk = 64
    f32 = jnp.float32

    @pl.when(k == 0)
    def _():
        acc[...] = jnp.zeros_like(acc)

    def mix(i, carry):
        r = pl.ds(pl.multiple_of(i * chunk, chunk), chunk)
        for j, (on_ref, pv_ref) in enumerate(((go_ref, gp_ref), (uo_ref, upv_ref))):
            on = on_ref[r, :].astype(f32)
            pv = pv_ref[r, :].astype(f32)
            tbuf[j, r, :] = (POLYAK * on + (1.0 - POLYAK) * pv).astype(tbuf.dtype)
        return carry

    lax.fori_loop(0, go_ref.shape[0] // chunk, mix, 0)

    def mm(i, carry):
        r = pl.ds(pl.multiple_of(i * tile, tile), tile)
        hs = h_ref[r, :]
        acc[0, r, :] += jnp.dot(hs, go_ref[...], preferred_element_type=f32)
        acc[1, r, :] += jnp.dot(hs, tbuf[0], preferred_element_type=f32)
        acc[2, r, :] += jnp.dot(hs, uo_ref[...], preferred_element_type=f32)
        acc[3, r, :] += jnp.dot(hs, tbuf[1], preferred_element_type=f32)
        return carry

    lax.fori_loop(0, h_ref.shape[0] // tile, mm, 0)

    @pl.when(k == pl.num_programs(0) - 1)
    def _():
        def finish(i, carry):
            r = pl.ds(pl.multiple_of(i * chunk, chunk), chunk)
            io_ref[r, :] = (jax.nn.silu(acc[0, r, :]) * acc[2, r, :]).astype(io_ref.dtype)
            it_ref[r, :] = (jax.nn.silu(acc[1, r, :]) * acc[3, r, :]).astype(it_ref.dtype)
            return carry

        lax.fori_loop(0, io_ref.shape[0] // chunk, finish, 0)


def gate_up(h_full, go, gp, uo, upv, kb):
    tokens, kdim = h_full.shape
    ff = go.shape[1]
    wspec = pl.BlockSpec((kb, ff), lambda k: (k, 0))
    ospec = pl.BlockSpec((tokens, ff), lambda k: (0, 0))
    flops = 8 * tokens * kdim * ff
    nbytes = 2 * (tokens * kdim + 4 * kdim * ff + 2 * tokens * ff)
    return pl.pallas_call(
        gate_up_kernel,
        grid=(kdim // kb,),
        out_shape=(jax.ShapeDtypeStruct((tokens, ff), jnp.bfloat16),) * 2,
        in_specs=[pl.BlockSpec((tokens, kb), lambda k: (0, k))] + [wspec] * 4,
        out_specs=[ospec, ospec],
        scratch_shapes=[pltpu.VMEM((4, tokens, ff), jnp.float32),
                        pltpu.VMEM((2, kb, ff), jnp.bfloat16)],
        compiler_params=pltpu.CompilerParams(vmem_limit_bytes=48 * 1024 * 1024),
        cost_estimate=pl.CostEstimate(flops=flops, bytes_accessed=nbytes,
                                      transcendentals=2 * tokens * ff),
    )(h_full, go, gp, uo, upv)


def local(ndp, nmp, hidden_states, gate_online, up_online, down_online, gate_previous,
          up_previous, down_previous):
    if ndp == 8 and nmp == 16:
        features_all, gate_full, up_full, down_full = gather_relay(
            hidden_states, gate_online, up_online, down_online, ndp)
    else:
        features_all = lax.all_gather(hidden_states, "mp", axis=1, tiled=True)
        gate_full, up_full, down_full = gather_weights_direct(gate_online, up_online,
                                                              down_online, ndp)

    inner_o, inner_t = gate_up(features_all, gate_full, gate_previous, up_full, up_previous,
                               2 * gate_online.shape[0])
    target_down = blend(down_full, down_previous)
    online_part = jnp.dot(inner_o, down_full, preferred_element_type=jnp.float32)
    target_part = jnp.dot(inner_t, target_down, preferred_element_type=jnp.float32)
    if nmp == 16:
        result = split_reduce_scatter(online_part.astype(jnp.bfloat16),
                                      target_part.astype(jnp.bfloat16))
    else:
        terms = jnp.stack([online_part, target_part], axis=0).astype(jnp.bfloat16)
        result = reduce_scatter(terms, nmp)
    return (result[0], result[1])


def solution(mesh):
    ndp = mesh.shape["dp"]
    nmp = mesh.shape["mp"]
    in_specs = (
        P("dp", "mp"),
        P("dp", "mp"),
        P("dp", "mp"),
        P("mp", "dp"),
        P(None, "mp"),
        P(None, "mp"),
        P("mp", None),
    )
    out_specs = (P("dp", "mp"), P("dp", "mp"))
    return jax.shard_map(functools.partial(local, ndp, nmp), mesh=mesh, in_specs=in_specs,
                         out_specs=out_specs, check_vma=False)
```

```python
import functools

import jax
import jax.numpy as jnp
from jax import lax
from jax.experimental import pallas as pl
from jax.experimental.pallas import tpu as pltpu
from jax.sharding import PartitionSpec as P

POLYAK = 0.25
MESH = pl.DeviceIdType.MESH


def blend(online, previous):
    return (
        POLYAK * online.astype(jnp.float32) + (1.0 - POLYAK) * previous.astype(jnp.float32)
    ).astype(jnp.bfloat16)


def gather_kernel(ndp, g_ref, u_ref, dn_ref, gf_ref, uf_ref, df_ref, send_sem, recv_sem,
                  local_sem):
    d = lax.axis_index("dp")
    m = lax.axis_index("mp")
    kr = g_ref.shape[0]
    dc = dn_ref.shape[1]
    rows = pl.ds(pl.multiple_of(d * kr, kr), kr)
    cols = pl.ds(pl.multiple_of(d * dc, dc), dc)

    locals_ = [
        pltpu.make_async_copy(g_ref, gf_ref.at[rows], local_sem.at[0]),
        pltpu.make_async_copy(u_ref, uf_ref.at[rows], local_sem.at[1]),
        pltpu.make_async_copy(dn_ref, df_ref.at[:, cols], local_sem.at[2]),
    ]
    for c in locals_:
        c.start()

    copies = []
    k = 0
    for s in range(1, ndp):
        peer = lax.rem(d + s, ndp)
        for src, dst in ((g_ref, gf_ref.at[rows]), (u_ref, uf_ref.at[rows]),
                         (dn_ref, df_ref.at[:, cols])):
            copies.append(pltpu.make_async_remote_copy(
                src_ref=src, dst_ref=dst, send_sem=send_sem.at[k], recv_sem=recv_sem.at[k],
                device_id=(peer, m), device_id_type=MESH))
            k += 1
    for c in copies:
        c.start()
    for c in locals_:
        c.wait()
    for c in copies:
        c.wait()


def gather_weights_direct(g, u, dn, ndp):
    n_copies = 3 * (ndp - 1)
    any_spec = pl.BlockSpec(memory_space=pl.ANY)
    out_shape = (
        jax.ShapeDtypeStruct((g.shape[0] * ndp, g.shape[1]), g.dtype),
        jax.ShapeDtypeStruct((u.shape[0] * ndp, u.shape[1]), u.dtype),
        jax.ShapeDtypeStruct((dn.shape[0], dn.shape[1] * ndp), dn.dtype),
    )
    return pl.pallas_call(
        functools.partial(gather_kernel, ndp),
        out_shape=out_shape,
        in_specs=[any_spec] * 3,
        out_specs=[any_spec] * 3,
        scratch_shapes=[
            pltpu.SemaphoreType.DMA((n_copies,)),
            pltpu.SemaphoreType.DMA((n_copies,)),
            pltpu.SemaphoreType.DMA((3,)),
        ],
        compiler_params=pltpu.CompilerParams(has_side_effects=True),
    )(g, u, dn)


def relay_gather_kernel(h_ref, g_ref, u_ref, dn_ref, hf_ref, gf_ref, uf_ref, df_ref, send_sem,
                        recv_sem, local_sem, hsend, hrecv):
    ndp = 8
    d = lax.axis_index("dp")
    m = lax.axis_index("mp")
    lo = d % 2
    partner = d - lo + (1 - lo)
    nxt = (d + 2) % ndp
    prv = (d + ndp - 2) % ndp
    far = (d + 4) % ndp
    owns = (g_ref, u_ref, dn_ref)
    fulls = (gf_ref, uf_ref, df_ref)

    def slot(w, idx, half=None):
        if w < 2:
            kr = owns[w].shape[0]
            if half is None:
                return fulls[w].at[pl.ds(pl.multiple_of(idx * kr, kr), kr)]
            hk = kr // 2
            return fulls[w].at[pl.ds(pl.multiple_of(idx * kr + half * hk, hk), hk)]
        rr, dc = owns[w].shape
        cols = pl.ds(pl.multiple_of(idx * dc, dc), dc)
        if half is None:
            return fulls[w].at[:, cols]
        hr = rr // 2
        return fulls[w].at[pl.ds(half * hr, hr), cols]

    def rc(w, k, src, dst, target):
        i = w * 8 + k
        return pltpu.make_async_remote_copy(
            src_ref=src, dst_ref=dst, send_sem=send_sem.at[i], recv_sem=recv_sem.at[i],
            device_id=(target, m), device_id_type=MESH)

    locals_ = [pltpu.make_async_copy(owns[w], slot(w, d), local_sem.at[w]) for w in range(3)]
    c = {}
    for w in range(3):
        c[w, 0] = rc(w, 0, owns[w], slot(w, d), partner)
        c[w, 1] = rc(w, 1, owns[w], slot(w, d), nxt)
        c[w, 2] = rc(w, 2, owns[w], slot(w, d), prv)
        c[w, 3] = rc(w, 3, slot(w, partner), slot(w, partner), nxt)
        c[w, 4] = rc(w, 4, slot(w, partner), slot(w, partner), prv)
        c[w, 5] = rc(w, 5, slot(w, prv, 0), slot(w, prv, 0), nxt)
        c[w, 6] = rc(w, 6, slot(w, nxt, 1), slot(w, nxt, 1), prv)
        c[w, 7] = rc(w, 7, slot(w, far), slot(w, far), partner)
    nmp = 16
    hc = h_ref.shape[1]
    hmine = hf_ref.at[:, pl.ds(pl.multiple_of(m * hc, hc), hc)]
    hlocal = pltpu.make_async_copy(h_ref, hmine, local_sem.at[3])
    hcopies = []
    for s in range(1, nmp):
        hcopies.append(pltpu.make_async_remote_copy(
            src_ref=h_ref, dst_ref=hmine, send_sem=hsend.at[s - 1], recv_sem=hrecv.at[s - 1],
            device_id=(d, lax.rem(m + s, nmp)), device_id_type=MESH))
    for w in range(3):
        locals_[w].start()
        for k in range(3):
            c[w, k].start()
    hlocal.start()
    for cp in hcopies:
        cp.start()
    for w in range(3):
        c[w, 1].wait_recv()
        c[w, 5].start()
        c[w, 2].wait_recv()
        c[w, 6].start()
    for w in range(3):
        c[w, 5].wait_recv()
        c[w, 6].wait_recv()
        c[w, 7].start()
    for w in range(3):
        c[w, 0].wait_recv()
        c[w, 3].start()
        c[w, 4].start()
    for w in range(3):
        for k in (3, 4, 7):
            c[w, k].wait_recv()
    for w in range(3):
        for k in range(8):
            c[w, k].wait_send()
        locals_[w].wait()
    hlocal.wait()
    for cp in hcopies:
        cp.wait()


def gather_relay(h, g, u, dn, ndp):
    any_spec = pl.BlockSpec(memory_space=pl.ANY)
    out_shape = (
        jax.ShapeDtypeStruct((g.shape[0] * ndp, g.shape[1]), g.dtype),
        jax.ShapeDtypeStruct((u.shape[0] * ndp, u.shape[1]), u.dtype),
        jax.ShapeDtypeStruct((dn.shape[0], dn.shape[1] * ndp), dn.dtype),
    )
    return pl.pallas_call(
        relay_gather_kernel,
        out_shape=(jax.ShapeDtypeStruct((h.shape[0], h.shape[1] * 16), h.dtype),) + out_shape,
        in_specs=[any_spec] * 4,
        out_specs=[any_spec] * 4,
        scratch_shapes=[
            pltpu.SemaphoreType.DMA((24,)),
            pltpu.SemaphoreType.DMA((24,)),
            pltpu.SemaphoreType.DMA((4,)),
            pltpu.SemaphoreType.DMA((15,)),
            pltpu.SemaphoreType.DMA((15,)),
        ],
        compiler_params=pltpu.CompilerParams(has_side_effects=True),
    )(h, g, u, dn)


def reduce_kernel(nmp, t_ref, o_ref, buf, send_sem, recv_sem, local_sem):
    d = lax.axis_index("dp")
    m = lax.axis_index("mp")
    w = o_ref.shape[2]
    mine = pl.ds(pl.multiple_of(m * w, w), w)
    local_copy = pltpu.make_async_copy(t_ref.at[:, :, mine], buf.at[0], local_sem.at[0])
    local_copy.start()
    copies = []
    for s in range(1, nmp):
        peer = lax.rem(m + s, nmp)
        theirs = pl.ds(pl.multiple_of(peer * w, w), w)
        copies.append(pltpu.make_async_remote_copy(
            src_ref=t_ref.at[:, :, theirs], dst_ref=buf.at[s], send_sem=send_sem.at[s],
            recv_sem=recv_sem.at[s], device_id=(d, peer), device_id_type=MESH))
    for c in copies:
        c.start()
    local_copy.wait()
    for c in copies:
        c.wait()
    rows = 32

    def body(i, carry):
        r = pl.ds(pl.multiple_of(i * rows, rows), rows)
        for k in range(o_ref.shape[0]):
            acc = buf[0, k, r, :].astype(jnp.float32)
            for s in range(1, nmp):
                acc = acc + buf[s, k, r, :].astype(jnp.float32)
            o_ref[k, r, :] = acc.astype(o_ref.dtype)
        return carry

    lax.fori_loop(0, o_ref.shape[1] // rows, body, 0)


def reduce_scatter(terms, nmp):
    n, t, width = terms.shape
    w = width // nmp
    return pl.pallas_call(
        functools.partial(reduce_kernel, nmp),
        out_shape=jax.ShapeDtypeStruct((n, t, w), jnp.bfloat16),
        in_specs=[pl.BlockSpec(memory_space=pl.ANY)],
        out_specs=pl.BlockSpec(memory_space=pltpu.VMEM),
        scratch_shapes=[
            pltpu.VMEM((nmp, n, t, w), jnp.bfloat16),
            pltpu.SemaphoreType.DMA((nmp,)),
            pltpu.SemaphoreType.DMA((nmp,)),
            pltpu.SemaphoreType.DMA((1,)),
        ],
        compiler_params=pltpu.CompilerParams(has_side_effects=True,
                                             vmem_limit_bytes=48 * 1024 * 1024),
    )(terms)


def hier_reduce_kernel(ta_ref, tb_ref, o_ref, own, r1, sb2, r2, s2, sb3, r3,
                       ls, ss1, rs1, ss2, rs2, ss3, rs3):
    d = lax.axis_index("dp")
    m = lax.axis_index("mp")
    c = m % 2
    z = (m // 2) % 4
    xh = m // 8
    w = o_ref.shape[2]
    rows = 32
    nchunk = o_ref.shape[1] // rows

    def blk(b, k):
        return (ta_ref, tb_ref)[k].at[:, pl.ds(pl.multiple_of(b * w, w), w)]

    def dev(mm):
        return (d, mm)

    locs = []
    st1 = []
    for j in range(16):
        bx, bz, k = j // 8, (j // 2) % 4, j % 2
        jj = bx * 4 + bz
        locs.append(pltpu.make_async_copy(blk(bx * 8 + bz * 2 + c, k), own.at[jj, k],
                                          ls.at[j]))
        st1.append(pltpu.make_async_remote_copy(
            src_ref=blk(bx * 8 + bz * 2 + (1 - c), k), dst_ref=r1.at[jj, k], send_sem=ss1.at[j],
            recv_sem=rs1.at[j], device_id=dev(m + 1 - 2 * c), device_id_type=MESH))
    for j in range(16):
        st1[j].start()
        locs[j].start()
    for j in range(16):
        locs[j].wait()
        st1[j].wait()

    st2 = []
    for s in range(1, 4):
        zt = (z + s) % 4

        def fill(i, carry, s=s, zt=zt):
            r = pl.ds(pl.multiple_of(i * rows, rows), rows)
            for bx in range(2):
                idx = bx * 4 + zt
                sb2[s - 1, bx, :, r, :] = (own[idx, :, r, :].astype(jnp.float32)
                                           + r1[idx, :, r, :].astype(jnp.float32)
                                           ).astype(sb2.dtype)
            return carry

        lax.fori_loop(0, nchunk, fill, 0)
        cp = pltpu.make_async_remote_copy(
            src_ref=sb2.at[s - 1], dst_ref=r2.at[s - 1], send_sem=ss2.at[s - 1],
            recv_sem=rs2.at[s - 1], device_id=dev(xh * 8 + zt * 2 + c), device_id_type=MESH)
        cp.start()
        st2.append(cp)
    for cp in st2:
        cp.wait()

    def sum2(i, carry):
        r = pl.ds(pl.multiple_of(i * rows, rows), rows)
        for bx in range(2):
            idx = bx * 4 + z
            acc = own[idx, :, r, :].astype(jnp.float32) + r1[idx, :, r, :].astype(jnp.float32)
            for k in range(3):
                acc = acc + r2[k, bx, :, r, :].astype(jnp.float32)
            s2[bx, :, r, :] = acc
        return carry

    lax.fori_loop(0, nchunk, sum2, 0)
    sb3[...] = s2[1 - xh].astype(sb3.dtype)
    cp3 = pltpu.make_async_remote_copy(
        src_ref=sb3, dst_ref=r3, send_sem=ss3.at[0], recv_sem=rs3.at[0],
        device_id=dev(m + 8 - 16 * xh), device_id_type=MESH)
    cp3.start()
    cp3.wait()
    o_ref[...] = (s2[xh] + r3[...].astype(jnp.float32)).astype(o_ref.dtype)


def hier_reduce_scatter(ta, tb):
    n = 2
    t, width = ta.shape
    w = width // 16
    bf = jnp.bfloat16
    dma = pltpu.SemaphoreType.DMA
    return pl.pallas_call(
        hier_reduce_kernel,
        out_shape=jax.ShapeDtypeStruct((n, t, w), bf),
        in_specs=[pl.BlockSpec(memory_space=pl.ANY)] * 2,
        out_specs=pl.BlockSpec(memory_space=pltpu.VMEM),
        scratch_shapes=[
            pltpu.VMEM((8, n, t, w), bf),
            pltpu.VMEM((8, n, t, w), bf),
            pltpu.VMEM((3, 2, n, t, w), bf),
            pltpu.VMEM((3, 2, n, t, w), bf),
            pltpu.VMEM((2, n, t, w), jnp.float32),
            pltpu.VMEM((n, t, w), bf),
            pltpu.VMEM((n, t, w), bf),
            dma((16,)), dma((16,)), dma((16,)), dma((3,)), dma((3,)), dma((1,)), dma((1,)),
        ],
        compiler_params=pltpu.CompilerParams(has_side_effects=True,
                                             vmem_limit_bytes=56 * 1024 * 1024),
    )(ta, tb)


def split_reduce_kernel(ta_ref, tb_ref, o_ref, own, r1, sa2, ra2, fa2, sa3, ra3,
                        sb2, rb2, fb2, sb3, rb3, ls, ss1, rs1, ssa2, rsa2, ssa3, rsa3,
                        ssb2, rsb2, ssb3, rsb3):
    d = lax.axis_index("dp")
    m = lax.axis_index("mp")
    c = m % 2
    z = (m // 2) % 4
    xh = m // 8
    w = o_ref.shape[2]
    half = o_ref.shape[1] // 2
    ra = pl.ds(0, half)
    rb = pl.ds(half, half)
    rows = 32
    nchunk = half // rows
    f32 = jnp.float32
    xpeer = m + 8 - 16 * xh

    def blk(b, k):
        return (ta_ref, tb_ref)[k].at[:, pl.ds(pl.multiple_of(b * w, w), w)]

    def rcopy(src, dst, ss, rs, mm):
        return pltpu.make_async_remote_copy(src_ref=src, dst_ref=dst, send_sem=ss, recv_sem=rs,
                                            device_id=(d, mm), device_id_type=MESH)

    locs = []
    st1 = []
    for j in range(16):
        bx, bz, k = j // 8, (j // 2) % 4, j % 2
        jj = bx * 4 + bz
        locs.append(pltpu.make_async_copy(blk(bx * 8 + bz * 2 + c, k), own.at[jj, k],
                                          ls.at[j]))
        st1.append(rcopy(blk(bx * 8 + bz * 2 + (1 - c), k), r1.at[jj, k], ss1.at[j], rs1.at[j],
                         m + 1 - 2 * c))
    for j in range(16):
        st1[j].start()
        locs[j].start()
    for j in range(16):
        locs[j].wait()
        st1[j].wait()

    def pair_sum(idx, r):
        return own[idx, :, r, :].astype(f32) + r1[idx, :, r, :].astype(f32)

    def fill_b2(i, carry):
        r = pl.ds(pl.multiple_of(half + i * rows, rows), rows)
        q = pl.ds(pl.multiple_of(i * rows, rows), rows)
        for bz in range(4):
            sb2[bz, :, q, :] = pair_sum((1 - xh) * 4 + bz, r).astype(sb2.dtype)
        return carry

    lax.fori_loop(0, nchunk, fill_b2, 0)
    cb2 = rcopy(sb2, rb2, ssb2.at[0], rsb2.at[0], xpeer)
    cb2.start()
    ca2 = []
    for s in range(1, 4):
        zt = (z + s) % 4

        def fill_a2(i, carry, s=s, zt=zt):
            q = pl.ds(pl.multiple_of(i * rows, rows), rows)
            for bx in range(2):
                sa2[s - 1, bx, :, q, :] = pair_sum(bx * 4 + zt, q).astype(sa2.dtype)
            return carry

        lax.fori_loop(0, nchunk, fill_a2, 0)
        cp = rcopy(sa2.at[s - 1], ra2.at[s - 1], ssa2.at[s - 1], rsa2.at[s - 1],
                   xh * 8 + zt * 2 + c)
        cp.start()
        ca2.append(cp)

    cb2.wait()

    def sum_b2(i, carry):
        r = pl.ds(pl.multiple_of(half + i * rows, rows), rows)
        q = pl.ds(pl.multiple_of(i * rows, rows), rows)
        for bz in range(4):
            fb2[bz, :, q, :] = pair_sum(xh * 4 + bz, r) + rb2[bz, :, q, :].astype(f32)
        return carry

    lax.fori_loop(0, nchunk, sum_b2, 0)
    cb3 = []
    for s in range(1, 4):
        zt = (z + s) % 4
        sb3[s - 1] = fb2[zt].astype(sb3.dtype)
        cp = rcopy(sb3.at[s - 1], rb3.at[s - 1], ssb3.at[s - 1], rsb3.at[s - 1],
                   xh * 8 + zt * 2 + c)
        cp.start()
        cb3.append(cp)

    for cp in ca2:
        cp.wait()

    def sum_a2(i, carry):
        q = pl.ds(pl.multiple_of(i * rows, rows), rows)
        for bx in range(2):
            acc = pair_sum(bx * 4 + z, q)
            for k in range(3):
                acc = acc + ra2[k, bx, :, q, :].astype(f32)
            fa2[bx, :, q, :] = acc
        return carry

    lax.fori_loop(0, nchunk, sum_a2, 0)
    sa3[...] = fa2[1 - xh].astype(sa3.dtype)
    ca3 = rcopy(sa3, ra3, ssa3.at[0], rsa3.at[0], xpeer)
    ca3.start()
    for cp in cb3:
        cp.wait()
    acc = fb2[z]
    for k in range(3):
        acc = acc + rb3[k].astype(f32)
    o_ref[:, rb, :] = acc.astype(o_ref.dtype)
    ca3.wait()
    o_ref[:, ra, :] = (fa2[xh] + ra3[...].astype(f32)).astype(o_ref.dtype)


def split_reduce_scatter(ta, tb):
    n = 2
    t, width = ta.shape
    w = width // 16
    h = t // 2
    bf = jnp.bfloat16
    f32 = jnp.float32
    dma = pltpu.SemaphoreType.DMA
    return pl.pallas_call(
        split_reduce_kernel,
        out_shape=jax.ShapeDtypeStruct((n, t, w), bf),
        in_specs=[pl.BlockSpec(memory_space=pl.ANY)] * 2,
        out_specs=pl.BlockSpec(memory_space=pltpu.VMEM),
        scratch_shapes=[
            pltpu.VMEM((8, n, t, w), bf),
            pltpu.VMEM((8, n, t, w), bf),
            pltpu.VMEM((3, 2, n, h, w), bf),
            pltpu.VMEM((3, 2, n, h, w), bf),
            pltpu.VMEM((2, n, h, w), f32),
            pltpu.VMEM((n, h, w), bf),
            pltpu.VMEM((n, h, w), bf),
            pltpu.VMEM((4, n, h, w), bf),
            pltpu.VMEM((4, n, h, w), bf),
            pltpu.VMEM((4, n, h, w), f32),
            pltpu.VMEM((3, n, h, w), bf),
            pltpu.VMEM((3, n, h, w), bf),
            dma((16,)), dma((16,)), dma((16,)),
            dma((3,)), dma((3,)), dma((1,)), dma((1,)),
            dma((1,)), dma((1,)), dma((3,)), dma((3,)),
        ],
        compiler_params=pltpu.CompilerParams(has_side_effects=True,
                                             vmem_limit_bytes=56 * 1024 * 1024),
    )(ta, tb)


def gate_up_kernel(h_ref, go_ref, gp_ref, uo_ref, upv_ref, io_ref, it_ref, acc, tbuf):
    k = pl.program_id(0)
    tile = 256
    chunk = 64
    f32 = jnp.float32

    @pl.when(k == 0)
    def _():
        acc[...] = jnp.zeros_like(acc)

    def mix(i, carry):
        r = pl.ds(pl.multiple_of(i * chunk, chunk), chunk)
        for j, (on_ref, pv_ref) in enumerate(((go_ref, gp_ref), (uo_ref, upv_ref))):
            on = on_ref[r, :].astype(f32)
            pv = pv_ref[r, :].astype(f32)
            tbuf[j, r, :] = (POLYAK * on + (1.0 - POLYAK) * pv).astype(tbuf.dtype)
        return carry

    lax.fori_loop(0, go_ref.shape[0] // chunk, mix, 0)

    def mm(i, carry):
        r = pl.ds(pl.multiple_of(i * tile, tile), tile)
        hs = h_ref[r, :]
        acc[0, r, :] += jnp.dot(hs, go_ref[...], preferred_element_type=f32)
        acc[1, r, :] += jnp.dot(hs, tbuf[0], preferred_element_type=f32)
        acc[2, r, :] += jnp.dot(hs, uo_ref[...], preferred_element_type=f32)
        acc[3, r, :] += jnp.dot(hs, tbuf[1], preferred_element_type=f32)
        return carry

    lax.fori_loop(0, h_ref.shape[0] // tile, mm, 0)

    @pl.when(k == pl.num_programs(0) - 1)
    def _():
        def finish(i, carry):
            r = pl.ds(pl.multiple_of(i * chunk, chunk), chunk)
            io_ref[r, :] = (jax.nn.silu(acc[0, r, :]) * acc[2, r, :]).astype(io_ref.dtype)
            it_ref[r, :] = (jax.nn.silu(acc[1, r, :]) * acc[3, r, :]).astype(it_ref.dtype)
            return carry

        lax.fori_loop(0, io_ref.shape[0] // chunk, finish, 0)


def gate_up(h_full, go, gp, uo, upv, kb):
    tokens, kdim = h_full.shape
    ff = go.shape[1]
    wspec = pl.BlockSpec((kb, ff), lambda k: (k, 0))
    ospec = pl.BlockSpec((tokens, ff), lambda k: (0, 0))
    flops = 8 * tokens * kdim * ff
    nbytes = 2 * (tokens * kdim + 4 * kdim * ff + 2 * tokens * ff)
    return pl.pallas_call(
        gate_up_kernel,
        grid=(kdim // kb,),
        out_shape=(jax.ShapeDtypeStruct((tokens, ff), jnp.bfloat16),) * 2,
        in_specs=[pl.BlockSpec((tokens, kb), lambda k: (0, k))] + [wspec] * 4,
        out_specs=[ospec, ospec],
        scratch_shapes=[pltpu.VMEM((4, tokens, ff), jnp.float32),
                        pltpu.VMEM((2, kb, ff), jnp.bfloat16)],
        compiler_params=pltpu.CompilerParams(vmem_limit_bytes=48 * 1024 * 1024),
        cost_estimate=pl.CostEstimate(flops=flops, bytes_accessed=nbytes,
                                      transcendentals=2 * tokens * ff),
    )(h_full, go, gp, uo, upv)


def local(ndp, nmp, hidden_states, gate_online, up_online, down_online, gate_previous,
          up_previous, down_previous):
    if ndp == 8 and nmp == 16:
        features_all, gate_full, up_full, down_full = gather_relay(
            hidden_states, gate_online, up_online, down_online, ndp)
    else:
        features_all = lax.all_gather(hidden_states, "mp", axis=1, tiled=True)
        gate_full, up_full, down_full = gather_weights_direct(gate_online, up_online,
                                                              down_online, ndp)

    inner_o, inner_t = gate_up(features_all, gate_full, gate_previous, up_full, up_previous,
                               2 * gate_online.shape[0])
    target_down = blend(down_full, down_previous)
    online_part = jnp.dot(inner_o, down_full, preferred_element_type=jnp.float32)
    target_part = jnp.dot(inner_t, target_down, preferred_element_type=jnp.float32)
    if nmp == 16:
        result = split_reduce_scatter(online_part.astype(jnp.bfloat16),
                                      target_part.astype(jnp.bfloat16))
    else:
        terms = jnp.stack([online_part, target_part], axis=0).astype(jnp.bfloat16)
        result = reduce_scatter(terms, nmp)
    return (result[0], result[1])


def solution(mesh):
    ndp = mesh.shape["dp"]
    nmp = mesh.shape["mp"]
    in_specs = (
        P("dp", "mp"),
        P("dp", "mp"),
        P("dp", "mp"),
        P("mp", "dp"),
        P(None, "mp"),
        P(None, "mp"),
        P("mp", None),
    )
    out_specs = (P("dp", "mp"), P("dp", "mp"))
    return jax.shard_map(functools.partial(local, ndp, nmp), mesh=mesh, in_specs=in_specs,
                         out_specs=out_specs, check_vma=False)
```

```python
import functools

import jax
import jax.numpy as jnp
from jax import lax
from jax.experimental import pallas as pl
from jax.experimental.pallas import tpu as pltpu
from jax.sharding import PartitionSpec as P

POLYAK = 0.25
MESH = pl.DeviceIdType.MESH


def blend(online, previous):
    return (
        POLYAK * online.astype(jnp.float32) + (1.0 - POLYAK) * previous.astype(jnp.float32)
    ).astype(jnp.bfloat16)


def gather_kernel(ndp, g_ref, u_ref, dn_ref, gf_ref, uf_ref, df_ref, send_sem, recv_sem,
                  local_sem):
    d = lax.axis_index("dp")
    m = lax.axis_index("mp")
    kr = g_ref.shape[0]
    dc = dn_ref.shape[1]
    rows = pl.ds(pl.multiple_of(d * kr, kr), kr)
    cols = pl.ds(pl.multiple_of(d * dc, dc), dc)

    locals_ = [
        pltpu.make_async_copy(g_ref, gf_ref.at[rows], local_sem.at[0]),
        pltpu.make_async_copy(u_ref, uf_ref.at[rows], local_sem.at[1]),
        pltpu.make_async_copy(dn_ref, df_ref.at[:, cols], local_sem.at[2]),
    ]
    for c in locals_:
        c.start()

    copies = []
    k = 0
    for s in range(1, ndp):
        peer = lax.rem(d + s, ndp)
        for src, dst in ((g_ref, gf_ref.at[rows]), (u_ref, uf_ref.at[rows]),
                         (dn_ref, df_ref.at[:, cols])):
            copies.append(pltpu.make_async_remote_copy(
                src_ref=src, dst_ref=dst, send_sem=send_sem.at[k], recv_sem=recv_sem.at[k],
                device_id=(peer, m), device_id_type=MESH))
            k += 1
    for c in copies:
        c.start()
    for c in locals_:
        c.wait()
    for c in copies:
        c.wait()


def gather_weights_direct(g, u, dn, ndp):
    n_copies = 3 * (ndp - 1)
    any_spec = pl.BlockSpec(memory_space=pl.ANY)
    out_shape = (
        jax.ShapeDtypeStruct((g.shape[0] * ndp, g.shape[1]), g.dtype),
        jax.ShapeDtypeStruct((u.shape[0] * ndp, u.shape[1]), u.dtype),
        jax.ShapeDtypeStruct((dn.shape[0], dn.shape[1] * ndp), dn.dtype),
    )
    return pl.pallas_call(
        functools.partial(gather_kernel, ndp),
        out_shape=out_shape,
        in_specs=[any_spec] * 3,
        out_specs=[any_spec] * 3,
        scratch_shapes=[
            pltpu.SemaphoreType.DMA((n_copies,)),
            pltpu.SemaphoreType.DMA((n_copies,)),
            pltpu.SemaphoreType.DMA((3,)),
        ],
        compiler_params=pltpu.CompilerParams(has_side_effects=True),
    )(g, u, dn)


def relay_gather_kernel(h_ref, g_ref, u_ref, dn_ref, gp_ref, upv_ref, hf_ref, gf_ref, uf_ref,
                        df_ref, pg_ref, pu_ref, send_sem, recv_sem, local_sem, hsend, hrecv,
                        hv, wb, wsem):
    ndp = 8
    d = lax.axis_index("dp")
    m = lax.axis_index("mp")
    lo = d % 2
    partner = d - lo + (1 - lo)
    nxt = (d + 2) % ndp
    prv = (d + ndp - 2) % ndp
    far = (d + 4) % ndp
    owns = (g_ref, u_ref, dn_ref)
    fulls = (gf_ref, uf_ref, df_ref)

    def slot(w, idx, half=None):
        if w < 2:
            kr = owns[w].shape[0]
            if half is None:
                return fulls[w].at[pl.ds(pl.multiple_of(idx * kr, kr), kr)]
            hk = kr // 2
            return fulls[w].at[pl.ds(pl.multiple_of(idx * kr + half * hk, hk), hk)]
        rr, dc = owns[w].shape
        cols = pl.ds(pl.multiple_of(idx * dc, dc), dc)
        if half is None:
            return fulls[w].at[:, cols]
        hr = rr // 2
        return fulls[w].at[pl.ds(half * hr, hr), cols]

    def rc(w, k, src, dst, target):
        i = w * 8 + k
        return pltpu.make_async_remote_copy(
            src_ref=src, dst_ref=dst, send_sem=send_sem.at[i], recv_sem=recv_sem.at[i],
            device_id=(target, m), device_id_type=MESH)

    locals_ = [pltpu.make_async_copy(owns[w], slot(w, d), local_sem.at[w]) for w in range(3)]
    c = {}
    for w in range(3):
        c[w, 0] = rc(w, 0, owns[w], slot(w, d), partner)
        c[w, 1] = rc(w, 1, owns[w], slot(w, d), nxt)
        c[w, 2] = rc(w, 2, owns[w], slot(w, d), prv)
        c[w, 3] = rc(w, 3, slot(w, partner), slot(w, partner), nxt)
        c[w, 4] = rc(w, 4, slot(w, partner), slot(w, partner), prv)
        c[w, 5] = rc(w, 5, slot(w, prv, 0), slot(w, prv, 0), nxt)
        c[w, 6] = rc(w, 6, slot(w, nxt, 1), slot(w, nxt, 1), prv)
        c[w, 7] = rc(w, 7, slot(w, far), slot(w, far), partner)
    nmp = 16
    hc = h_ref.shape[1]
    hmine = hf_ref.at[:, pl.ds(pl.multiple_of(m * hc, hc), hc)]
    hlocal = pltpu.make_async_copy(h_ref, hmine, local_sem.at[3])
    hcopies = []
    for s in range(1, nmp):
        hcopies.append(pltpu.make_async_remote_copy(
            src_ref=h_ref, dst_ref=hmine, send_sem=hsend.at[s - 1], recv_sem=hrecv.at[s - 1],
            device_id=(d, lax.rem(m + s, nmp)), device_id_type=MESH))
    for w in range(3):
        locals_[w].start()
        for k in range(3):
            c[w, k].start()
    hlocal.start()
    for cp in hcopies:
        cp.start()
    for w in range(3):
        c[w, 1].wait_recv()
        c[w, 5].start()
        c[w, 2].wait_recv()
        c[w, 6].start()
    for w in range(3):
        c[w, 5].wait_recv()
        c[w, 6].wait_recv()
        c[w, 7].start()
    for w in range(3):
        c[w, 0].wait_recv()
        c[w, 3].start()
        c[w, 4].start()

    hlocal.wait()
    for cp in hcopies:
        cp.wait_recv()
    hload = pltpu.make_async_copy(hf_ref, hv, wsem.at[2])
    hload.start()
    hload.wait()
    pg_ref[...] = jnp.zeros_like(pg_ref)
    pu_ref[...] = jnp.zeros_like(pu_ref)
    kr = g_ref.shape[0]
    tile = 256
    for slot_i in range(ndp):
        rows = pl.ds(slot_i * kr, kr)
        lg = pltpu.make_async_copy(gp_ref.at[rows], wb.at[0], wsem.at[0])
        lu = pltpu.make_async_copy(upv_ref.at[rows], wb.at[1], wsem.at[1])
        lg.start()
        lu.start()
        lg.wait()
        lu.wait()

        def mm(i, carry, rows=rows):
            r = pl.ds(pl.multiple_of(i * tile, tile), tile)
            hs = hv[r, rows]
            pg_ref[r, :] += jnp.dot(hs, wb[0], preferred_element_type=jnp.float32)
            pu_ref[r, :] += jnp.dot(hs, wb[1], preferred_element_type=jnp.float32)
            return carry

        lax.fori_loop(0, hv.shape[0] // tile, mm, 0)

    for w in range(3):
        for k in (3, 4, 7):
            c[w, k].wait_recv()
    for w in range(3):
        for k in range(8):
            c[w, k].wait_send()
        locals_[w].wait()
    for cp in hcopies:
        cp.wait_send()


def gather_relay(h, g, u, dn, gp, upv, ndp):
    any_spec = pl.BlockSpec(memory_space=pl.ANY)
    out_shape = (
        jax.ShapeDtypeStruct((g.shape[0] * ndp, g.shape[1]), g.dtype),
        jax.ShapeDtypeStruct((u.shape[0] * ndp, u.shape[1]), u.dtype),
        jax.ShapeDtypeStruct((dn.shape[0], dn.shape[1] * ndp), dn.dtype),
    )
    tokens, ff = h.shape[0], g.shape[1]
    prod = jax.ShapeDtypeStruct((tokens, ff), jnp.float32)
    vspec = pl.BlockSpec(memory_space=pltpu.VMEM)
    return pl.pallas_call(
        relay_gather_kernel,
        out_shape=(jax.ShapeDtypeStruct((tokens, h.shape[1] * 16), h.dtype),) + out_shape
        + (prod, prod),
        in_specs=[any_spec] * 6,
        out_specs=[any_spec] * 4 + [vspec] * 2,
        scratch_shapes=[
            pltpu.SemaphoreType.DMA((24,)),
            pltpu.SemaphoreType.DMA((24,)),
            pltpu.SemaphoreType.DMA((4,)),
            pltpu.SemaphoreType.DMA((15,)),
            pltpu.SemaphoreType.DMA((15,)),
            pltpu.VMEM((tokens, h.shape[1] * 16), h.dtype),
            pltpu.VMEM((2, g.shape[0], ff), g.dtype),
            pltpu.SemaphoreType.DMA((3,)),
        ],
        compiler_params=pltpu.CompilerParams(has_side_effects=True,
                                             vmem_limit_bytes=48 * 1024 * 1024),
    )(h, g, u, dn, gp, upv)


def reduce_kernel(nmp, t_ref, o_ref, buf, send_sem, recv_sem, local_sem):
    d = lax.axis_index("dp")
    m = lax.axis_index("mp")
    w = o_ref.shape[2]
    mine = pl.ds(pl.multiple_of(m * w, w), w)
    local_copy = pltpu.make_async_copy(t_ref.at[:, :, mine], buf.at[0], local_sem.at[0])
    local_copy.start()
    copies = []
    for s in range(1, nmp):
        peer = lax.rem(m + s, nmp)
        theirs = pl.ds(pl.multiple_of(peer * w, w), w)
        copies.append(pltpu.make_async_remote_copy(
            src_ref=t_ref.at[:, :, theirs], dst_ref=buf.at[s], send_sem=send_sem.at[s],
            recv_sem=recv_sem.at[s], device_id=(d, peer), device_id_type=MESH))
    for c in copies:
        c.start()
    local_copy.wait()
    for c in copies:
        c.wait()
    rows = 32

    def body(i, carry):
        r = pl.ds(pl.multiple_of(i * rows, rows), rows)
        for k in range(o_ref.shape[0]):
            acc = buf[0, k, r, :].astype(jnp.float32)
            for s in range(1, nmp):
                acc = acc + buf[s, k, r, :].astype(jnp.float32)
            o_ref[k, r, :] = acc.astype(o_ref.dtype)
        return carry

    lax.fori_loop(0, o_ref.shape[1] // rows, body, 0)


def reduce_scatter(terms, nmp):
    n, t, width = terms.shape
    w = width // nmp
    return pl.pallas_call(
        functools.partial(reduce_kernel, nmp),
        out_shape=jax.ShapeDtypeStruct((n, t, w), jnp.bfloat16),
        in_specs=[pl.BlockSpec(memory_space=pl.ANY)],
        out_specs=pl.BlockSpec(memory_space=pltpu.VMEM),
        scratch_shapes=[
            pltpu.VMEM((nmp, n, t, w), jnp.bfloat16),
            pltpu.SemaphoreType.DMA((nmp,)),
            pltpu.SemaphoreType.DMA((nmp,)),
            pltpu.SemaphoreType.DMA((1,)),
        ],
        compiler_params=pltpu.CompilerParams(has_side_effects=True,
                                             vmem_limit_bytes=48 * 1024 * 1024),
    )(terms)


def hier_reduce_kernel(ta_ref, tb_ref, o_ref, own, r1, sb2, r2, s2, sb3, r3,
                       ls, ss1, rs1, ss2, rs2, ss3, rs3):
    d = lax.axis_index("dp")
    m = lax.axis_index("mp")
    c = m % 2
    z = (m // 2) % 4
    xh = m // 8
    w = o_ref.shape[2]
    rows = 32
    nchunk = o_ref.shape[1] // rows

    def blk(b, k):
        return (ta_ref, tb_ref)[k].at[:, pl.ds(pl.multiple_of(b * w, w), w)]

    def dev(mm):
        return (d, mm)

    locs = []
    st1 = []
    for j in range(16):
        bx, bz, k = j // 8, (j // 2) % 4, j % 2
        jj = bx * 4 + bz
        locs.append(pltpu.make_async_copy(blk(bx * 8 + bz * 2 + c, k), own.at[jj, k],
                                          ls.at[j]))
        st1.append(pltpu.make_async_remote_copy(
            src_ref=blk(bx * 8 + bz * 2 + (1 - c), k), dst_ref=r1.at[jj, k], send_sem=ss1.at[j],
            recv_sem=rs1.at[j], device_id=dev(m + 1 - 2 * c), device_id_type=MESH))
    for j in range(16):
        st1[j].start()
        locs[j].start()
    for j in range(16):
        locs[j].wait()
        st1[j].wait()

    st2 = []
    for s in range(1, 4):
        zt = (z + s) % 4

        def fill(i, carry, s=s, zt=zt):
            r = pl.ds(pl.multiple_of(i * rows, rows), rows)
            for bx in range(2):
                idx = bx * 4 + zt
                sb2[s - 1, bx, :, r, :] = (own[idx, :, r, :].astype(jnp.float32)
                                           + r1[idx, :, r, :].astype(jnp.float32)
                                           ).astype(sb2.dtype)
            return carry

        lax.fori_loop(0, nchunk, fill, 0)
        cp = pltpu.make_async_remote_copy(
            src_ref=sb2.at[s - 1], dst_ref=r2.at[s - 1], send_sem=ss2.at[s - 1],
            recv_sem=rs2.at[s - 1], device_id=dev(xh * 8 + zt * 2 + c), device_id_type=MESH)
        cp.start()
        st2.append(cp)
    for cp in st2:
        cp.wait()

    def sum2(i, carry):
        r = pl.ds(pl.multiple_of(i * rows, rows), rows)
        for bx in range(2):
            idx = bx * 4 + z
            acc = own[idx, :, r, :].astype(jnp.float32) + r1[idx, :, r, :].astype(jnp.float32)
            for k in range(3):
                acc = acc + r2[k, bx, :, r, :].astype(jnp.float32)
            s2[bx, :, r, :] = acc
        return carry

    lax.fori_loop(0, nchunk, sum2, 0)
    sb3[...] = s2[1 - xh].astype(sb3.dtype)
    cp3 = pltpu.make_async_remote_copy(
        src_ref=sb3, dst_ref=r3, send_sem=ss3.at[0], recv_sem=rs3.at[0],
        device_id=dev(m + 8 - 16 * xh), device_id_type=MESH)
    cp3.start()
    cp3.wait()
    o_ref[...] = (s2[xh] + r3[...].astype(jnp.float32)).astype(o_ref.dtype)


def hier_reduce_scatter(ta, tb):
    n = 2
    t, width = ta.shape
    w = width // 16
    bf = jnp.bfloat16
    dma = pltpu.SemaphoreType.DMA
    return pl.pallas_call(
        hier_reduce_kernel,
        out_shape=jax.ShapeDtypeStruct((n, t, w), bf),
        in_specs=[pl.BlockSpec(memory_space=pl.ANY)] * 2,
        out_specs=pl.BlockSpec(memory_space=pltpu.VMEM),
        scratch_shapes=[
            pltpu.VMEM((8, n, t, w), bf),
            pltpu.VMEM((8, n, t, w), bf),
            pltpu.VMEM((3, 2, n, t, w), bf),
            pltpu.VMEM((3, 2, n, t, w), bf),
            pltpu.VMEM((2, n, t, w), jnp.float32),
            pltpu.VMEM((n, t, w), bf),
            pltpu.VMEM((n, t, w), bf),
            dma((16,)), dma((16,)), dma((16,)), dma((3,)), dma((3,)), dma((1,)), dma((1,)),
        ],
        compiler_params=pltpu.CompilerParams(has_side_effects=True,
                                             vmem_limit_bytes=56 * 1024 * 1024),
    )(ta, tb)


def split_reduce_kernel(ta_ref, tb_ref, o_ref, own, r1, sa2, ra2, fa2, sa3, ra3,
                        sb2, rb2, fb2, sb3, rb3, ls, ss1, rs1, ssa2, rsa2, ssa3, rsa3,
                        ssb2, rsb2, ssb3, rsb3):
    d = lax.axis_index("dp")
    m = lax.axis_index("mp")
    c = m % 2
    z = (m // 2) % 4
    xh = m // 8
    w = o_ref.shape[2]
    half = o_ref.shape[1] // 2
    ra = pl.ds(0, half)
    rb = pl.ds(half, half)
    rows = 32
    nchunk = half // rows
    f32 = jnp.float32
    xpeer = m + 8 - 16 * xh

    def blk(b, k):
        return (ta_ref, tb_ref)[k].at[:, pl.ds(pl.multiple_of(b * w, w), w)]

    def rcopy(src, dst, ss, rs, mm):
        return pltpu.make_async_remote_copy(src_ref=src, dst_ref=dst, send_sem=ss, recv_sem=rs,
                                            device_id=(d, mm), device_id_type=MESH)

    locs = []
    st1 = []
    for j in range(16):
        bx, bz, k = j // 8, (j // 2) % 4, j % 2
        jj = bx * 4 + bz
        locs.append(pltpu.make_async_copy(blk(bx * 8 + bz * 2 + c, k), own.at[jj, k],
                                          ls.at[j]))
        st1.append(rcopy(blk(bx * 8 + bz * 2 + (1 - c), k), r1.at[jj, k], ss1.at[j], rs1.at[j],
                         m + 1 - 2 * c))
    for j in range(16):
        st1[j].start()
        locs[j].start()
    for j in range(16):
        locs[j].wait()
        st1[j].wait()

    def pair_sum(idx, r):
        return own[idx, :, r, :].astype(f32) + r1[idx, :, r, :].astype(f32)

    def fill_b2(i, carry):
        r = pl.ds(pl.multiple_of(half + i * rows, rows), rows)
        q = pl.ds(pl.multiple_of(i * rows, rows), rows)
        for bz in range(4):
            sb2[bz, :, q, :] = pair_sum((1 - xh) * 4 + bz, r).astype(sb2.dtype)
        return carry

    lax.fori_loop(0, nchunk, fill_b2, 0)
    cb2 = rcopy(sb2, rb2, ssb2.at[0], rsb2.at[0], xpeer)
    cb2.start()
    ca2 = []
    for s in range(1, 4):
        zt = (z + s) % 4

        def fill_a2(i, carry, s=s, zt=zt):
            q = pl.ds(pl.multiple_of(i * rows, rows), rows)
            for bx in range(2):
                sa2[s - 1, bx, :, q, :] = pair_sum(bx * 4 + zt, q).astype(sa2.dtype)
            return carry

        lax.fori_loop(0, nchunk, fill_a2, 0)
        cp = rcopy(sa2.at[s - 1], ra2.at[s - 1], ssa2.at[s - 1], rsa2.at[s - 1],
                   xh * 8 + zt * 2 + c)
        cp.start()
        ca2.append(cp)

    cb2.wait()

    def sum_b2(i, carry):
        r = pl.ds(pl.multiple_of(half + i * rows, rows), rows)
        q = pl.ds(pl.multiple_of(i * rows, rows), rows)
        for bz in range(4):
            fb2[bz, :, q, :] = pair_sum(xh * 4 + bz, r) + rb2[bz, :, q, :].astype(f32)
        return carry

    lax.fori_loop(0, nchunk, sum_b2, 0)
    cb3 = []
    for s in range(1, 4):
        zt = (z + s) % 4
        sb3[s - 1] = fb2[zt].astype(sb3.dtype)
        cp = rcopy(sb3.at[s - 1], rb3.at[s - 1], ssb3.at[s - 1], rsb3.at[s - 1],
                   xh * 8 + zt * 2 + c)
        cp.start()
        cb3.append(cp)

    for cp in ca2:
        cp.wait()

    def sum_a2(i, carry):
        q = pl.ds(pl.multiple_of(i * rows, rows), rows)
        for bx in range(2):
            acc = pair_sum(bx * 4 + z, q)
            for k in range(3):
                acc = acc + ra2[k, bx, :, q, :].astype(f32)
            fa2[bx, :, q, :] = acc
        return carry

    lax.fori_loop(0, nchunk, sum_a2, 0)
    sa3[...] = fa2[1 - xh].astype(sa3.dtype)
    ca3 = rcopy(sa3, ra3, ssa3.at[0], rsa3.at[0], xpeer)
    ca3.start()
    for cp in cb3:
        cp.wait()
    acc = fb2[z]
    for k in range(3):
        acc = acc + rb3[k].astype(f32)
    o_ref[:, rb, :] = acc.astype(o_ref.dtype)
    ca3.wait()
    o_ref[:, ra, :] = (fa2[xh] + ra3[...].astype(f32)).astype(o_ref.dtype)


def split_reduce_scatter(ta, tb):
    n = 2
    t, width = ta.shape
    w = width // 16
    h = t // 2
    bf = jnp.bfloat16
    f32 = jnp.float32
    dma = pltpu.SemaphoreType.DMA
    return pl.pallas_call(
        split_reduce_kernel,
        out_shape=jax.ShapeDtypeStruct((n, t, w), bf),
        in_specs=[pl.BlockSpec(memory_space=pl.ANY)] * 2,
        out_specs=pl.BlockSpec(memory_space=pltpu.VMEM),
        scratch_shapes=[
            pltpu.VMEM((8, n, t, w), bf),
            pltpu.VMEM((8, n, t, w), bf),
            pltpu.VMEM((3, 2, n, h, w), bf),
            pltpu.VMEM((3, 2, n, h, w), bf),
            pltpu.VMEM((2, n, h, w), f32),
            pltpu.VMEM((n, h, w), bf),
            pltpu.VMEM((n, h, w), bf),
            pltpu.VMEM((4, n, h, w), bf),
            pltpu.VMEM((4, n, h, w), bf),
            pltpu.VMEM((4, n, h, w), f32),
            pltpu.VMEM((3, n, h, w), bf),
            pltpu.VMEM((3, n, h, w), bf),
            dma((16,)), dma((16,)), dma((16,)),
            dma((3,)), dma((3,)), dma((1,)), dma((1,)),
            dma((1,)), dma((1,)), dma((3,)), dma((3,)),
        ],
        compiler_params=pltpu.CompilerParams(has_side_effects=True,
                                             vmem_limit_bytes=56 * 1024 * 1024),
    )(ta, tb)


def gate_up_kernel(h_ref, go_ref, gp_ref, uo_ref, upv_ref, io_ref, it_ref, acc, tbuf):
    k = pl.program_id(0)
    tile = 256
    chunk = 64
    f32 = jnp.float32

    @pl.when(k == 0)
    def _():
        acc[...] = jnp.zeros_like(acc)

    def mix(i, carry):
        r = pl.ds(pl.multiple_of(i * chunk, chunk), chunk)
        for j, (on_ref, pv_ref) in enumerate(((go_ref, gp_ref), (uo_ref, upv_ref))):
            on = on_ref[r, :].astype(f32)
            pv = pv_ref[r, :].astype(f32)
            tbuf[j, r, :] = (POLYAK * on + (1.0 - POLYAK) * pv).astype(tbuf.dtype)
        return carry

    lax.fori_loop(0, go_ref.shape[0] // chunk, mix, 0)

    def mm(i, carry):
        r = pl.ds(pl.multiple_of(i * tile, tile), tile)
        hs = h_ref[r, :]
        acc[0, r, :] += jnp.dot(hs, go_ref[...], preferred_element_type=f32)
        acc[1, r, :] += jnp.dot(hs, tbuf[0], preferred_element_type=f32)
        acc[2, r, :] += jnp.dot(hs, uo_ref[...], preferred_element_type=f32)
        acc[3, r, :] += jnp.dot(hs, tbuf[1], preferred_element_type=f32)
        return carry

    lax.fori_loop(0, h_ref.shape[0] // tile, mm, 0)

    @pl.when(k == pl.num_programs(0) - 1)
    def _():
        def finish(i, carry):
            r = pl.ds(pl.multiple_of(i * chunk, chunk), chunk)
            io_ref[r, :] = (jax.nn.silu(acc[0, r, :]) * acc[2, r, :]).astype(io_ref.dtype)
            it_ref[r, :] = (jax.nn.silu(acc[1, r, :]) * acc[3, r, :]).astype(it_ref.dtype)
            return carry

        lax.fori_loop(0, io_ref.shape[0] // chunk, finish, 0)


def gate_up(h_full, go, gp, uo, upv, kb):
    tokens, kdim = h_full.shape
    ff = go.shape[1]
    wspec = pl.BlockSpec((kb, ff), lambda k: (k, 0))
    ospec = pl.BlockSpec((tokens, ff), lambda k: (0, 0))
    flops = 8 * tokens * kdim * ff
    nbytes = 2 * (tokens * kdim + 4 * kdim * ff + 2 * tokens * ff)
    return pl.pallas_call(
        gate_up_kernel,
        grid=(kdim // kb,),
        out_shape=(jax.ShapeDtypeStruct((tokens, ff), jnp.bfloat16),) * 2,
        in_specs=[pl.BlockSpec((tokens, kb), lambda k: (0, k))] + [wspec] * 4,
        out_specs=[ospec, ospec],
        scratch_shapes=[pltpu.VMEM((4, tokens, ff), jnp.float32),
                        pltpu.VMEM((2, kb, ff), jnp.bfloat16)],
        compiler_params=pltpu.CompilerParams(vmem_limit_bytes=48 * 1024 * 1024),
        cost_estimate=pl.CostEstimate(flops=flops, bytes_accessed=nbytes,
                                      transcendentals=2 * tokens * ff),
    )(h_full, go, gp, uo, upv)


def gate_up_online_kernel(h_ref, go_ref, uo_ref, pg_ref, pu_ref, io_ref, it_ref, acc):
    k = pl.program_id(0)
    tile = 256
    chunk = 64
    f32 = jnp.float32

    @pl.when(k == 0)
    def _():
        acc[...] = jnp.zeros_like(acc)

    def mm(i, carry):
        r = pl.ds(pl.multiple_of(i * tile, tile), tile)
        hs = h_ref[r, :]
        acc[0, r, :] += jnp.dot(hs, go_ref[...], preferred_element_type=f32)
        acc[1, r, :] += jnp.dot(hs, uo_ref[...], preferred_element_type=f32)
        return carry

    lax.fori_loop(0, h_ref.shape[0] // tile, mm, 0)

    @pl.when(k == pl.num_programs(0) - 1)
    def _():
        def finish(i, carry):
            r = pl.ds(pl.multiple_of(i * chunk, chunk), chunk)
            g_o = acc[0, r, :]
            u_o = acc[1, r, :]
            g_t = POLYAK * g_o + (1.0 - POLYAK) * pg_ref[r, :]
            u_t = POLYAK * u_o + (1.0 - POLYAK) * pu_ref[r, :]
            io_ref[r, :] = (jax.nn.silu(g_o) * u_o).astype(io_ref.dtype)
            it_ref[r, :] = (jax.nn.silu(g_t) * u_t).astype(it_ref.dtype)
            return carry

        lax.fori_loop(0, io_ref.shape[0] // chunk, finish, 0)


def gate_up_online(h_full, go, uo, pg, pu, kb):
    tokens, kdim = h_full.shape
    ff = go.shape[1]
    wspec = pl.BlockSpec((kb, ff), lambda k: (k, 0))
    ospec = pl.BlockSpec((tokens, ff), lambda k: (0, 0))
    return pl.pallas_call(
        gate_up_online_kernel,
        grid=(kdim // kb,),
        out_shape=(jax.ShapeDtypeStruct((tokens, ff), jnp.bfloat16),) * 2,
        in_specs=[pl.BlockSpec((tokens, kb), lambda k: (0, k)), wspec, wspec, ospec, ospec],
        out_specs=[ospec, ospec],
        scratch_shapes=[pltpu.VMEM((2, tokens, ff), jnp.float32)],
        compiler_params=pltpu.CompilerParams(vmem_limit_bytes=48 * 1024 * 1024),
        cost_estimate=pl.CostEstimate(flops=4 * tokens * kdim * ff,
                                      bytes_accessed=2 * (tokens * kdim + 2 * kdim * ff),
                                      transcendentals=2 * tokens * ff),
    )(h_full, go, uo, pg, pu)


def local(ndp, nmp, hidden_states, gate_online, up_online, down_online, gate_previous,
          up_previous, down_previous):
    kb = 2 * gate_online.shape[0]
    if ndp == 8 and nmp == 16:
        features_all, gate_full, up_full, down_full, prev_g, prev_u = gather_relay(
            hidden_states, gate_online, up_online, down_online, gate_previous, up_previous, ndp)
        inner_o, inner_t = gate_up_online(features_all, gate_full, up_full, prev_g, prev_u, kb)
    else:
        features_all = lax.all_gather(hidden_states, "mp", axis=1, tiled=True)
        gate_full, up_full, down_full = gather_weights_direct(gate_online, up_online,
                                                              down_online, ndp)
        inner_o, inner_t = gate_up(features_all, gate_full, gate_previous, up_full, up_previous,
                                   kb)
    target_down = blend(down_full, down_previous)
    online_part = jnp.dot(inner_o, down_full, preferred_element_type=jnp.float32)
    target_part = jnp.dot(inner_t, target_down, preferred_element_type=jnp.float32)
    if nmp == 16:
        result = split_reduce_scatter(online_part.astype(jnp.bfloat16),
                                      target_part.astype(jnp.bfloat16))
    else:
        terms = jnp.stack([online_part, target_part], axis=0).astype(jnp.bfloat16)
        result = reduce_scatter(terms, nmp)
    return (result[0], result[1])


def solution(mesh):
    ndp = mesh.shape["dp"]
    nmp = mesh.shape["mp"]
    in_specs = (
        P("dp", "mp"),
        P("dp", "mp"),
        P("dp", "mp"),
        P("mp", "dp"),
        P(None, "mp"),
        P(None, "mp"),
        P("mp", None),
    )
    out_specs = (P("dp", "mp"), P("dp", "mp"))
    return jax.shard_map(functools.partial(local, ndp, nmp), mesh=mesh, in_specs=in_specs,
                         out_specs=out_specs, check_vma=False)
```

```python
import functools

import jax
import jax.numpy as jnp
from jax import lax
from jax.experimental import pallas as pl
from jax.experimental.pallas import tpu as pltpu
from jax.sharding import PartitionSpec as P

POLYAK = 0.25
MESH = pl.DeviceIdType.MESH


def blend(online, previous):
    return (
        POLYAK * online.astype(jnp.float32) + (1.0 - POLYAK) * previous.astype(jnp.float32)
    ).astype(jnp.bfloat16)


def gather_kernel(ndp, g_ref, u_ref, dn_ref, gf_ref, uf_ref, df_ref, send_sem, recv_sem,
                  local_sem):
    d = lax.axis_index("dp")
    m = lax.axis_index("mp")
    kr = g_ref.shape[0]
    dc = dn_ref.shape[1]
    rows = pl.ds(pl.multiple_of(d * kr, kr), kr)
    cols = pl.ds(pl.multiple_of(d * dc, dc), dc)

    locals_ = [
        pltpu.make_async_copy(g_ref, gf_ref.at[rows], local_sem.at[0]),
        pltpu.make_async_copy(u_ref, uf_ref.at[rows], local_sem.at[1]),
        pltpu.make_async_copy(dn_ref, df_ref.at[:, cols], local_sem.at[2]),
    ]
    for c in locals_:
        c.start()

    copies = []
    k = 0
    for s in range(1, ndp):
        peer = lax.rem(d + s, ndp)
        for src, dst in ((g_ref, gf_ref.at[rows]), (u_ref, uf_ref.at[rows]),
                         (dn_ref, df_ref.at[:, cols])):
            copies.append(pltpu.make_async_remote_copy(
                src_ref=src, dst_ref=dst, send_sem=send_sem.at[k], recv_sem=recv_sem.at[k],
                device_id=(peer, m), device_id_type=MESH))
            k += 1
    for c in copies:
        c.start()
    for c in locals_:
        c.wait()
    for c in copies:
        c.wait()


def gather_weights_direct(g, u, dn, ndp):
    n_copies = 3 * (ndp - 1)
    any_spec = pl.BlockSpec(memory_space=pl.ANY)
    out_shape = (
        jax.ShapeDtypeStruct((g.shape[0] * ndp, g.shape[1]), g.dtype),
        jax.ShapeDtypeStruct((u.shape[0] * ndp, u.shape[1]), u.dtype),
        jax.ShapeDtypeStruct((dn.shape[0], dn.shape[1] * ndp), dn.dtype),
    )
    return pl.pallas_call(
        functools.partial(gather_kernel, ndp),
        out_shape=out_shape,
        in_specs=[any_spec] * 3,
        out_specs=[any_spec] * 3,
        scratch_shapes=[
            pltpu.SemaphoreType.DMA((n_copies,)),
            pltpu.SemaphoreType.DMA((n_copies,)),
            pltpu.SemaphoreType.DMA((3,)),
        ],
        compiler_params=pltpu.CompilerParams(has_side_effects=True),
    )(g, u, dn)


def relay_gather_kernel(h_ref, g_ref, u_ref, dn_ref, gp_ref, upv_ref, hf_ref, gf_ref, uf_ref,
                        df_ref, pg_ref, pu_ref, send_sem, recv_sem, local_sem, hsend, hrecv,
                        hv, wb, wsem):
    ndp = 8
    d = lax.axis_index("dp")
    m = lax.axis_index("mp")
    lo = d % 2
    partner = d - lo + (1 - lo)
    nxt = (d + 2) % ndp
    prv = (d + ndp - 2) % ndp
    far = (d + 4) % ndp
    owns = (g_ref, u_ref, dn_ref)
    fulls = (gf_ref, uf_ref, df_ref)

    def slot(w, idx, half=None):
        if w < 2:
            kr = owns[w].shape[0]
            if half is None:
                return fulls[w].at[pl.ds(pl.multiple_of(idx * kr, kr), kr)]
            hk = kr // 2
            return fulls[w].at[pl.ds(pl.multiple_of(idx * kr + half * hk, hk), hk)]
        rr, dc = owns[w].shape
        cols = pl.ds(pl.multiple_of(idx * dc, dc), dc)
        if half is None:
            return fulls[w].at[:, cols]
        hr = rr // 2
        return fulls[w].at[pl.ds(half * hr, hr), cols]

    def rc(w, k, src, dst, target):
        i = w * 8 + k
        return pltpu.make_async_remote_copy(
            src_ref=src, dst_ref=dst, send_sem=send_sem.at[i], recv_sem=recv_sem.at[i],
            device_id=(target, m), device_id_type=MESH)

    locals_ = [pltpu.make_async_copy(owns[w], slot(w, d), local_sem.at[w]) for w in range(3)]
    c = {}
    for w in range(3):
        c[w, 0] = rc(w, 0, owns[w], slot(w, d), partner)
        c[w, 1] = rc(w, 1, owns[w], slot(w, d), nxt)
        c[w, 2] = rc(w, 2, owns[w], slot(w, d), prv)
        c[w, 3] = rc(w, 3, slot(w, partner), slot(w, partner), nxt)
        c[w, 4] = rc(w, 4, slot(w, partner), slot(w, partner), prv)
        c[w, 5] = rc(w, 5, slot(w, prv, 0), slot(w, prv, 0), nxt)
        c[w, 6] = rc(w, 6, slot(w, nxt, 1), slot(w, nxt, 1), prv)
        c[w, 7] = rc(w, 7, slot(w, far), slot(w, far), partner)
    nmp = 16
    hc = h_ref.shape[1]
    hmine = hf_ref.at[:, pl.ds(pl.multiple_of(m * hc, hc), hc)]
    hlocal = pltpu.make_async_copy(h_ref, hmine, local_sem.at[3])
    hcopies = []
    for s in range(1, nmp):
        hcopies.append(pltpu.make_async_remote_copy(
            src_ref=h_ref, dst_ref=hmine, send_sem=hsend.at[s - 1], recv_sem=hrecv.at[s - 1],
            device_id=(d, lax.rem(m + s, nmp)), device_id_type=MESH))
    for w in range(3):
        locals_[w].start()
        for k in range(3):
            c[w, k].start()
    hlocal.start()
    for cp in hcopies:
        cp.start()
    for w in range(3):
        c[w, 1].wait_recv()
        c[w, 5].start()
        c[w, 2].wait_recv()
        c[w, 6].start()
    for w in range(3):
        c[w, 5].wait_recv()
        c[w, 6].wait_recv()
        c[w, 7].start()
    for w in range(3):
        c[w, 0].wait_recv()
        c[w, 3].start()
        c[w, 4].start()

    hlocal.wait()
    for cp in hcopies:
        cp.wait_recv()
    hload = pltpu.make_async_copy(hf_ref, hv, wsem.at[2])
    hload.start()
    hload.wait()
    pg_ref[...] = jnp.zeros_like(pg_ref)
    pu_ref[...] = jnp.zeros_like(pu_ref)
    kr = g_ref.shape[0]
    tile = 256
    for slot_i in range(ndp):
        rows = pl.ds(slot_i * kr, kr)
        lg = pltpu.make_async_copy(gp_ref.at[rows], wb.at[0], wsem.at[0])
        lu = pltpu.make_async_copy(upv_ref.at[rows], wb.at[1], wsem.at[1])
        lg.start()
        lu.start()
        lg.wait()
        lu.wait()

        def mm(i, carry, rows=rows):
            r = pl.ds(pl.multiple_of(i * tile, tile), tile)
            hs = hv[r, rows]
            pg_ref[r, :] += jnp.dot(hs, wb[0], preferred_element_type=jnp.float32)
            pu_ref[r, :] += jnp.dot(hs, wb[1], preferred_element_type=jnp.float32)
            return carry

        lax.fori_loop(0, hv.shape[0] // tile, mm, 0)

    for w in range(3):
        for k in (3, 4, 7):
            c[w, k].wait_recv()
    for w in range(3):
        for k in range(8):
            c[w, k].wait_send()
        locals_[w].wait()
    for cp in hcopies:
        cp.wait_send()


def gather_relay(h, g, u, dn, gp, upv, ndp):
    any_spec = pl.BlockSpec(memory_space=pl.ANY)
    out_shape = (
        jax.ShapeDtypeStruct((g.shape[0] * ndp, g.shape[1]), g.dtype),
        jax.ShapeDtypeStruct((u.shape[0] * ndp, u.shape[1]), u.dtype),
        jax.ShapeDtypeStruct((dn.shape[0], dn.shape[1] * ndp), dn.dtype),
    )
    tokens, ff = h.shape[0], g.shape[1]
    prod = jax.ShapeDtypeStruct((tokens, ff), jnp.float32)
    vspec = pl.BlockSpec(memory_space=pltpu.VMEM)
    return pl.pallas_call(
        relay_gather_kernel,
        out_shape=(jax.ShapeDtypeStruct((tokens, h.shape[1] * 16), h.dtype),) + out_shape
        + (prod, prod),
        in_specs=[any_spec] * 6,
        out_specs=[any_spec] * 4 + [vspec] * 2,
        scratch_shapes=[
            pltpu.SemaphoreType.DMA((24,)),
            pltpu.SemaphoreType.DMA((24,)),
            pltpu.SemaphoreType.DMA((4,)),
            pltpu.SemaphoreType.DMA((15,)),
            pltpu.SemaphoreType.DMA((15,)),
            pltpu.VMEM((tokens, h.shape[1] * 16), h.dtype),
            pltpu.VMEM((2, g.shape[0], ff), g.dtype),
            pltpu.SemaphoreType.DMA((3,)),
        ],
        compiler_params=pltpu.CompilerParams(has_side_effects=True,
                                             vmem_limit_bytes=48 * 1024 * 1024),
    )(h, g, u, dn, gp, upv)


def reduce_kernel(nmp, t_ref, o_ref, buf, send_sem, recv_sem, local_sem):
    d = lax.axis_index("dp")
    m = lax.axis_index("mp")
    w = o_ref.shape[2]
    mine = pl.ds(pl.multiple_of(m * w, w), w)
    local_copy = pltpu.make_async_copy(t_ref.at[:, :, mine], buf.at[0], local_sem.at[0])
    local_copy.start()
    copies = []
    for s in range(1, nmp):
        peer = lax.rem(m + s, nmp)
        theirs = pl.ds(pl.multiple_of(peer * w, w), w)
        copies.append(pltpu.make_async_remote_copy(
            src_ref=t_ref.at[:, :, theirs], dst_ref=buf.at[s], send_sem=send_sem.at[s],
            recv_sem=recv_sem.at[s], device_id=(d, peer), device_id_type=MESH))
    for c in copies:
        c.start()
    local_copy.wait()
    for c in copies:
        c.wait()
    rows = 32

    def body(i, carry):
        r = pl.ds(pl.multiple_of(i * rows, rows), rows)
        for k in range(o_ref.shape[0]):
            acc = buf[0, k, r, :].astype(jnp.float32)
            for s in range(1, nmp):
                acc = acc + buf[s, k, r, :].astype(jnp.float32)
            o_ref[k, r, :] = acc.astype(o_ref.dtype)
        return carry

    lax.fori_loop(0, o_ref.shape[1] // rows, body, 0)


def reduce_scatter(terms, nmp):
    n, t, width = terms.shape
    w = width // nmp
    return pl.pallas_call(
        functools.partial(reduce_kernel, nmp),
        out_shape=jax.ShapeDtypeStruct((n, t, w), jnp.bfloat16),
        in_specs=[pl.BlockSpec(memory_space=pl.ANY)],
        out_specs=pl.BlockSpec(memory_space=pltpu.VMEM),
        scratch_shapes=[
            pltpu.VMEM((nmp, n, t, w), jnp.bfloat16),
            pltpu.SemaphoreType.DMA((nmp,)),
            pltpu.SemaphoreType.DMA((nmp,)),
            pltpu.SemaphoreType.DMA((1,)),
        ],
        compiler_params=pltpu.CompilerParams(has_side_effects=True,
                                             vmem_limit_bytes=48 * 1024 * 1024),
    )(terms)


def hier_reduce_kernel(ta_ref, tb_ref, o_ref, own, r1, sb2, r2, s2, sb3, r3,
                       ls, ss1, rs1, ss2, rs2, ss3, rs3):
    d = lax.axis_index("dp")
    m = lax.axis_index("mp")
    c = m % 2
    z = (m // 2) % 4
    xh = m // 8
    w = o_ref.shape[2]
    rows = 32
    nchunk = o_ref.shape[1] // rows

    def blk(b, k):
        return (ta_ref, tb_ref)[k].at[:, pl.ds(pl.multiple_of(b * w, w), w)]

    def dev(mm):
        return (d, mm)

    locs = []
    st1 = []
    for j in range(16):
        bx, bz, k = j // 8, (j // 2) % 4, j % 2
        jj = bx * 4 + bz
        locs.append(pltpu.make_async_copy(blk(bx * 8 + bz * 2 + c, k), own.at[jj, k],
                                          ls.at[j]))
        st1.append(pltpu.make_async_remote_copy(
            src_ref=blk(bx * 8 + bz * 2 + (1 - c), k), dst_ref=r1.at[jj, k], send_sem=ss1.at[j],
            recv_sem=rs1.at[j], device_id=dev(m + 1 - 2 * c), device_id_type=MESH))
    for j in range(16):
        st1[j].start()
        locs[j].start()
    for j in range(16):
        locs[j].wait()
        st1[j].wait()

    st2 = []
    for s in range(1, 4):
        zt = (z + s) % 4

        def fill(i, carry, s=s, zt=zt):
            r = pl.ds(pl.multiple_of(i * rows, rows), rows)
            for bx in range(2):
                idx = bx * 4 + zt
                sb2[s - 1, bx, :, r, :] = (own[idx, :, r, :].astype(jnp.float32)
                                           + r1[idx, :, r, :].astype(jnp.float32)
                                           ).astype(sb2.dtype)
            return carry

        lax.fori_loop(0, nchunk, fill, 0)
        cp = pltpu.make_async_remote_copy(
            src_ref=sb2.at[s - 1], dst_ref=r2.at[s - 1], send_sem=ss2.at[s - 1],
            recv_sem=rs2.at[s - 1], device_id=dev(xh * 8 + zt * 2 + c), device_id_type=MESH)
        cp.start()
        st2.append(cp)
    for cp in st2:
        cp.wait()

    def sum2(i, carry):
        r = pl.ds(pl.multiple_of(i * rows, rows), rows)
        for bx in range(2):
            idx = bx * 4 + z
            acc = own[idx, :, r, :].astype(jnp.float32) + r1[idx, :, r, :].astype(jnp.float32)
            for k in range(3):
                acc = acc + r2[k, bx, :, r, :].astype(jnp.float32)
            s2[bx, :, r, :] = acc
        return carry

    lax.fori_loop(0, nchunk, sum2, 0)
    sb3[...] = s2[1 - xh].astype(sb3.dtype)
    cp3 = pltpu.make_async_remote_copy(
        src_ref=sb3, dst_ref=r3, send_sem=ss3.at[0], recv_sem=rs3.at[0],
        device_id=dev(m + 8 - 16 * xh), device_id_type=MESH)
    cp3.start()
    cp3.wait()
    o_ref[...] = (s2[xh] + r3[...].astype(jnp.float32)).astype(o_ref.dtype)


def hier_reduce_scatter(ta, tb):
    n = 2
    t, width = ta.shape
    w = width // 16
    bf = jnp.bfloat16
    dma = pltpu.SemaphoreType.DMA
    return pl.pallas_call(
        hier_reduce_kernel,
        out_shape=jax.ShapeDtypeStruct((n, t, w), bf),
        in_specs=[pl.BlockSpec(memory_space=pl.ANY)] * 2,
        out_specs=pl.BlockSpec(memory_space=pltpu.VMEM),
        scratch_shapes=[
            pltpu.VMEM((8, n, t, w), bf),
            pltpu.VMEM((8, n, t, w), bf),
            pltpu.VMEM((3, 2, n, t, w), bf),
            pltpu.VMEM((3, 2, n, t, w), bf),
            pltpu.VMEM((2, n, t, w), jnp.float32),
            pltpu.VMEM((n, t, w), bf),
            pltpu.VMEM((n, t, w), bf),
            dma((16,)), dma((16,)), dma((16,)), dma((3,)), dma((3,)), dma((1,)), dma((1,)),
        ],
        compiler_params=pltpu.CompilerParams(has_side_effects=True,
                                             vmem_limit_bytes=56 * 1024 * 1024),
    )(ta, tb)


def split_reduce_kernel(ta_ref, tb_ref, o_ref, own, r1, sa2, ra2, fa2, sa3, ra3,
                        sb2, rb2, fb2, sb3, rb3, ls, ss1, rs1, ssa2, rsa2, ssa3, rsa3,
                        ssb2, rsb2, ssb3, rsb3):
    d = lax.axis_index("dp")
    m = lax.axis_index("mp")
    c = m % 2
    z = (m // 2) % 4
    xh = m // 8
    w = o_ref.shape[2]
    half = o_ref.shape[1] // 2
    ra = pl.ds(0, half)
    rb = pl.ds(half, half)
    rows = 32
    nchunk = half // rows
    f32 = jnp.float32
    xpeer = m + 8 - 16 * xh

    def blk(b, k):
        return (ta_ref, tb_ref)[k].at[:, pl.ds(pl.multiple_of(b * w, w), w)]

    def rcopy(src, dst, ss, rs, mm):
        return pltpu.make_async_remote_copy(src_ref=src, dst_ref=dst, send_sem=ss, recv_sem=rs,
                                            device_id=(d, mm), device_id_type=MESH)

    locs = []
    st1 = []
    for j in range(16):
        bx, bz, k = j // 8, (j // 2) % 4, j % 2
        jj = bx * 4 + bz
        locs.append(pltpu.make_async_copy(blk(bx * 8 + bz * 2 + c, k), own.at[jj, k],
                                          ls.at[j]))
        st1.append(rcopy(blk(bx * 8 + bz * 2 + (1 - c), k), r1.at[jj, k], ss1.at[j], rs1.at[j],
                         m + 1 - 2 * c))
    for j in range(16):
        st1[j].start()
        locs[j].start()
    for j in range(16):
        locs[j].wait()
        st1[j].wait()

    def pair_sum(idx, r):
        return own[idx, :, r, :].astype(f32) + r1[idx, :, r, :].astype(f32)

    def fill_b2(i, carry):
        r = pl.ds(pl.multiple_of(half + i * rows, rows), rows)
        q = pl.ds(pl.multiple_of(i * rows, rows), rows)
        for bz in range(4):
            sb2[bz, :, q, :] = pair_sum((1 - xh) * 4 + bz, r).astype(sb2.dtype)
        return carry

    lax.fori_loop(0, nchunk, fill_b2, 0)
    cb2 = rcopy(sb2, rb2, ssb2.at[0], rsb2.at[0], xpeer)
    cb2.start()
    ca2 = []
    for s in range(1, 4):
        zt = (z + s) % 4

        def fill_a2(i, carry, s=s, zt=zt):
            q = pl.ds(pl.multiple_of(i * rows, rows), rows)
            for bx in range(2):
                sa2[s - 1, bx, :, q, :] = pair_sum(bx * 4 + zt, q).astype(sa2.dtype)
            return carry

        lax.fori_loop(0, nchunk, fill_a2, 0)
        cp = rcopy(sa2.at[s - 1], ra2.at[s - 1], ssa2.at[s - 1], rsa2.at[s - 1],
                   xh * 8 + zt * 2 + c)
        cp.start()
        ca2.append(cp)

    cb2.wait()

    def sum_b2(i, carry):
        r = pl.ds(pl.multiple_of(half + i * rows, rows), rows)
        q = pl.ds(pl.multiple_of(i * rows, rows), rows)
        for bz in range(4):
            fb2[bz, :, q, :] = pair_sum(xh * 4 + bz, r) + rb2[bz, :, q, :].astype(f32)
        return carry

    lax.fori_loop(0, nchunk, sum_b2, 0)
    cb3 = []
    for s in range(1, 4):
        zt = (z + s) % 4
        sb3[s - 1] = fb2[zt].astype(sb3.dtype)
        cp = rcopy(sb3.at[s - 1], rb3.at[s - 1], ssb3.at[s - 1], rsb3.at[s - 1],
                   xh * 8 + zt * 2 + c)
        cp.start()
        cb3.append(cp)

    for cp in ca2:
        cp.wait()

    def sum_a2(i, carry):
        q = pl.ds(pl.multiple_of(i * rows, rows), rows)
        for bx in range(2):
            acc = pair_sum(bx * 4 + z, q)
            for k in range(3):
                acc = acc + ra2[k, bx, :, q, :].astype(f32)
            fa2[bx, :, q, :] = acc
        return carry

    lax.fori_loop(0, nchunk, sum_a2, 0)
    sa3[...] = fa2[1 - xh].astype(sa3.dtype)
    ca3 = rcopy(sa3, ra3, ssa3.at[0], rsa3.at[0], xpeer)
    ca3.start()
    for cp in cb3:
        cp.wait()
    acc = fb2[z]
    for k in range(3):
        acc = acc + rb3[k].astype(f32)
    o_ref[:, rb, :] = acc.astype(o_ref.dtype)
    ca3.wait()
    o_ref[:, ra, :] = (fa2[xh] + ra3[...].astype(f32)).astype(o_ref.dtype)


def split_reduce_scatter(ta, tb):
    n = 2
    t, width = ta.shape
    w = width // 16
    h = t // 2
    bf = jnp.bfloat16
    f32 = jnp.float32
    dma = pltpu.SemaphoreType.DMA
    return pl.pallas_call(
        split_reduce_kernel,
        out_shape=jax.ShapeDtypeStruct((n, t, w), bf),
        in_specs=[pl.BlockSpec(memory_space=pl.ANY)] * 2,
        out_specs=pl.BlockSpec(memory_space=pltpu.VMEM),
        scratch_shapes=[
            pltpu.VMEM((8, n, t, w), bf),
            pltpu.VMEM((8, n, t, w), bf),
            pltpu.VMEM((3, 2, n, h, w), bf),
            pltpu.VMEM((3, 2, n, h, w), bf),
            pltpu.VMEM((2, n, h, w), f32),
            pltpu.VMEM((n, h, w), bf),
            pltpu.VMEM((n, h, w), bf),
            pltpu.VMEM((4, n, h, w), bf),
            pltpu.VMEM((4, n, h, w), bf),
            pltpu.VMEM((4, n, h, w), f32),
            pltpu.VMEM((3, n, h, w), bf),
            pltpu.VMEM((3, n, h, w), bf),
            dma((16,)), dma((16,)), dma((16,)),
            dma((3,)), dma((3,)), dma((1,)), dma((1,)),
            dma((1,)), dma((1,)), dma((3,)), dma((3,)),
        ],
        compiler_params=pltpu.CompilerParams(has_side_effects=True,
                                             vmem_limit_bytes=56 * 1024 * 1024),
    )(ta, tb)


def gate_up_kernel(h_ref, go_ref, gp_ref, uo_ref, upv_ref, io_ref, it_ref, acc, tbuf):
    k = pl.program_id(0)
    tile = 256
    chunk = 64
    f32 = jnp.float32

    @pl.when(k == 0)
    def _():
        acc[...] = jnp.zeros_like(acc)

    def mix(i, carry):
        r = pl.ds(pl.multiple_of(i * chunk, chunk), chunk)
        for j, (on_ref, pv_ref) in enumerate(((go_ref, gp_ref), (uo_ref, upv_ref))):
            on = on_ref[r, :].astype(f32)
            pv = pv_ref[r, :].astype(f32)
            tbuf[j, r, :] = (POLYAK * on + (1.0 - POLYAK) * pv).astype(tbuf.dtype)
        return carry

    lax.fori_loop(0, go_ref.shape[0] // chunk, mix, 0)

    def mm(i, carry):
        r = pl.ds(pl.multiple_of(i * tile, tile), tile)
        hs = h_ref[r, :]
        acc[0, r, :] += jnp.dot(hs, go_ref[...], preferred_element_type=f32)
        acc[1, r, :] += jnp.dot(hs, tbuf[0], preferred_element_type=f32)
        acc[2, r, :] += jnp.dot(hs, uo_ref[...], preferred_element_type=f32)
        acc[3, r, :] += jnp.dot(hs, tbuf[1], preferred_element_type=f32)
        return carry

    lax.fori_loop(0, h_ref.shape[0] // tile, mm, 0)

    @pl.when(k == pl.num_programs(0) - 1)
    def _():
        def finish(i, carry):
            r = pl.ds(pl.multiple_of(i * chunk, chunk), chunk)
            io_ref[r, :] = (jax.nn.silu(acc[0, r, :]) * acc[2, r, :]).astype(io_ref.dtype)
            it_ref[r, :] = (jax.nn.silu(acc[1, r, :]) * acc[3, r, :]).astype(it_ref.dtype)
            return carry

        lax.fori_loop(0, io_ref.shape[0] // chunk, finish, 0)


def gate_up(h_full, go, gp, uo, upv, kb):
    tokens, kdim = h_full.shape
    ff = go.shape[1]
    wspec = pl.BlockSpec((kb, ff), lambda k: (k, 0))
    ospec = pl.BlockSpec((tokens, ff), lambda k: (0, 0))
    flops = 8 * tokens * kdim * ff
    nbytes = 2 * (tokens * kdim + 4 * kdim * ff + 2 * tokens * ff)
    return pl.pallas_call(
        gate_up_kernel,
        grid=(kdim // kb,),
        out_shape=(jax.ShapeDtypeStruct((tokens, ff), jnp.bfloat16),) * 2,
        in_specs=[pl.BlockSpec((tokens, kb), lambda k: (0, k))] + [wspec] * 4,
        out_specs=[ospec, ospec],
        scratch_shapes=[pltpu.VMEM((4, tokens, ff), jnp.float32),
                        pltpu.VMEM((2, kb, ff), jnp.bfloat16)],
        compiler_params=pltpu.CompilerParams(vmem_limit_bytes=48 * 1024 * 1024),
        cost_estimate=pl.CostEstimate(flops=flops, bytes_accessed=nbytes,
                                      transcendentals=2 * tokens * ff),
    )(h_full, go, gp, uo, upv)


def gate_up_online_kernel(h_ref, go_ref, uo_ref, pg_ref, pu_ref, io_ref, it_ref, acc):
    k = pl.program_id(0)
    tile = 256
    chunk = 64
    f32 = jnp.float32

    @pl.when(k == 0)
    def _():
        acc[...] = jnp.zeros_like(acc)

    def mm(i, carry):
        r = pl.ds(pl.multiple_of(i * tile, tile), tile)
        hs = h_ref[r, :]
        acc[0, r, :] += jnp.dot(hs, go_ref[...], preferred_element_type=f32)
        acc[1, r, :] += jnp.dot(hs, uo_ref[...], preferred_element_type=f32)
        return carry

    lax.fori_loop(0, h_ref.shape[0] // tile, mm, 0)

    @pl.when(k == pl.num_programs(0) - 1)
    def _():
        def finish(i, carry):
            r = pl.ds(pl.multiple_of(i * chunk, chunk), chunk)
            g_o = acc[0, r, :]
            u_o = acc[1, r, :]
            g_t = POLYAK * g_o + (1.0 - POLYAK) * pg_ref[r, :]
            u_t = POLYAK * u_o + (1.0 - POLYAK) * pu_ref[r, :]
            io_ref[r, :] = (jax.nn.silu(g_o) * u_o).astype(io_ref.dtype)
            it_ref[r, :] = (jax.nn.silu(g_t) * u_t).astype(it_ref.dtype)
            return carry

        lax.fori_loop(0, io_ref.shape[0] // chunk, finish, 0)


def gate_up_online(h_full, go, uo, pg, pu, kb):
    tokens, kdim = h_full.shape
    ff = go.shape[1]
    wspec = pl.BlockSpec((kb, ff), lambda k: (k, 0))
    ospec = pl.BlockSpec((tokens, ff), lambda k: (0, 0))
    return pl.pallas_call(
        gate_up_online_kernel,
        grid=(kdim // kb,),
        out_shape=(jax.ShapeDtypeStruct((tokens, ff), jnp.bfloat16),) * 2,
        in_specs=[pl.BlockSpec((tokens, kb), lambda k: (0, k)), wspec, wspec, ospec, ospec],
        out_specs=[ospec, ospec],
        scratch_shapes=[pltpu.VMEM((2, tokens, ff), jnp.float32)],
        compiler_params=pltpu.CompilerParams(vmem_limit_bytes=48 * 1024 * 1024),
        cost_estimate=pl.CostEstimate(flops=4 * tokens * kdim * ff,
                                      bytes_accessed=2 * (tokens * kdim + 2 * kdim * ff),
                                      transcendentals=2 * tokens * ff),
    )(h_full, go, uo, pg, pu)


def down_kernel(io_ref, it_ref, do_ref, dp_ref, oo_ref, ot_ref):
    f32 = jnp.float32
    wt = (POLYAK * do_ref[...].astype(f32)
          + (1.0 - POLYAK) * dp_ref[...].astype(f32)).astype(do_ref.dtype)
    oo_ref[...] = jnp.dot(io_ref[...], do_ref[...], preferred_element_type=f32).astype(oo_ref.dtype)
    ot_ref[...] = jnp.dot(it_ref[...], wt, preferred_element_type=f32).astype(ot_ref.dtype)


def down_products(inner_o, inner_t, down_full, down_previous, cb):
    tokens, ff = inner_o.shape
    width = down_full.shape[1]
    ispec = pl.BlockSpec((tokens, ff), lambda j: (0, 0))
    wspec = pl.BlockSpec((ff, cb), lambda j: (0, j))
    ospec = pl.BlockSpec((tokens, cb), lambda j: (0, j))
    return pl.pallas_call(
        down_kernel,
        grid=(width // cb,),
        out_shape=(jax.ShapeDtypeStruct((tokens, width), jnp.bfloat16),) * 2,
        in_specs=[ispec, ispec, wspec, wspec],
        out_specs=[ospec, ospec],
        compiler_params=pltpu.CompilerParams(vmem_limit_bytes=32 * 1024 * 1024),
        cost_estimate=pl.CostEstimate(flops=4 * tokens * ff * width,
                                      bytes_accessed=2 * (2 * tokens * ff + 2 * ff * width
                                                          + 2 * tokens * width),
                                      transcendentals=0),
    )(inner_o, inner_t, down_full, down_previous)


def local(ndp, nmp, hidden_states, gate_online, up_online, down_online, gate_previous,
          up_previous, down_previous):
    kb = 2 * gate_online.shape[0]
    if ndp == 8 and nmp == 16:
        features_all, gate_full, up_full, down_full, prev_g, prev_u = gather_relay(
            hidden_states, gate_online, up_online, down_online, gate_previous, up_previous, ndp)
        inner_o, inner_t = gate_up_online(features_all, gate_full, up_full, prev_g, prev_u, kb)
    else:
        features_all = lax.all_gather(hidden_states, "mp", axis=1, tiled=True)
        gate_full, up_full, down_full = gather_weights_direct(gate_online, up_online,
                                                              down_online, ndp)
        inner_o, inner_t = gate_up(features_all, gate_full, gate_previous, up_full, up_previous,
                                   kb)
    if nmp == 16:
        online_part, target_part = down_products(inner_o, inner_t, down_full, down_previous,
                                                 down_online.shape[1])
        result = split_reduce_scatter(online_part, target_part)
    else:
        target_down = blend(down_full, down_previous)
        online_part = jnp.dot(inner_o, down_full, preferred_element_type=jnp.float32)
        target_part = jnp.dot(inner_t, target_down, preferred_element_type=jnp.float32)
        terms = jnp.stack([online_part, target_part], axis=0).astype(jnp.bfloat16)
        result = reduce_scatter(terms, nmp)
    return (result[0], result[1])


def solution(mesh):
    ndp = mesh.shape["dp"]
    nmp = mesh.shape["mp"]
    in_specs = (
        P("dp", "mp"),
        P("dp", "mp"),
        P("dp", "mp"),
        P("mp", "dp"),
        P(None, "mp"),
        P(None, "mp"),
        P("mp", None),
    )
    out_specs = (P("dp", "mp"), P("dp", "mp"))
    return jax.shard_map(functools.partial(local, ndp, nmp), mesh=mesh, in_specs=in_specs,
                         out_specs=out_specs, check_vma=False)
```

```python
import functools

import jax
import jax.numpy as jnp
from jax import lax
from jax.experimental import pallas as pl
from jax.experimental.pallas import tpu as pltpu
from jax.sharding import PartitionSpec as P

POLYAK = 0.25
MESH = pl.DeviceIdType.MESH


def blend(online, previous):
    return (
        POLYAK * online.astype(jnp.float32) + (1.0 - POLYAK) * previous.astype(jnp.float32)
    ).astype(jnp.bfloat16)


def gather_kernel(ndp, g_ref, u_ref, dn_ref, gf_ref, uf_ref, df_ref, send_sem, recv_sem,
                  local_sem):
    d = lax.axis_index("dp")
    m = lax.axis_index("mp")
    kr = g_ref.shape[0]
    dc = dn_ref.shape[1]
    rows = pl.ds(pl.multiple_of(d * kr, kr), kr)
    cols = pl.ds(pl.multiple_of(d * dc, dc), dc)

    locals_ = [
        pltpu.make_async_copy(g_ref, gf_ref.at[rows], local_sem.at[0]),
        pltpu.make_async_copy(u_ref, uf_ref.at[rows], local_sem.at[1]),
        pltpu.make_async_copy(dn_ref, df_ref.at[:, cols], local_sem.at[2]),
    ]
    for c in locals_:
        c.start()

    copies = []
    k = 0
    for s in range(1, ndp):
        peer = lax.rem(d + s, ndp)
        for src, dst in ((g_ref, gf_ref.at[rows]), (u_ref, uf_ref.at[rows]),
                         (dn_ref, df_ref.at[:, cols])):
            copies.append(pltpu.make_async_remote_copy(
                src_ref=src, dst_ref=dst, send_sem=send_sem.at[k], recv_sem=recv_sem.at[k],
                device_id=(peer, m), device_id_type=MESH))
            k += 1
    for c in copies:
        c.start()
    for c in locals_:
        c.wait()
    for c in copies:
        c.wait()


def gather_weights_direct(g, u, dn, ndp):
    n_copies = 3 * (ndp - 1)
    any_spec = pl.BlockSpec(memory_space=pl.ANY)
    out_shape = (
        jax.ShapeDtypeStruct((g.shape[0] * ndp, g.shape[1]), g.dtype),
        jax.ShapeDtypeStruct((u.shape[0] * ndp, u.shape[1]), u.dtype),
        jax.ShapeDtypeStruct((dn.shape[0], dn.shape[1] * ndp), dn.dtype),
    )
    return pl.pallas_call(
        functools.partial(gather_kernel, ndp),
        out_shape=out_shape,
        in_specs=[any_spec] * 3,
        out_specs=[any_spec] * 3,
        scratch_shapes=[
            pltpu.SemaphoreType.DMA((n_copies,)),
            pltpu.SemaphoreType.DMA((n_copies,)),
            pltpu.SemaphoreType.DMA((3,)),
        ],
        compiler_params=pltpu.CompilerParams(has_side_effects=True),
    )(g, u, dn)


def relay_gather_kernel(h_ref, g_ref, u_ref, dn_ref, gp_ref, upv_ref, hf_ref, gf_ref, uf_ref,
                        df_ref, io_ref, it_ref, send_sem, recv_sem, local_sem, hsend, hrecv,
                        hv, wb, wsem, acc):
    ndp = 8
    d = lax.axis_index("dp")
    m = lax.axis_index("mp")
    lo = d % 2
    partner = d - lo + (1 - lo)
    nxt = (d + 2) % ndp
    prv = (d + ndp - 2) % ndp
    far = (d + 4) % ndp
    owns = (g_ref, u_ref, dn_ref)
    fulls = (gf_ref, uf_ref, df_ref)

    def slot(w, idx, half=None):
        if w < 2:
            kr = owns[w].shape[0]
            if half is None:
                return fulls[w].at[pl.ds(pl.multiple_of(idx * kr, kr), kr)]
            hk = kr // 2
            return fulls[w].at[pl.ds(pl.multiple_of(idx * kr + half * hk, hk), hk)]
        rr, dc = owns[w].shape
        cols = pl.ds(pl.multiple_of(idx * dc, dc), dc)
        if half is None:
            return fulls[w].at[:, cols]
        hr = rr // 2
        return fulls[w].at[pl.ds(half * hr, hr), cols]

    def rc(w, k, src, dst, target):
        i = w * 8 + k
        return pltpu.make_async_remote_copy(
            src_ref=src, dst_ref=dst, send_sem=send_sem.at[i], recv_sem=recv_sem.at[i],
            device_id=(target, m), device_id_type=MESH)

    locals_ = [pltpu.make_async_copy(owns[w], slot(w, d), local_sem.at[w]) for w in range(3)]
    c = {}
    for w in range(3):
        c[w, 0] = rc(w, 0, owns[w], slot(w, d), partner)
        c[w, 1] = rc(w, 1, owns[w], slot(w, d), nxt)
        c[w, 2] = rc(w, 2, owns[w], slot(w, d), prv)
        c[w, 3] = rc(w, 3, slot(w, partner), slot(w, partner), nxt)
        c[w, 4] = rc(w, 4, slot(w, partner), slot(w, partner), prv)
        c[w, 5] = rc(w, 5, slot(w, prv, 0), slot(w, prv, 0), nxt)
        c[w, 6] = rc(w, 6, slot(w, nxt, 1), slot(w, nxt, 1), prv)
        c[w, 7] = rc(w, 7, slot(w, far), slot(w, far), partner)
    nmp = 16
    hc = h_ref.shape[1]
    hmine = hf_ref.at[:, pl.ds(pl.multiple_of(m * hc, hc), hc)]
    hlocal = pltpu.make_async_copy(h_ref, hmine, local_sem.at[3])
    hcopies = []
    for s in range(1, nmp):
        hcopies.append(pltpu.make_async_remote_copy(
            src_ref=h_ref, dst_ref=hmine, send_sem=hsend.at[s - 1], recv_sem=hrecv.at[s - 1],
            device_id=(d, lax.rem(m + s, nmp)), device_id_type=MESH))
    for w in range(3):
        locals_[w].start()
        for k in range(3):
            c[w, k].start()
    hlocal.start()
    for cp in hcopies:
        cp.start()
    for w in range(3):
        c[w, 1].wait_recv()
        c[w, 5].start()
        c[w, 2].wait_recv()
        c[w, 6].start()
    for w in range(3):
        c[w, 5].wait_recv()
        c[w, 6].wait_recv()
        c[w, 7].start()
    for w in range(3):
        c[w, 0].wait_recv()
        c[w, 3].start()
        c[w, 4].start()

    hlocal.wait()
    for cp in hcopies:
        cp.wait_recv()
    for w in range(3):
        locals_[w].wait()
    hload = pltpu.make_async_copy(hf_ref, hv, wsem.at[2])
    hload.start()
    hload.wait()
    acc[...] = jnp.zeros_like(acc)
    kr = g_ref.shape[0]
    tile = 256

    def products(a_ref, b_ref, idx, first):
        rows = pl.ds(pl.multiple_of(idx * kr, kr), kr)
        la = pltpu.make_async_copy(a_ref.at[rows], wb.at[0], wsem.at[0])
        lb = pltpu.make_async_copy(b_ref.at[rows], wb.at[1], wsem.at[1])
        la.start()
        lb.start()
        la.wait()
        lb.wait()

        def mm(i, carry):
            r = pl.ds(pl.multiple_of(i * tile, tile), tile)
            hs = hv[r, rows]
            acc[first, r, :] += jnp.dot(hs, wb[0], preferred_element_type=jnp.float32)
            acc[first + 1, r, :] += jnp.dot(hs, wb[1], preferred_element_type=jnp.float32)
            return carry

        lax.fori_loop(0, hv.shape[0] // tile, mm, 0)

    def prev_slot(i, carry):
        products(gp_ref, upv_ref, i, 2)
        return carry

    lax.fori_loop(0, ndp, prev_slot, 0)
    for idx in (d, partner, prv, nxt, far):
        products(gf_ref, uf_ref, idx, 0)

    for w in range(3):
        for k in (3, 4, 7):
            c[w, k].wait_recv()
    for idx in ((partner + 2) % ndp, (partner + ndp - 2) % ndp, (partner + 4) % ndp):
        products(gf_ref, uf_ref, idx, 0)

    chunk = 64

    def finish(i, carry):
        r = pl.ds(pl.multiple_of(i * chunk, chunk), chunk)
        g_o = acc[0, r, :]
        u_o = acc[1, r, :]
        g_t = POLYAK * g_o + (1.0 - POLYAK) * acc[2, r, :]
        u_t = POLYAK * u_o + (1.0 - POLYAK) * acc[3, r, :]
        io_ref[r, :] = (jax.nn.silu(g_o) * u_o).astype(io_ref.dtype)
        it_ref[r, :] = (jax.nn.silu(g_t) * u_t).astype(it_ref.dtype)
        return carry

    lax.fori_loop(0, io_ref.shape[0] // chunk, finish, 0)
    for w in range(3):
        for k in range(8):
            c[w, k].wait_send()
    for cp in hcopies:
        cp.wait_send()


def gather_relay(h, g, u, dn, gp, upv, ndp):
    any_spec = pl.BlockSpec(memory_space=pl.ANY)
    out_shape = (
        jax.ShapeDtypeStruct((g.shape[0] * ndp, g.shape[1]), g.dtype),
        jax.ShapeDtypeStruct((u.shape[0] * ndp, u.shape[1]), u.dtype),
        jax.ShapeDtypeStruct((dn.shape[0], dn.shape[1] * ndp), dn.dtype),
    )
    tokens, ff = h.shape[0], g.shape[1]
    prod = jax.ShapeDtypeStruct((tokens, ff), jnp.bfloat16)
    vspec = pl.BlockSpec(memory_space=pltpu.VMEM)
    return pl.pallas_call(
        relay_gather_kernel,
        out_shape=(jax.ShapeDtypeStruct((tokens, h.shape[1] * 16), h.dtype),) + out_shape
        + (prod, prod),
        in_specs=[any_spec] * 6,
        out_specs=[any_spec] * 4 + [vspec] * 2,
        scratch_shapes=[
            pltpu.SemaphoreType.DMA((24,)),
            pltpu.SemaphoreType.DMA((24,)),
            pltpu.SemaphoreType.DMA((4,)),
            pltpu.SemaphoreType.DMA((15,)),
            pltpu.SemaphoreType.DMA((15,)),
            pltpu.VMEM((tokens, h.shape[1] * 16), h.dtype),
            pltpu.VMEM((2, g.shape[0], ff), g.dtype),
            pltpu.SemaphoreType.DMA((3,)),
            pltpu.VMEM((4, tokens, ff), jnp.float32),
        ],
        compiler_params=pltpu.CompilerParams(has_side_effects=True,
                                             vmem_limit_bytes=48 * 1024 * 1024),
    )(h, g, u, dn, gp, upv)


def reduce_kernel(nmp, t_ref, o_ref, buf, send_sem, recv_sem, local_sem):
    d = lax.axis_index("dp")
    m = lax.axis_index("mp")
    w = o_ref.shape[2]
    mine = pl.ds(pl.multiple_of(m * w, w), w)
    local_copy = pltpu.make_async_copy(t_ref.at[:, :, mine], buf.at[0], local_sem.at[0])
    local_copy.start()
    copies = []
    for s in range(1, nmp):
        peer = lax.rem(m + s, nmp)
        theirs = pl.ds(pl.multiple_of(peer * w, w), w)
        copies.append(pltpu.make_async_remote_copy(
            src_ref=t_ref.at[:, :, theirs], dst_ref=buf.at[s], send_sem=send_sem.at[s],
            recv_sem=recv_sem.at[s], device_id=(d, peer), device_id_type=MESH))
    for c in copies:
        c.start()
    local_copy.wait()
    for c in copies:
        c.wait()
    rows = 32

    def body(i, carry):
        r = pl.ds(pl.multiple_of(i * rows, rows), rows)
        for k in range(o_ref.shape[0]):
            acc = buf[0, k, r, :].astype(jnp.float32)
            for s in range(1, nmp):
                acc = acc + buf[s, k, r, :].astype(jnp.float32)
            o_ref[k, r, :] = acc.astype(o_ref.dtype)
        return carry

    lax.fori_loop(0, o_ref.shape[1] // rows, body, 0)


def reduce_scatter(terms, nmp):
    n, t, width = terms.shape
    w = width // nmp
    return pl.pallas_call(
        functools.partial(reduce_kernel, nmp),
        out_shape=jax.ShapeDtypeStruct((n, t, w), jnp.bfloat16),
        in_specs=[pl.BlockSpec(memory_space=pl.ANY)],
        out_specs=pl.BlockSpec(memory_space=pltpu.VMEM),
        scratch_shapes=[
            pltpu.VMEM((nmp, n, t, w), jnp.bfloat16),
            pltpu.SemaphoreType.DMA((nmp,)),
            pltpu.SemaphoreType.DMA((nmp,)),
            pltpu.SemaphoreType.DMA((1,)),
        ],
        compiler_params=pltpu.CompilerParams(has_side_effects=True,
                                             vmem_limit_bytes=48 * 1024 * 1024),
    )(terms)


def hier_reduce_kernel(ta_ref, tb_ref, o_ref, own, r1, sb2, r2, s2, sb3, r3,
                       ls, ss1, rs1, ss2, rs2, ss3, rs3):
    d = lax.axis_index("dp")
    m = lax.axis_index("mp")
    c = m % 2
    z = (m // 2) % 4
    xh = m // 8
    w = o_ref.shape[2]
    rows = 32
    nchunk = o_ref.shape[1] // rows

    def blk(b, k):
        return (ta_ref, tb_ref)[k].at[:, pl.ds(pl.multiple_of(b * w, w), w)]

    def dev(mm):
        return (d, mm)

    locs = []
    st1 = []
    for j in range(16):
        bx, bz, k = j // 8, (j // 2) % 4, j % 2
        jj = bx * 4 + bz
        locs.append(pltpu.make_async_copy(blk(bx * 8 + bz * 2 + c, k), own.at[jj, k],
                                          ls.at[j]))
        st1.append(pltpu.make_async_remote_copy(
            src_ref=blk(bx * 8 + bz * 2 + (1 - c), k), dst_ref=r1.at[jj, k], send_sem=ss1.at[j],
            recv_sem=rs1.at[j], device_id=dev(m + 1 - 2 * c), device_id_type=MESH))
    for j in range(16):
        st1[j].start()
        locs[j].start()
    for j in range(16):
        locs[j].wait()
        st1[j].wait()

    st2 = []
    for s in range(1, 4):
        zt = (z + s) % 4

        def fill(i, carry, s=s, zt=zt):
            r = pl.ds(pl.multiple_of(i * rows, rows), rows)
            for bx in range(2):
                idx = bx * 4 + zt
                sb2[s - 1, bx, :, r, :] = (own[idx, :, r, :].astype(jnp.float32)
                                           + r1[idx, :, r, :].astype(jnp.float32)
                                           ).astype(sb2.dtype)
            return carry

        lax.fori_loop(0, nchunk, fill, 0)
        cp = pltpu.make_async_remote_copy(
            src_ref=sb2.at[s - 1], dst_ref=r2.at[s - 1], send_sem=ss2.at[s - 1],
            recv_sem=rs2.at[s - 1], device_id=dev(xh * 8 + zt * 2 + c), device_id_type=MESH)
        cp.start()
        st2.append(cp)
    for cp in st2:
        cp.wait()

    def sum2(i, carry):
        r = pl.ds(pl.multiple_of(i * rows, rows), rows)
        for bx in range(2):
            idx = bx * 4 + z
            acc = own[idx, :, r, :].astype(jnp.float32) + r1[idx, :, r, :].astype(jnp.float32)
            for k in range(3):
                acc = acc + r2[k, bx, :, r, :].astype(jnp.float32)
            s2[bx, :, r, :] = acc
        return carry

    lax.fori_loop(0, nchunk, sum2, 0)
    sb3[...] = s2[1 - xh].astype(sb3.dtype)
    cp3 = pltpu.make_async_remote_copy(
        src_ref=sb3, dst_ref=r3, send_sem=ss3.at[0], recv_sem=rs3.at[0],
        device_id=dev(m + 8 - 16 * xh), device_id_type=MESH)
    cp3.start()
    cp3.wait()
    o_ref[...] = (s2[xh] + r3[...].astype(jnp.float32)).astype(o_ref.dtype)


def hier_reduce_scatter(ta, tb):
    n = 2
    t, width = ta.shape
    w = width // 16
    bf = jnp.bfloat16
    dma = pltpu.SemaphoreType.DMA
    return pl.pallas_call(
        hier_reduce_kernel,
        out_shape=jax.ShapeDtypeStruct((n, t, w), bf),
        in_specs=[pl.BlockSpec(memory_space=pl.ANY)] * 2,
        out_specs=pl.BlockSpec(memory_space=pltpu.VMEM),
        scratch_shapes=[
            pltpu.VMEM((8, n, t, w), bf),
            pltpu.VMEM((8, n, t, w), bf),
            pltpu.VMEM((3, 2, n, t, w), bf),
            pltpu.VMEM((3, 2, n, t, w), bf),
            pltpu.VMEM((2, n, t, w), jnp.float32),
            pltpu.VMEM((n, t, w), bf),
            pltpu.VMEM((n, t, w), bf),
            dma((16,)), dma((16,)), dma((16,)), dma((3,)), dma((3,)), dma((1,)), dma((1,)),
        ],
        compiler_params=pltpu.CompilerParams(has_side_effects=True,
                                             vmem_limit_bytes=56 * 1024 * 1024),
    )(ta, tb)


def split_reduce_kernel(ta_ref, tb_ref, o_ref, own, r1, sa2, ra2, fa2, sa3, ra3,
                        sb2, rb2, fb2, sb3, rb3, ls, ss1, rs1, ssa2, rsa2, ssa3, rsa3,
                        ssb2, rsb2, ssb3, rsb3):
    d = lax.axis_index("dp")
    m = lax.axis_index("mp")
    c = m % 2
    z = (m // 2) % 4
    xh = m // 8
    w = o_ref.shape[2]
    half = o_ref.shape[1] // 2
    ra = pl.ds(0, half)
    rb = pl.ds(half, half)
    rows = 32
    nchunk = half // rows
    f32 = jnp.float32
    xpeer = m + 8 - 16 * xh

    def blk(b, k):
        return (ta_ref, tb_ref)[k].at[:, pl.ds(pl.multiple_of(b * w, w), w)]

    def rcopy(src, dst, ss, rs, mm):
        return pltpu.make_async_remote_copy(src_ref=src, dst_ref=dst, send_sem=ss, recv_sem=rs,
                                            device_id=(d, mm), device_id_type=MESH)

    locs = []
    st1 = []
    for j in range(16):
        bx, bz, k = j // 8, (j // 2) % 4, j % 2
        jj = bx * 4 + bz
        locs.append(pltpu.make_async_copy(blk(bx * 8 + bz * 2 + c, k), own.at[jj, k],
                                          ls.at[j]))
        st1.append(rcopy(blk(bx * 8 + bz * 2 + (1 - c), k), r1.at[jj, k], ss1.at[j], rs1.at[j],
                         m + 1 - 2 * c))
    for j in range(16):
        st1[j].start()
        locs[j].start()
    for j in range(16):
        locs[j].wait()
        st1[j].wait()

    def pair_sum(idx, r):
        return own[idx, :, r, :].astype(f32) + r1[idx, :, r, :].astype(f32)

    def fill_b2(i, carry):
        r = pl.ds(pl.multiple_of(half + i * rows, rows), rows)
        q = pl.ds(pl.multiple_of(i * rows, rows), rows)
        for bz in range(4):
            sb2[bz, :, q, :] = pair_sum((1 - xh) * 4 + bz, r).astype(sb2.dtype)
        return carry

    lax.fori_loop(0, nchunk, fill_b2, 0)
    cb2 = rcopy(sb2, rb2, ssb2.at[0], rsb2.at[0], xpeer)
    cb2.start()
    ca2 = []
    for s in range(1, 4):
        zt = (z + s) % 4

        def fill_a2(i, carry, s=s, zt=zt):
            q = pl.ds(pl.multiple_of(i * rows, rows), rows)
            for bx in range(2):
                sa2[s - 1, bx, :, q, :] = pair_sum(bx * 4 + zt, q).astype(sa2.dtype)
            return carry

        lax.fori_loop(0, nchunk, fill_a2, 0)
        cp = rcopy(sa2.at[s - 1], ra2.at[s - 1], ssa2.at[s - 1], rsa2.at[s - 1],
                   xh * 8 + zt * 2 + c)
        cp.start()
        ca2.append(cp)

    cb2.wait()

    def sum_b2(i, carry):
        r = pl.ds(pl.multiple_of(half + i * rows, rows), rows)
        q = pl.ds(pl.multiple_of(i * rows, rows), rows)
        for bz in range(4):
            fb2[bz, :, q, :] = pair_sum(xh * 4 + bz, r) + rb2[bz, :, q, :].astype(f32)
        return carry

    lax.fori_loop(0, nchunk, sum_b2, 0)
    cb3 = []
    for s in range(1, 4):
        zt = (z + s) % 4
        sb3[s - 1] = fb2[zt].astype(sb3.dtype)
        cp = rcopy(sb3.at[s - 1], rb3.at[s - 1], ssb3.at[s - 1], rsb3.at[s - 1],
                   xh * 8 + zt * 2 + c)
        cp.start()
        cb3.append(cp)

    for cp in ca2:
        cp.wait()

    def sum_a2(i, carry):
        q = pl.ds(pl.multiple_of(i * rows, rows), rows)
        for bx in range(2):
            acc = pair_sum(bx * 4 + z, q)
            for k in range(3):
                acc = acc + ra2[k, bx, :, q, :].astype(f32)
            fa2[bx, :, q, :] = acc
        return carry

    lax.fori_loop(0, nchunk, sum_a2, 0)
    sa3[...] = fa2[1 - xh].astype(sa3.dtype)
    ca3 = rcopy(sa3, ra3, ssa3.at[0], rsa3.at[0], xpeer)
    ca3.start()
    for cp in cb3:
        cp.wait()
    acc = fb2[z]
    for k in range(3):
        acc = acc + rb3[k].astype(f32)
    o_ref[:, rb, :] = acc.astype(o_ref.dtype)
    ca3.wait()
    o_ref[:, ra, :] = (fa2[xh] + ra3[...].astype(f32)).astype(o_ref.dtype)


def split_reduce_scatter(ta, tb):
    n = 2
    t, width = ta.shape
    w = width // 16
    h = t // 2
    bf = jnp.bfloat16
    f32 = jnp.float32
    dma = pltpu.SemaphoreType.DMA
    return pl.pallas_call(
        split_reduce_kernel,
        out_shape=jax.ShapeDtypeStruct((n, t, w), bf),
        in_specs=[pl.BlockSpec(memory_space=pl.ANY)] * 2,
        out_specs=pl.BlockSpec(memory_space=pltpu.VMEM),
        scratch_shapes=[
            pltpu.VMEM((8, n, t, w), bf),
            pltpu.VMEM((8, n, t, w), bf),
            pltpu.VMEM((3, 2, n, h, w), bf),
            pltpu.VMEM((3, 2, n, h, w), bf),
            pltpu.VMEM((2, n, h, w), f32),
            pltpu.VMEM((n, h, w), bf),
            pltpu.VMEM((n, h, w), bf),
            pltpu.VMEM((4, n, h, w), bf),
            pltpu.VMEM((4, n, h, w), bf),
            pltpu.VMEM((4, n, h, w), f32),
            pltpu.VMEM((3, n, h, w), bf),
            pltpu.VMEM((3, n, h, w), bf),
            dma((16,)), dma((16,)), dma((16,)),
            dma((3,)), dma((3,)), dma((1,)), dma((1,)),
            dma((1,)), dma((1,)), dma((3,)), dma((3,)),
        ],
        compiler_params=pltpu.CompilerParams(has_side_effects=True,
                                             vmem_limit_bytes=56 * 1024 * 1024),
    )(ta, tb)


def gate_up_kernel(h_ref, go_ref, gp_ref, uo_ref, upv_ref, io_ref, it_ref, acc, tbuf):
    k = pl.program_id(0)
    tile = 256
    chunk = 64
    f32 = jnp.float32

    @pl.when(k == 0)
    def _():
        acc[...] = jnp.zeros_like(acc)

    def mix(i, carry):
        r = pl.ds(pl.multiple_of(i * chunk, chunk), chunk)
        for j, (on_ref, pv_ref) in enumerate(((go_ref, gp_ref), (uo_ref, upv_ref))):
            on = on_ref[r, :].astype(f32)
            pv = pv_ref[r, :].astype(f32)
            tbuf[j, r, :] = (POLYAK * on + (1.0 - POLYAK) * pv).astype(tbuf.dtype)
        return carry

    lax.fori_loop(0, go_ref.shape[0] // chunk, mix, 0)

    def mm(i, carry):
        r = pl.ds(pl.multiple_of(i * tile, tile), tile)
        hs = h_ref[r, :]
        acc[0, r, :] += jnp.dot(hs, go_ref[...], preferred_element_type=f32)
        acc[1, r, :] += jnp.dot(hs, tbuf[0], preferred_element_type=f32)
        acc[2, r, :] += jnp.dot(hs, uo_ref[...], preferred_element_type=f32)
        acc[3, r, :] += jnp.dot(hs, tbuf[1], preferred_element_type=f32)
        return carry

    lax.fori_loop(0, h_ref.shape[0] // tile, mm, 0)

    @pl.when(k == pl.num_programs(0) - 1)
    def _():
        def finish(i, carry):
            r = pl.ds(pl.multiple_of(i * chunk, chunk), chunk)
            io_ref[r, :] = (jax.nn.silu(acc[0, r, :]) * acc[2, r, :]).astype(io_ref.dtype)
            it_ref[r, :] = (jax.nn.silu(acc[1, r, :]) * acc[3, r, :]).astype(it_ref.dtype)
            return carry

        lax.fori_loop(0, io_ref.shape[0] // chunk, finish, 0)


def gate_up(h_full, go, gp, uo, upv, kb):
    tokens, kdim = h_full.shape
    ff = go.shape[1]
    wspec = pl.BlockSpec((kb, ff), lambda k: (k, 0))
    ospec = pl.BlockSpec((tokens, ff), lambda k: (0, 0))
    flops = 8 * tokens * kdim * ff
    nbytes = 2 * (tokens * kdim + 4 * kdim * ff + 2 * tokens * ff)
    return pl.pallas_call(
        gate_up_kernel,
        grid=(kdim // kb,),
        out_shape=(jax.ShapeDtypeStruct((tokens, ff), jnp.bfloat16),) * 2,
        in_specs=[pl.BlockSpec((tokens, kb), lambda k: (0, k))] + [wspec] * 4,
        out_specs=[ospec, ospec],
        scratch_shapes=[pltpu.VMEM((4, tokens, ff), jnp.float32),
                        pltpu.VMEM((2, kb, ff), jnp.bfloat16)],
        compiler_params=pltpu.CompilerParams(vmem_limit_bytes=48 * 1024 * 1024),
        cost_estimate=pl.CostEstimate(flops=flops, bytes_accessed=nbytes,
                                      transcendentals=2 * tokens * ff),
    )(h_full, go, gp, uo, upv)


def gate_up_online_kernel(h_ref, go_ref, uo_ref, pg_ref, pu_ref, io_ref, it_ref, acc):
    k = pl.program_id(0)
    tile = 256
    chunk = 64
    f32 = jnp.float32

    @pl.when(k == 0)
    def _():
        acc[...] = jnp.zeros_like(acc)

    def mm(i, carry):
        r = pl.ds(pl.multiple_of(i * tile, tile), tile)
        hs = h_ref[r, :]
        acc[0, r, :] += jnp.dot(hs, go_ref[...], preferred_element_type=f32)
        acc[1, r, :] += jnp.dot(hs, uo_ref[...], preferred_element_type=f32)
        return carry

    lax.fori_loop(0, h_ref.shape[0] // tile, mm, 0)

    @pl.when(k == pl.num_programs(0) - 1)
    def _():
        def finish(i, carry):
            r = pl.ds(pl.multiple_of(i * chunk, chunk), chunk)
            g_o = acc[0, r, :]
            u_o = acc[1, r, :]
            g_t = POLYAK * g_o + (1.0 - POLYAK) * pg_ref[r, :]
            u_t = POLYAK * u_o + (1.0 - POLYAK) * pu_ref[r, :]
            io_ref[r, :] = (jax.nn.silu(g_o) * u_o).astype(io_ref.dtype)
            it_ref[r, :] = (jax.nn.silu(g_t) * u_t).astype(it_ref.dtype)
            return carry

        lax.fori_loop(0, io_ref.shape[0] // chunk, finish, 0)


def gate_up_online(h_full, go, uo, pg, pu, kb):
    tokens, kdim = h_full.shape
    ff = go.shape[1]
    wspec = pl.BlockSpec((kb, ff), lambda k: (k, 0))
    ospec = pl.BlockSpec((tokens, ff), lambda k: (0, 0))
    return pl.pallas_call(
        gate_up_online_kernel,
        grid=(kdim // kb,),
        out_shape=(jax.ShapeDtypeStruct((tokens, ff), jnp.bfloat16),) * 2,
        in_specs=[pl.BlockSpec((tokens, kb), lambda k: (0, k)), wspec, wspec, ospec, ospec],
        out_specs=[ospec, ospec],
        scratch_shapes=[pltpu.VMEM((2, tokens, ff), jnp.float32)],
        compiler_params=pltpu.CompilerParams(vmem_limit_bytes=48 * 1024 * 1024),
        cost_estimate=pl.CostEstimate(flops=4 * tokens * kdim * ff,
                                      bytes_accessed=2 * (tokens * kdim + 2 * kdim * ff),
                                      transcendentals=2 * tokens * ff),
    )(h_full, go, uo, pg, pu)


def down_kernel(io_ref, it_ref, do_ref, dp_ref, oo_ref, ot_ref):
    f32 = jnp.float32
    wt = (POLYAK * do_ref[...].astype(f32)
          + (1.0 - POLYAK) * dp_ref[...].astype(f32)).astype(do_ref.dtype)
    oo_ref[...] = jnp.dot(io_ref[...], do_ref[...], preferred_element_type=f32).astype(oo_ref.dtype)
    ot_ref[...] = jnp.dot(it_ref[...], wt, preferred_element_type=f32).astype(ot_ref.dtype)


def down_products(inner_o, inner_t, down_full, down_previous, cb):
    tokens, ff = inner_o.shape
    width = down_full.shape[1]
    ispec = pl.BlockSpec((tokens, ff), lambda j: (0, 0))
    wspec = pl.BlockSpec((ff, cb), lambda j: (0, j))
    ospec = pl.BlockSpec((tokens, cb), lambda j: (0, j))
    return pl.pallas_call(
        down_kernel,
        grid=(width // cb,),
        out_shape=(jax.ShapeDtypeStruct((tokens, width), jnp.bfloat16),) * 2,
        in_specs=[ispec, ispec, wspec, wspec],
        out_specs=[ospec, ospec],
        compiler_params=pltpu.CompilerParams(vmem_limit_bytes=32 * 1024 * 1024),
        cost_estimate=pl.CostEstimate(flops=4 * tokens * ff * width,
                                      bytes_accessed=2 * (2 * tokens * ff + 2 * ff * width
                                                          + 2 * tokens * width),
                                      transcendentals=0),
    )(inner_o, inner_t, down_full, down_previous)


def local(ndp, nmp, hidden_states, gate_online, up_online, down_online, gate_previous,
          up_previous, down_previous):
    kb = 2 * gate_online.shape[0]
    if ndp == 8 and nmp == 16:
        _, _, _, down_full, inner_o, inner_t = gather_relay(
            hidden_states, gate_online, up_online, down_online, gate_previous, up_previous, ndp)
    else:
        features_all = lax.all_gather(hidden_states, "mp", axis=1, tiled=True)
        gate_full, up_full, down_full = gather_weights_direct(gate_online, up_online,
                                                              down_online, ndp)
        inner_o, inner_t = gate_up(features_all, gate_full, gate_previous, up_full, up_previous,
                                   kb)
    if nmp == 16:
        online_part, target_part = down_products(inner_o, inner_t, down_full, down_previous,
                                                 down_online.shape[1])
        result = split_reduce_scatter(online_part, target_part)
    else:
        target_down = blend(down_full, down_previous)
        online_part = jnp.dot(inner_o, down_full, preferred_element_type=jnp.float32)
        target_part = jnp.dot(inner_t, target_down, preferred_element_type=jnp.float32)
        terms = jnp.stack([online_part, target_part], axis=0).astype(jnp.bfloat16)
        result = reduce_scatter(terms, nmp)
    return (result[0], result[1])


def solution(mesh):
    ndp = mesh.shape["dp"]
    nmp = mesh.shape["mp"]
    in_specs = (
        P("dp", "mp"),
        P("dp", "mp"),
        P("dp", "mp"),
        P("mp", "dp"),
        P(None, "mp"),
        P(None, "mp"),
        P("mp", None),
    )
    out_specs = (P("dp", "mp"), P("dp", "mp"))
    return jax.shard_map(functools.partial(local, ndp, nmp), mesh=mesh, in_specs=in_specs,
                         out_specs=out_specs, check_vma=False)
```

```python
import functools

import jax
import jax.numpy as jnp
from jax import lax
from jax.experimental import pallas as pl
from jax.experimental.pallas import tpu as pltpu
from jax.sharding import PartitionSpec as P

POLYAK = 0.25
MESH = pl.DeviceIdType.MESH


def blend(online, previous):
    return (
        POLYAK * online.astype(jnp.float32) + (1.0 - POLYAK) * previous.astype(jnp.float32)
    ).astype(jnp.bfloat16)


def gather_kernel(ndp, g_ref, u_ref, dn_ref, gf_ref, uf_ref, df_ref, send_sem, recv_sem,
                  local_sem):
    d = lax.axis_index("dp")
    m = lax.axis_index("mp")
    kr = g_ref.shape[0]
    dc = dn_ref.shape[1]
    rows = pl.ds(pl.multiple_of(d * kr, kr), kr)
    cols = pl.ds(pl.multiple_of(d * dc, dc), dc)

    locals_ = [
        pltpu.make_async_copy(g_ref, gf_ref.at[rows], local_sem.at[0]),
        pltpu.make_async_copy(u_ref, uf_ref.at[rows], local_sem.at[1]),
        pltpu.make_async_copy(dn_ref, df_ref.at[:, cols], local_sem.at[2]),
    ]
    for c in locals_:
        c.start()

    copies = []
    k = 0
    for s in range(1, ndp):
        peer = lax.rem(d + s, ndp)
        for src, dst in ((g_ref, gf_ref.at[rows]), (u_ref, uf_ref.at[rows]),
                         (dn_ref, df_ref.at[:, cols])):
            copies.append(pltpu.make_async_remote_copy(
                src_ref=src, dst_ref=dst, send_sem=send_sem.at[k], recv_sem=recv_sem.at[k],
                device_id=(peer, m), device_id_type=MESH))
            k += 1
    for c in copies:
        c.start()
    for c in locals_:
        c.wait()
    for c in copies:
        c.wait()


def gather_weights_direct(g, u, dn, ndp):
    n_copies = 3 * (ndp - 1)
    any_spec = pl.BlockSpec(memory_space=pl.ANY)
    out_shape = (
        jax.ShapeDtypeStruct((g.shape[0] * ndp, g.shape[1]), g.dtype),
        jax.ShapeDtypeStruct((u.shape[0] * ndp, u.shape[1]), u.dtype),
        jax.ShapeDtypeStruct((dn.shape[0], dn.shape[1] * ndp), dn.dtype),
    )
    return pl.pallas_call(
        functools.partial(gather_kernel, ndp),
        out_shape=out_shape,
        in_specs=[any_spec] * 3,
        out_specs=[any_spec] * 3,
        scratch_shapes=[
            pltpu.SemaphoreType.DMA((n_copies,)),
            pltpu.SemaphoreType.DMA((n_copies,)),
            pltpu.SemaphoreType.DMA((3,)),
        ],
        compiler_params=pltpu.CompilerParams(has_side_effects=True),
    )(g, u, dn)


def relay_gather_kernel(h_ref, g_ref, u_ref, dn_ref, gp_ref, upv_ref, hf_ref, gf_ref, uf_ref,
                        df_ref, io_ref, it_ref, send_sem, recv_sem, local_sem, hsend, hrecv,
                        hv, wb, wsem, acc):
    ndp = 8
    d = lax.axis_index("dp")
    m = lax.axis_index("mp")
    lo = d % 2
    partner = d - lo + (1 - lo)
    nxt = (d + 2) % ndp
    prv = (d + ndp - 2) % ndp
    far = (d + 4) % ndp
    owns = (g_ref, u_ref, dn_ref)
    fulls = (gf_ref, uf_ref, df_ref)

    def slot(w, idx, half=None):
        if w < 2:
            kr = owns[w].shape[0]
            if half is None:
                return fulls[w].at[pl.ds(pl.multiple_of(idx * kr, kr), kr)]
            hk = kr // 2
            return fulls[w].at[pl.ds(pl.multiple_of(idx * kr + half * hk, hk), hk)]
        rr, dc = owns[w].shape
        cols = pl.ds(pl.multiple_of(idx * dc, dc), dc)
        if half is None:
            return fulls[w].at[:, cols]
        hr = rr // 2
        return fulls[w].at[pl.ds(half * hr, hr), cols]

    def rc(w, k, src, dst, target):
        i = w * 8 + k
        return pltpu.make_async_remote_copy(
            src_ref=src, dst_ref=dst, send_sem=send_sem.at[i], recv_sem=recv_sem.at[i],
            device_id=(target, m), device_id_type=MESH)

    locals_ = [pltpu.make_async_copy(owns[w], slot(w, d), local_sem.at[w]) for w in range(3)]
    c = {}
    for w in range(3):
        c[w, 0] = rc(w, 0, owns[w], slot(w, d), partner)
        c[w, 1] = rc(w, 1, owns[w], slot(w, d), nxt)
        c[w, 2] = rc(w, 2, owns[w], slot(w, d), prv)
        c[w, 3] = rc(w, 3, slot(w, partner), slot(w, partner), nxt)
        c[w, 4] = rc(w, 4, slot(w, partner), slot(w, partner), prv)
        c[w, 5] = rc(w, 5, slot(w, prv, 0), slot(w, prv, 0), nxt)
        c[w, 6] = rc(w, 6, slot(w, nxt, 1), slot(w, nxt, 1), prv)
        c[w, 7] = rc(w, 7, slot(w, far), slot(w, far), partner)
    nmp = 16
    hc = h_ref.shape[1]
    hmine = hf_ref.at[:, pl.ds(pl.multiple_of(m * hc, hc), hc)]
    hlocal = pltpu.make_async_copy(h_ref, hmine, local_sem.at[3])
    hcopies = []
    for s in range(1, nmp):
        hcopies.append(pltpu.make_async_remote_copy(
            src_ref=h_ref, dst_ref=hmine, send_sem=hsend.at[s - 1], recv_sem=hrecv.at[s - 1],
            device_id=(d, lax.rem(m + s, nmp)), device_id_type=MESH))
    for w in range(3):
        locals_[w].start()
        for k in range(3):
            c[w, k].start()
    hlocal.start()
    for cp in hcopies:
        cp.start()
    for w in range(3):
        c[w, 1].wait_recv()
        c[w, 5].start()
        c[w, 2].wait_recv()
        c[w, 6].start()
    for w in range(3):
        c[w, 5].wait_recv()
        c[w, 6].wait_recv()
        c[w, 7].start()
    for w in range(3):
        c[w, 0].wait_recv()
        c[w, 3].start()
        c[w, 4].start()

    hlocal.wait()
    for cp in hcopies:
        cp.wait_recv()
    for w in range(3):
        locals_[w].wait()
    hload = pltpu.make_async_copy(hf_ref, hv, wsem.at[2])
    hload.start()
    hload.wait()
    acc[...] = jnp.zeros_like(acc)
    kr = g_ref.shape[0]
    tile = 256

    def products(a_ref, b_ref, idx, first):
        rows = pl.ds(pl.multiple_of(idx * kr, kr), kr)
        la = pltpu.make_async_copy(a_ref.at[rows], wb.at[0], wsem.at[0])
        lb = pltpu.make_async_copy(b_ref.at[rows], wb.at[1], wsem.at[1])
        la.start()
        lb.start()
        la.wait()
        lb.wait()

        def mm(i, carry):
            r = pl.ds(pl.multiple_of(i * tile, tile), tile)
            hs = hv[r, rows]
            acc[first, r, :] += jnp.dot(hs, wb[0], preferred_element_type=jnp.float32)
            acc[first + 1, r, :] += jnp.dot(hs, wb[1], preferred_element_type=jnp.float32)
            return carry

        lax.fori_loop(0, hv.shape[0] // tile, mm, 0)

    def prev_slot(i, carry):
        products(gp_ref, upv_ref, i, 2)
        return carry

    lax.fori_loop(0, ndp, prev_slot, 0)
    for idx in (d, partner, prv, nxt, far):
        products(gf_ref, uf_ref, idx, 0)

    for w in range(3):
        c[w, 7].wait_recv()
    products(gf_ref, uf_ref, (partner + 4) % ndp, 0)
    for w in range(3):
        c[w, 3].wait_recv()
        c[w, 4].wait_recv()
    for idx in ((partner + 2) % ndp, (partner + ndp - 2) % ndp):
        products(gf_ref, uf_ref, idx, 0)

    chunk = 64

    def finish(i, carry):
        r = pl.ds(pl.multiple_of(i * chunk, chunk), chunk)
        g_o = acc[0, r, :]
        u_o = acc[1, r, :]
        g_t = POLYAK * g_o + (1.0 - POLYAK) * acc[2, r, :]
        u_t = POLYAK * u_o + (1.0 - POLYAK) * acc[3, r, :]
        io_ref[r, :] = (jax.nn.silu(g_o) * u_o).astype(io_ref.dtype)
        it_ref[r, :] = (jax.nn.silu(g_t) * u_t).astype(it_ref.dtype)
        return carry

    lax.fori_loop(0, io_ref.shape[0] // chunk, finish, 0)
    for w in range(3):
        for k in range(8):
            c[w, k].wait_send()
    for cp in hcopies:
        cp.wait_send()


def gather_relay(h, g, u, dn, gp, upv, ndp):
    any_spec = pl.BlockSpec(memory_space=pl.ANY)
    out_shape = (
        jax.ShapeDtypeStruct((g.shape[0] * ndp, g.shape[1]), g.dtype),
        jax.ShapeDtypeStruct((u.shape[0] * ndp, u.shape[1]), u.dtype),
        jax.ShapeDtypeStruct((dn.shape[0], dn.shape[1] * ndp), dn.dtype),
    )
    tokens, ff = h.shape[0], g.shape[1]
    prod = jax.ShapeDtypeStruct((tokens, ff), jnp.bfloat16)
    vspec = pl.BlockSpec(memory_space=pltpu.VMEM)
    return pl.pallas_call(
        relay_gather_kernel,
        out_shape=(jax.ShapeDtypeStruct((tokens, h.shape[1] * 16), h.dtype),) + out_shape
        + (prod, prod),
        in_specs=[any_spec] * 6,
        out_specs=[any_spec] * 4 + [vspec] * 2,
        scratch_shapes=[
            pltpu.SemaphoreType.DMA((24,)),
            pltpu.SemaphoreType.DMA((24,)),
            pltpu.SemaphoreType.DMA((4,)),
            pltpu.SemaphoreType.DMA((15,)),
            pltpu.SemaphoreType.DMA((15,)),
            pltpu.VMEM((tokens, h.shape[1] * 16), h.dtype),
            pltpu.VMEM((2, g.shape[0], ff), g.dtype),
            pltpu.SemaphoreType.DMA((3,)),
            pltpu.VMEM((4, tokens, ff), jnp.float32),
        ],
        compiler_params=pltpu.CompilerParams(has_side_effects=True,
                                             vmem_limit_bytes=48 * 1024 * 1024),
    )(h, g, u, dn, gp, upv)


def reduce_kernel(nmp, t_ref, o_ref, buf, send_sem, recv_sem, local_sem):
    d = lax.axis_index("dp")
    m = lax.axis_index("mp")
    w = o_ref.shape[2]
    mine = pl.ds(pl.multiple_of(m * w, w), w)
    local_copy = pltpu.make_async_copy(t_ref.at[:, :, mine], buf.at[0], local_sem.at[0])
    local_copy.start()
    copies = []
    for s in range(1, nmp):
        peer = lax.rem(m + s, nmp)
        theirs = pl.ds(pl.multiple_of(peer * w, w), w)
        copies.append(pltpu.make_async_remote_copy(
            src_ref=t_ref.at[:, :, theirs], dst_ref=buf.at[s], send_sem=send_sem.at[s],
            recv_sem=recv_sem.at[s], device_id=(d, peer), device_id_type=MESH))
    for c in copies:
        c.start()
    local_copy.wait()
    for c in copies:
        c.wait()
    rows = 32

    def body(i, carry):
        r = pl.ds(pl.multiple_of(i * rows, rows), rows)
        for k in range(o_ref.shape[0]):
            acc = buf[0, k, r, :].astype(jnp.float32)
            for s in range(1, nmp):
                acc = acc + buf[s, k, r, :].astype(jnp.float32)
            o_ref[k, r, :] = acc.astype(o_ref.dtype)
        return carry

    lax.fori_loop(0, o_ref.shape[1] // rows, body, 0)


def reduce_scatter(terms, nmp):
    n, t, width = terms.shape
    w = width // nmp
    return pl.pallas_call(
        functools.partial(reduce_kernel, nmp),
        out_shape=jax.ShapeDtypeStruct((n, t, w), jnp.bfloat16),
        in_specs=[pl.BlockSpec(memory_space=pl.ANY)],
        out_specs=pl.BlockSpec(memory_space=pltpu.VMEM),
        scratch_shapes=[
            pltpu.VMEM((nmp, n, t, w), jnp.bfloat16),
            pltpu.SemaphoreType.DMA((nmp,)),
            pltpu.SemaphoreType.DMA((nmp,)),
            pltpu.SemaphoreType.DMA((1,)),
        ],
        compiler_params=pltpu.CompilerParams(has_side_effects=True,
                                             vmem_limit_bytes=48 * 1024 * 1024),
    )(terms)


def hier_reduce_kernel(ta_ref, tb_ref, o_ref, own, r1, sb2, r2, s2, sb3, r3,
                       ls, ss1, rs1, ss2, rs2, ss3, rs3):
    d = lax.axis_index("dp")
    m = lax.axis_index("mp")
    c = m % 2
    z = (m // 2) % 4
    xh = m // 8
    w = o_ref.shape[2]
    rows = 32
    nchunk = o_ref.shape[1] // rows

    def blk(b, k):
        return (ta_ref, tb_ref)[k].at[:, pl.ds(pl.multiple_of(b * w, w), w)]

    def dev(mm):
        return (d, mm)

    locs = []
    st1 = []
    for j in range(16):
        bx, bz, k = j // 8, (j // 2) % 4, j % 2
        jj = bx * 4 + bz
        locs.append(pltpu.make_async_copy(blk(bx * 8 + bz * 2 + c, k), own.at[jj, k],
                                          ls.at[j]))
        st1.append(pltpu.make_async_remote_copy(
            src_ref=blk(bx * 8 + bz * 2 + (1 - c), k), dst_ref=r1.at[jj, k], send_sem=ss1.at[j],
            recv_sem=rs1.at[j], device_id=dev(m + 1 - 2 * c), device_id_type=MESH))
    for j in range(16):
        st1[j].start()
        locs[j].start()
    for j in range(16):
        locs[j].wait()
        st1[j].wait()

    st2 = []
    for s in range(1, 4):
        zt = (z + s) % 4

        def fill(i, carry, s=s, zt=zt):
            r = pl.ds(pl.multiple_of(i * rows, rows), rows)
            for bx in range(2):
                idx = bx * 4 + zt
                sb2[s - 1, bx, :, r, :] = (own[idx, :, r, :].astype(jnp.float32)
                                           + r1[idx, :, r, :].astype(jnp.float32)
                                           ).astype(sb2.dtype)
            return carry

        lax.fori_loop(0, nchunk, fill, 0)
        cp = pltpu.make_async_remote_copy(
            src_ref=sb2.at[s - 1], dst_ref=r2.at[s - 1], send_sem=ss2.at[s - 1],
            recv_sem=rs2.at[s - 1], device_id=dev(xh * 8 + zt * 2 + c), device_id_type=MESH)
        cp.start()
        st2.append(cp)
    for cp in st2:
        cp.wait()

    def sum2(i, carry):
        r = pl.ds(pl.multiple_of(i * rows, rows), rows)
        for bx in range(2):
            idx = bx * 4 + z
            acc = own[idx, :, r, :].astype(jnp.float32) + r1[idx, :, r, :].astype(jnp.float32)
            for k in range(3):
                acc = acc + r2[k, bx, :, r, :].astype(jnp.float32)
            s2[bx, :, r, :] = acc
        return carry

    lax.fori_loop(0, nchunk, sum2, 0)
    sb3[...] = s2[1 - xh].astype(sb3.dtype)
    cp3 = pltpu.make_async_remote_copy(
        src_ref=sb3, dst_ref=r3, send_sem=ss3.at[0], recv_sem=rs3.at[0],
        device_id=dev(m + 8 - 16 * xh), device_id_type=MESH)
    cp3.start()
    cp3.wait()
    o_ref[...] = (s2[xh] + r3[...].astype(jnp.float32)).astype(o_ref.dtype)


def hier_reduce_scatter(ta, tb):
    n = 2
    t, width = ta.shape
    w = width // 16
    bf = jnp.bfloat16
    dma = pltpu.SemaphoreType.DMA
    return pl.pallas_call(
        hier_reduce_kernel,
        out_shape=jax.ShapeDtypeStruct((n, t, w), bf),
        in_specs=[pl.BlockSpec(memory_space=pl.ANY)] * 2,
        out_specs=pl.BlockSpec(memory_space=pltpu.VMEM),
        scratch_shapes=[
            pltpu.VMEM((8, n, t, w), bf),
            pltpu.VMEM((8, n, t, w), bf),
            pltpu.VMEM((3, 2, n, t, w), bf),
            pltpu.VMEM((3, 2, n, t, w), bf),
            pltpu.VMEM((2, n, t, w), jnp.float32),
            pltpu.VMEM((n, t, w), bf),
            pltpu.VMEM((n, t, w), bf),
            dma((16,)), dma((16,)), dma((16,)), dma((3,)), dma((3,)), dma((1,)), dma((1,)),
        ],
        compiler_params=pltpu.CompilerParams(has_side_effects=True,
                                             vmem_limit_bytes=56 * 1024 * 1024),
    )(ta, tb)


def split_reduce_kernel(ta_ref, tb_ref, o_ref, own, r1, sa2, ra2, fa2, sa3, ra3,
                        sb2, rb2, fb2, sb3, rb3, ls, ss1, rs1, ssa2, rsa2, ssa3, rsa3,
                        ssb2, rsb2, ssb3, rsb3):
    d = lax.axis_index("dp")
    m = lax.axis_index("mp")
    c = m % 2
    z = (m // 2) % 4
    xh = m // 8
    w = o_ref.shape[2]
    half = o_ref.shape[1] // 2
    ra = pl.ds(0, half)
    rb = pl.ds(half, half)
    rows = 32
    nchunk = half // rows
    f32 = jnp.float32
    xpeer = m + 8 - 16 * xh

    def blk(b, k):
        return (ta_ref, tb_ref)[k].at[:, pl.ds(pl.multiple_of(b * w, w), w)]

    def rcopy(src, dst, ss, rs, mm):
        return pltpu.make_async_remote_copy(src_ref=src, dst_ref=dst, send_sem=ss, recv_sem=rs,
                                            device_id=(d, mm), device_id_type=MESH)

    locs = []
    st1 = []
    for j in range(16):
        bx, bz, k = j // 8, (j // 2) % 4, j % 2
        jj = bx * 4 + bz
        locs.append(pltpu.make_async_copy(blk(bx * 8 + bz * 2 + c, k), own.at[jj, k],
                                          ls.at[j]))
        st1.append(rcopy(blk(bx * 8 + bz * 2 + (1 - c), k), r1.at[jj, k], ss1.at[j], rs1.at[j],
                         m + 1 - 2 * c))
    for j in range(16):
        st1[j].start()
        locs[j].start()
    for j in range(16):
        locs[j].wait()
        st1[j].wait()

    def pair_sum(idx, r):
        return own[idx, :, r, :].astype(f32) + r1[idx, :, r, :].astype(f32)

    def fill_b2(i, carry):
        r = pl.ds(pl.multiple_of(half + i * rows, rows), rows)
        q = pl.ds(pl.multiple_of(i * rows, rows), rows)
        for bz in range(4):
            sb2[bz, :, q, :] = pair_sum((1 - xh) * 4 + bz, r).astype(sb2.dtype)
        return carry

    lax.fori_loop(0, nchunk, fill_b2, 0)
    cb2 = rcopy(sb2, rb2, ssb2.at[0], rsb2.at[0], xpeer)
    cb2.start()
    ca2 = []
    for s in range(1, 4):
        zt = (z + s) % 4

        def fill_a2(i, carry, s=s, zt=zt):
            q = pl.ds(pl.multiple_of(i * rows, rows), rows)
            for bx in range(2):
                sa2[s - 1, bx, :, q, :] = pair_sum(bx * 4 + zt, q).astype(sa2.dtype)
            return carry

        lax.fori_loop(0, nchunk, fill_a2, 0)
        cp = rcopy(sa2.at[s - 1], ra2.at[s - 1], ssa2.at[s - 1], rsa2.at[s - 1],
                   xh * 8 + zt * 2 + c)
        cp.start()
        ca2.append(cp)

    cb2.wait()

    def sum_b2(i, carry):
        r = pl.ds(pl.multiple_of(half + i * rows, rows), rows)
        q = pl.ds(pl.multiple_of(i * rows, rows), rows)
        for bz in range(4):
            fb2[bz, :, q, :] = pair_sum(xh * 4 + bz, r) + rb2[bz, :, q, :].astype(f32)
        return carry

    lax.fori_loop(0, nchunk, sum_b2, 0)
    cb3 = []
    for s in range(1, 4):
        zt = (z + s) % 4
        sb3[s - 1] = fb2[zt].astype(sb3.dtype)
        cp = rcopy(sb3.at[s - 1], rb3.at[s - 1], ssb3.at[s - 1], rsb3.at[s - 1],
                   xh * 8 + zt * 2 + c)
        cp.start()
        cb3.append(cp)

    for cp in ca2:
        cp.wait()

    def sum_a2(i, carry):
        q = pl.ds(pl.multiple_of(i * rows, rows), rows)
        for bx in range(2):
            acc = pair_sum(bx * 4 + z, q)
            for k in range(3):
                acc = acc + ra2[k, bx, :, q, :].astype(f32)
            fa2[bx, :, q, :] = acc
        return carry

    lax.fori_loop(0, nchunk, sum_a2, 0)
    sa3[...] = fa2[1 - xh].astype(sa3.dtype)
    ca3 = rcopy(sa3, ra3, ssa3.at[0], rsa3.at[0], xpeer)
    ca3.start()
    for cp in cb3:
        cp.wait()
    acc = fb2[z]
    for k in range(3):
        acc = acc + rb3[k].astype(f32)
    o_ref[:, rb, :] = acc.astype(o_ref.dtype)
    ca3.wait()
    o_ref[:, ra, :] = (fa2[xh] + ra3[...].astype(f32)).astype(o_ref.dtype)


def split_reduce_scatter(ta, tb):
    n = 2
    t, width = ta.shape
    w = width // 16
    h = t // 2
    bf = jnp.bfloat16
    f32 = jnp.float32
    dma = pltpu.SemaphoreType.DMA
    return pl.pallas_call(
        split_reduce_kernel,
        out_shape=jax.ShapeDtypeStruct((n, t, w), bf),
        in_specs=[pl.BlockSpec(memory_space=pl.ANY)] * 2,
        out_specs=pl.BlockSpec(memory_space=pltpu.VMEM),
        scratch_shapes=[
            pltpu.VMEM((8, n, t, w), bf),
            pltpu.VMEM((8, n, t, w), bf),
            pltpu.VMEM((3, 2, n, h, w), bf),
            pltpu.VMEM((3, 2, n, h, w), bf),
            pltpu.VMEM((2, n, h, w), f32),
            pltpu.VMEM((n, h, w), bf),
            pltpu.VMEM((n, h, w), bf),
            pltpu.VMEM((4, n, h, w), bf),
            pltpu.VMEM((4, n, h, w), bf),
            pltpu.VMEM((4, n, h, w), f32),
            pltpu.VMEM((3, n, h, w), bf),
            pltpu.VMEM((3, n, h, w), bf),
            dma((16,)), dma((16,)), dma((16,)),
            dma((3,)), dma((3,)), dma((1,)), dma((1,)),
            dma((1,)), dma((1,)), dma((3,)), dma((3,)),
        ],
        compiler_params=pltpu.CompilerParams(has_side_effects=True,
                                             vmem_limit_bytes=56 * 1024 * 1024),
    )(ta, tb)


def gate_up_kernel(h_ref, go_ref, gp_ref, uo_ref, upv_ref, io_ref, it_ref, acc, tbuf):
    k = pl.program_id(0)
    tile = 256
    chunk = 64
    f32 = jnp.float32

    @pl.when(k == 0)
    def _():
        acc[...] = jnp.zeros_like(acc)

    def mix(i, carry):
        r = pl.ds(pl.multiple_of(i * chunk, chunk), chunk)
        for j, (on_ref, pv_ref) in enumerate(((go_ref, gp_ref), (uo_ref, upv_ref))):
            on = on_ref[r, :].astype(f32)
            pv = pv_ref[r, :].astype(f32)
            tbuf[j, r, :] = (POLYAK * on + (1.0 - POLYAK) * pv).astype(tbuf.dtype)
        return carry

    lax.fori_loop(0, go_ref.shape[0] // chunk, mix, 0)

    def mm(i, carry):
        r = pl.ds(pl.multiple_of(i * tile, tile), tile)
        hs = h_ref[r, :]
        acc[0, r, :] += jnp.dot(hs, go_ref[...], preferred_element_type=f32)
        acc[1, r, :] += jnp.dot(hs, tbuf[0], preferred_element_type=f32)
        acc[2, r, :] += jnp.dot(hs, uo_ref[...], preferred_element_type=f32)
        acc[3, r, :] += jnp.dot(hs, tbuf[1], preferred_element_type=f32)
        return carry

    lax.fori_loop(0, h_ref.shape[0] // tile, mm, 0)

    @pl.when(k == pl.num_programs(0) - 1)
    def _():
        def finish(i, carry):
            r = pl.ds(pl.multiple_of(i * chunk, chunk), chunk)
            io_ref[r, :] = (jax.nn.silu(acc[0, r, :]) * acc[2, r, :]).astype(io_ref.dtype)
            it_ref[r, :] = (jax.nn.silu(acc[1, r, :]) * acc[3, r, :]).astype(it_ref.dtype)
            return carry

        lax.fori_loop(0, io_ref.shape[0] // chunk, finish, 0)


def gate_up(h_full, go, gp, uo, upv, kb):
    tokens, kdim = h_full.shape
    ff = go.shape[1]
    wspec = pl.BlockSpec((kb, ff), lambda k: (k, 0))
    ospec = pl.BlockSpec((tokens, ff), lambda k: (0, 0))
    flops = 8 * tokens * kdim * ff
    nbytes = 2 * (tokens * kdim + 4 * kdim * ff + 2 * tokens * ff)
    return pl.pallas_call(
        gate_up_kernel,
        grid=(kdim // kb,),
        out_shape=(jax.ShapeDtypeStruct((tokens, ff), jnp.bfloat16),) * 2,
        in_specs=[pl.BlockSpec((tokens, kb), lambda k: (0, k))] + [wspec] * 4,
        out_specs=[ospec, ospec],
        scratch_shapes=[pltpu.VMEM((4, tokens, ff), jnp.float32),
                        pltpu.VMEM((2, kb, ff), jnp.bfloat16)],
        compiler_params=pltpu.CompilerParams(vmem_limit_bytes=48 * 1024 * 1024),
        cost_estimate=pl.CostEstimate(flops=flops, bytes_accessed=nbytes,
                                      transcendentals=2 * tokens * ff),
    )(h_full, go, gp, uo, upv)


def gate_up_online_kernel(h_ref, go_ref, uo_ref, pg_ref, pu_ref, io_ref, it_ref, acc):
    k = pl.program_id(0)
    tile = 256
    chunk = 64
    f32 = jnp.float32

    @pl.when(k == 0)
    def _():
        acc[...] = jnp.zeros_like(acc)

    def mm(i, carry):
        r = pl.ds(pl.multiple_of(i * tile, tile), tile)
        hs = h_ref[r, :]
        acc[0, r, :] += jnp.dot(hs, go_ref[...], preferred_element_type=f32)
        acc[1, r, :] += jnp.dot(hs, uo_ref[...], preferred_element_type=f32)
        return carry

    lax.fori_loop(0, h_ref.shape[0] // tile, mm, 0)

    @pl.when(k == pl.num_programs(0) - 1)
    def _():
        def finish(i, carry):
            r = pl.ds(pl.multiple_of(i * chunk, chunk), chunk)
            g_o = acc[0, r, :]
            u_o = acc[1, r, :]
            g_t = POLYAK * g_o + (1.0 - POLYAK) * pg_ref[r, :]
            u_t = POLYAK * u_o + (1.0 - POLYAK) * pu_ref[r, :]
            io_ref[r, :] = (jax.nn.silu(g_o) * u_o).astype(io_ref.dtype)
            it_ref[r, :] = (jax.nn.silu(g_t) * u_t).astype(it_ref.dtype)
            return carry

        lax.fori_loop(0, io_ref.shape[0] // chunk, finish, 0)


def gate_up_online(h_full, go, uo, pg, pu, kb):
    tokens, kdim = h_full.shape
    ff = go.shape[1]
    wspec = pl.BlockSpec((kb, ff), lambda k: (k, 0))
    ospec = pl.BlockSpec((tokens, ff), lambda k: (0, 0))
    return pl.pallas_call(
        gate_up_online_kernel,
        grid=(kdim // kb,),
        out_shape=(jax.ShapeDtypeStruct((tokens, ff), jnp.bfloat16),) * 2,
        in_specs=[pl.BlockSpec((tokens, kb), lambda k: (0, k)), wspec, wspec, ospec, ospec],
        out_specs=[ospec, ospec],
        scratch_shapes=[pltpu.VMEM((2, tokens, ff), jnp.float32)],
        compiler_params=pltpu.CompilerParams(vmem_limit_bytes=48 * 1024 * 1024),
        cost_estimate=pl.CostEstimate(flops=4 * tokens * kdim * ff,
                                      bytes_accessed=2 * (tokens * kdim + 2 * kdim * ff),
                                      transcendentals=2 * tokens * ff),
    )(h_full, go, uo, pg, pu)


def down_kernel(io_ref, it_ref, do_ref, dp_ref, oo_ref, ot_ref):
    f32 = jnp.float32
    wt = (POLYAK * do_ref[...].astype(f32)
          + (1.0 - POLYAK) * dp_ref[...].astype(f32)).astype(do_ref.dtype)
    oo_ref[...] = jnp.dot(io_ref[...], do_ref[...], preferred_element_type=f32).astype(oo_ref.dtype)
    ot_ref[...] = jnp.dot(it_ref[...], wt, preferred_element_type=f32).astype(ot_ref.dtype)


def down_products(inner_o, inner_t, down_full, down_previous, cb):
    tokens, ff = inner_o.shape
    width = down_full.shape[1]
    ispec = pl.BlockSpec((tokens, ff), lambda j: (0, 0))
    wspec = pl.BlockSpec((ff, cb), lambda j: (0, j))
    ospec = pl.BlockSpec((tokens, cb), lambda j: (0, j))
    return pl.pallas_call(
        down_kernel,
        grid=(width // cb,),
        out_shape=(jax.ShapeDtypeStruct((tokens, width), jnp.bfloat16),) * 2,
        in_specs=[ispec, ispec, wspec, wspec],
        out_specs=[ospec, ospec],
        compiler_params=pltpu.CompilerParams(vmem_limit_bytes=32 * 1024 * 1024),
        cost_estimate=pl.CostEstimate(flops=4 * tokens * ff * width,
                                      bytes_accessed=2 * (2 * tokens * ff + 2 * ff * width
                                                          + 2 * tokens * width),
                                      transcendentals=0),
    )(inner_o, inner_t, down_full, down_previous)


def local(ndp, nmp, hidden_states, gate_online, up_online, down_online, gate_previous,
          up_previous, down_previous):
    kb = 2 * gate_online.shape[0]
    if ndp == 8 and nmp == 16:
        _, _, _, down_full, inner_o, inner_t = gather_relay(
            hidden_states, gate_online, up_online, down_online, gate_previous, up_previous, ndp)
    else:
        features_all = lax.all_gather(hidden_states, "mp", axis=1, tiled=True)
        gate_full, up_full, down_full = gather_weights_direct(gate_online, up_online,
                                                              down_online, ndp)
        inner_o, inner_t = gate_up(features_all, gate_full, gate_previous, up_full, up_previous,
                                   kb)
    if nmp == 16:
        online_part, target_part = down_products(inner_o, inner_t, down_full, down_previous,
                                                 down_online.shape[1])
        result = split_reduce_scatter(online_part, target_part)
    else:
        target_down = blend(down_full, down_previous)
        online_part = jnp.dot(inner_o, down_full, preferred_element_type=jnp.float32)
        target_part = jnp.dot(inner_t, target_down, preferred_element_type=jnp.float32)
        terms = jnp.stack([online_part, target_part], axis=0).astype(jnp.bfloat16)
        result = reduce_scatter(terms, nmp)
    return (result[0], result[1])


def solution(mesh):
    ndp = mesh.shape["dp"]
    nmp = mesh.shape["mp"]
    in_specs = (
        P("dp", "mp"),
        P("dp", "mp"),
        P("dp", "mp"),
        P("mp", "dp"),
        P(None, "mp"),
        P(None, "mp"),
        P("mp", None),
    )
    out_specs = (P("dp", "mp"), P("dp", "mp"))
    return jax.shard_map(functools.partial(local, ndp, nmp), mesh=mesh, in_specs=in_specs,
                         out_specs=out_specs, check_vma=False)
```

```python
import functools

import jax
import jax.numpy as jnp
from jax import lax
from jax.experimental import pallas as pl
from jax.experimental.pallas import tpu as pltpu
from jax.sharding import PartitionSpec as P

POLYAK = 0.25
MESH = pl.DeviceIdType.MESH


def blend(online, previous):
    return (
        POLYAK * online.astype(jnp.float32) + (1.0 - POLYAK) * previous.astype(jnp.float32)
    ).astype(jnp.bfloat16)


def gather_kernel(ndp, g_ref, u_ref, dn_ref, gf_ref, uf_ref, df_ref, send_sem, recv_sem,
                  local_sem):
    d = lax.axis_index("dp")
    m = lax.axis_index("mp")
    kr = g_ref.shape[0]
    dc = dn_ref.shape[1]
    rows = pl.ds(pl.multiple_of(d * kr, kr), kr)
    cols = pl.ds(pl.multiple_of(d * dc, dc), dc)

    locals_ = [
        pltpu.make_async_copy(g_ref, gf_ref.at[rows], local_sem.at[0]),
        pltpu.make_async_copy(u_ref, uf_ref.at[rows], local_sem.at[1]),
        pltpu.make_async_copy(dn_ref, df_ref.at[:, cols], local_sem.at[2]),
    ]
    for c in locals_:
        c.start()

    copies = []
    k = 0
    for s in range(1, ndp):
        peer = lax.rem(d + s, ndp)
        for src, dst in ((g_ref, gf_ref.at[rows]), (u_ref, uf_ref.at[rows]),
                         (dn_ref, df_ref.at[:, cols])):
            copies.append(pltpu.make_async_remote_copy(
                src_ref=src, dst_ref=dst, send_sem=send_sem.at[k], recv_sem=recv_sem.at[k],
                device_id=(peer, m), device_id_type=MESH))
            k += 1
    for c in copies:
        c.start()
    for c in locals_:
        c.wait()
    for c in copies:
        c.wait()


def gather_weights_direct(g, u, dn, ndp):
    n_copies = 3 * (ndp - 1)
    any_spec = pl.BlockSpec(memory_space=pl.ANY)
    out_shape = (
        jax.ShapeDtypeStruct((g.shape[0] * ndp, g.shape[1]), g.dtype),
        jax.ShapeDtypeStruct((u.shape[0] * ndp, u.shape[1]), u.dtype),
        jax.ShapeDtypeStruct((dn.shape[0], dn.shape[1] * ndp), dn.dtype),
    )
    return pl.pallas_call(
        functools.partial(gather_kernel, ndp),
        out_shape=out_shape,
        in_specs=[any_spec] * 3,
        out_specs=[any_spec] * 3,
        scratch_shapes=[
            pltpu.SemaphoreType.DMA((n_copies,)),
            pltpu.SemaphoreType.DMA((n_copies,)),
            pltpu.SemaphoreType.DMA((3,)),
        ],
        compiler_params=pltpu.CompilerParams(has_side_effects=True),
    )(g, u, dn)


def relay_gather_kernel(h_ref, g_ref, u_ref, dn_ref, gp_ref, upv_ref, hf_ref, gf_ref, uf_ref,
                        df_ref, io_ref, it_ref, send_sem, recv_sem, local_sem, hsend, hrecv,
                        hv, wb, wsem, acc):
    ndp = 8
    d = lax.axis_index("dp")
    m = lax.axis_index("mp")
    lo = d % 2
    partner = d - lo + (1 - lo)
    nxt = (d + 2) % ndp
    prv = (d + ndp - 2) % ndp
    far = (d + 4) % ndp
    owns = (g_ref, u_ref, dn_ref)
    fulls = (gf_ref, uf_ref, df_ref)

    def slot(w, idx, half=None):
        if w < 2:
            kr = owns[w].shape[0]
            if half is None:
                return fulls[w].at[pl.ds(pl.multiple_of(idx * kr, kr), kr)]
            hk = kr // 2
            return fulls[w].at[pl.ds(pl.multiple_of(idx * kr + half * hk, hk), hk)]
        rr, dc = owns[w].shape
        cols = pl.ds(pl.multiple_of(idx * dc, dc), dc)
        if half is None:
            return fulls[w].at[:, cols]
        hr = rr // 2
        return fulls[w].at[pl.ds(half * hr, hr), cols]

    def rc(w, k, src, dst, target):
        i = w * 8 + k
        return pltpu.make_async_remote_copy(
            src_ref=src, dst_ref=dst, send_sem=send_sem.at[i], recv_sem=recv_sem.at[i],
            device_id=(target, m), device_id_type=MESH)

    locals_ = [pltpu.make_async_copy(owns[w], slot(w, d), local_sem.at[w]) for w in range(3)]
    c = {}
    for w in range(3):
        c[w, 0] = rc(w, 0, owns[w], slot(w, d), partner)
        c[w, 1] = rc(w, 1, owns[w], slot(w, d), nxt)
        c[w, 2] = rc(w, 2, owns[w], slot(w, d), prv)
        c[w, 3] = rc(w, 3, slot(w, partner), slot(w, partner), nxt)
        c[w, 4] = rc(w, 4, slot(w, partner), slot(w, partner), prv)
        c[w, 5] = rc(w, 5, slot(w, prv, 0), slot(w, prv, 0), nxt)
        c[w, 6] = rc(w, 6, slot(w, nxt, 1), slot(w, nxt, 1), prv)
        c[w, 7] = rc(w, 7, slot(w, far), slot(w, far), partner)
    nmp = 16
    hc = h_ref.shape[1]
    hmine = hf_ref.at[:, pl.ds(pl.multiple_of(m * hc, hc), hc)]
    hlocal = pltpu.make_async_copy(h_ref, hmine, local_sem.at[3])
    hcopies = []
    for s in range(1, nmp):
        hcopies.append(pltpu.make_async_remote_copy(
            src_ref=h_ref, dst_ref=hmine, send_sem=hsend.at[s - 1], recv_sem=hrecv.at[s - 1],
            device_id=(d, lax.rem(m + s, nmp)), device_id_type=MESH))
    for w in range(3):
        locals_[w].start()
        for k in range(3):
            c[w, k].start()
    hlocal.start()
    for cp in hcopies:
        cp.start()
    for w in range(3):
        c[w, 1].wait_recv()
        c[w, 5].start()
        c[w, 2].wait_recv()
        c[w, 6].start()
    for w in range(3):
        c[w, 5].wait_recv()
        c[w, 6].wait_recv()
        c[w, 7].start()
    for w in range(3):
        c[w, 0].wait_recv()
        c[w, 3].start()
        c[w, 4].start()

    hlocal.wait()
    for cp in hcopies:
        cp.wait_recv()
    for w in range(3):
        locals_[w].wait()
    hload = pltpu.make_async_copy(hf_ref, hv, wsem.at[2])
    hload.start()
    hload.wait()
    acc[...] = jnp.zeros_like(acc)
    kr = g_ref.shape[0]
    tile = 256

    def products(a_ref, b_ref, idx, first):
        rows = pl.ds(pl.multiple_of(idx * kr, kr), kr)
        la = pltpu.make_async_copy(a_ref.at[rows], wb.at[0], wsem.at[0])
        lb = pltpu.make_async_copy(b_ref.at[rows], wb.at[1], wsem.at[1])
        la.start()
        lb.start()
        la.wait()
        lb.wait()

        def mm(i, carry):
            r = pl.ds(pl.multiple_of(i * tile, tile), tile)
            hs = hv[r, rows]
            acc[first, r, :] += jnp.dot(hs, wb[0], preferred_element_type=jnp.float32)
            acc[first + 1, r, :] += jnp.dot(hs, wb[1], preferred_element_type=jnp.float32)
            return carry

        lax.fori_loop(0, hv.shape[0] // tile, mm, 0)

    def prev_slot(i, carry):
        products(gp_ref, upv_ref, i, 2)
        return carry

    lax.fori_loop(0, ndp, prev_slot, 0)
    for idx in (d, partner, prv, nxt, far):
        products(gf_ref, uf_ref, idx, 0)

    for w in range(3):
        c[w, 7].wait_recv()
    products(gf_ref, uf_ref, (partner + 4) % ndp, 0)
    for w in range(3):
        c[w, 3].wait_recv()
        c[w, 4].wait_recv()
    for idx in ((partner + 2) % ndp, (partner + ndp - 2) % ndp):
        products(gf_ref, uf_ref, idx, 0)

    chunk = 64

    def finish(i, carry):
        r = pl.ds(pl.multiple_of(i * chunk, chunk), chunk)
        g_o = acc[0, r, :]
        u_o = acc[1, r, :]
        g_t = POLYAK * g_o + (1.0 - POLYAK) * acc[2, r, :]
        u_t = POLYAK * u_o + (1.0 - POLYAK) * acc[3, r, :]
        io_ref[r, :] = (jax.nn.silu(g_o) * u_o).astype(io_ref.dtype)
        it_ref[r, :] = (jax.nn.silu(g_t) * u_t).astype(it_ref.dtype)
        return carry

    lax.fori_loop(0, io_ref.shape[0] // chunk, finish, 0)
    for w in range(3):
        for k in range(8):
            c[w, k].wait_send()
    for cp in hcopies:
        cp.wait_send()


def gather_relay(h, g, u, dn, gp, upv, ndp):
    any_spec = pl.BlockSpec(memory_space=pl.ANY)
    out_shape = (
        jax.ShapeDtypeStruct((g.shape[0] * ndp, g.shape[1]), g.dtype),
        jax.ShapeDtypeStruct((u.shape[0] * ndp, u.shape[1]), u.dtype),
        jax.ShapeDtypeStruct((dn.shape[0], dn.shape[1] * ndp), dn.dtype),
    )
    tokens, ff = h.shape[0], g.shape[1]
    prod = jax.ShapeDtypeStruct((tokens, ff), jnp.bfloat16)
    vspec = pl.BlockSpec(memory_space=pltpu.VMEM)
    return pl.pallas_call(
        relay_gather_kernel,
        out_shape=(jax.ShapeDtypeStruct((tokens, h.shape[1] * 16), h.dtype),) + out_shape
        + (prod, prod),
        in_specs=[any_spec] * 6,
        out_specs=[any_spec] * 4 + [vspec] * 2,
        scratch_shapes=[
            pltpu.SemaphoreType.DMA((24,)),
            pltpu.SemaphoreType.DMA((24,)),
            pltpu.SemaphoreType.DMA((4,)),
            pltpu.SemaphoreType.DMA((15,)),
            pltpu.SemaphoreType.DMA((15,)),
            pltpu.VMEM((tokens, h.shape[1] * 16), h.dtype),
            pltpu.VMEM((2, g.shape[0], ff), g.dtype),
            pltpu.SemaphoreType.DMA((3,)),
            pltpu.VMEM((4, tokens, ff), jnp.float32),
        ],
        compiler_params=pltpu.CompilerParams(has_side_effects=True,
                                             vmem_limit_bytes=48 * 1024 * 1024),
    )(h, g, u, dn, gp, upv)


def reduce_kernel(nmp, t_ref, o_ref, buf, send_sem, recv_sem, local_sem):
    d = lax.axis_index("dp")
    m = lax.axis_index("mp")
    w = o_ref.shape[2]
    mine = pl.ds(pl.multiple_of(m * w, w), w)
    local_copy = pltpu.make_async_copy(t_ref.at[:, :, mine], buf.at[0], local_sem.at[0])
    local_copy.start()
    copies = []
    for s in range(1, nmp):
        peer = lax.rem(m + s, nmp)
        theirs = pl.ds(pl.multiple_of(peer * w, w), w)
        copies.append(pltpu.make_async_remote_copy(
            src_ref=t_ref.at[:, :, theirs], dst_ref=buf.at[s], send_sem=send_sem.at[s],
            recv_sem=recv_sem.at[s], device_id=(d, peer), device_id_type=MESH))
    for c in copies:
        c.start()
    local_copy.wait()
    for c in copies:
        c.wait()
    rows = 32

    def body(i, carry):
        r = pl.ds(pl.multiple_of(i * rows, rows), rows)
        for k in range(o_ref.shape[0]):
            acc = buf[0, k, r, :].astype(jnp.float32)
            for s in range(1, nmp):
                acc = acc + buf[s, k, r, :].astype(jnp.float32)
            o_ref[k, r, :] = acc.astype(o_ref.dtype)
        return carry

    lax.fori_loop(0, o_ref.shape[1] // rows, body, 0)


def reduce_scatter(terms, nmp):
    n, t, width = terms.shape
    w = width // nmp
    return pl.pallas_call(
        functools.partial(reduce_kernel, nmp),
        out_shape=jax.ShapeDtypeStruct((n, t, w), jnp.bfloat16),
        in_specs=[pl.BlockSpec(memory_space=pl.ANY)],
        out_specs=pl.BlockSpec(memory_space=pltpu.VMEM),
        scratch_shapes=[
            pltpu.VMEM((nmp, n, t, w), jnp.bfloat16),
            pltpu.SemaphoreType.DMA((nmp,)),
            pltpu.SemaphoreType.DMA((nmp,)),
            pltpu.SemaphoreType.DMA((1,)),
        ],
        compiler_params=pltpu.CompilerParams(has_side_effects=True,
                                             vmem_limit_bytes=48 * 1024 * 1024),
    )(terms)


def hier_reduce_kernel(ta_ref, tb_ref, o_ref, own, r1, sb2, r2, s2, sb3, r3,
                       ls, ss1, rs1, ss2, rs2, ss3, rs3):
    d = lax.axis_index("dp")
    m = lax.axis_index("mp")
    c = m % 2
    z = (m // 2) % 4
    xh = m // 8
    w = o_ref.shape[2]
    rows = 32
    nchunk = o_ref.shape[1] // rows

    def blk(b, k):
        return (ta_ref, tb_ref)[k].at[:, pl.ds(pl.multiple_of(b * w, w), w)]

    def dev(mm):
        return (d, mm)

    locs = []
    st1 = []
    for j in range(16):
        bx, bz, k = j // 8, (j // 2) % 4, j % 2
        jj = bx * 4 + bz
        locs.append(pltpu.make_async_copy(blk(bx * 8 + bz * 2 + c, k), own.at[jj, k],
                                          ls.at[j]))
        st1.append(pltpu.make_async_remote_copy(
            src_ref=blk(bx * 8 + bz * 2 + (1 - c), k), dst_ref=r1.at[jj, k], send_sem=ss1.at[j],
            recv_sem=rs1.at[j], device_id=dev(m + 1 - 2 * c), device_id_type=MESH))
    for j in range(16):
        st1[j].start()
        locs[j].start()
    for j in range(16):
        locs[j].wait()
        st1[j].wait()

    st2 = []
    for s in range(1, 4):
        zt = (z + s) % 4

        def fill(i, carry, s=s, zt=zt):
            r = pl.ds(pl.multiple_of(i * rows, rows), rows)
            for bx in range(2):
                idx = bx * 4 + zt
                sb2[s - 1, bx, :, r, :] = (own[idx, :, r, :].astype(jnp.float32)
                                           + r1[idx, :, r, :].astype(jnp.float32)
                                           ).astype(sb2.dtype)
            return carry

        lax.fori_loop(0, nchunk, fill, 0)
        cp = pltpu.make_async_remote_copy(
            src_ref=sb2.at[s - 1], dst_ref=r2.at[s - 1], send_sem=ss2.at[s - 1],
            recv_sem=rs2.at[s - 1], device_id=dev(xh * 8 + zt * 2 + c), device_id_type=MESH)
        cp.start()
        st2.append(cp)
    for cp in st2:
        cp.wait()

    def sum2(i, carry):
        r = pl.ds(pl.multiple_of(i * rows, rows), rows)
        for bx in range(2):
            idx = bx * 4 + z
            acc = own[idx, :, r, :].astype(jnp.float32) + r1[idx, :, r, :].astype(jnp.float32)
            for k in range(3):
                acc = acc + r2[k, bx, :, r, :].astype(jnp.float32)
            s2[bx, :, r, :] = acc
        return carry

    lax.fori_loop(0, nchunk, sum2, 0)
    sb3[...] = s2[1 - xh].astype(sb3.dtype)
    cp3 = pltpu.make_async_remote_copy(
        src_ref=sb3, dst_ref=r3, send_sem=ss3.at[0], recv_sem=rs3.at[0],
        device_id=dev(m + 8 - 16 * xh), device_id_type=MESH)
    cp3.start()
    cp3.wait()
    o_ref[...] = (s2[xh] + r3[...].astype(jnp.float32)).astype(o_ref.dtype)


def hier_reduce_scatter(ta, tb):
    n = 2
    t, width = ta.shape
    w = width // 16
    bf = jnp.bfloat16
    dma = pltpu.SemaphoreType.DMA
    return pl.pallas_call(
        hier_reduce_kernel,
        out_shape=jax.ShapeDtypeStruct((n, t, w), bf),
        in_specs=[pl.BlockSpec(memory_space=pl.ANY)] * 2,
        out_specs=pl.BlockSpec(memory_space=pltpu.VMEM),
        scratch_shapes=[
            pltpu.VMEM((8, n, t, w), bf),
            pltpu.VMEM((8, n, t, w), bf),
            pltpu.VMEM((3, 2, n, t, w), bf),
            pltpu.VMEM((3, 2, n, t, w), bf),
            pltpu.VMEM((2, n, t, w), jnp.float32),
            pltpu.VMEM((n, t, w), bf),
            pltpu.VMEM((n, t, w), bf),
            dma((16,)), dma((16,)), dma((16,)), dma((3,)), dma((3,)), dma((1,)), dma((1,)),
        ],
        compiler_params=pltpu.CompilerParams(has_side_effects=True,
                                             vmem_limit_bytes=56 * 1024 * 1024),
    )(ta, tb)


def split_reduce_kernel(ta_ref, tb_ref, o_ref, own, r1, sa2, ra2, fa2, sa3, ra3,
                        sb2, rb2, fb2, sb3, rb3, ls, ss1, rs1, ssa2, rsa2, ssa3, rsa3,
                        ssb2, rsb2, ssb3, rsb3):
    d = lax.axis_index("dp")
    m = lax.axis_index("mp")
    c = m % 2
    z = (m // 2) % 4
    xh = m // 8
    w = o_ref.shape[2]
    half = o_ref.shape[1] // 2
    ra = pl.ds(0, half)
    rb = pl.ds(half, half)
    rows = 32
    nchunk = half // rows
    f32 = jnp.float32
    xpeer = m + 8 - 16 * xh

    def blk(b, k):
        return (ta_ref, tb_ref)[k].at[:, pl.ds(pl.multiple_of(b * w, w), w)]

    def rcopy(src, dst, ss, rs, mm):
        return pltpu.make_async_remote_copy(src_ref=src, dst_ref=dst, send_sem=ss, recv_sem=rs,
                                            device_id=(d, mm), device_id_type=MESH)

    locs = []
    st1 = []
    for j in range(16):
        bx, bz, k = j // 8, (j // 2) % 4, j % 2
        jj = bx * 4 + bz
        locs.append(pltpu.make_async_copy(blk(bx * 8 + bz * 2 + c, k), own.at[jj, k],
                                          ls.at[j]))
        st1.append(rcopy(blk(bx * 8 + bz * 2 + (1 - c), k), r1.at[jj, k], ss1.at[j], rs1.at[j],
                         m + 1 - 2 * c))
    for j in range(16):
        st1[j].start()
        locs[j].start()
    for j in range(16):
        locs[j].wait()
        st1[j].wait()

    def pair_sum(idx, r):
        return own[idx, :, r, :].astype(f32) + r1[idx, :, r, :].astype(f32)

    def fill_b2(i, carry):
        r = pl.ds(pl.multiple_of(half + i * rows, rows), rows)
        q = pl.ds(pl.multiple_of(i * rows, rows), rows)
        for bz in range(4):
            sb2[bz, :, q, :] = pair_sum((1 - xh) * 4 + bz, r).astype(sb2.dtype)
        return carry

    lax.fori_loop(0, nchunk, fill_b2, 0)
    cb2 = rcopy(sb2, rb2, ssb2.at[0], rsb2.at[0], xpeer)
    cb2.start()
    ca2 = []
    for s in range(1, 4):
        zt = (z + s) % 4

        def fill_a2(i, carry, s=s, zt=zt):
            q = pl.ds(pl.multiple_of(i * rows, rows), rows)
            for bx in range(2):
                sa2[s - 1, bx, :, q, :] = pair_sum(bx * 4 + zt, q).astype(sa2.dtype)
            return carry

        lax.fori_loop(0, nchunk, fill_a2, 0)
        cp = rcopy(sa2.at[s - 1], ra2.at[s - 1], ssa2.at[s - 1], rsa2.at[s - 1],
                   xh * 8 + zt * 2 + c)
        cp.start()
        ca2.append(cp)

    cb2.wait()

    def sum_b2(i, carry):
        r = pl.ds(pl.multiple_of(half + i * rows, rows), rows)
        q = pl.ds(pl.multiple_of(i * rows, rows), rows)
        for bz in range(4):
            fb2[bz, :, q, :] = pair_sum(xh * 4 + bz, r) + rb2[bz, :, q, :].astype(f32)
        return carry

    lax.fori_loop(0, nchunk, sum_b2, 0)
    cb3 = []
    for s in range(1, 4):
        zt = (z + s) % 4
        sb3[s - 1] = fb2[zt].astype(sb3.dtype)
        cp = rcopy(sb3.at[s - 1], rb3.at[s - 1], ssb3.at[s - 1], rsb3.at[s - 1],
                   xh * 8 + zt * 2 + c)
        cp.start()
        cb3.append(cp)

    for cp in ca2:
        cp.wait()

    def sum_a2(i, carry):
        q = pl.ds(pl.multiple_of(i * rows, rows), rows)
        for bx in range(2):
            acc = pair_sum(bx * 4 + z, q)
            for k in range(3):
                acc = acc + ra2[k, bx, :, q, :].astype(f32)
            fa2[bx, :, q, :] = acc
        return carry

    lax.fori_loop(0, nchunk, sum_a2, 0)
    sa3[...] = fa2[1 - xh].astype(sa3.dtype)
    ca3 = rcopy(sa3, ra3, ssa3.at[0], rsa3.at[0], xpeer)
    ca3.start()
    for cp in cb3:
        cp.wait()
    acc = fb2[z]
    for k in range(3):
        acc = acc + rb3[k].astype(f32)
    o_ref[:, rb, :] = acc.astype(o_ref.dtype)
    ca3.wait()
    o_ref[:, ra, :] = (fa2[xh] + ra3[...].astype(f32)).astype(o_ref.dtype)


def split_reduce_scatter(ta, tb):
    n = 2
    t, width = ta.shape
    w = width // 16
    h = t // 2
    bf = jnp.bfloat16
    f32 = jnp.float32
    dma = pltpu.SemaphoreType.DMA
    return pl.pallas_call(
        split_reduce_kernel,
        out_shape=jax.ShapeDtypeStruct((n, t, w), bf),
        in_specs=[pl.BlockSpec(memory_space=pl.ANY)] * 2,
        out_specs=pl.BlockSpec(memory_space=pltpu.VMEM),
        scratch_shapes=[
            pltpu.VMEM((8, n, t, w), bf),
            pltpu.VMEM((8, n, t, w), bf),
            pltpu.VMEM((3, 2, n, h, w), bf),
            pltpu.VMEM((3, 2, n, h, w), bf),
            pltpu.VMEM((2, n, h, w), f32),
            pltpu.VMEM((n, h, w), bf),
            pltpu.VMEM((n, h, w), bf),
            pltpu.VMEM((4, n, h, w), bf),
            pltpu.VMEM((4, n, h, w), bf),
            pltpu.VMEM((4, n, h, w), f32),
            pltpu.VMEM((3, n, h, w), bf),
            pltpu.VMEM((3, n, h, w), bf),
            dma((16,)), dma((16,)), dma((16,)),
            dma((3,)), dma((3,)), dma((1,)), dma((1,)),
            dma((1,)), dma((1,)), dma((3,)), dma((3,)),
        ],
        compiler_params=pltpu.CompilerParams(has_side_effects=True,
                                             vmem_limit_bytes=56 * 1024 * 1024),
    )(ta, tb)


def gate_up_kernel(h_ref, go_ref, gp_ref, uo_ref, upv_ref, io_ref, it_ref, acc, tbuf):
    k = pl.program_id(0)
    tile = 256
    chunk = 64
    f32 = jnp.float32

    @pl.when(k == 0)
    def _():
        acc[...] = jnp.zeros_like(acc)

    def mix(i, carry):
        r = pl.ds(pl.multiple_of(i * chunk, chunk), chunk)
        for j, (on_ref, pv_ref) in enumerate(((go_ref, gp_ref), (uo_ref, upv_ref))):
            on = on_ref[r, :].astype(f32)
            pv = pv_ref[r, :].astype(f32)
            tbuf[j, r, :] = (POLYAK * on + (1.0 - POLYAK) * pv).astype(tbuf.dtype)
        return carry

    lax.fori_loop(0, go_ref.shape[0] // chunk, mix, 0)

    def mm(i, carry):
        r = pl.ds(pl.multiple_of(i * tile, tile), tile)
        hs = h_ref[r, :]
        acc[0, r, :] += jnp.dot(hs, go_ref[...], preferred_element_type=f32)
        acc[1, r, :] += jnp.dot(hs, tbuf[0], preferred_element_type=f32)
        acc[2, r, :] += jnp.dot(hs, uo_ref[...], preferred_element_type=f32)
        acc[3, r, :] += jnp.dot(hs, tbuf[1], preferred_element_type=f32)
        return carry

    lax.fori_loop(0, h_ref.shape[0] // tile, mm, 0)

    @pl.when(k == pl.num_programs(0) - 1)
    def _():
        def finish(i, carry):
            r = pl.ds(pl.multiple_of(i * chunk, chunk), chunk)
            io_ref[r, :] = (jax.nn.silu(acc[0, r, :]) * acc[2, r, :]).astype(io_ref.dtype)
            it_ref[r, :] = (jax.nn.silu(acc[1, r, :]) * acc[3, r, :]).astype(it_ref.dtype)
            return carry

        lax.fori_loop(0, io_ref.shape[0] // chunk, finish, 0)


def gate_up(h_full, go, gp, uo, upv, kb):
    tokens, kdim = h_full.shape
    ff = go.shape[1]
    wspec = pl.BlockSpec((kb, ff), lambda k: (k, 0))
    ospec = pl.BlockSpec((tokens, ff), lambda k: (0, 0))
    flops = 8 * tokens * kdim * ff
    nbytes = 2 * (tokens * kdim + 4 * kdim * ff + 2 * tokens * ff)
    return pl.pallas_call(
        gate_up_kernel,
        grid=(kdim // kb,),
        out_shape=(jax.ShapeDtypeStruct((tokens, ff), jnp.bfloat16),) * 2,
        in_specs=[pl.BlockSpec((tokens, kb), lambda k: (0, k))] + [wspec] * 4,
        out_specs=[ospec, ospec],
        scratch_shapes=[pltpu.VMEM((4, tokens, ff), jnp.float32),
                        pltpu.VMEM((2, kb, ff), jnp.bfloat16)],
        compiler_params=pltpu.CompilerParams(vmem_limit_bytes=48 * 1024 * 1024),
        cost_estimate=pl.CostEstimate(flops=flops, bytes_accessed=nbytes,
                                      transcendentals=2 * tokens * ff),
    )(h_full, go, gp, uo, upv)


def gate_up_online_kernel(h_ref, go_ref, uo_ref, pg_ref, pu_ref, io_ref, it_ref, acc):
    k = pl.program_id(0)
    tile = 256
    chunk = 64
    f32 = jnp.float32

    @pl.when(k == 0)
    def _():
        acc[...] = jnp.zeros_like(acc)

    def mm(i, carry):
        r = pl.ds(pl.multiple_of(i * tile, tile), tile)
        hs = h_ref[r, :]
        acc[0, r, :] += jnp.dot(hs, go_ref[...], preferred_element_type=f32)
        acc[1, r, :] += jnp.dot(hs, uo_ref[...], preferred_element_type=f32)
        return carry

    lax.fori_loop(0, h_ref.shape[0] // tile, mm, 0)

    @pl.when(k == pl.num_programs(0) - 1)
    def _():
        def finish(i, carry):
            r = pl.ds(pl.multiple_of(i * chunk, chunk), chunk)
            g_o = acc[0, r, :]
            u_o = acc[1, r, :]
            g_t = POLYAK * g_o + (1.0 - POLYAK) * pg_ref[r, :]
            u_t = POLYAK * u_o + (1.0 - POLYAK) * pu_ref[r, :]
            io_ref[r, :] = (jax.nn.silu(g_o) * u_o).astype(io_ref.dtype)
            it_ref[r, :] = (jax.nn.silu(g_t) * u_t).astype(it_ref.dtype)
            return carry

        lax.fori_loop(0, io_ref.shape[0] // chunk, finish, 0)


def gate_up_online(h_full, go, uo, pg, pu, kb):
    tokens, kdim = h_full.shape
    ff = go.shape[1]
    wspec = pl.BlockSpec((kb, ff), lambda k: (k, 0))
    ospec = pl.BlockSpec((tokens, ff), lambda k: (0, 0))
    return pl.pallas_call(
        gate_up_online_kernel,
        grid=(kdim // kb,),
        out_shape=(jax.ShapeDtypeStruct((tokens, ff), jnp.bfloat16),) * 2,
        in_specs=[pl.BlockSpec((tokens, kb), lambda k: (0, k)), wspec, wspec, ospec, ospec],
        out_specs=[ospec, ospec],
        scratch_shapes=[pltpu.VMEM((2, tokens, ff), jnp.float32)],
        compiler_params=pltpu.CompilerParams(vmem_limit_bytes=48 * 1024 * 1024),
        cost_estimate=pl.CostEstimate(flops=4 * tokens * kdim * ff,
                                      bytes_accessed=2 * (tokens * kdim + 2 * kdim * ff),
                                      transcendentals=2 * tokens * ff),
    )(h_full, go, uo, pg, pu)


def down_kernel(io_ref, it_ref, do_ref, dp_ref, oo_ref, ot_ref):
    f32 = jnp.float32
    wt = (POLYAK * do_ref[...].astype(f32)
          + (1.0 - POLYAK) * dp_ref[...].astype(f32)).astype(do_ref.dtype)
    oo_ref[...] = jnp.dot(io_ref[...], do_ref[...], preferred_element_type=f32).astype(oo_ref.dtype)
    ot_ref[...] = jnp.dot(it_ref[...], wt, preferred_element_type=f32).astype(ot_ref.dtype)


def down_products(inner_o, inner_t, down_full, down_previous, cb):
    tokens, ff = inner_o.shape
    width = down_full.shape[1]
    ispec = pl.BlockSpec((tokens, ff), lambda j: (0, 0))
    wspec = pl.BlockSpec((ff, cb), lambda j: (0, j))
    ospec = pl.BlockSpec((tokens, cb), lambda j: (0, j))
    return pl.pallas_call(
        down_kernel,
        grid=(width // cb,),
        out_shape=(jax.ShapeDtypeStruct((tokens, width), jnp.bfloat16),) * 2,
        in_specs=[ispec, ispec, wspec, wspec],
        out_specs=[ospec, ospec],
        compiler_params=pltpu.CompilerParams(vmem_limit_bytes=32 * 1024 * 1024),
        cost_estimate=pl.CostEstimate(flops=4 * tokens * ff * width,
                                      bytes_accessed=2 * (2 * tokens * ff + 2 * ff * width
                                                          + 2 * tokens * width),
                                      transcendentals=0),
    )(inner_o, inner_t, down_full, down_previous)


def local(ndp, nmp, hidden_states, gate_online, up_online, down_online, gate_previous,
          up_previous, down_previous):
    kb = 2 * gate_online.shape[0]
    if ndp == 8 and nmp == 16:
        _, _, _, down_full, inner_o, inner_t = gather_relay(
            hidden_states, gate_online, up_online, down_online, gate_previous, up_previous, ndp)
    else:
        features_all = lax.all_gather(hidden_states, "mp", axis=1, tiled=True)
        gate_full, up_full, down_full = gather_weights_direct(gate_online, up_online,
                                                              down_online, ndp)
        inner_o, inner_t = gate_up(features_all, gate_full, gate_previous, up_full, up_previous,
                                   kb)
    if nmp == 16:
        online_part, target_part = down_products(inner_o, inner_t, down_full, down_previous,
                                                 2 * down_online.shape[1])
        result = split_reduce_scatter(online_part, target_part)
    else:
        target_down = blend(down_full, down_previous)
        online_part = jnp.dot(inner_o, down_full, preferred_element_type=jnp.float32)
        target_part = jnp.dot(inner_t, target_down, preferred_element_type=jnp.float32)
        terms = jnp.stack([online_part, target_part], axis=0).astype(jnp.bfloat16)
        result = reduce_scatter(terms, nmp)
    return (result[0], result[1])


def solution(mesh):
    ndp = mesh.shape["dp"]
    nmp = mesh.shape["mp"]
    in_specs = (
        P("dp", "mp"),
        P("dp", "mp"),
        P("dp", "mp"),
        P("mp", "dp"),
        P(None, "mp"),
        P(None, "mp"),
        P("mp", None),
    )
    out_specs = (P("dp", "mp"), P("dp", "mp"))
    return jax.shard_map(functools.partial(local, ndp, nmp), mesh=mesh, in_specs=in_specs,
                         out_specs=out_specs, check_vma=False)
```

```python
import functools

import jax
import jax.numpy as jnp
from jax import lax
from jax.experimental import pallas as pl
from jax.experimental.pallas import tpu as pltpu
from jax.sharding import PartitionSpec as P

POLYAK = 0.25
MESH = pl.DeviceIdType.MESH


def blend(online, previous):
    return (
        POLYAK * online.astype(jnp.float32) + (1.0 - POLYAK) * previous.astype(jnp.float32)
    ).astype(jnp.bfloat16)


def gather_kernel(ndp, g_ref, u_ref, dn_ref, gf_ref, uf_ref, df_ref, send_sem, recv_sem,
                  local_sem):
    d = lax.axis_index("dp")
    m = lax.axis_index("mp")
    kr = g_ref.shape[0]
    dc = dn_ref.shape[1]
    rows = pl.ds(pl.multiple_of(d * kr, kr), kr)
    cols = pl.ds(pl.multiple_of(d * dc, dc), dc)

    locals_ = [
        pltpu.make_async_copy(g_ref, gf_ref.at[rows], local_sem.at[0]),
        pltpu.make_async_copy(u_ref, uf_ref.at[rows], local_sem.at[1]),
        pltpu.make_async_copy(dn_ref, df_ref.at[:, cols], local_sem.at[2]),
    ]
    for c in locals_:
        c.start()

    copies = []
    k = 0
    for s in range(1, ndp):
        peer = lax.rem(d + s, ndp)
        for src, dst in ((g_ref, gf_ref.at[rows]), (u_ref, uf_ref.at[rows]),
                         (dn_ref, df_ref.at[:, cols])):
            copies.append(pltpu.make_async_remote_copy(
                src_ref=src, dst_ref=dst, send_sem=send_sem.at[k], recv_sem=recv_sem.at[k],
                device_id=(peer, m), device_id_type=MESH))
            k += 1
    for c in copies:
        c.start()
    for c in locals_:
        c.wait()
    for c in copies:
        c.wait()


def gather_weights_direct(g, u, dn, ndp):
    n_copies = 3 * (ndp - 1)
    any_spec = pl.BlockSpec(memory_space=pl.ANY)
    out_shape = (
        jax.ShapeDtypeStruct((g.shape[0] * ndp, g.shape[1]), g.dtype),
        jax.ShapeDtypeStruct((u.shape[0] * ndp, u.shape[1]), u.dtype),
        jax.ShapeDtypeStruct((dn.shape[0], dn.shape[1] * ndp), dn.dtype),
    )
    return pl.pallas_call(
        functools.partial(gather_kernel, ndp),
        out_shape=out_shape,
        in_specs=[any_spec] * 3,
        out_specs=[any_spec] * 3,
        scratch_shapes=[
            pltpu.SemaphoreType.DMA((n_copies,)),
            pltpu.SemaphoreType.DMA((n_copies,)),
            pltpu.SemaphoreType.DMA((3,)),
        ],
        compiler_params=pltpu.CompilerParams(has_side_effects=True),
    )(g, u, dn)


def relay_gather_kernel(h_ref, g_ref, u_ref, dn_ref, gp_ref, upv_ref, hf_ref, gf_ref, uf_ref,
                        df_ref, io_ref, it_ref, send_sem, recv_sem, local_sem, hsend, hrecv,
                        hv, wb, wsem, acc):
    ndp = 8
    d = lax.axis_index("dp")
    m = lax.axis_index("mp")
    lo = d % 2
    partner = d - lo + (1 - lo)
    nxt = (d + 2) % ndp
    prv = (d + ndp - 2) % ndp
    far = (d + 4) % ndp
    owns = (g_ref, u_ref, dn_ref)
    fulls = (gf_ref, uf_ref, df_ref)

    def slot(w, idx, half=None):
        if w < 2:
            kr = owns[w].shape[0]
            if half is None:
                return fulls[w].at[pl.ds(pl.multiple_of(idx * kr, kr), kr)]
            hk = kr // 2
            return fulls[w].at[pl.ds(pl.multiple_of(idx * kr + half * hk, hk), hk)]
        rr, dc = owns[w].shape
        cols = pl.ds(pl.multiple_of(idx * dc, dc), dc)
        if half is None:
            return fulls[w].at[:, cols]
        hr = rr // 2
        return fulls[w].at[pl.ds(half * hr, hr), cols]

    def rc(w, k, src, dst, target):
        i = w * 8 + k
        return pltpu.make_async_remote_copy(
            src_ref=src, dst_ref=dst, send_sem=send_sem.at[i], recv_sem=recv_sem.at[i],
            device_id=(target, m), device_id_type=MESH)

    locals_ = [pltpu.make_async_copy(owns[w], slot(w, d), local_sem.at[w]) for w in range(3)]
    c = {}
    for w in range(3):
        c[w, 0] = rc(w, 0, owns[w], slot(w, d), partner)
        c[w, 1] = rc(w, 1, owns[w], slot(w, d), nxt)
        c[w, 2] = rc(w, 2, owns[w], slot(w, d), prv)
        c[w, 3] = rc(w, 3, slot(w, partner), slot(w, partner), nxt)
        c[w, 4] = rc(w, 4, slot(w, partner), slot(w, partner), prv)
        c[w, 5] = rc(w, 5, slot(w, prv, 0), slot(w, prv, 0), nxt)
        c[w, 6] = rc(w, 6, slot(w, nxt, 1), slot(w, nxt, 1), prv)
        c[w, 7] = rc(w, 7, slot(w, far), slot(w, far), partner)
    nmp = 16
    hc = h_ref.shape[1]
    hmine = hf_ref.at[:, pl.ds(pl.multiple_of(m * hc, hc), hc)]
    hlocal = pltpu.make_async_copy(h_ref, hmine, local_sem.at[3])
    hcopies = []
    for s in range(1, nmp):
        hcopies.append(pltpu.make_async_remote_copy(
            src_ref=h_ref, dst_ref=hmine, send_sem=hsend.at[s - 1], recv_sem=hrecv.at[s - 1],
            device_id=(d, lax.rem(m + s, nmp)), device_id_type=MESH))
    for w in range(3):
        locals_[w].start()
        for k in range(3):
            c[w, k].start()
    hlocal.start()
    for cp in hcopies:
        cp.start()
    for w in range(3):
        c[w, 1].wait_recv()
        c[w, 5].start()
        c[w, 2].wait_recv()
        c[w, 6].start()
    for w in range(3):
        c[w, 5].wait_recv()
        c[w, 6].wait_recv()
        c[w, 7].start()
    for w in range(3):
        c[w, 0].wait_recv()
        c[w, 3].start()
        c[w, 4].start()

    hlocal.wait()
    for cp in hcopies:
        cp.wait_recv()
    for w in range(3):
        locals_[w].wait()
    hload = pltpu.make_async_copy(hf_ref, hv, wsem.at[2])
    hload.start()
    hload.wait()
    acc[...] = jnp.zeros_like(acc)
    kr = g_ref.shape[0]
    tile = 512

    def products(a_ref, b_ref, idx, first):
        rows = pl.ds(pl.multiple_of(idx * kr, kr), kr)
        la = pltpu.make_async_copy(a_ref.at[rows], wb.at[0], wsem.at[0])
        lb = pltpu.make_async_copy(b_ref.at[rows], wb.at[1], wsem.at[1])
        la.start()
        lb.start()
        la.wait()
        lb.wait()

        def mm(i, carry):
            r = pl.ds(pl.multiple_of(i * tile, tile), tile)
            hs = hv[r, rows]
            acc[first, r, :] += jnp.dot(hs, wb[0], preferred_element_type=jnp.float32)
            acc[first + 1, r, :] += jnp.dot(hs, wb[1], preferred_element_type=jnp.float32)
            return carry

        lax.fori_loop(0, hv.shape[0] // tile, mm, 0)

    def prev_slot(i, carry):
        products(gp_ref, upv_ref, i, 2)
        return carry

    lax.fori_loop(0, ndp, prev_slot, 0)
    for idx in (d, partner, prv, nxt, far):
        products(gf_ref, uf_ref, idx, 0)

    for w in range(3):
        c[w, 7].wait_recv()
    products(gf_ref, uf_ref, (partner + 4) % ndp, 0)
    for w in range(3):
        c[w, 3].wait_recv()
        c[w, 4].wait_recv()
    for idx in ((partner + 2) % ndp, (partner + ndp - 2) % ndp):
        products(gf_ref, uf_ref, idx, 0)

    chunk = 64

    def finish(i, carry):
        r = pl.ds(pl.multiple_of(i * chunk, chunk), chunk)
        g_o = acc[0, r, :]
        u_o = acc[1, r, :]
        g_t = POLYAK * g_o + (1.0 - POLYAK) * acc[2, r, :]
        u_t = POLYAK * u_o + (1.0 - POLYAK) * acc[3, r, :]
        io_ref[r, :] = (jax.nn.silu(g_o) * u_o).astype(io_ref.dtype)
        it_ref[r, :] = (jax.nn.silu(g_t) * u_t).astype(it_ref.dtype)
        return carry

    lax.fori_loop(0, io_ref.shape[0] // chunk, finish, 0)
    for w in range(3):
        for k in range(8):
            c[w, k].wait_send()
    for cp in hcopies:
        cp.wait_send()


def gather_relay(h, g, u, dn, gp, upv, ndp):
    any_spec = pl.BlockSpec(memory_space=pl.ANY)
    out_shape = (
        jax.ShapeDtypeStruct((g.shape[0] * ndp, g.shape[1]), g.dtype),
        jax.ShapeDtypeStruct((u.shape[0] * ndp, u.shape[1]), u.dtype),
        jax.ShapeDtypeStruct((dn.shape[0], dn.shape[1] * ndp), dn.dtype),
    )
    tokens, ff = h.shape[0], g.shape[1]
    prod = jax.ShapeDtypeStruct((tokens, ff), jnp.bfloat16)
    vspec = pl.BlockSpec(memory_space=pltpu.VMEM)
    return pl.pallas_call(
        relay_gather_kernel,
        out_shape=(jax.ShapeDtypeStruct((tokens, h.shape[1] * 16), h.dtype),) + out_shape
        + (prod, prod),
        in_specs=[any_spec] * 6,
        out_specs=[any_spec] * 4 + [vspec] * 2,
        scratch_shapes=[
            pltpu.SemaphoreType.DMA((24,)),
            pltpu.SemaphoreType.DMA((24,)),
            pltpu.SemaphoreType.DMA((4,)),
            pltpu.SemaphoreType.DMA((15,)),
            pltpu.SemaphoreType.DMA((15,)),
            pltpu.VMEM((tokens, h.shape[1] * 16), h.dtype),
            pltpu.VMEM((2, g.shape[0], ff), g.dtype),
            pltpu.SemaphoreType.DMA((3,)),
            pltpu.VMEM((4, tokens, ff), jnp.float32),
        ],
        compiler_params=pltpu.CompilerParams(has_side_effects=True,
                                             vmem_limit_bytes=48 * 1024 * 1024),
    )(h, g, u, dn, gp, upv)


def reduce_kernel(nmp, t_ref, o_ref, buf, send_sem, recv_sem, local_sem):
    d = lax.axis_index("dp")
    m = lax.axis_index("mp")
    w = o_ref.shape[2]
    mine = pl.ds(pl.multiple_of(m * w, w), w)
    local_copy = pltpu.make_async_copy(t_ref.at[:, :, mine], buf.at[0], local_sem.at[0])
    local_copy.start()
    copies = []
    for s in range(1, nmp):
        peer = lax.rem(m + s, nmp)
        theirs = pl.ds(pl.multiple_of(peer * w, w), w)
        copies.append(pltpu.make_async_remote_copy(
            src_ref=t_ref.at[:, :, theirs], dst_ref=buf.at[s], send_sem=send_sem.at[s],
            recv_sem=recv_sem.at[s], device_id=(d, peer), device_id_type=MESH))
    for c in copies:
        c.start()
    local_copy.wait()
    for c in copies:
        c.wait()
    rows = 32

    def body(i, carry):
        r = pl.ds(pl.multiple_of(i * rows, rows), rows)
        for k in range(o_ref.shape[0]):
            acc = buf[0, k, r, :].astype(jnp.float32)
            for s in range(1, nmp):
                acc = acc + buf[s, k, r, :].astype(jnp.float32)
            o_ref[k, r, :] = acc.astype(o_ref.dtype)
        return carry

    lax.fori_loop(0, o_ref.shape[1] // rows, body, 0)


def reduce_scatter(terms, nmp):
    n, t, width = terms.shape
    w = width // nmp
    return pl.pallas_call(
        functools.partial(reduce_kernel, nmp),
        out_shape=jax.ShapeDtypeStruct((n, t, w), jnp.bfloat16),
        in_specs=[pl.BlockSpec(memory_space=pl.ANY)],
        out_specs=pl.BlockSpec(memory_space=pltpu.VMEM),
        scratch_shapes=[
            pltpu.VMEM((nmp, n, t, w), jnp.bfloat16),
            pltpu.SemaphoreType.DMA((nmp,)),
            pltpu.SemaphoreType.DMA((nmp,)),
            pltpu.SemaphoreType.DMA((1,)),
        ],
        compiler_params=pltpu.CompilerParams(has_side_effects=True,
                                             vmem_limit_bytes=48 * 1024 * 1024),
    )(terms)


def hier_reduce_kernel(ta_ref, tb_ref, o_ref, own, r1, sb2, r2, s2, sb3, r3,
                       ls, ss1, rs1, ss2, rs2, ss3, rs3):
    d = lax.axis_index("dp")
    m = lax.axis_index("mp")
    c = m % 2
    z = (m // 2) % 4
    xh = m // 8
    w = o_ref.shape[2]
    rows = 32
    nchunk = o_ref.shape[1] // rows

    def blk(b, k):
        return (ta_ref, tb_ref)[k].at[:, pl.ds(pl.multiple_of(b * w, w), w)]

    def dev(mm):
        return (d, mm)

    locs = []
    st1 = []
    for j in range(16):
        bx, bz, k = j // 8, (j // 2) % 4, j % 2
        jj = bx * 4 + bz
        locs.append(pltpu.make_async_copy(blk(bx * 8 + bz * 2 + c, k), own.at[jj, k],
                                          ls.at[j]))
        st1.append(pltpu.make_async_remote_copy(
            src_ref=blk(bx * 8 + bz * 2 + (1 - c), k), dst_ref=r1.at[jj, k], send_sem=ss1.at[j],
            recv_sem=rs1.at[j], device_id=dev(m + 1 - 2 * c), device_id_type=MESH))
    for j in range(16):
        st1[j].start()
        locs[j].start()
    for j in range(16):
        locs[j].wait()
        st1[j].wait()

    st2 = []
    for s in range(1, 4):
        zt = (z + s) % 4

        def fill(i, carry, s=s, zt=zt):
            r = pl.ds(pl.multiple_of(i * rows, rows), rows)
            for bx in range(2):
                idx = bx * 4 + zt
                sb2[s - 1, bx, :, r, :] = (own[idx, :, r, :].astype(jnp.float32)
                                           + r1[idx, :, r, :].astype(jnp.float32)
                                           ).astype(sb2.dtype)
            return carry

        lax.fori_loop(0, nchunk, fill, 0)
        cp = pltpu.make_async_remote_copy(
            src_ref=sb2.at[s - 1], dst_ref=r2.at[s - 1], send_sem=ss2.at[s - 1],
            recv_sem=rs2.at[s - 1], device_id=dev(xh * 8 + zt * 2 + c), device_id_type=MESH)
        cp.start()
        st2.append(cp)
    for cp in st2:
        cp.wait()

    def sum2(i, carry):
        r = pl.ds(pl.multiple_of(i * rows, rows), rows)
        for bx in range(2):
            idx = bx * 4 + z
            acc = own[idx, :, r, :].astype(jnp.float32) + r1[idx, :, r, :].astype(jnp.float32)
            for k in range(3):
                acc = acc + r2[k, bx, :, r, :].astype(jnp.float32)
            s2[bx, :, r, :] = acc
        return carry

    lax.fori_loop(0, nchunk, sum2, 0)
    sb3[...] = s2[1 - xh].astype(sb3.dtype)
    cp3 = pltpu.make_async_remote_copy(
        src_ref=sb3, dst_ref=r3, send_sem=ss3.at[0], recv_sem=rs3.at[0],
        device_id=dev(m + 8 - 16 * xh), device_id_type=MESH)
    cp3.start()
    cp3.wait()
    o_ref[...] = (s2[xh] + r3[...].astype(jnp.float32)).astype(o_ref.dtype)


def hier_reduce_scatter(ta, tb):
    n = 2
    t, width = ta.shape
    w = width // 16
    bf = jnp.bfloat16
    dma = pltpu.SemaphoreType.DMA
    return pl.pallas_call(
        hier_reduce_kernel,
        out_shape=jax.ShapeDtypeStruct((n, t, w), bf),
        in_specs=[pl.BlockSpec(memory_space=pl.ANY)] * 2,
        out_specs=pl.BlockSpec(memory_space=pltpu.VMEM),
        scratch_shapes=[
            pltpu.VMEM((8, n, t, w), bf),
            pltpu.VMEM((8, n, t, w), bf),
            pltpu.VMEM((3, 2, n, t, w), bf),
            pltpu.VMEM((3, 2, n, t, w), bf),
            pltpu.VMEM((2, n, t, w), jnp.float32),
            pltpu.VMEM((n, t, w), bf),
            pltpu.VMEM((n, t, w), bf),
            dma((16,)), dma((16,)), dma((16,)), dma((3,)), dma((3,)), dma((1,)), dma((1,)),
        ],
        compiler_params=pltpu.CompilerParams(has_side_effects=True,
                                             vmem_limit_bytes=56 * 1024 * 1024),
    )(ta, tb)


def split_reduce_kernel(ta_ref, tb_ref, o_ref, own, r1, sa2, ra2, fa2, sa3, ra3,
                        sb2, rb2, fb2, sb3, rb3, ls, ss1, rs1, ssa2, rsa2, ssa3, rsa3,
                        ssb2, rsb2, ssb3, rsb3):
    d = lax.axis_index("dp")
    m = lax.axis_index("mp")
    c = m % 2
    z = (m // 2) % 4
    xh = m // 8
    w = o_ref.shape[2]
    half = o_ref.shape[1] // 2
    ra = pl.ds(0, half)
    rb = pl.ds(half, half)
    rows = 32
    nchunk = half // rows
    f32 = jnp.float32
    xpeer = m + 8 - 16 * xh

    def blk(b, k):
        return (ta_ref, tb_ref)[k].at[:, pl.ds(pl.multiple_of(b * w, w), w)]

    def rcopy(src, dst, ss, rs, mm):
        return pltpu.make_async_remote_copy(src_ref=src, dst_ref=dst, send_sem=ss, recv_sem=rs,
                                            device_id=(d, mm), device_id_type=MESH)

    locs = []
    st1 = []
    for j in range(16):
        bx, bz, k = j // 8, (j // 2) % 4, j % 2
        jj = bx * 4 + bz
        locs.append(pltpu.make_async_copy(blk(bx * 8 + bz * 2 + c, k), own.at[jj, k],
                                          ls.at[j]))
        st1.append(rcopy(blk(bx * 8 + bz * 2 + (1 - c), k), r1.at[jj, k], ss1.at[j], rs1.at[j],
                         m + 1 - 2 * c))
    for j in range(16):
        st1[j].start()
        locs[j].start()
    for j in range(16):
        locs[j].wait()
        st1[j].wait()

    def pair_sum(idx, r):
        return own[idx, :, r, :].astype(f32) + r1[idx, :, r, :].astype(f32)

    def fill_b2(i, carry):
        r = pl.ds(pl.multiple_of(half + i * rows, rows), rows)
        q = pl.ds(pl.multiple_of(i * rows, rows), rows)
        for bz in range(4):
            sb2[bz, :, q, :] = pair_sum((1 - xh) * 4 + bz, r).astype(sb2.dtype)
        return carry

    lax.fori_loop(0, nchunk, fill_b2, 0)
    cb2 = rcopy(sb2, rb2, ssb2.at[0], rsb2.at[0], xpeer)
    cb2.start()
    ca2 = []
    for s in range(1, 4):
        zt = (z + s) % 4

        def fill_a2(i, carry, s=s, zt=zt):
            q = pl.ds(pl.multiple_of(i * rows, rows), rows)
            for bx in range(2):
                sa2[s - 1, bx, :, q, :] = pair_sum(bx * 4 + zt, q).astype(sa2.dtype)
            return carry

        lax.fori_loop(0, nchunk, fill_a2, 0)
        cp = rcopy(sa2.at[s - 1], ra2.at[s - 1], ssa2.at[s - 1], rsa2.at[s - 1],
                   xh * 8 + zt * 2 + c)
        cp.start()
        ca2.append(cp)

    cb2.wait()

    def sum_b2(i, carry):
        r = pl.ds(pl.multiple_of(half + i * rows, rows), rows)
        q = pl.ds(pl.multiple_of(i * rows, rows), rows)
        for bz in range(4):
            fb2[bz, :, q, :] = pair_sum(xh * 4 + bz, r) + rb2[bz, :, q, :].astype(f32)
        return carry

    lax.fori_loop(0, nchunk, sum_b2, 0)
    cb3 = []
    for s in range(1, 4):
        zt = (z + s) % 4
        sb3[s - 1] = fb2[zt].astype(sb3.dtype)
        cp = rcopy(sb3.at[s - 1], rb3.at[s - 1], ssb3.at[s - 1], rsb3.at[s - 1],
                   xh * 8 + zt * 2 + c)
        cp.start()
        cb3.append(cp)

    for cp in ca2:
        cp.wait()

    def sum_a2(i, carry):
        q = pl.ds(pl.multiple_of(i * rows, rows), rows)
        for bx in range(2):
            acc = pair_sum(bx * 4 + z, q)
            for k in range(3):
                acc = acc + ra2[k, bx, :, q, :].astype(f32)
            fa2[bx, :, q, :] = acc
        return carry

    lax.fori_loop(0, nchunk, sum_a2, 0)
    sa3[...] = fa2[1 - xh].astype(sa3.dtype)
    ca3 = rcopy(sa3, ra3, ssa3.at[0], rsa3.at[0], xpeer)
    ca3.start()
    for cp in cb3:
        cp.wait()
    acc = fb2[z]
    for k in range(3):
        acc = acc + rb3[k].astype(f32)
    o_ref[:, rb, :] = acc.astype(o_ref.dtype)
    ca3.wait()
    o_ref[:, ra, :] = (fa2[xh] + ra3[...].astype(f32)).astype(o_ref.dtype)


def split_reduce_scatter(ta, tb):
    n = 2
    t, width = ta.shape
    w = width // 16
    h = t // 2
    bf = jnp.bfloat16
    f32 = jnp.float32
    dma = pltpu.SemaphoreType.DMA
    return pl.pallas_call(
        split_reduce_kernel,
        out_shape=jax.ShapeDtypeStruct((n, t, w), bf),
        in_specs=[pl.BlockSpec(memory_space=pl.ANY)] * 2,
        out_specs=pl.BlockSpec(memory_space=pltpu.VMEM),
        scratch_shapes=[
            pltpu.VMEM((8, n, t, w), bf),
            pltpu.VMEM((8, n, t, w), bf),
            pltpu.VMEM((3, 2, n, h, w), bf),
            pltpu.VMEM((3, 2, n, h, w), bf),
            pltpu.VMEM((2, n, h, w), f32),
            pltpu.VMEM((n, h, w), bf),
            pltpu.VMEM((n, h, w), bf),
            pltpu.VMEM((4, n, h, w), bf),
            pltpu.VMEM((4, n, h, w), bf),
            pltpu.VMEM((4, n, h, w), f32),
            pltpu.VMEM((3, n, h, w), bf),
            pltpu.VMEM((3, n, h, w), bf),
            dma((16,)), dma((16,)), dma((16,)),
            dma((3,)), dma((3,)), dma((1,)), dma((1,)),
            dma((1,)), dma((1,)), dma((3,)), dma((3,)),
        ],
        compiler_params=pltpu.CompilerParams(has_side_effects=True,
                                             vmem_limit_bytes=56 * 1024 * 1024),
    )(ta, tb)


def gate_up_kernel(h_ref, go_ref, gp_ref, uo_ref, upv_ref, io_ref, it_ref, acc, tbuf):
    k = pl.program_id(0)
    tile = 256
    chunk = 64
    f32 = jnp.float32

    @pl.when(k == 0)
    def _():
        acc[...] = jnp.zeros_like(acc)

    def mix(i, carry):
        r = pl.ds(pl.multiple_of(i * chunk, chunk), chunk)
        for j, (on_ref, pv_ref) in enumerate(((go_ref, gp_ref), (uo_ref, upv_ref))):
            on = on_ref[r, :].astype(f32)
            pv = pv_ref[r, :].astype(f32)
            tbuf[j, r, :] = (POLYAK * on + (1.0 - POLYAK) * pv).astype(tbuf.dtype)
        return carry

    lax.fori_loop(0, go_ref.shape[0] // chunk, mix, 0)

    def mm(i, carry):
        r = pl.ds(pl.multiple_of(i * tile, tile), tile)
        hs = h_ref[r, :]
        acc[0, r, :] += jnp.dot(hs, go_ref[...], preferred_element_type=f32)
        acc[1, r, :] += jnp.dot(hs, tbuf[0], preferred_element_type=f32)
        acc[2, r, :] += jnp.dot(hs, uo_ref[...], preferred_element_type=f32)
        acc[3, r, :] += jnp.dot(hs, tbuf[1], preferred_element_type=f32)
        return carry

    lax.fori_loop(0, h_ref.shape[0] // tile, mm, 0)

    @pl.when(k == pl.num_programs(0) - 1)
    def _():
        def finish(i, carry):
            r = pl.ds(pl.multiple_of(i * chunk, chunk), chunk)
            io_ref[r, :] = (jax.nn.silu(acc[0, r, :]) * acc[2, r, :]).astype(io_ref.dtype)
            it_ref[r, :] = (jax.nn.silu(acc[1, r, :]) * acc[3, r, :]).astype(it_ref.dtype)
            return carry

        lax.fori_loop(0, io_ref.shape[0] // chunk, finish, 0)


def gate_up(h_full, go, gp, uo, upv, kb):
    tokens, kdim = h_full.shape
    ff = go.shape[1]
    wspec = pl.BlockSpec((kb, ff), lambda k: (k, 0))
    ospec = pl.BlockSpec((tokens, ff), lambda k: (0, 0))
    flops = 8 * tokens * kdim * ff
    nbytes = 2 * (tokens * kdim + 4 * kdim * ff + 2 * tokens * ff)
    return pl.pallas_call(
        gate_up_kernel,
        grid=(kdim // kb,),
        out_shape=(jax.ShapeDtypeStruct((tokens, ff), jnp.bfloat16),) * 2,
        in_specs=[pl.BlockSpec((tokens, kb), lambda k: (0, k))] + [wspec] * 4,
        out_specs=[ospec, ospec],
        scratch_shapes=[pltpu.VMEM((4, tokens, ff), jnp.float32),
                        pltpu.VMEM((2, kb, ff), jnp.bfloat16)],
        compiler_params=pltpu.CompilerParams(vmem_limit_bytes=48 * 1024 * 1024),
        cost_estimate=pl.CostEstimate(flops=flops, bytes_accessed=nbytes,
                                      transcendentals=2 * tokens * ff),
    )(h_full, go, gp, uo, upv)


def gate_up_online_kernel(h_ref, go_ref, uo_ref, pg_ref, pu_ref, io_ref, it_ref, acc):
    k = pl.program_id(0)
    tile = 256
    chunk = 64
    f32 = jnp.float32

    @pl.when(k == 0)
    def _():
        acc[...] = jnp.zeros_like(acc)

    def mm(i, carry):
        r = pl.ds(pl.multiple_of(i * tile, tile), tile)
        hs = h_ref[r, :]
        acc[0, r, :] += jnp.dot(hs, go_ref[...], preferred_element_type=f32)
        acc[1, r, :] += jnp.dot(hs, uo_ref[...], preferred_element_type=f32)
        return carry

    lax.fori_loop(0, h_ref.shape[0] // tile, mm, 0)

    @pl.when(k == pl.num_programs(0) - 1)
    def _():
        def finish(i, carry):
            r = pl.ds(pl.multiple_of(i * chunk, chunk), chunk)
            g_o = acc[0, r, :]
            u_o = acc[1, r, :]
            g_t = POLYAK * g_o + (1.0 - POLYAK) * pg_ref[r, :]
            u_t = POLYAK * u_o + (1.0 - POLYAK) * pu_ref[r, :]
            io_ref[r, :] = (jax.nn.silu(g_o) * u_o).astype(io_ref.dtype)
            it_ref[r, :] = (jax.nn.silu(g_t) * u_t).astype(it_ref.dtype)
            return carry

        lax.fori_loop(0, io_ref.shape[0] // chunk, finish, 0)


def gate_up_online(h_full, go, uo, pg, pu, kb):
    tokens, kdim = h_full.shape
    ff = go.shape[1]
    wspec = pl.BlockSpec((kb, ff), lambda k: (k, 0))
    ospec = pl.BlockSpec((tokens, ff), lambda k: (0, 0))
    return pl.pallas_call(
        gate_up_online_kernel,
        grid=(kdim // kb,),
        out_shape=(jax.ShapeDtypeStruct((tokens, ff), jnp.bfloat16),) * 2,
        in_specs=[pl.BlockSpec((tokens, kb), lambda k: (0, k)), wspec, wspec, ospec, ospec],
        out_specs=[ospec, ospec],
        scratch_shapes=[pltpu.VMEM((2, tokens, ff), jnp.float32)],
        compiler_params=pltpu.CompilerParams(vmem_limit_bytes=48 * 1024 * 1024),
        cost_estimate=pl.CostEstimate(flops=4 * tokens * kdim * ff,
                                      bytes_accessed=2 * (tokens * kdim + 2 * kdim * ff),
                                      transcendentals=2 * tokens * ff),
    )(h_full, go, uo, pg, pu)


def down_kernel(io_ref, it_ref, do_ref, dp_ref, oo_ref, ot_ref):
    f32 = jnp.float32
    wt = (POLYAK * do_ref[...].astype(f32)
          + (1.0 - POLYAK) * dp_ref[...].astype(f32)).astype(do_ref.dtype)
    oo_ref[...] = jnp.dot(io_ref[...], do_ref[...], preferred_element_type=f32).astype(oo_ref.dtype)
    ot_ref[...] = jnp.dot(it_ref[...], wt, preferred_element_type=f32).astype(ot_ref.dtype)


def down_products(inner_o, inner_t, down_full, down_previous, cb):
    tokens, ff = inner_o.shape
    width = down_full.shape[1]
    ispec = pl.BlockSpec((tokens, ff), lambda j: (0, 0))
    wspec = pl.BlockSpec((ff, cb), lambda j: (0, j))
    ospec = pl.BlockSpec((tokens, cb), lambda j: (0, j))
    return pl.pallas_call(
        down_kernel,
        grid=(width // cb,),
        out_shape=(jax.ShapeDtypeStruct((tokens, width), jnp.bfloat16),) * 2,
        in_specs=[ispec, ispec, wspec, wspec],
        out_specs=[ospec, ospec],
        compiler_params=pltpu.CompilerParams(vmem_limit_bytes=32 * 1024 * 1024),
        cost_estimate=pl.CostEstimate(flops=4 * tokens * ff * width,
                                      bytes_accessed=2 * (2 * tokens * ff + 2 * ff * width
                                                          + 2 * tokens * width),
                                      transcendentals=0),
    )(inner_o, inner_t, down_full, down_previous)


def local(ndp, nmp, hidden_states, gate_online, up_online, down_online, gate_previous,
          up_previous, down_previous):
    kb = 2 * gate_online.shape[0]
    if ndp == 8 and nmp == 16:
        _, _, _, down_full, inner_o, inner_t = gather_relay(
            hidden_states, gate_online, up_online, down_online, gate_previous, up_previous, ndp)
    else:
        features_all = lax.all_gather(hidden_states, "mp", axis=1, tiled=True)
        gate_full, up_full, down_full = gather_weights_direct(gate_online, up_online,
                                                              down_online, ndp)
        inner_o, inner_t = gate_up(features_all, gate_full, gate_previous, up_full, up_previous,
                                   kb)
    if nmp == 16:
        online_part, target_part = down_products(inner_o, inner_t, down_full, down_previous,
                                                 2 * down_online.shape[1])
        result = split_reduce_scatter(online_part, target_part)
    else:
        target_down = blend(down_full, down_previous)
        online_part = jnp.dot(inner_o, down_full, preferred_element_type=jnp.float32)
        target_part = jnp.dot(inner_t, target_down, preferred_element_type=jnp.float32)
        terms = jnp.stack([online_part, target_part], axis=0).astype(jnp.bfloat16)
        result = reduce_scatter(terms, nmp)
    return (result[0], result[1])


def solution(mesh):
    ndp = mesh.shape["dp"]
    nmp = mesh.shape["mp"]
    in_specs = (
        P("dp", "mp"),
        P("dp", "mp"),
        P("dp", "mp"),
        P("mp", "dp"),
        P(None, "mp"),
        P(None, "mp"),
        P("mp", None),
    )
    out_specs = (P("dp", "mp"), P("dp", "mp"))
    return jax.shard_map(functools.partial(local, ndp, nmp), mesh=mesh, in_specs=in_specs,
                         out_specs=out_specs, check_vma=False)
```
